32 devices in a mesh: grp: 4 (over y, x), mem: 8 (over z, core).
Axes of the slice: x: 2, y: 2, z: 4, core: 2. Of those that a mesh axis runs over, the one named last changes fastest.
Arguments:
- tokens: bfloat16 [4096, 1024], P(('grp', 'mem')), may hold values from -6 to 6
- segment_ids: int32 [4096], P('grp'), may hold values from 0 to 127, never falling along the last dimension, each value on 1 to 512 neighbouring positions
- picks: int32 [4096, 4, 32], P(('grp', 'mem')), may hold values from 0 to 65535, as said below
- attn_gain: bfloat16 [1024], P('mem'), may hold values from 0.5 to 1.5
- qkv_weight: bfloat16 [1024, 3072], P('mem'), may hold values from -0.1875 to 0.1875
- attn_proj: bfloat16 [1024, 1024], P('mem'), may hold values from -1 to 1
- mem_gain: bfloat16 [1024], P('mem'), may hold values from 0.5 to 1.5
- query_weight: bfloat16 [1024, 4096], P('mem'), may hold values from -0.1875 to 0.1875
- half_keys: bfloat16 [2048, 512], P('mem'), may hold values from -0.29882812 to 0.29882812
- memory_values: bfloat16 [65536, 1024], P(('grp', 'mem')), may hold values from -6 to 6
- gate_weight: bfloat16 [1024, 1024], P('mem'), may hold values from -0.1875 to 0.1875
- out_weight: bfloat16 [1024, 1024], P('mem'), may hold values from -0.25 to 0.25
- out_cotangent: bfloat16 [4096, 1024], P(('grp', 'mem')), may hold values from -6 to 6
Outputs:
- block_out: bfloat16 [4096, 1024], P(('grp', 'mem'))
- tokens_grad: float32 [4096, 1024], P(('grp', 'mem'))
- attn_gain_grad: float32 [1024], P('mem')
- qkv_weight_grad: float32 [1024, 3072], P('mem')
- attn_proj_grad: float32 [1024, 1024], P('mem')
- mem_gain_grad: float32 [1024], P('mem')
- query_weight_grad: float32 [1024, 4096], P('mem')
- half_keys_grad: float32 [2048, 512], P('mem')
- memory_values_grad: float32 [65536, 1024], P(('grp', 'mem'))
- gate_weight_grad: float32 [1024, 1024], P('mem')
- out_weight_grad: float32 [1024, 1024], P('mem')
The draws below stay inside these ranges and needn't reach their ends.
Inputs may be any that keep to these rules, and one draw needn't show every extreme that they name: Of the picks of the 128 tokens that one device of grp+mem holds, at most 1024 fall in the 2048 value rows that any one device holds; one such block of rows receives exactly 1024 from every device.
All inputs are finite; a program needn't handle non-finite values.
Results may differ from the reference program's by a relative error of at most 0.02.
Values may be sent and summed in bfloat16 or wider, within the bound.
A program may use at most 384 MiB of HBM per device.

```python
import math
import jax
import jax.numpy as jnp
import numpy as np
from jax import lax

D = 1024
HEADS = 16
HDIM = 64
MHEADS = 4
NK = 256
HALF = 512
TOPK = 32
TOK_DEV = 128
VROWS = 65536
LEN = 1024
TOKENS = 4096
CAP = 1024
N_GRP = 4
DEVICES = 32


def draw_picks(key, part):
    per_device = TOK_DEV * MHEADS * TOPK
    slot_total = DEVICES * CAP
    local_rows = VROWS // DEVICES
    hot_owner = jax.random.randint(jax.random.fold_in(key, 1), (), 0, DEVICES)
    owner_bias = jax.random.randint(jax.random.fold_in(key, 2), (DEVICES,), 0, 1024)
    slot_owner = jnp.repeat(jnp.arange(DEVICES, dtype=jnp.int32), CAP, total_repeat_length=slot_total)
    slot_index = jnp.arange(slot_total, dtype=jnp.int32)

    def one_source(source):
        source_key = jax.random.fold_in(jax.random.fold_in(key, 3), source)
        noise_draw = jax.random.randint(jax.random.fold_in(source_key, 1), (slot_total,), 0, 1024)
        priority = noise_draw + owner_bias[slot_owner]
        forced = (slot_owner == hot_owner) | (slot_index == 0) | (slot_index == slot_total - CAP)
        priority = jnp.where(forced, 4096, priority)
        shuffle = jax.random.permutation(jax.random.fold_in(source_key, 2), slot_total)
        ranking = shuffle[jnp.argsort(-priority[shuffle], stable=True)]
        chosen = ranking[:per_device]
        local_row = jax.random.randint(jax.random.fold_in(source_key, 3), (per_device,), 0, local_rows)
        local_row = jnp.where(chosen == 0, 0, jnp.where(chosen == slot_total - CAP, local_rows - 1, local_row))
        values = slot_owner[chosen] * local_rows + local_row
        values = jax.random.permutation(jax.random.fold_in(source_key, 4), values)
        return values.reshape(TOK_DEV, MHEADS, TOPK)
    drawn = jax.vmap(one_source)(jnp.arange(DEVICES, dtype=jnp.int32))
    return drawn.reshape(TOKENS, MHEADS, TOPK).astype(jnp.int32)


def shard_levels(own_key, dims, split, least, top_value):
    level = 1.0
    for dim, parts in split:
        heights = jax.random.uniform(jax.random.fold_in(jax.random.fold_in(own_key, 6), dim), (parts,), jnp.float32, least / len(split), top_value / len(split))
        level = level * jnp.repeat(jnp.exp(heights), dims[dim] // parts).reshape((-1,) + (1,) * (len(dims) - 1 - dim))
    return level


def split_up(amount, total, most, lean):
    portions = [(1 << 20) // math.isqrt(standing ** lean) + 1 for standing in range(2, amount + 1)]
    spare, holding = total - most - (amount - 1), [1] * (amount - 1)
    while spare > 0:
        movable = [i for i in range(amount - 1) if holding[i] < most]
        whole, remaining = sum([portions[i] for i in movable]), spare
        for i in movable:
            more = min(most - holding[i], max(1, remaining * portions[i] // whole), spare)
            holding[i] = holding[i] + more
            spare = spare - more
    return np.array([most] + holding)


def ragged_sizes(stream_key, amount, total, reach, lean):
    if amount == 2:
        one = jax.random.randint(stream_key, (), max(1, total - reach), min(reach, total - 1) + 1)
        return jnp.stack([one, total - one])
    sizes = jnp.asarray(split_up(amount, total, reach, lean), jnp.int32)
    twos = (amount - 1) // 2
    source_of, sink = sizes[1:1 + 2 * twos:2], sizes[2:2 + 2 * twos:2]
    room = jnp.minimum(source_of - 1, reach - sink)
    passed = jax.random.randint(jax.random.fold_in(stream_key, 1), (twos,), 0, 1 << 20) % (room + 1)
    sizes = sizes.at[1:1 + 2 * twos:2].set(source_of - passed).at[2:2 + 2 * twos:2].set(sink + passed)
    return sizes[jax.random.permutation(jax.random.fold_in(stream_key, 2), amount)]


def gaussian(rng, extent, spread, limit, shards=(), kind=jnp.bfloat16):
    factor_of = shard_levels(rng, extent, shards, -0.22, 0.18) if shards else 1.0
    entries = jax.random.normal(rng, extent, jnp.float32) * spread * factor_of
    return jnp.minimum(jnp.maximum(entries, -limit), limit).astype(kind)


def setup_inputs(seed: int = 0) -> dict:
    key_list = jax.random.split(jax.random.key(seed), 14)
    return {
        "tokens": gaussian(key_list[0], (TOKENS, D), 1.0, 6.0, ((0, 32),)),
        "segment_ids": jnp.searchsorted(jnp.cumsum(ragged_sizes(key_list[1], TOKENS // 32, TOKENS, LEN // 2, 2)), jnp.arange(TOKENS), side="right").astype(jnp.int32),
        "picks": draw_picks(jax.random.fold_in(key_list[13], 71), 0),
        "attn_gain": jnp.clip(1.0 + 0.1 * jax.random.normal(key_list[3], (D,), jnp.float32), 0.5, 1.5).astype(jnp.bfloat16),
        "qkv_weight": gaussian(key_list[4], (D, 3 * D), D ** -0.5, 0.1875, ((0, 8),)),
        "attn_proj": gaussian(key_list[5], (D, D), (D // 32) ** -0.5, 1.0, ((0, 8),)),
        "mem_gain": jnp.clip(1.0 + 0.1 * jax.random.normal(key_list[6], (D,), jnp.float32), 0.5, 1.5).astype(jnp.bfloat16),
        "query_weight": gaussian(key_list[7], (D, MHEADS * 2 * HALF), D ** -0.5, 0.1875, ((0, 8),)),
        "half_keys": gaussian(key_list[8], (MHEADS * 2 * NK, HALF), 0.05, 0.29882812, ((0, 8),)),
        "memory_values": gaussian(key_list[9], (VROWS, D), 1.0, 6.0, ((0, 32),)),
        "gate_weight": gaussian(key_list[10], (D, D), D ** -0.5, 0.1875, ((0, 8),)),
        "out_weight": gaussian(key_list[11], (D, D), (D // 2) ** -0.5, 0.25, ((0, 8),)),
        "out_cotangent": gaussian(key_list[12], (TOKENS, D), 1.0, 6.0, ((0, 32),)),
    }


@jax.custom_vjp
def low(v):
    return lax.optimization_barrier(v.astype(jnp.bfloat16)).astype(jnp.float32)

@jax.custom_vjp
def low_back(v):
    return v

def low_keep(v):
    return (low(v), None)

def low_pass(kept, grad):
    return (grad,)

def back_keep(v):
    return (v, None)

def back_low(kept, grad):
    return (low(grad),)
low.defvjp(low_keep, low_pass)
low_back.defvjp(back_keep, back_low)

def round_both(values):
    return low_back(low(values))

def matmul(left, right):
    return jnp.dot(left, right, precision=lax.Precision.HIGHEST, preferred_element_type=jnp.float32)

def rms_norm(values, gain):
    return values * lax.rsqrt(lax.optimization_barrier(jnp.mean(values * values, axis=-1, keepdims=True)) + 1e-05) * gain

def attend_sequence(queries, keys_seq, values_seq, segments):
    block_len = min(512, LEN)
    block_count = LEN // block_len
    key_heads = keys_seq.reshape(LEN, HEADS, HDIM)
    value_heads = values_seq.reshape(LEN, HEADS, HDIM)
    key_pos = jnp.arange(LEN, dtype=jnp.int32)

    def one_block(pieces):
        query_block, positions, query_seg = pieces
        scores = jnp.einsum('qhd,khd->hqk', query_block, key_heads, precision=lax.Precision.HIGHEST, preferred_element_type=jnp.float32) * 0.125
        scores = low_back(scores)
        allowed = (key_pos[None, :] <= positions[:, None]) & (segments[None, :] == query_seg[:, None])
        scores = jnp.where(allowed[None], scores, -1e+30)
        probs = jax.nn.softmax(scores, axis=-1)
        output = jnp.einsum('hqk,khd->qhd', low(probs), value_heads, precision=lax.Precision.HIGHEST, preferred_element_type=jnp.float32)
        return output.reshape(block_len, D)
    outputs = lax.map(jax.checkpoint(one_block), (queries.reshape(block_count, block_len, HEADS, HDIM), key_pos.reshape(block_count, block_len), segments.reshape(block_count, block_len)))
    return outputs.reshape(LEN, D)

def memory_block(query_block, pick_block, key_table, value_table):
    block_len = query_block.shape[0]
    half_query = query_block.reshape(block_len, MHEADS, 2, HALF)
    table = key_table.reshape(MHEADS, 2, NK, HALF)
    half_scores = jnp.einsum('thcf,hcnf->thcn', half_query, table, precision=lax.Precision.HIGHEST, preferred_element_type=jnp.float32)
    first_index = pick_block // NK
    second_index = pick_block % NK
    pick_scores = jnp.take_along_axis(half_scores[:, :, 0], first_index, axis=2) + jnp.take_along_axis(half_scores[:, :, 1], second_index, axis=2)
    pick_scores = low_back(pick_scores)
    weights = jax.nn.softmax(pick_scores, axis=-1)
    picked_rows = low_back(value_table[pick_block])
    output = jnp.einsum('thj,thjd->td', low(weights), picked_rows, precision=lax.Precision.HIGHEST, preferred_element_type=jnp.float32)
    return low_back(output)

def reference(tokens, segment_ids, picks, attn_gain, qkv_weight, attn_proj, mem_gain, query_weight, half_keys, memory_values, gate_weight, out_weight, out_cotangent):

    def forward(inputs, gain_one, qkv_full, proj_full, gain_two, query_full, key_table, value_table, gate_full, output_full):
        first = low(rms_norm(inputs, gain_one))
        projected = matmul(first, qkv_full)
        queries = round_both(projected[:, :D])
        keys_all = round_both(projected[:, D:2 * D])
        values_all = round_both(projected[:, 2 * D:])
        attended = lax.map(lambda pieces: attend_sequence(*pieces), (queries.reshape(N_GRP, LEN, D), keys_all.reshape(N_GRP, LEN, D), values_all.reshape(N_GRP, LEN, D), segment_ids.reshape(N_GRP, LEN)))
        attended = round_both(attended.reshape(TOKENS, D))
        residual = inputs + low_back(matmul(attended, proj_full))
        second = low(rms_norm(residual, gain_two))
        mem_query = round_both(matmul(second, query_full))
        mem_block = min(256, TOKENS)
        memory_out = lax.map(jax.checkpoint(lambda pieces: memory_block(pieces[0], pieces[1], key_table, value_table)), (mem_query.reshape(TOKENS // mem_block, mem_block, MHEADS * 2 * HALF), picks.reshape(TOKENS // mem_block, mem_block, MHEADS, TOPK)))
        memory_out = memory_out.reshape(TOKENS, D)
        gate_pre = low_back(matmul(second, gate_full))
        mixed = low(memory_out * jax.nn.silu(gate_pre))
        return residual + matmul(mixed, output_full)
    params = tuple((item.astype(jnp.float32) for item in (tokens, attn_gain, qkv_weight, attn_proj, mem_gain, query_weight, half_keys, memory_values, gate_weight, out_weight)))
    result, backward = jax.vjp(forward, *params)
    grads = backward(out_cotangent.astype(jnp.float32))
    return (result.astype(jnp.bfloat16), grads[0], grads[1], grads[2], grads[3], grads[4], grads[5], grads[6], grads[7], grads[8], grads[9])
```

```python
import functools

import jax
import jax.numpy as jnp
from jax import lax
from jax.experimental import pallas as pl
from jax.experimental.pallas import tpu as pltpu
from jax.sharding import PartitionSpec as P

HEADS = 16
HDIM = 64
MHEADS = 4
NK = 256
HALF = 512
TOPK = 32
EPS = 1e-05
LANES = 128
ALL = ("grp", "mem")
BF = jnp.bfloat16
F32 = jnp.float32
NEG = -1e30


def dot(left, right, dims=((1,), (0,))):
    return lax.dot_general(left, right, (dims, ((), ())), preferred_element_type=F32)


NT = ((1,), (1,))
TN = ((0,), (0,))


def iota(shape, dim):
    return lax.broadcasted_iota(jnp.int32, shape, dim)


def lane_halves(rows):
    first = iota((rows, LANES), 1) < HDIM
    return first


def half_masks():
    lane = iota((1, LANES), 1)
    return ((lane < HDIM).astype(BF), (lane >= HDIM).astype(BF))


def attn_fwd_kernel(rows, win, pos_ref, q_ref, k_ref, v_ref, qseg_ref, kseg_ref, out_ref, lse_ref):
    pair = pl.program_id(0)
    row0 = pos_ref[0] * rows
    start = pl.multiple_of(jnp.maximum(row0 + rows - win, 0), LANES)
    keys = k_ref[pl.ds(start, win), :]
    values = v_ref[pl.ds(start, win), :]
    key_pos = start + iota((rows, win), 1)
    query_pos = row0 + iota((rows, win), 0)
    allowed = (key_pos <= query_pos) & (kseg_ref[:, pl.ds(start, win)] == qseg_ref[...])
    lane = iota((rows, LANES), 1)
    masks = half_masks()
    outs = []
    lse = jnp.where(pair == 0, jnp.zeros((rows, LANES), F32), lse_ref[...])
    for half in range(2):
        scores = dot(q_ref[...] * masks[half], keys, NT) * 0.125
        scores = jnp.where(allowed, scores, NEG)
        top = jnp.max(scores, axis=1, keepdims=True)
        weights = jnp.exp(scores - top)
        total = jnp.sum(weights, axis=1, keepdims=True)
        probs = weights * (1.0 / total)
        outs.append(dot(probs.astype(BF), values))
        lse = jnp.where(lane == pair * 2 + half, top + jnp.log(total), lse)
    out_ref[...] = jnp.where(lane < HDIM, outs[0], outs[1])
    lse_ref[...] = lse


def attn_fwd(pos, qkv, seg_row, seg_col, rows):
    group_len, width = qkv.shape[0], qkv.shape[1] // 3
    pairs = width // LANES
    win = min(group_len, group_len // 2 + rows)
    return pl.pallas_call(
        functools.partial(attn_fwd_kernel, rows, win),
        grid_spec=pltpu.PrefetchScalarGridSpec(
            num_scalar_prefetch=1,
            grid=(pairs,),
            in_specs=[
                pl.BlockSpec((rows, LANES), lambda h, p: (p[0], h)),
                pl.BlockSpec((group_len, LANES), lambda h, p: (0, pairs + h)),
                pl.BlockSpec((group_len, LANES), lambda h, p: (0, 2 * pairs + h)),
                pl.BlockSpec((rows, 1), lambda h, p: (p[0], 0)),
                pl.BlockSpec((1, group_len), lambda h, p: (0, 0)),
            ],
            out_specs=[
                pl.BlockSpec((rows, LANES), lambda h, p: (0, h)),
                pl.BlockSpec((rows, LANES), lambda h, p: (0, 0)),
            ],
        ),
        out_shape=[
            jax.ShapeDtypeStruct((rows, width), F32),
            jax.ShapeDtypeStruct((rows, LANES), F32),
        ],
        cost_estimate=pl.CostEstimate(
            flops=4 * rows * win * width,
            bytes_accessed=group_len * width * 4,
            transcendentals=rows * win * HEADS,
        ),
        name="attn_fwd",
    )(pos, qkv, qkv, qkv, seg_col, seg_row)


def attn_bwd_kernel(
    rows, win, pairs, pos_ref, q_ref, k_ref, v_ref, da_ref, stat_ref, segc_ref, segr_ref, out_ref
):
    pair = pl.program_id(0)
    group_len = k_ref.shape[0]
    row0 = pl.multiple_of(pos_ref[0] * rows, LANES)
    start = pl.multiple_of(jnp.maximum(row0 + rows - win, 0), LANES)
    qstart = pl.multiple_of(jnp.minimum(row0, group_len - win), LANES)
    own, back, ahead = pl.ds(row0, rows), pl.ds(start, win), pl.ds(qstart, win)
    masks = half_masks()
    lane = iota((rows, LANES), 1)

    def stat(where, index, count):
        table = stat_ref[where, :]
        return jnp.sum(
            jnp.where(iota((count, table.shape[1]), 1) == index, table, 0.0),
            axis=1,
            keepdims=True,
        )

    allowed = (start + iota((rows, win), 1) <= row0 + iota((rows, win), 0)) & (
        segr_ref[:, back] == segc_ref[own, :]
    )
    allowed_two = (row0 + iota((win, rows), 1) <= qstart + iota((win, rows), 0)) & (
        segr_ref[:, own] == segc_ref[ahead, :]
    )
    dqs, dks, dvs = [], [], []
    for half in range(2):
        head = pair * 2 + half
        lse, delta = stat(own, head, rows), stat(own, HEADS + head, rows)
        keys = k_ref[back, :]
        scores = dot(q_ref[own, :] * masks[half], keys, NT) * 0.125
        probs = jnp.exp(jnp.where(allowed, scores - lse, NEG))
        dprobs = dot(da_ref[own, :] * masks[half], v_ref[back, :], NT)
        grads = (probs * (dprobs - delta)).astype(BF)
        dqs.append(dot(grads, keys))
        lse, delta = stat(ahead, head, win), stat(ahead, HEADS + head, win)
        queries, douts = q_ref[ahead, :], da_ref[ahead, :]
        scores = dot(queries * masks[half], k_ref[own, :], NT) * 0.125
        probs = jnp.exp(jnp.where(allowed_two, scores - lse, NEG))
        dprobs = dot(douts * masks[half], v_ref[own, :], NT)
        grads = (probs * (dprobs - delta)).astype(BF)
        dks.append(dot(grads, queries, TN))
        dvs.append(dot(probs.astype(BF), douts, TN))
    width = pairs * LANES
    for i, (parts, scale) in enumerate(((dqs, 0.125), (dks, 0.125), (dvs, 1.0))):
        column = pl.multiple_of(i * width + pair * LANES, LANES)
        out_ref[:, pl.ds(column, LANES)] = (
            jnp.where(lane < HDIM, parts[0], parts[1]) * scale
        ).astype(BF)


def attn_bwd(pos, qkv, douts, stats, seg_row, seg_col, rows):
    group_len, width = douts.shape
    pairs = width // LANES
    win = min(group_len, group_len // 2 + rows)
    return pl.pallas_call(
        functools.partial(attn_bwd_kernel, rows, win, pairs),
        grid_spec=pltpu.PrefetchScalarGridSpec(
            num_scalar_prefetch=1,
            grid=(pairs,),
            in_specs=[
                pl.BlockSpec((group_len, LANES), lambda h, p: (0, h)),
                pl.BlockSpec((group_len, LANES), lambda h, p: (0, pairs + h)),
                pl.BlockSpec((group_len, LANES), lambda h, p: (0, 2 * pairs + h)),
                pl.BlockSpec((group_len, LANES), lambda h, p: (0, h)),
                pl.BlockSpec(stats.shape, lambda h, p: (0, 0)),
                pl.BlockSpec((group_len, 1), lambda h, p: (0, 0)),
                pl.BlockSpec((1, group_len), lambda h, p: (0, 0)),
            ],
            out_specs=pl.BlockSpec((rows, 3 * width), lambda h, p: (0, 0)),
        ),
        out_shape=jax.ShapeDtypeStruct((rows, 3 * width), BF),
        cost_estimate=pl.CostEstimate(
            flops=14 * rows * win * width,
            bytes_accessed=group_len * width * 8,
            transcendentals=2 * rows * win * HEADS,
        ),
        name="attn_bwd",
    )(pos, qkv, qkv, qkv, douts, stats, seg_col, seg_row)


def by_head(lane, reduce, fill, values):
    spread = jnp.zeros_like(values)
    for c in range(MHEADS):
        inside = lane // TOPK == c
        spread = jnp.where(
            inside, reduce(jnp.where(inside, values, fill), axis=1, keepdims=True), spread
        )
    return spread


def pick_fwd_kernel(scores_ref, picks_ref, weight_ref, low_ref):
    rows = picks_ref.shape[0]
    lane = iota((rows, LANES), 1)
    picks = picks_ref[...]
    index = (picks // NK, picks % NK)
    total = jnp.zeros((rows, LANES), F32)
    for c in range(MHEADS):
        both = jnp.zeros((rows, LANES), F32)
        for e in range(2):
            base = (c * 2 + e) * NK
            for part in range(NK // LANES):
                table = scores_ref[:, base + part * LANES : base + (part + 1) * LANES]
                found = jnp.take_along_axis(table, index[e] % LANES, axis=1)
                both = both + jnp.where(index[e] // LANES == part, found, 0.0)
        total = jnp.where(lane // TOPK == c, both, total)
    top = by_head(lane, jnp.max, NEG, total)
    weights = jnp.exp(total - top)
    weights = weights / by_head(lane, jnp.sum, 0.0, weights)
    weight_ref[...] = weights
    low_ref[...] = weights.astype(BF)


def pick_fwd(half_scores, picks):
    rows = picks.shape[0]
    return pl.pallas_call(
        pick_fwd_kernel,
        out_shape=[
            jax.ShapeDtypeStruct((rows, LANES), F32),
            jax.ShapeDtypeStruct((rows, LANES), BF),
        ],
        name="pick_fwd",
    )(half_scores, picks)


def pick_bwd_kernel(weight_ref, grad_ref, picks_ref, out_ref):
    rows = picks_ref.shape[0]
    lane = iota((rows, LANES), 1)
    weights, grads, picks = weight_ref[...], grad_ref[...], picks_ref[...]
    score = (weights * (grads - by_head(lane, jnp.sum, 0.0, weights * grads))).astype(BF)
    score = score.astype(F32)
    index = (picks // NK, picks % NK)
    key = iota((rows, NK), 1)
    for c in range(MHEADS):
        totals = [jnp.zeros((rows, NK), F32) for _ in range(2)]
        for j in range(TOPK):
            column = slice(c * TOPK + j, c * TOPK + j + 1)
            for e in range(2):
                totals[e] = totals[e] + jnp.where(
                    key == index[e][:, column], score[:, column], 0.0
                )
        for e in range(2):
            base = (c * 2 + e) * NK
            out_ref[:, base : base + NK] = totals[e].astype(BF)


def pick_bwd(weights, grads, picks):
    rows = picks.shape[0]
    block = 32
    spec = pl.BlockSpec((block, LANES), lambda i: (i, 0))
    return pl.pallas_call(
        pick_bwd_kernel,
        grid=(rows // block,),
        in_specs=[spec, spec, spec],
        out_specs=pl.BlockSpec((block, MHEADS * 2 * NK), lambda i: (i, 0)),
        out_shape=jax.ShapeDtypeStruct((rows, MHEADS * 2 * NK), BF),
        name="pick_bwd",
    )(weights, grads, picks)


def owner_kernel(
    his, flat_bits, local_rows, keys_ref, sent_ref, values_ref, part_ref, spread_ref
):
    rows = part_ref.shape[0]
    width = values_ref.shape[1]
    slots = keys_ref.shape[-1]
    low_rows = local_rows // his
    key = keys_ref[0]
    flat = key & ((1 << flat_bits) - 1)
    dummy = ((key >> flat_bits) & 1) == 1
    row = (key >> (flat_bits + 1)) % local_rows
    token = flat // LANES
    pick = flat % LANES
    token = jnp.where(dummy, -1, token)
    block = jnp.where(dummy, -1, (row // low_rows) * rows + token)
    low_row = row % low_rows
    grad = sent_ref[:, :width]
    weights = sent_ref[:, width:]
    is_token = iota((rows, slots), 0) == token
    is_pick = iota((LANES, slots), 0) == pick
    token_hot = is_token.astype(F32).astype(BF)
    found = dot(weights, token_hot, TN)
    weight = jnp.sum(jnp.where(is_pick, found, 0.0), axis=0, keepdims=True)
    is_block = iota((his * rows, slots), 0) == block
    is_low = iota((low_rows, slots), 0) == low_row
    low_hot = is_low.astype(F32).astype(BF)
    spread = dot(jnp.where(is_block, weight, 0.0).astype(BF), low_hot, NT).astype(BF)
    total = jnp.zeros((rows, width), F32)
    products = []
    for h in range(his):
        table = values_ref[h * low_rows : (h + 1) * low_rows, :]
        piece = spread[h * rows : (h + 1) * rows, :]
        spread_ref[h] = piece
        total = total + dot(piece, table)
        products.append(dot(grad, table, NT).astype(BF))
    picked = dot(jnp.concatenate(products, axis=0), is_block.astype(F32).astype(BF), TN)
    picked = jnp.sum(jnp.where(is_low, picked, 0.0), axis=0, keepdims=True)
    part_ref[:, :width] = total.astype(BF)
    part_ref[:, width:] = dot(
        jnp.where(is_token, picked, 0.0).astype(BF), is_pick.astype(F32).astype(BF), NT
    ).astype(BF)


def owner_call(keys, sent, values, flat_bits):
    owners, slots = keys.shape
    rows = sent.shape[0] // owners
    local_rows, width = values.shape
    his = 4
    low_rows = local_rows // his
    return pl.pallas_call(
        functools.partial(owner_kernel, his, flat_bits, local_rows),
        grid=(owners,),
        in_specs=[
            pl.BlockSpec((1, 1, slots), lambda s: (s, 0, 0)),
            pl.BlockSpec((rows, width + LANES), lambda s: (s, 0)),
            pl.BlockSpec((local_rows, width), lambda s: (0, 0)),
        ],
        out_specs=[
            pl.BlockSpec((rows, width + LANES), lambda s: (s, 0)),
            pl.BlockSpec((his, rows, low_rows), lambda s: (0, s, 0)),
        ],
        out_shape=[
            jax.ShapeDtypeStruct((owners * rows, width + LANES), BF),
            jax.ShapeDtypeStruct((his, owners * rows, low_rows), BF),
        ],
        compiler_params=pltpu.CompilerParams(vmem_limit_bytes=48 * 1024 * 1024),
        cost_estimate=pl.CostEstimate(
            flops=2 * owners * rows * local_rows * (2 * slots + 2 * width),
            bytes_accessed=owners * rows * (2 * width + local_rows) * 2,
            transcendentals=0,
        ),
        name="owner",
    )(keys.reshape(owners, 1, slots), sent, values)


def route(picks, owners, local_rows, capacity, flat_bits):
    total = picks.size
    rows_of = picks.reshape(total)
    flat = jnp.arange(total, dtype=jnp.int32)
    each = jnp.arange(owners, dtype=jnp.int32)
    counts = jnp.sum((rows_of[:, None] // local_rows == each[None, :]).astype(jnp.int32), axis=0)
    ends = jnp.cumsum(capacity - counts)
    spares = owners * capacity - total
    spare_owner = jnp.sum(
        (jnp.arange(spares, dtype=jnp.int32)[:, None] >= ends[None, :]).astype(jnp.int32), axis=1
    )
    real = (rows_of << (flat_bits + 1)) + flat
    spare = ((spare_owner * local_rows + local_rows - 1) << (flat_bits + 1)) + (1 << flat_bits)
    keys = lax.sort(jnp.concatenate([real, spare]))
    return keys.reshape(owners, capacity)


def rms_scale(values):
    return lax.rsqrt(jnp.mean(values * values, axis=-1, keepdims=True) + EPS)


def rms_back(values, scale, gain, grad):
    scaled = grad * gain
    inner = jnp.mean(values * scaled, axis=-1, keepdims=True)
    gain_grad = jnp.sum(grad * values * scale, axis=0)
    return scale * scaled - values * (scale * scale * scale * inner), gain_grad


def per_device(
    tokens,
    segment_ids,
    picks,
    attn_gain,
    qkv_weight,
    attn_proj,
    mem_gain,
    query_weight,
    half_keys,
    memory_values,
    gate_weight,
    out_weight,
    out_cotangent,
):
    rows, width = tokens.shape
    owners = lax.axis_size("grp") * lax.axis_size("mem")
    local_rows = memory_values.shape[0]
    total_picks = rows * MHEADS * TOPK
    flat_bits = (total_picks - 1).bit_length()
    capacity = 2 * total_picks // owners
    group_len = segment_ids.shape[0]
    position = lax.axis_index("mem").astype(jnp.int32)
    pos = position.reshape(1)

    def gather(x, axes="mem"):
        return lax.all_gather(x, axes, axis=0, tiled=True)

    gains = lax.all_gather(jnp.stack([attn_gain, mem_gain]), "mem", axis=1, tiled=True)
    gains = gains.astype(F32)
    gain_one, gain_two = gains[0:1], gains[1:2]
    tokens_all = gather(tokens)
    qkv_full = gather(qkv_weight)
    proj_full = gather(attn_proj)
    query_full = gather(query_weight)
    keys_full = gather(half_keys)
    gate_full = gather(gate_weight)
    output_full = gather(out_weight)

    requests = route(picks, owners, local_rows, capacity, flat_bits)
    arrived = lax.all_to_all(requests, ALL, split_axis=0, concat_axis=0, tiled=True)

    inputs_all = tokens_all.astype(F32)
    first_all = (inputs_all * rms_scale(inputs_all) * gain_one).astype(BF)
    qkv_all = dot(first_all, qkv_full).astype(BF)
    seg_row, seg_col = segment_ids.reshape(1, group_len), segment_ids.reshape(group_len, 1)
    attn_sum, lse = attn_fwd(pos, qkv_all, seg_row, seg_col, rows)
    attended = attn_sum.astype(BF)
    inputs = tokens.astype(F32)
    residual = inputs + dot(attended, proj_full)
    scale_two = rms_scale(residual)
    second = (residual * scale_two * gain_two).astype(BF)
    mem_query = dot(second, query_full).astype(BF)
    gate_pre = dot(second, gate_full)
    mixed_grad = dot(out_cotangent, output_full, NT)
    sig = jax.nn.sigmoid(gate_pre)
    gate_act = gate_pre * sig
    memory_grad = (mixed_grad * gate_act).astype(BF)
    key_table = keys_full.reshape(MHEADS * 2, NK, HALF)
    half_scores = jnp.einsum(
        "tcf,cnf->tcn",
        mem_query.reshape(rows, MHEADS * 2, HALF),
        key_table,
        preferred_element_type=F32,
    ).reshape(rows, MHEADS * 2 * NK)
    flat_picks = picks.reshape(rows, MHEADS * TOPK)
    pick_weights, weights_low = pick_fwd(half_scores, flat_picks)

    sent = gather(jnp.concatenate([memory_grad, weights_low], axis=1), ALL)
    part, spread = owner_call(arrived, sent, memory_values, flat_bits)
    back = lax.psum_scatter(part, "grp", scatter_dimension=0, tiled=True)
    back = lax.psum_scatter(back, "mem", scatter_dimension=0, tiled=True)
    values_grad = jnp.einsum(
        "hkl,kd->hld", spread, sent[:, :width], preferred_element_type=F32
    ).reshape(local_rows, width)

    memory_out = back[:, :width].astype(F32)
    weight_grad = back[:, width:].astype(F32)
    mixed = (memory_out * gate_act).astype(BF)
    block_out = (residual + dot(mixed, output_full)).astype(BF)
    out_w_grad = dot(mixed, out_cotangent, TN)
    gate_grad = (mixed_grad * memory_out * (sig * (1.0 + gate_pre * (1.0 - sig)))).astype(BF)
    gate_w_grad = dot(second, gate_grad, TN)
    half_grad = pick_bwd(pick_weights, weight_grad, flat_picks)
    half_cube = half_grad.reshape(rows, MHEADS * 2, NK)
    query_grad = (
        jnp.einsum("tcn,cnf->tcf", half_cube, key_table, preferred_element_type=F32)
        .astype(BF)
        .reshape(rows, MHEADS * 2 * HALF)
    )
    keys_grad = jnp.einsum(
        "tcn,tcf->cnf",
        half_cube,
        mem_query.reshape(rows, MHEADS * 2, HALF),
        preferred_element_type=F32,
    ).reshape(MHEADS * 2 * NK, HALF)
    query_w_grad = dot(second, query_grad, TN)
    second_grad = dot(gate_grad, gate_full, NT) + dot(query_grad, query_full, NT)
    resid_from_norm, gain_two_grad = rms_back(residual, scale_two, gain_two, second_grad)
    resid_grad = out_cotangent.astype(F32) + resid_from_norm
    resid_low = resid_grad.astype(BF)
    proj_grad = dot(attended, resid_low, TN)
    attn_grad = dot(resid_low, proj_full, NT).astype(BF)
    delta = jnp.sum(
        (attn_grad.astype(F32) * attn_sum).reshape(rows, HEADS, HDIM), axis=-1
    )
    stats = jnp.concatenate([lse[:, :HEADS], delta], axis=1)
    stats_high = lax.reduce_precision(stats, 8, 7)
    stats_low = stats - stats_high
    shared = gather(
        jnp.concatenate(
            [
                resid_low,
                stats_high.astype(BF),
                stats_low.astype(BF),
                jnp.zeros((rows, LANES - 4 * HEADS), BF),
            ],
            axis=1,
        )
    )
    stats_all = shared[:, width : width + 2 * HEADS].astype(F32) + shared[
        :, width + 2 * HEADS : width + 4 * HEADS
    ].astype(F32)
    attn_grad_all = dot(shared[:, :width], proj_full, NT).astype(BF)
    qkv_rows = attn_bwd(pos, qkv_all, attn_grad_all, stats_all, seg_row, seg_col, rows)
    scale_one = rms_scale(inputs)
    first_low = (inputs * scale_one * gain_one).astype(BF)
    qkv_w_grad = dot(first_low, qkv_rows, TN)
    first_grad = dot(qkv_rows, qkv_full, NT)
    input_from_norm, gain_one_grad = rms_back(inputs, scale_one, gain_one, first_grad)
    tokens_grad = resid_grad + input_from_norm

    def scatter(x):
        return lax.psum_scatter(x.astype(BF), "mem", scatter_dimension=0, tiled=True)

    shares = [
        scatter(x) for x in (out_w_grad, gate_w_grad, keys_grad, query_w_grad, proj_grad, qkv_w_grad)
    ]
    shares = lax.psum(tuple(shares), "grp")
    gain_sums = lax.psum(jnp.stack([gain_one_grad, gain_two_grad]), ALL)
    gain_sums = lax.dynamic_slice_in_dim(
        gain_sums, position * attn_gain.shape[0], attn_gain.shape[0], axis=1
    )
    out_share, gate_share, keys_share, query_share, proj_share, qkv_share = (
        x.astype(F32) for x in shares
    )
    return (
        block_out,
        tokens_grad,
        gain_sums[0],
        qkv_share,
        proj_share,
        gain_sums[1],
        query_share,
        keys_share,
        values_grad,
        gate_share,
        out_share,
    )


def solution(mesh):
    placed = (
        P(ALL, None),
        P("grp"),
        P(ALL, None, None),
        P("mem"),
        P("mem", None),
        P("mem", None),
        P("mem"),
        P("mem", None),
        P("mem", None),
        P(ALL, None),
        P("mem", None),
        P("mem", None),
        P(ALL, None),
    )
    return jax.shard_map(
        per_device,
        mesh=mesh,
        in_specs=placed,
        out_specs=(
            P(ALL, None),
            P(ALL, None),
            P("mem"),
            P("mem", None),
            P("mem", None),
            P("mem"),
            P("mem", None),
            P("mem", None),
            P(ALL, None),
            P("mem", None),
            P("mem", None),
        ),
        check_vma=False,
    )
```

```python
import functools

import jax
import jax.numpy as jnp
from jax import lax
from jax.experimental import pallas as pl
from jax.experimental.pallas import tpu as pltpu
from jax.sharding import PartitionSpec as P

HEADS = 16
HDIM = 64
MHEADS = 4
NK = 256
HALF = 512
TOPK = 32
EPS = 1e-05
LANES = 128
ALL = ("grp", "mem")
BF = jnp.bfloat16
F32 = jnp.float32
NEG = -1e30


def dot(left, right, dims=((1,), (0,))):
    return lax.dot_general(left, right, (dims, ((), ())), preferred_element_type=F32)


NT = ((1,), (1,))
TN = ((0,), (0,))


def iota(shape, dim):
    return lax.broadcasted_iota(jnp.int32, shape, dim)


def lane_halves(rows):
    first = iota((rows, LANES), 1) < HDIM
    return first


def half_masks():
    lane = iota((1, LANES), 1)
    return ((lane < HDIM).astype(BF), (lane >= HDIM).astype(BF))


def attn_fwd_kernel(rows, win, pos_ref, q_ref, k_ref, v_ref, qseg_ref, kseg_ref, out_ref, lse_ref):
    pair = pl.program_id(0)
    row0 = pos_ref[0] * rows
    start = pl.multiple_of(jnp.maximum(row0 + rows - win, 0), LANES)
    keys = k_ref[pl.ds(start, win), :]
    values = v_ref[pl.ds(start, win), :]
    key_pos = start + iota((rows, win), 1)
    query_pos = row0 + iota((rows, win), 0)
    allowed = (key_pos <= query_pos) & (kseg_ref[:, pl.ds(start, win)] == qseg_ref[...])
    lane = iota((rows, LANES), 1)
    masks = half_masks()
    outs = []
    lse = jnp.where(pair == 0, jnp.zeros((rows, LANES), F32), lse_ref[...])
    for half in range(2):
        scores = dot(q_ref[...] * masks[half], keys, NT) * 0.125
        scores = jnp.where(allowed, scores, NEG)
        top = jnp.max(scores, axis=1, keepdims=True)
        weights = jnp.exp(scores - top)
        total = jnp.sum(weights, axis=1, keepdims=True)
        probs = weights * (1.0 / total)
        outs.append(dot(probs.astype(BF), values))
        lse = jnp.where(lane == pair * 2 + half, top + jnp.log(total), lse)
    out_ref[...] = jnp.where(lane < HDIM, outs[0], outs[1])
    lse_ref[...] = lse


def attn_fwd(pos, qkv, seg_row, seg_col, rows):
    group_len, width = qkv.shape[0], qkv.shape[1] // 3
    pairs = width // LANES
    win = min(group_len, group_len // 2 + rows)
    return pl.pallas_call(
        functools.partial(attn_fwd_kernel, rows, win),
        grid_spec=pltpu.PrefetchScalarGridSpec(
            num_scalar_prefetch=1,
            grid=(pairs,),
            in_specs=[
                pl.BlockSpec((rows, LANES), lambda h, p: (p[0], h)),
                pl.BlockSpec((group_len, LANES), lambda h, p: (0, pairs + h)),
                pl.BlockSpec((group_len, LANES), lambda h, p: (0, 2 * pairs + h)),
                pl.BlockSpec((rows, 1), lambda h, p: (p[0], 0)),
                pl.BlockSpec((1, group_len), lambda h, p: (0, 0)),
            ],
            out_specs=[
                pl.BlockSpec((rows, LANES), lambda h, p: (0, h)),
                pl.BlockSpec((rows, LANES), lambda h, p: (0, 0)),
            ],
        ),
        out_shape=[
            jax.ShapeDtypeStruct((rows, width), F32),
            jax.ShapeDtypeStruct((rows, LANES), F32),
        ],
        cost_estimate=pl.CostEstimate(
            flops=4 * rows * win * width,
            bytes_accessed=group_len * width * 4,
            transcendentals=rows * win * HEADS,
        ),
        name="attn_fwd",
    )(pos, qkv, qkv, qkv, seg_col, seg_row)


def attn_bwd_kernel(
    rows, win, pairs, pos_ref, q_ref, k_ref, v_ref, da_ref, stat_ref, segc_ref, segr_ref, out_ref
):
    pair = pl.program_id(0)
    group_len = k_ref.shape[0]
    row0 = pl.multiple_of(pos_ref[0] * rows, LANES)
    start = pl.multiple_of(jnp.maximum(row0 + rows - win, 0), LANES)
    qstart = pl.multiple_of(jnp.minimum(row0, group_len - win), LANES)
    own, back, ahead = pl.ds(row0, rows), pl.ds(start, win), pl.ds(qstart, win)
    masks = half_masks()
    lane = iota((rows, LANES), 1)

    def stat(where, index, count):
        table = stat_ref[where, :]
        return jnp.sum(
            jnp.where(iota((count, table.shape[1]), 1) == index, table, 0.0),
            axis=1,
            keepdims=True,
        )

    allowed = (start + iota((rows, win), 1) <= row0 + iota((rows, win), 0)) & (
        segr_ref[:, back] == segc_ref[own, :]
    )
    allowed_two = (row0 + iota((win, rows), 1) <= qstart + iota((win, rows), 0)) & (
        segr_ref[:, own] == segc_ref[ahead, :]
    )
    dqs, dks, dvs = [], [], []
    for half in range(2):
        head = pair * 2 + half
        lse, delta = stat(own, head, rows), stat(own, HEADS + head, rows)
        keys = k_ref[back, :]
        scores = dot(q_ref[own, :] * masks[half], keys, NT) * 0.125
        probs = jnp.exp(jnp.where(allowed, scores - lse, NEG))
        dprobs = dot(da_ref[own, :] * masks[half], v_ref[back, :], NT)
        grads = (probs * (dprobs - delta)).astype(BF)
        dqs.append(dot(grads, keys))
        lse, delta = stat(ahead, head, win), stat(ahead, HEADS + head, win)
        queries, douts = q_ref[ahead, :], da_ref[ahead, :]
        scores = dot(queries * masks[half], k_ref[own, :], NT) * 0.125
        probs = jnp.exp(jnp.where(allowed_two, scores - lse, NEG))
        dprobs = dot(douts * masks[half], v_ref[own, :], NT)
        grads = (probs * (dprobs - delta)).astype(BF)
        dks.append(dot(grads, queries, TN))
        dvs.append(dot(probs.astype(BF), douts, TN))
    width = pairs * LANES
    for i, (parts, scale) in enumerate(((dqs, 0.125), (dks, 0.125), (dvs, 1.0))):
        column = pl.multiple_of(i * width + pair * LANES, LANES)
        out_ref[:, pl.ds(column, LANES)] = (
            jnp.where(lane < HDIM, parts[0], parts[1]) * scale
        ).astype(BF)


def attn_bwd(pos, qkv, douts, stats, seg_row, seg_col, rows):
    group_len, width = douts.shape
    pairs = width // LANES
    win = min(group_len, group_len // 2 + rows)
    return pl.pallas_call(
        functools.partial(attn_bwd_kernel, rows, win, pairs),
        grid_spec=pltpu.PrefetchScalarGridSpec(
            num_scalar_prefetch=1,
            grid=(pairs,),
            in_specs=[
                pl.BlockSpec((group_len, LANES), lambda h, p: (0, h)),
                pl.BlockSpec((group_len, LANES), lambda h, p: (0, pairs + h)),
                pl.BlockSpec((group_len, LANES), lambda h, p: (0, 2 * pairs + h)),
                pl.BlockSpec((group_len, LANES), lambda h, p: (0, h)),
                pl.BlockSpec(stats.shape, lambda h, p: (0, 0)),
                pl.BlockSpec((group_len, 1), lambda h, p: (0, 0)),
                pl.BlockSpec((1, group_len), lambda h, p: (0, 0)),
            ],
            out_specs=pl.BlockSpec((rows, 3 * width), lambda h, p: (0, 0)),
        ),
        out_shape=jax.ShapeDtypeStruct((rows, 3 * width), BF),
        cost_estimate=pl.CostEstimate(
            flops=14 * rows * win * width,
            bytes_accessed=group_len * width * 8,
            transcendentals=2 * rows * win * HEADS,
        ),
        name="attn_bwd",
    )(pos, qkv, qkv, qkv, douts, stats, seg_col, seg_row)


def by_head(lane, reduce, fill, values):
    spread = jnp.zeros_like(values)
    for c in range(MHEADS):
        inside = lane // TOPK == c
        spread = jnp.where(
            inside, reduce(jnp.where(inside, values, fill), axis=1, keepdims=True), spread
        )
    return spread


def pick_fwd_kernel(scores_ref, picks_ref, weight_ref, low_ref):
    rows = picks_ref.shape[0]
    lane = iota((rows, LANES), 1)
    picks = picks_ref[...]
    index = (picks // NK, picks % NK)
    total = jnp.zeros((rows, LANES), F32)
    for c in range(MHEADS):
        both = jnp.zeros((rows, LANES), F32)
        for e in range(2):
            base = (c * 2 + e) * NK
            for part in range(NK // LANES):
                table = scores_ref[:, base + part * LANES : base + (part + 1) * LANES]
                found = jnp.take_along_axis(table, index[e] % LANES, axis=1)
                both = both + jnp.where(index[e] // LANES == part, found, 0.0)
        total = jnp.where(lane // TOPK == c, both, total)
    top = by_head(lane, jnp.max, NEG, total)
    weights = jnp.exp(total - top)
    weights = weights / by_head(lane, jnp.sum, 0.0, weights)
    weight_ref[...] = weights
    low_ref[...] = weights.astype(BF)


def pick_fwd(half_scores, picks):
    rows = picks.shape[0]
    return pl.pallas_call(
        pick_fwd_kernel,
        out_shape=[
            jax.ShapeDtypeStruct((rows, LANES), F32),
            jax.ShapeDtypeStruct((rows, LANES), BF),
        ],
        name="pick_fwd",
    )(half_scores, picks)


def pick_bwd_kernel(weight_ref, grad_ref, picks_ref, out_ref):
    rows = picks_ref.shape[0]
    lane = iota((rows, LANES), 1)
    weights, grads, picks = weight_ref[...], grad_ref[...], picks_ref[...]
    score = (weights * (grads - by_head(lane, jnp.sum, 0.0, weights * grads))).astype(BF)
    score = score.astype(F32)
    index = (picks // NK, picks % NK)
    key = iota((rows, NK), 1)
    for c in range(MHEADS):
        totals = [jnp.zeros((rows, NK), F32) for _ in range(2)]
        for j in range(TOPK):
            column = slice(c * TOPK + j, c * TOPK + j + 1)
            for e in range(2):
                totals[e] = totals[e] + jnp.where(
                    key == index[e][:, column], score[:, column], 0.0
                )
        for e in range(2):
            base = (c * 2 + e) * NK
            out_ref[:, base : base + NK] = totals[e].astype(BF)


def pick_bwd(weights, grads, picks):
    rows = picks.shape[0]
    block = 32
    spec = pl.BlockSpec((block, LANES), lambda i: (i, 0))
    return pl.pallas_call(
        pick_bwd_kernel,
        grid=(rows // block,),
        in_specs=[spec, spec, spec],
        out_specs=pl.BlockSpec((block, MHEADS * 2 * NK), lambda i: (i, 0)),
        out_shape=jax.ShapeDtypeStruct((rows, MHEADS * 2 * NK), BF),
        name="pick_bwd",
    )(weights, grads, picks)


def owner_kernel(
    his, flat_bits, local_rows, keys_ref, sent_ref, values_ref, part_ref, spread_ref
):
    rows = part_ref.shape[0]
    width = values_ref.shape[1]
    slots = keys_ref.shape[-1]
    low_rows = local_rows // his
    key = keys_ref[0]
    flat = key & ((1 << flat_bits) - 1)
    dummy = ((key >> flat_bits) & 1) == 1
    row = (key >> (flat_bits + 1)) % local_rows
    token = flat // LANES
    pick = flat % LANES
    token = jnp.where(dummy, -1, token)
    block = jnp.where(dummy, -1, (row // low_rows) * rows + token)
    low_row = row % low_rows
    grad = sent_ref[:, :width]
    weights = sent_ref[:, width:]
    is_token = iota((rows, slots), 0) == token
    is_pick = iota((LANES, slots), 0) == pick
    token_hot = is_token.astype(F32).astype(BF)
    found = dot(weights, token_hot, TN)
    weight = jnp.sum(jnp.where(is_pick, found, 0.0), axis=0, keepdims=True)
    is_block = iota((his * rows, slots), 0) == block
    is_low = iota((low_rows, slots), 0) == low_row
    low_hot = is_low.astype(F32).astype(BF)
    spread = dot(jnp.where(is_block, weight, 0.0).astype(BF), low_hot, NT).astype(BF)
    total = jnp.zeros((rows, width), F32)
    products = []
    for h in range(his):
        table = values_ref[h * low_rows : (h + 1) * low_rows, :]
        piece = spread[h * rows : (h + 1) * rows, :]
        spread_ref[h] = piece
        total = total + dot(piece, table)
        products.append(dot(grad, table, NT).astype(BF))
    picked = dot(jnp.concatenate(products, axis=0), is_block.astype(F32).astype(BF), TN)
    picked = jnp.sum(jnp.where(is_low, picked, 0.0), axis=0, keepdims=True)
    part_ref[:, :width] = total.astype(BF)
    part_ref[:, width:] = dot(
        jnp.where(is_token, picked, 0.0).astype(BF), is_pick.astype(F32).astype(BF), NT
    ).astype(BF)


def owner_call(keys, sent, values, flat_bits, order):
    owners, slots = keys.shape
    rows = sent.shape[0] // owners
    local_rows, width = values.shape
    his = 4
    low_rows = local_rows // his
    return pl.pallas_call(
        functools.partial(owner_kernel, his, flat_bits, local_rows),
        grid=(owners,),
        in_specs=[
            pl.BlockSpec((1, 1, slots), lambda s: (s, 0, 0)),
            pl.BlockSpec((rows, width + LANES), lambda s: (s, 0)),
            pl.BlockSpec((local_rows, width), lambda s: (0, 0)),
        ],
        out_specs=[
            pl.BlockSpec((rows, width + LANES), lambda s: (order(s), 0)),
            pl.BlockSpec((his, rows, low_rows), lambda s: (0, s, 0)),
        ],
        out_shape=[
            jax.ShapeDtypeStruct((owners * rows, width + LANES), BF),
            jax.ShapeDtypeStruct((his, owners * rows, low_rows), BF),
        ],
        compiler_params=pltpu.CompilerParams(vmem_limit_bytes=48 * 1024 * 1024),
        cost_estimate=pl.CostEstimate(
            flops=2 * owners * rows * local_rows * (2 * slots + 2 * width),
            bytes_accessed=owners * rows * (2 * width + local_rows) * 2,
            transcendentals=0,
        ),
        name="owner",
    )(keys.reshape(owners, 1, slots), sent, values)


def route(picks, owners, local_rows, capacity, flat_bits):
    total = picks.size
    rows_of = picks.reshape(total)
    flat = jnp.arange(total, dtype=jnp.int32)
    each = jnp.arange(owners, dtype=jnp.int32)
    counts = jnp.sum((rows_of[:, None] // local_rows == each[None, :]).astype(jnp.int32), axis=0)
    ends = jnp.cumsum(capacity - counts)
    spares = owners * capacity - total
    spare_owner = jnp.sum(
        (jnp.arange(spares, dtype=jnp.int32)[:, None] >= ends[None, :]).astype(jnp.int32), axis=1
    )
    real = (rows_of << (flat_bits + 1)) + flat
    spare = ((spare_owner * local_rows + local_rows - 1) << (flat_bits + 1)) + (1 << flat_bits)
    keys = lax.sort(jnp.concatenate([real, spare]))
    return keys.reshape(owners, capacity)


MESH = pl.DeviceIdType.MESH


def places():
    g, m = lax.axis_index("grp"), lax.axis_index("mem")
    across = g + 1 - 2 * (g % 2)
    along = (g + 2) % 4
    sibling = m + 1 - 2 * (m % 2)
    return g, m, across, along, sibling


def enter(peers):
    barrier = pltpu.get_barrier_semaphore()
    for peer in peers:
        pl.semaphore_signal(barrier, inc=1, device_id=peer, device_id_type=MESH)
    pl.semaphore_wait(barrier, len(peers))


def push(src, dst, send, recv, peer):
    copy = pltpu.make_async_remote_copy(
        src_ref=src, dst_ref=dst, send_sem=send, recv_sem=recv, device_id=peer, device_id_type=MESH
    )
    copy.start()
    return copy


def reduce_planes(held, ready, x1, y1, x2, y2, zin, send, recv):
    g, m, across, along, _ = places()
    diagonal = 3 - g
    half = held.shape[2] // 2
    low, high = pl.ds(0, half), pl.ds(half, half)
    to_x, to_y = (across, m), (along, m)
    sent, ones, twos, threes = [], [], [], []
    for k in range(4):
        ready(k)
        a = push(held.at[k, diagonal, low], x1.at[k], send.at[0, k], recv.at[0, k], to_x)
        b = push(held.at[k, diagonal, high], y1.at[k], send.at[1, k], recv.at[1, k], to_y)
        ones.append((a, b))
    for k in range(4):
        a, b = ones[k]
        a.wait_recv()
        b.wait_recv()
        held[k, along, low] = held[k, along, low] + x1[k]
        held[k, across, high] = held[k, across, high] + y1[k]
        a = push(held.at[k, across], x2.at[k], send.at[2, k], recv.at[2, k], to_x)
        b = push(held.at[k, along], y2.at[k], send.at[3, k], recv.at[3, k], to_y)
        twos.append((a, b))
    total = None
    for k in range(4):
        a, b = twos[k]
        a.wait_recv()
        b.wait_recv()
        total = held[k, g].astype(F32) + x2[k].astype(F32) + y2[k].astype(F32)
        if k < 3:
            held[k, g] = total.astype(BF)
            peer = (g, (m + 2 * (3 - k)) % 8)
            threes.append(push(held.at[k, g], zin.at[k], send.at[4, k], recv.at[4, k], peer))
    for k in range(3):
        threes[k].wait_recv()
        total = total + zin[k].astype(F32)
    for pair in ones + twos:
        sent.extend(pair)
    for copy in sent + threes:
        copy.wait_send()
    return total


def plane_peers():
    g, m, across, along, sibling = places()
    return [(across, m), (along, m), (g, sibling)] + [(g, (m + 2 * d) % 8) for d in (1, 2, 3)]


def return_kernel(part_ref, out_ref, held, sib, x1, y1, x2, y2, zin, local_sem, send, recv):
    g, m, _, _, sibling = places()
    core, z = m % 2, m // 2
    enter(plane_peers())
    locals_, remotes = [], []
    for k in range(4):
        level = (z + 3 - k) % 4
        copy = pltpu.make_async_copy(part_ref.at[core, level], held.at[k], local_sem.at[k])
        copy.start()
        locals_.append(copy)
        remotes.append(
            push(
                part_ref.at[1 - core, level], sib.at[k], send.at[5, k], recv.at[5, k], (g, sibling)
            )
        )

    def ready(k):
        locals_[k].wait()
        remotes[k].wait_recv()
        for i in range(4):
            held[k, i] = held[k, i] + sib[k, i]

    out_ref[...] = reduce_planes(held, ready, x1, y1, x2, y2, zin, send, recv)
    for copy in remotes:
        copy.wait_send()


def plane_scratch(rows, columns):
    return [
        pltpu.VMEM((4, rows // 2, columns), BF),
        pltpu.VMEM((4, rows // 2, columns), BF),
        pltpu.VMEM((4, rows, columns), BF),
        pltpu.VMEM((4, rows, columns), BF),
        pltpu.VMEM((3, rows, columns), BF),
    ]


def return_rows(part, rows):
    columns = part.shape[1]
    return pl.pallas_call(
        return_kernel,
        in_specs=[pl.BlockSpec(memory_space=pl.ANY)],
        out_specs=pl.BlockSpec(memory_space=pltpu.VMEM),
        out_shape=jax.ShapeDtypeStruct((rows, columns), F32),
        scratch_shapes=[
            pltpu.VMEM((4, 4, rows, columns), BF),
            pltpu.VMEM((4, 4, rows, columns), BF),
            *plane_scratch(rows, columns),
            pltpu.SemaphoreType.DMA((4,)),
            pltpu.SemaphoreType.DMA((6, 4)),
            pltpu.SemaphoreType.DMA((6, 4)),
        ],
        compiler_params=pltpu.CompilerParams(
            collective_id=1, has_side_effects=True, vmem_limit_bytes=48 * 1024 * 1024
        ),
        name="return_rows",
    )(part.reshape(2, 4, 4, rows, columns))


WIDTH = HEADS * HDIM
KEYS = MHEADS * 2 * NK
QUERIES = MHEADS * 2 * HALF
F_MIXED, F_SECOND, F_ATTENDED, F_FIRST, F_COT, F_GATE, F_RESID = (i * WIDTH for i in range(7))
F_HALF = 7 * WIDTH
F_QKV = F_HALF + KEYS
F_QUERY = F_QKV + 3 * WIDTH
F_ALL = F_QUERY + QUERIES
G_OUT, G_GATE, G_PROJ, G_HALF = 0, WIDTH, 2 * WIDTH, 3 * WIDTH
G_QKV = G_HALF + KEYS
G_KEYS = G_QKV + 3 * WIDTH
G_GAIN = G_KEYS + 2 * HALF
G_ALL = G_GAIN + LANES
PRODUCTS = (
    (F_MIXED, F_COT, WIDTH, G_OUT),
    (F_SECOND, F_GATE, WIDTH, G_GATE),
    (F_ATTENDED, F_RESID, WIDTH, G_PROJ),
    (F_SECOND, F_HALF, KEYS, G_HALF),
    (F_FIRST, F_QKV, 3 * WIDTH, G_QKV),
)


def grads_kernel(
    fact_ref, gain_ref, out_ref, fact, gains, held, x1, y1, x2, y2, zin, quarter, local_sem, send, recv
):
    g, m, across, along, sibling = places()
    core, z = m % 2, m // 2
    rows = fact_ref.shape[0]
    enter(plane_peers())
    copies = []
    for i, (src, dst, count) in enumerate(((fact_ref, fact, rows), (gain_ref, gains, 16))):
        near = pltpu.make_async_copy(src, dst.at[pl.ds(0, count)], local_sem.at[i])
        near.start()
        far = push(
            src, dst.at[pl.ds(count, count)], send.at[5, i], recv.at[5, i], (g, sibling)
        )
        copies.append((near, far))
    for near, far in copies:
        near.wait()
        far.wait_recv()
    row = iota((32, LANES), 0) % 16
    column = iota((32, LANES), 1)
    select = ((row < 4) & (row // 2 == column)).astype(F32).astype(BF)
    chunk = WIDTH

    def ready(k):
        block = (z + 3 - k) % 4 * 2 + core

        def store(value, at):
            for i in range(4):
                held[k, i, :, at : at + value.shape[1]] = value[i * 32 : (i + 1) * 32].astype(BF)

        for left, right, count, at in PRODUCTS:
            lhs = fact[:, pl.ds(pl.multiple_of(left + block * LANES, LANES), LANES)]
            for j in range(0, count, chunk):
                store(dot(lhs, fact[:, right + j : right + j + chunk], TN), at + j)
        lhs = fact[:, pl.ds(pl.multiple_of(F_HALF + block * NK, LANES), NK)]
        rhs = fact[:, pl.ds(pl.multiple_of(F_QUERY + block * HALF, LANES), HALF)]
        value = dot(lhs, rhs, TN)
        for i in range(4):
            for h in range(2):
                first = i * 64 + h * 32
                held[k, i, :, G_KEYS + h * HALF : G_KEYS + (h + 1) * HALF] = value[
                    first : first + 32
                ].astype(BF)
        lhs = gains[:, pl.ds(pl.multiple_of(block * LANES, LANES), LANES)]
        store(dot(lhs, select, TN), G_GAIN)

    total = reduce_planes(held, ready, x1, y1, x2, y2, zin, send, recv)
    quarter[g] = total.astype(BF)
    to_x, to_y = (across, m), (along, m)
    low, high = pl.ds(0, 16), pl.ds(16, 16)
    a = push(quarter.at[g], quarter.at[g], send.at[6, 0], recv.at[6, 0], to_x)
    b = push(quarter.at[g], quarter.at[g], send.at[6, 1], recv.at[6, 1], to_y)
    a.wait_recv()
    c = push(quarter.at[across, low], quarter.at[across, low], send.at[6, 2], recv.at[6, 2], to_y)
    b.wait_recv()
    d = push(quarter.at[along, high], quarter.at[along, high], send.at[6, 3], recv.at[6, 3], to_x)
    c.wait_recv()
    d.wait_recv()
    for copy in (a, b, c, d):
        copy.wait_send()
    for _, far in copies:
        far.wait_send()
    out_ref[...] = quarter[...]


def reduce_grads(factors, gains):
    rows = factors.shape[0]
    return pl.pallas_call(
        grads_kernel,
        in_specs=[pl.BlockSpec(memory_space=pl.ANY)] * 2,
        out_specs=pl.BlockSpec(memory_space=pltpu.VMEM),
        out_shape=jax.ShapeDtypeStruct((4, 32, G_ALL), BF),
        scratch_shapes=[
            pltpu.VMEM((2 * rows, F_ALL), BF),
            pltpu.VMEM((32, WIDTH), BF),
            pltpu.VMEM((4, 4, 32, G_ALL), BF),
            *plane_scratch(32, G_ALL),
            pltpu.VMEM((4, 32, G_ALL), BF),
            pltpu.SemaphoreType.DMA((2,)),
            pltpu.SemaphoreType.DMA((7, 4)),
            pltpu.SemaphoreType.DMA((7, 4)),
        ],
        compiler_params=pltpu.CompilerParams(
            collective_id=2, has_side_effects=True, vmem_limit_bytes=56 * 1024 * 1024
        ),
        name="reduce_grads",
    )(factors, gains).reshape(4 * 32, G_ALL)


def rms_scale(values):
    return lax.rsqrt(jnp.mean(values * values, axis=-1, keepdims=True) + EPS)


def rms_back(values, scale, gain, grad):
    scaled = grad * gain
    inner = jnp.mean(values * scaled, axis=-1, keepdims=True)
    gain_grad = jnp.sum(grad * values * scale, axis=0)
    return scale * scaled - values * (scale * scale * scale * inner), gain_grad


def per_device(
    tokens,
    segment_ids,
    picks,
    attn_gain,
    qkv_weight,
    attn_proj,
    mem_gain,
    query_weight,
    half_keys,
    memory_values,
    gate_weight,
    out_weight,
    out_cotangent,
):
    rows, width = tokens.shape
    owners = lax.axis_size("grp") * lax.axis_size("mem")
    local_rows = memory_values.shape[0]
    total_picks = rows * MHEADS * TOPK
    flat_bits = (total_picks - 1).bit_length()
    capacity = 2 * total_picks // owners
    group_len = segment_ids.shape[0]
    linked = (lax.axis_size("grp"), lax.axis_size("mem"), rows) == (4, 8, LANES)
    position = lax.axis_index("mem").astype(jnp.int32)
    pos = position.reshape(1)

    def gather(x, axes="mem"):
        return lax.all_gather(x, axes, axis=0, tiled=True)

    gains = lax.all_gather(jnp.stack([attn_gain, mem_gain]), "mem", axis=1, tiled=True)
    gains = gains.astype(F32)
    gain_one, gain_two = gains[0:1], gains[1:2]
    tokens_all = gather(tokens)
    qkv_full = gather(qkv_weight)
    proj_full = gather(attn_proj)
    query_full = gather(query_weight)
    keys_full = gather(half_keys)
    gate_full = gather(gate_weight)
    output_full = gather(out_weight)

    requests = route(picks, owners, local_rows, capacity, flat_bits)
    arrived = lax.all_to_all(requests, ALL, split_axis=0, concat_axis=0, tiled=True)

    inputs_all = tokens_all.astype(F32)
    first_all = (inputs_all * rms_scale(inputs_all) * gain_one).astype(BF)
    qkv_all = dot(first_all, qkv_full).astype(BF)
    seg_row, seg_col = segment_ids.reshape(1, group_len), segment_ids.reshape(group_len, 1)
    attn_sum, lse = attn_fwd(pos, qkv_all, seg_row, seg_col, rows)
    attended = attn_sum.astype(BF)
    inputs = tokens.astype(F32)
    residual = inputs + dot(attended, proj_full)
    scale_two = rms_scale(residual)
    second = (residual * scale_two * gain_two).astype(BF)
    mem_query = dot(second, query_full).astype(BF)
    gate_pre = dot(second, gate_full)
    mixed_grad = dot(out_cotangent, output_full, NT)
    sig = jax.nn.sigmoid(gate_pre)
    gate_act = gate_pre * sig
    memory_grad = (mixed_grad * gate_act).astype(BF)
    key_table = keys_full.reshape(MHEADS * 2, NK, HALF)
    half_scores = jnp.einsum(
        "tcf,cnf->tcn",
        mem_query.reshape(rows, MHEADS * 2, HALF),
        key_table,
        preferred_element_type=F32,
    ).reshape(rows, MHEADS * 2 * NK)
    flat_picks = picks.reshape(rows, MHEADS * TOPK)
    pick_weights, weights_low = pick_fwd(half_scores, flat_picks)

    sent = gather(jnp.concatenate([memory_grad, weights_low], axis=1), ALL)
    if linked:
        part, spread = owner_call(
            arrived, sent, memory_values, flat_bits, lambda s: s % 2 * 16 + s // 2 % 4 * 4 + s // 8
        )
        back = return_rows(part, rows)
    else:
        part, spread = owner_call(arrived, sent, memory_values, flat_bits, lambda s: s)
        back = lax.psum_scatter(part, "grp", scatter_dimension=0, tiled=True)
        back = lax.psum_scatter(back, "mem", scatter_dimension=0, tiled=True)
    values_grad = jnp.einsum(
        "hkl,kd->hld", spread, sent[:, :width], preferred_element_type=F32
    ).reshape(local_rows, width)

    memory_out = back[:, :width].astype(F32)
    weight_grad = back[:, width:].astype(F32)
    mixed = (memory_out * gate_act).astype(BF)
    block_out = (residual + dot(mixed, output_full)).astype(BF)
    gate_grad = (mixed_grad * memory_out * (sig * (1.0 + gate_pre * (1.0 - sig)))).astype(BF)
    half_grad = pick_bwd(pick_weights, weight_grad, flat_picks)
    half_cube = half_grad.reshape(rows, MHEADS * 2, NK)
    query_grad = (
        jnp.einsum("tcn,cnf->tcf", half_cube, key_table, preferred_element_type=F32)
        .astype(BF)
        .reshape(rows, MHEADS * 2 * HALF)
    )
    second_grad = dot(gate_grad, gate_full, NT) + dot(query_grad, query_full, NT)
    resid_from_norm, gain_two_grad = rms_back(residual, scale_two, gain_two, second_grad)
    resid_grad = out_cotangent.astype(F32) + resid_from_norm
    resid_low = resid_grad.astype(BF)
    attn_grad = dot(resid_low, proj_full, NT).astype(BF)
    delta = jnp.sum(
        (attn_grad.astype(F32) * attn_sum).reshape(rows, HEADS, HDIM), axis=-1
    )
    stats = jnp.concatenate([lse[:, :HEADS], delta], axis=1)
    stats_high = lax.reduce_precision(stats, 8, 7)
    stats_low = stats - stats_high
    shared = gather(
        jnp.concatenate(
            [
                resid_low,
                stats_high.astype(BF),
                stats_low.astype(BF),
                jnp.zeros((rows, LANES - 4 * HEADS), BF),
            ],
            axis=1,
        )
    )
    stats_all = shared[:, width : width + 2 * HEADS].astype(F32) + shared[
        :, width + 2 * HEADS : width + 4 * HEADS
    ].astype(F32)
    attn_grad_all = dot(shared[:, :width], proj_full, NT).astype(BF)
    qkv_rows = attn_bwd(pos, qkv_all, attn_grad_all, stats_all, seg_row, seg_col, rows)
    scale_one = rms_scale(inputs)
    first_low = (inputs * scale_one * gain_one).astype(BF)
    first_grad = dot(qkv_rows, qkv_full, NT)
    input_from_norm, gain_one_grad = rms_back(inputs, scale_one, gain_one, first_grad)
    tokens_grad = resid_grad + input_from_norm

    if linked:
        factors = jnp.concatenate(
            [
                mixed,
                second,
                attended,
                first_low,
                out_cotangent,
                gate_grad,
                resid_low,
                half_grad,
                qkv_rows,
                mem_query,
            ],
            axis=1,
        )
        sums = jnp.stack([gain_one_grad, gain_two_grad])
        sums_high = lax.reduce_precision(sums, 8, 7)
        gain_rows = jnp.stack([sums_high, sums - sums_high], axis=1).reshape(4, width)
        gain_rows = jnp.concatenate([gain_rows.astype(BF), jnp.zeros((12, width), BF)])
        reduced = reduce_grads(factors, gain_rows).astype(F32)
        out_share = reduced[:, G_OUT : G_OUT + width]
        gate_share = reduced[:, G_GATE : G_GATE + width]
        proj_share = reduced[:, G_PROJ : G_PROJ + width]
        qkv_share = reduced[:, G_QKV : G_QKV + 3 * width]
        keys_share = (
            reduced[:, G_KEYS : G_KEYS + 2 * HALF]
            .reshape(4, 32, 2, HALF)
            .transpose(0, 2, 1, 3)
            .reshape(half_keys.shape)
        )
        query_share = jnp.einsum(
            "rcn,cnf->rcf",
            reduced[:, G_HALF : G_HALF + KEYS].astype(BF).reshape(rows, MHEADS * 2, NK),
            key_table,
            preferred_element_type=F32,
        ).reshape(rows, QUERIES)
        gain_sums = reduced[:, G_GAIN : G_GAIN + 2].T
    else:
        keys_grad = jnp.einsum(
            "tcn,tcf->cnf",
            half_cube,
            mem_query.reshape(rows, MHEADS * 2, HALF),
            preferred_element_type=F32,
        ).reshape(KEYS, HALF)
        partials = (
            dot(mixed, out_cotangent, TN),
            dot(second, gate_grad, TN),
            keys_grad,
            dot(second, query_grad, TN),
            dot(attended, resid_low, TN),
            dot(first_low, qkv_rows, TN),
        )
        shares = [
            lax.psum_scatter(x.astype(BF), "mem", scatter_dimension=0, tiled=True)
            for x in partials
        ]
        shares = lax.psum(tuple(shares), "grp")
        gain_sums = lax.psum(jnp.stack([gain_one_grad, gain_two_grad]), ALL)
        gain_sums = lax.dynamic_slice_in_dim(
            gain_sums, position * attn_gain.shape[0], attn_gain.shape[0], axis=1
        )
        out_share, gate_share, keys_share, query_share, proj_share, qkv_share = (
            x.astype(F32) for x in shares
        )
    return (
        block_out,
        tokens_grad,
        gain_sums[0],
        qkv_share,
        proj_share,
        gain_sums[1],
        query_share,
        keys_share,
        values_grad,
        gate_share,
        out_share,
    )


def solution(mesh):
    placed = (
        P(ALL, None),
        P("grp"),
        P(ALL, None, None),
        P("mem"),
        P("mem", None),
        P("mem", None),
        P("mem"),
        P("mem", None),
        P("mem", None),
        P(ALL, None),
        P("mem", None),
        P("mem", None),
        P(ALL, None),
    )
    return jax.shard_map(
        per_device,
        mesh=mesh,
        in_specs=placed,
        out_specs=(
            P(ALL, None),
            P(ALL, None),
            P("mem"),
            P("mem", None),
            P("mem", None),
            P("mem"),
            P("mem", None),
            P("mem", None),
            P(ALL, None),
            P("mem", None),
            P("mem", None),
        ),
        check_vma=False,
    )
```

```python
import functools

import jax
import jax.numpy as jnp
from jax import lax
from jax.experimental import pallas as pl
from jax.experimental.pallas import tpu as pltpu
from jax.sharding import PartitionSpec as P

HEADS = 16
HDIM = 64
MHEADS = 4
NK = 256
HALF = 512
TOPK = 32
EPS = 1e-05
LANES = 128
ALL = ("grp", "mem")
BF = jnp.bfloat16
F32 = jnp.float32
NEG = -1e30


def dot(left, right, dims=((1,), (0,))):
    return lax.dot_general(left, right, (dims, ((), ())), preferred_element_type=F32)


NT = ((1,), (1,))
TN = ((0,), (0,))


def iota(shape, dim):
    return lax.broadcasted_iota(jnp.int32, shape, dim)


def lane_halves(rows):
    first = iota((rows, LANES), 1) < HDIM
    return first


def half_masks():
    lane = iota((1, LANES), 1)
    return ((lane < HDIM).astype(BF), (lane >= HDIM).astype(BF))


def attn_fwd_kernel(rows, win, pos_ref, q_ref, k_ref, v_ref, qseg_ref, kseg_ref, out_ref, lse_ref):
    pair = pl.program_id(0)
    row0 = pos_ref[0] * rows
    start = pl.multiple_of(jnp.maximum(row0 + rows - win, 0), LANES)
    keys = k_ref[pl.ds(start, win), :]
    values = v_ref[pl.ds(start, win), :]
    key_pos = start + iota((rows, win), 1)
    query_pos = row0 + iota((rows, win), 0)
    allowed = (key_pos <= query_pos) & (kseg_ref[:, pl.ds(start, win)] == qseg_ref[...])
    lane = iota((rows, LANES), 1)
    masks = half_masks()
    outs = []
    lse = jnp.where(pair == 0, jnp.zeros((rows, LANES), F32), lse_ref[...])
    for half in range(2):
        scores = dot(q_ref[...] * masks[half], keys, NT) * 0.125
        scores = jnp.where(allowed, scores, NEG)
        top = jnp.max(scores, axis=1, keepdims=True)
        weights = jnp.exp(scores - top)
        total = jnp.sum(weights, axis=1, keepdims=True)
        probs = weights * (1.0 / total)
        outs.append(dot(probs.astype(BF), values))
        lse = jnp.where(lane == pair * 2 + half, top + jnp.log(total), lse)
    out_ref[...] = jnp.where(lane < HDIM, outs[0], outs[1])
    lse_ref[...] = lse


def attn_fwd(pos, qkv, seg_row, seg_col, rows):
    group_len, width = qkv.shape[0], qkv.shape[1] // 3
    pairs = width // LANES
    win = min(group_len, group_len // 2 + rows)
    return pl.pallas_call(
        functools.partial(attn_fwd_kernel, rows, win),
        grid_spec=pltpu.PrefetchScalarGridSpec(
            num_scalar_prefetch=1,
            grid=(pairs,),
            in_specs=[
                pl.BlockSpec((rows, LANES), lambda h, p: (p[0], h)),
                pl.BlockSpec((group_len, LANES), lambda h, p: (0, pairs + h)),
                pl.BlockSpec((group_len, LANES), lambda h, p: (0, 2 * pairs + h)),
                pl.BlockSpec((rows, 1), lambda h, p: (p[0], 0)),
                pl.BlockSpec((1, group_len), lambda h, p: (0, 0)),
            ],
            out_specs=[
                pl.BlockSpec((rows, LANES), lambda h, p: (0, h)),
                pl.BlockSpec((rows, LANES), lambda h, p: (0, 0)),
            ],
        ),
        out_shape=[
            jax.ShapeDtypeStruct((rows, width), F32),
            jax.ShapeDtypeStruct((rows, LANES), F32),
        ],
        cost_estimate=pl.CostEstimate(
            flops=4 * rows * win * width,
            bytes_accessed=group_len * width * 4,
            transcendentals=rows * win * HEADS,
        ),
        name="attn_fwd",
    )(pos, qkv, qkv, qkv, seg_col, seg_row)


def attn_bwd_kernel(
    rows, win, pairs, pos_ref, q_ref, k_ref, v_ref, da_ref, stat_ref, segc_ref, segr_ref, out_ref
):
    pair = pl.program_id(0)
    group_len = k_ref.shape[0]
    row0 = pl.multiple_of(pos_ref[0] * rows, LANES)
    start = pl.multiple_of(jnp.maximum(row0 + rows - win, 0), LANES)
    qstart = pl.multiple_of(jnp.minimum(row0, group_len - win), LANES)
    own, back, ahead = pl.ds(row0, rows), pl.ds(start, win), pl.ds(qstart, win)
    masks = half_masks()
    lane = iota((rows, LANES), 1)

    def stat(where, index, count):
        table = stat_ref[where, :]
        return jnp.sum(
            jnp.where(iota((count, table.shape[1]), 1) == index, table, 0.0),
            axis=1,
            keepdims=True,
        )

    allowed = (start + iota((rows, win), 1) <= row0 + iota((rows, win), 0)) & (
        segr_ref[:, back] == segc_ref[own, :]
    )
    allowed_two = (row0 + iota((win, rows), 1) <= qstart + iota((win, rows), 0)) & (
        segr_ref[:, own] == segc_ref[ahead, :]
    )
    dqs, dks, dvs = [], [], []
    for half in range(2):
        head = pair * 2 + half
        lse, delta = stat(own, head, rows), stat(own, HEADS + head, rows)
        keys = k_ref[back, :]
        scores = dot(q_ref[own, :] * masks[half], keys, NT) * 0.125
        probs = jnp.exp(jnp.where(allowed, scores - lse, NEG))
        dprobs = dot(da_ref[own, :] * masks[half], v_ref[back, :], NT)
        grads = (probs * (dprobs - delta)).astype(BF)
        dqs.append(dot(grads, keys))
        lse, delta = stat(ahead, head, win), stat(ahead, HEADS + head, win)
        queries, douts = q_ref[ahead, :], da_ref[ahead, :]
        scores = dot(queries * masks[half], k_ref[own, :], NT) * 0.125
        probs = jnp.exp(jnp.where(allowed_two, scores - lse, NEG))
        dprobs = dot(douts * masks[half], v_ref[own, :], NT)
        grads = (probs * (dprobs - delta)).astype(BF)
        dks.append(dot(grads, queries, TN))
        dvs.append(dot(probs.astype(BF), douts, TN))
    width = pairs * LANES
    for i, (parts, scale) in enumerate(((dqs, 0.125), (dks, 0.125), (dvs, 1.0))):
        column = pl.multiple_of(i * width + pair * LANES, LANES)
        out_ref[:, pl.ds(column, LANES)] = (
            jnp.where(lane < HDIM, parts[0], parts[1]) * scale
        ).astype(BF)


def attn_bwd(pos, qkv, douts, stats, seg_row, seg_col, rows):
    group_len, width = douts.shape
    pairs = width // LANES
    win = min(group_len, group_len // 2 + rows)
    return pl.pallas_call(
        functools.partial(attn_bwd_kernel, rows, win, pairs),
        grid_spec=pltpu.PrefetchScalarGridSpec(
            num_scalar_prefetch=1,
            grid=(pairs,),
            in_specs=[
                pl.BlockSpec((group_len, LANES), lambda h, p: (0, h)),
                pl.BlockSpec((group_len, LANES), lambda h, p: (0, pairs + h)),
                pl.BlockSpec((group_len, LANES), lambda h, p: (0, 2 * pairs + h)),
                pl.BlockSpec((group_len, LANES), lambda h, p: (0, h)),
                pl.BlockSpec(stats.shape, lambda h, p: (0, 0)),
                pl.BlockSpec((group_len, 1), lambda h, p: (0, 0)),
                pl.BlockSpec((1, group_len), lambda h, p: (0, 0)),
            ],
            out_specs=pl.BlockSpec((rows, 3 * width), lambda h, p: (0, 0)),
        ),
        out_shape=jax.ShapeDtypeStruct((rows, 3 * width), BF),
        cost_estimate=pl.CostEstimate(
            flops=14 * rows * win * width,
            bytes_accessed=group_len * width * 8,
            transcendentals=2 * rows * win * HEADS,
        ),
        name="attn_bwd",
    )(pos, qkv, qkv, qkv, douts, stats, seg_col, seg_row)


def by_head(lane, reduce, fill, values):
    spread = jnp.zeros_like(values)
    for c in range(MHEADS):
        inside = lane // TOPK == c
        spread = jnp.where(
            inside, reduce(jnp.where(inside, values, fill), axis=1, keepdims=True), spread
        )
    return spread


def pick_fwd_kernel(scores_ref, picks_ref, weight_ref, low_ref):
    rows = picks_ref.shape[0]
    lane = iota((rows, LANES), 1)
    picks = picks_ref[...]
    index = (picks // NK, picks % NK)
    total = jnp.zeros((rows, LANES), F32)
    for c in range(MHEADS):
        both = jnp.zeros((rows, LANES), F32)
        for e in range(2):
            base = (c * 2 + e) * NK
            for part in range(NK // LANES):
                table = scores_ref[:, base + part * LANES : base + (part + 1) * LANES]
                found = jnp.take_along_axis(table, index[e] % LANES, axis=1)
                both = both + jnp.where(index[e] // LANES == part, found, 0.0)
        total = jnp.where(lane // TOPK == c, both, total)
    top = by_head(lane, jnp.max, NEG, total)
    weights = jnp.exp(total - top)
    weights = weights / by_head(lane, jnp.sum, 0.0, weights)
    weight_ref[...] = weights
    low_ref[...] = weights.astype(BF)


def pick_fwd(half_scores, picks):
    rows = picks.shape[0]
    return pl.pallas_call(
        pick_fwd_kernel,
        out_shape=[
            jax.ShapeDtypeStruct((rows, LANES), F32),
            jax.ShapeDtypeStruct((rows, LANES), BF),
        ],
        name="pick_fwd",
    )(half_scores, picks)


def pick_bwd_kernel(weight_ref, grad_ref, picks_ref, out_ref):
    rows = picks_ref.shape[0]
    lane = iota((rows, LANES), 1)
    weights, grads, picks = weight_ref[...], grad_ref[...], picks_ref[...]
    score = (weights * (grads - by_head(lane, jnp.sum, 0.0, weights * grads))).astype(BF)
    score = score.astype(F32)
    index = (picks // NK, picks % NK)
    key = iota((rows, NK), 1)
    for c in range(MHEADS):
        totals = [jnp.zeros((rows, NK), F32) for _ in range(2)]
        for j in range(TOPK):
            column = slice(c * TOPK + j, c * TOPK + j + 1)
            for e in range(2):
                totals[e] = totals[e] + jnp.where(
                    key == index[e][:, column], score[:, column], 0.0
                )
        for e in range(2):
            base = (c * 2 + e) * NK
            out_ref[:, base : base + NK] = totals[e].astype(BF)


def pick_bwd(weights, grads, picks):
    rows = picks.shape[0]
    block = 32
    spec = pl.BlockSpec((block, LANES), lambda i: (i, 0))
    return pl.pallas_call(
        pick_bwd_kernel,
        grid=(rows // block,),
        in_specs=[spec, spec, spec],
        out_specs=pl.BlockSpec((block, MHEADS * 2 * NK), lambda i: (i, 0)),
        out_shape=jax.ShapeDtypeStruct((rows, MHEADS * 2 * NK), BF),
        name="pick_bwd",
    )(weights, grads, picks)


def owner_kernel(
    his, flat_bits, local_rows, keys_ref, sent_ref, values_ref, part_ref, spread_ref
):
    rows = part_ref.shape[0]
    width = values_ref.shape[1]
    slots = keys_ref.shape[-1]
    low_rows = local_rows // his
    key = keys_ref[0]
    flat = key & ((1 << flat_bits) - 1)
    dummy = ((key >> flat_bits) & 1) == 1
    row = (key >> (flat_bits + 1)) % local_rows
    token = flat // LANES
    pick = flat % LANES
    token = jnp.where(dummy, -1, token)
    block = jnp.where(dummy, -1, (row // low_rows) * rows + token)
    low_row = row % low_rows
    grad = sent_ref[:, :width]
    weights = sent_ref[:, width:]
    is_token = iota((rows, slots), 0) == token
    is_pick = iota((LANES, slots), 0) == pick
    token_hot = is_token.astype(F32).astype(BF)
    found = dot(weights, token_hot, TN)
    weight = jnp.sum(jnp.where(is_pick, found, 0.0), axis=0, keepdims=True)
    is_block = iota((his * rows, slots), 0) == block
    is_low = iota((low_rows, slots), 0) == low_row
    low_hot = is_low.astype(F32).astype(BF)
    spread = dot(jnp.where(is_block, weight, 0.0).astype(BF), low_hot, NT).astype(BF)
    total = jnp.zeros((rows, width), F32)
    products = []
    for h in range(his):
        table = values_ref[h * low_rows : (h + 1) * low_rows, :]
        piece = spread[h * rows : (h + 1) * rows, :]
        spread_ref[h] = piece
        total = total + dot(piece, table)
        products.append(dot(grad, table, NT).astype(BF))
    picked = dot(jnp.concatenate(products, axis=0), is_block.astype(F32).astype(BF), TN)
    picked = jnp.sum(jnp.where(is_low, picked, 0.0), axis=0, keepdims=True)
    part_ref[:, :width] = total.astype(BF)
    part_ref[:, width:] = dot(
        jnp.where(is_token, picked, 0.0).astype(BF), is_pick.astype(F32).astype(BF), NT
    ).astype(BF)


def owner_call(keys, sent, values, flat_bits, order):
    owners, slots = keys.shape
    rows = sent.shape[0] // owners
    local_rows, width = values.shape
    his = 4
    low_rows = local_rows // his
    return pl.pallas_call(
        functools.partial(owner_kernel, his, flat_bits, local_rows),
        grid=(owners,),
        in_specs=[
            pl.BlockSpec((1, 1, slots), lambda s: (s, 0, 0)),
            pl.BlockSpec((rows, width + LANES), lambda s: (s, 0)),
            pl.BlockSpec((local_rows, width), lambda s: (0, 0)),
        ],
        out_specs=[
            pl.BlockSpec((rows, width + LANES), lambda s: (order(s), 0)),
            pl.BlockSpec((his, rows, low_rows), lambda s: (0, s, 0)),
        ],
        out_shape=[
            jax.ShapeDtypeStruct((owners * rows, width + LANES), BF),
            jax.ShapeDtypeStruct((his, owners * rows, low_rows), BF),
        ],
        compiler_params=pltpu.CompilerParams(vmem_limit_bytes=48 * 1024 * 1024),
        cost_estimate=pl.CostEstimate(
            flops=2 * owners * rows * local_rows * (2 * slots + 2 * width),
            bytes_accessed=owners * rows * (2 * width + local_rows) * 2,
            transcendentals=0,
        ),
        name="owner",
    )(keys.reshape(owners, 1, slots), sent, values)


def route(picks, owners, local_rows, capacity, flat_bits):
    total = picks.size
    rows_of = picks.reshape(total)
    flat = jnp.arange(total, dtype=jnp.int32)
    each = jnp.arange(owners, dtype=jnp.int32)
    counts = jnp.sum((rows_of[:, None] // local_rows == each[None, :]).astype(jnp.int32), axis=0)
    ends = jnp.cumsum(capacity - counts)
    spares = owners * capacity - total
    spare_owner = jnp.sum(
        (jnp.arange(spares, dtype=jnp.int32)[:, None] >= ends[None, :]).astype(jnp.int32), axis=1
    )
    real = (rows_of << (flat_bits + 1)) + flat
    spare = ((spare_owner * local_rows + local_rows - 1) << (flat_bits + 1)) + (1 << flat_bits)
    keys = lax.sort(jnp.concatenate([real, spare]))
    return keys.reshape(owners, capacity)


MESH = pl.DeviceIdType.MESH


def places():
    g, m = lax.axis_index("grp"), lax.axis_index("mem")
    across = g + 1 - 2 * (g % 2)
    along = (g + 2) % 4
    sibling = m + 1 - 2 * (m % 2)
    return g, m, across, along, sibling


def enter(peers):
    barrier = pltpu.get_barrier_semaphore()
    for peer in peers:
        pl.semaphore_signal(barrier, inc=1, device_id=peer, device_id_type=MESH)
    pl.semaphore_wait(barrier, len(peers))


def push(src, dst, send, recv, peer):
    copy = pltpu.make_async_remote_copy(
        src_ref=src, dst_ref=dst, send_sem=send, recv_sem=recv, device_id=peer, device_id_type=MESH
    )
    copy.start()
    return copy


def reduce_planes(held, ready, x1, y1, x2, y2, zin, send, recv):
    g, m, across, along, _ = places()
    diagonal = 3 - g
    half = held.shape[2] // 2
    low, high = pl.ds(0, half), pl.ds(half, half)
    to_x, to_y = (across, m), (along, m)
    sent, ones, twos, threes = [], [], [], []
    for k in range(4):
        ready(k)
        a = push(held.at[k, diagonal, low], x1.at[k], send.at[0, k], recv.at[0, k], to_x)
        b = push(held.at[k, diagonal, high], y1.at[k], send.at[1, k], recv.at[1, k], to_y)
        ones.append((a, b))
    for k in range(4):
        a, b = ones[k]
        a.wait_recv()
        b.wait_recv()
        held[k, along, low] = held[k, along, low] + x1[k]
        held[k, across, high] = held[k, across, high] + y1[k]
        a = push(held.at[k, across], x2.at[k], send.at[2, k], recv.at[2, k], to_x)
        b = push(held.at[k, along], y2.at[k], send.at[3, k], recv.at[3, k], to_y)
        twos.append((a, b))
    total = None
    for k in range(4):
        a, b = twos[k]
        a.wait_recv()
        b.wait_recv()
        total = held[k, g].astype(F32) + x2[k].astype(F32) + y2[k].astype(F32)
        if k < 3:
            held[k, g] = total.astype(BF)
            peer = (g, (m + 2 * (3 - k)) % 8)
            threes.append(push(held.at[k, g], zin.at[k], send.at[4, k], recv.at[4, k], peer))
    for k in range(3):
        threes[k].wait_recv()
        total = total + zin[k].astype(F32)
    for pair in ones + twos:
        sent.extend(pair)
    for copy in sent + threes:
        copy.wait_send()
    return total


def plane_peers():
    g, m, across, along, sibling = places()
    return [(across, m), (along, m), (g, sibling)] + [(g, (m + 2 * d) % 8) for d in (1, 2, 3)]


def return_kernel(part_ref, out_ref, held, sib, x1, y1, x2, y2, zin, local_sem, send, recv):
    g, m, _, _, sibling = places()
    core, z = m % 2, m // 2
    enter(plane_peers())
    locals_, remotes = [], []
    for k in range(4):
        level = (z + 3 - k) % 4
        copy = pltpu.make_async_copy(part_ref.at[core, level], held.at[k], local_sem.at[k])
        copy.start()
        locals_.append(copy)
        remotes.append(
            push(
                part_ref.at[1 - core, level], sib.at[k], send.at[5, k], recv.at[5, k], (g, sibling)
            )
        )

    def ready(k):
        locals_[k].wait()
        remotes[k].wait_recv()
        for i in range(4):
            held[k, i] = held[k, i] + sib[k, i]

    out_ref[...] = reduce_planes(held, ready, x1, y1, x2, y2, zin, send, recv)
    for copy in remotes:
        copy.wait_send()


def plane_scratch(rows, columns):
    return [
        pltpu.VMEM((4, rows // 2, columns), BF),
        pltpu.VMEM((4, rows // 2, columns), BF),
        pltpu.VMEM((4, rows, columns), BF),
        pltpu.VMEM((4, rows, columns), BF),
        pltpu.VMEM((3, rows, columns), BF),
    ]


def return_rows(part, rows):
    columns = part.shape[1]
    return pl.pallas_call(
        return_kernel,
        in_specs=[pl.BlockSpec(memory_space=pl.ANY)],
        out_specs=pl.BlockSpec(memory_space=pltpu.VMEM),
        out_shape=jax.ShapeDtypeStruct((rows, columns), F32),
        scratch_shapes=[
            pltpu.VMEM((4, 4, rows, columns), BF),
            pltpu.VMEM((4, 4, rows, columns), BF),
            *plane_scratch(rows, columns),
            pltpu.SemaphoreType.DMA((4,)),
            pltpu.SemaphoreType.DMA((6, 4)),
            pltpu.SemaphoreType.DMA((6, 4)),
        ],
        compiler_params=pltpu.CompilerParams(
            collective_id=1, has_side_effects=True, vmem_limit_bytes=48 * 1024 * 1024
        ),
        name="return_rows",
    )(part.reshape(2, 4, 4, rows, columns))


def gather_kernel(pieces, count, *refs):
    sources, targets = refs[:count], refs[count : 2 * count]
    local_sem, send, recv = refs[2 * count :]
    g, m, across, along, sibling = places()
    z = m // 2
    to_x, to_y, to_s = (across, m), (along, m), (g, sibling)
    enter(plane_peers())
    total = range(len(pieces))
    ways = [(sign, hop) for hop in (1, 2, 3) for sign in (1, -1)]

    def view(piece, owner, quarter=None, part=None):
        array, first, columns, _ = pieces[piece]
        ref = targets[array]
        size = ref.shape[0] // 8
        start = owner * size
        if quarter is not None:
            size = size // 4
            start = start + quarter * size
        if part is not None:
            size = size // 2
            start = start + part * size
        return ref.at[pl.ds(start, size), pl.ds(first, columns)]

    def copy(piece, index, block, peer, src=None):
        return pltpu.make_async_remote_copy(
            src_ref=block if src is None else src,
            dst_ref=block,
            send_sem=send.at[piece, index],
            recv_sem=recv.at[piece, index],
            device_id=peer,
            device_id_type=MESH,
        )

    def line(p, way, owner, src=None):
        block = view(p, owner, g if pieces[p][3] else None)
        peer = (g, (m + 8 + 2 * ways[way][0]) % 8)
        return copy(p, way, block, peer, src)

    def has(way, hop=None):
        sign, distance = ways[way]
        distance = distance if hop is None else hop
        return z >= distance if sign > 0 else z + distance <= 3

    def more(way):
        return z <= 2 if ways[way][0] > 0 else z >= 1

    def origin(way):
        sign, distance = ways[way]
        return (m + 8 - 2 * sign * distance) % 8

    def planes(p, way):
        block = view(p, origin(way), g)
        return copy(p, 6 + way, block, to_x), copy(p, 12 + way, block, to_y)

    def corners(p, way):
        owner = origin(way)
        return (
            copy(p, 18 + way, view(p, owner, across, 0), to_y),
            copy(p, 24 + way, view(p, owner, along, 1), to_x),
        )

    def core(p, way):
        return copy(p, 30 + way, view(p, origin(way)), to_s)

    def first(p):
        array, start, columns, shared = pieces[p]
        ref = sources[array]
        whole = ref.at[:, pl.ds(start, columns)]
        src = whole
        if shared:
            quarter = ref.shape[0] // 4
            src = ref.at[pl.ds(g * quarter, quarter), pl.ds(start, columns)]
        return (
            [line(p, way, m, src) for way in (0, 1)],
            pltpu.make_async_copy(whole, view(p, m), local_sem.at[p]),
            copy(p, 36, view(p, m), to_s, whole),
        )

    for p in total:
        out, near, side = first(p)
        for way in (0, 1):
            pl.when(more(way))(out[way].start)
        near.start()
        side.start()

    def arrive(p, hop):
        for way in (2 * hop - 2, 2 * hop - 1):

            @pl.when(has(way))
            def _():
                line(p, way, origin(way)).wait_recv()
                if hop < 3:
                    pl.when(more(way))(line(p, way + 2, origin(way)).start)
                if pieces[p][3]:
                    for item in planes(p, way):
                        item.start()
                else:
                    core(p, way).start()

    def turn(p, hop):
        for way in (2 * hop - 2, 2 * hop - 1):

            @pl.when(has(way))
            def _():
                for item, after in zip(planes(p, way), corners(p, way), strict=True):
                    item.wait_recv()
                    after.start()

    def cross(p, hop):
        for way in (2 * hop - 2, 2 * hop - 1):

            @pl.when(has(way))
            def _():
                for item in corners(p, way):
                    item.wait_recv()
                core(p, way).start()

    shared = [p for p in total if pieces[p][3]]
    for hop in range(1, 6):
        for p in total:
            if hop <= 3:
                arrive(p, hop)
            if p in shared and 1 <= hop - 1 <= 3:
                turn(p, hop - 1)
            if p in shared and 1 <= hop - 2 <= 3:
                cross(p, hop - 2)
    for p in total:
        out, near, side = first(p)
        near.wait()
        side.wait()
        for way in (0, 1):
            pl.when(more(way))(out[way].wait_send)
        for way in range(6):

            @pl.when(has(way))
            def _():
                core(p, way).wait()
                if ways[way][1] < 3:
                    pl.when(more(way))(line(p, way + 2, origin(way)).wait_send)
                if pieces[p][3]:
                    for item in planes(p, way) + corners(p, way):
                        item.wait_send()


def gather_weights(arrays, chunk, own_count):
    pieces = []
    for i, x in enumerate(arrays):
        columns = x.shape[1]
        for first in range(0, columns, chunk):
            pieces.append((i, first, min(chunk, columns - first), i >= own_count))
    count = len(arrays)
    return pl.pallas_call(
        functools.partial(gather_kernel, tuple(pieces), count),
        in_specs=[pl.BlockSpec(memory_space=pl.ANY)] * count,
        out_specs=[pl.BlockSpec(memory_space=pl.ANY)] * count,
        out_shape=[jax.ShapeDtypeStruct((8 * x.shape[0], x.shape[1]), x.dtype) for x in arrays],
        scratch_shapes=[
            pltpu.SemaphoreType.DMA((len(pieces),)),
            pltpu.SemaphoreType.DMA((len(pieces), 37)),
            pltpu.SemaphoreType.DMA((len(pieces), 37)),
        ],
        compiler_params=pltpu.CompilerParams(collective_id=3, has_side_effects=True),
        name="gather_weights",
    )(*arrays)


WIDTH = HEADS * HDIM
KEYS = MHEADS * 2 * NK
QUERIES = MHEADS * 2 * HALF
F_MIXED, F_SECOND, F_ATTENDED, F_FIRST, F_COT, F_GATE, F_RESID = (i * WIDTH for i in range(7))
F_HALF = 7 * WIDTH
F_QKV = F_HALF + KEYS
F_QUERY = F_QKV + 3 * WIDTH
F_ALL = F_QUERY + QUERIES
G_OUT, G_GATE, G_PROJ, G_HALF = 0, WIDTH, 2 * WIDTH, 3 * WIDTH
G_QKV = G_HALF + KEYS
G_KEYS = G_QKV + 3 * WIDTH
G_GAIN = G_KEYS + 2 * HALF
G_ALL = G_GAIN + LANES
PRODUCTS = (
    (F_MIXED, F_COT, WIDTH, G_OUT),
    (F_SECOND, F_GATE, WIDTH, G_GATE),
    (F_ATTENDED, F_RESID, WIDTH, G_PROJ),
    (F_SECOND, F_HALF, KEYS, G_HALF),
    (F_FIRST, F_QKV, 3 * WIDTH, G_QKV),
)


def grads_kernel(
    fact_ref, gain_ref, out_ref, fact, gains, held, x1, y1, x2, y2, zin, quarter, local_sem, send, recv
):
    g, m, across, along, sibling = places()
    core, z = m % 2, m // 2
    rows = fact_ref.shape[0]
    enter(plane_peers())
    copies = []
    for i, (src, dst, count) in enumerate(((fact_ref, fact, rows), (gain_ref, gains, 16))):
        near = pltpu.make_async_copy(src, dst.at[pl.ds(0, count)], local_sem.at[i])
        near.start()
        far = push(
            src, dst.at[pl.ds(count, count)], send.at[5, i], recv.at[5, i], (g, sibling)
        )
        copies.append((near, far))
    for near, far in copies:
        near.wait()
        far.wait_recv()
    row = iota((32, LANES), 0) % 16
    column = iota((32, LANES), 1)
    select = ((row < 4) & (row // 2 == column)).astype(F32).astype(BF)
    chunk = WIDTH

    def ready(k):
        block = (z + 3 - k) % 4 * 2 + core

        def store(value, at):
            for i in range(4):
                held[k, i, :, at : at + value.shape[1]] = value[i * 32 : (i + 1) * 32].astype(BF)

        for left, right, count, at in PRODUCTS:
            lhs = fact[:, pl.ds(pl.multiple_of(left + block * LANES, LANES), LANES)]
            for j in range(0, count, chunk):
                store(dot(lhs, fact[:, right + j : right + j + chunk], TN), at + j)
        lhs = fact[:, pl.ds(pl.multiple_of(F_HALF + block * NK, LANES), NK)]
        rhs = fact[:, pl.ds(pl.multiple_of(F_QUERY + block * HALF, LANES), HALF)]
        value = dot(lhs, rhs, TN)
        for i in range(4):
            for h in range(2):
                first = i * 64 + h * 32
                held[k, i, :, G_KEYS + h * HALF : G_KEYS + (h + 1) * HALF] = value[
                    first : first + 32
                ].astype(BF)
        lhs = gains[:, pl.ds(pl.multiple_of(block * LANES, LANES), LANES)]
        store(dot(lhs, select, TN), G_GAIN)

    total = reduce_planes(held, ready, x1, y1, x2, y2, zin, send, recv)
    quarter[g] = total.astype(BF)
    to_x, to_y = (across, m), (along, m)
    low, high = pl.ds(0, 16), pl.ds(16, 16)
    a = push(quarter.at[g], quarter.at[g], send.at[6, 0], recv.at[6, 0], to_x)
    b = push(quarter.at[g], quarter.at[g], send.at[6, 1], recv.at[6, 1], to_y)
    a.wait_recv()
    c = push(quarter.at[across, low], quarter.at[across, low], send.at[6, 2], recv.at[6, 2], to_y)
    b.wait_recv()
    d = push(quarter.at[along, high], quarter.at[along, high], send.at[6, 3], recv.at[6, 3], to_x)
    c.wait_recv()
    d.wait_recv()
    for copy in (a, b, c, d):
        copy.wait_send()
    for _, far in copies:
        far.wait_send()
    out_ref[...] = quarter[...]


def reduce_grads(factors, gains):
    rows = factors.shape[0]
    return pl.pallas_call(
        grads_kernel,
        in_specs=[pl.BlockSpec(memory_space=pl.ANY)] * 2,
        out_specs=pl.BlockSpec(memory_space=pltpu.VMEM),
        out_shape=jax.ShapeDtypeStruct((4, 32, G_ALL), BF),
        scratch_shapes=[
            pltpu.VMEM((2 * rows, F_ALL), BF),
            pltpu.VMEM((32, WIDTH), BF),
            pltpu.VMEM((4, 4, 32, G_ALL), BF),
            *plane_scratch(32, G_ALL),
            pltpu.VMEM((4, 32, G_ALL), BF),
            pltpu.SemaphoreType.DMA((2,)),
            pltpu.SemaphoreType.DMA((7, 4)),
            pltpu.SemaphoreType.DMA((7, 4)),
        ],
        compiler_params=pltpu.CompilerParams(
            collective_id=2, has_side_effects=True, vmem_limit_bytes=56 * 1024 * 1024
        ),
        name="reduce_grads",
    )(factors, gains).reshape(4 * 32, G_ALL)


def rms_scale(values):
    return lax.rsqrt(jnp.mean(values * values, axis=-1, keepdims=True) + EPS)


def rms_back(values, scale, gain, grad):
    scaled = grad * gain
    inner = jnp.mean(values * scaled, axis=-1, keepdims=True)
    gain_grad = jnp.sum(grad * values * scale, axis=0)
    return scale * scaled - values * (scale * scale * scale * inner), gain_grad


def per_device(
    tokens,
    segment_ids,
    picks,
    attn_gain,
    qkv_weight,
    attn_proj,
    mem_gain,
    query_weight,
    half_keys,
    memory_values,
    gate_weight,
    out_weight,
    out_cotangent,
):
    rows, width = tokens.shape
    owners = lax.axis_size("grp") * lax.axis_size("mem")
    local_rows = memory_values.shape[0]
    total_picks = rows * MHEADS * TOPK
    flat_bits = (total_picks - 1).bit_length()
    capacity = 2 * total_picks // owners
    group_len = segment_ids.shape[0]
    linked = (lax.axis_size("grp"), lax.axis_size("mem"), rows) == (4, 8, LANES)
    position = lax.axis_index("mem").astype(jnp.int32)
    pos = position.reshape(1)

    def gather(x, axes="mem"):
        return lax.all_gather(x, axes, axis=0, tiled=True)

    if linked:
        gain_block = jnp.concatenate(
            [attn_gain[None], mem_gain[None], jnp.zeros((14, LANES), BF)]
        )
        (
            tokens_all,
            gains,
            qkv_full,
            proj_full,
            keys_full,
            query_full,
            gate_full,
            output_full,
        ) = gather_weights(
            (
                tokens,
                gain_block,
                qkv_weight,
                attn_proj,
                half_keys,
                query_weight,
                gate_weight,
                out_weight,
            ),
            2 * width,
            2,
        )
        gains = gains.reshape(8, 16, LANES)[:, :2].transpose(1, 0, 2).reshape(2, width)
    else:
        gains = lax.all_gather(jnp.stack([attn_gain, mem_gain]), "mem", axis=1, tiled=True)
        tokens_all = gather(tokens)
        qkv_full = gather(qkv_weight)
        proj_full = gather(attn_proj)
        query_full = gather(query_weight)
        keys_full = gather(half_keys)
        gate_full = gather(gate_weight)
        output_full = gather(out_weight)
    gains = gains.astype(F32)
    gain_one, gain_two = gains[0:1], gains[1:2]

    requests = route(picks, owners, local_rows, capacity, flat_bits)
    arrived = lax.all_to_all(requests, ALL, split_axis=0, concat_axis=0, tiled=True)

    inputs_all = tokens_all.astype(F32)
    first_all = (inputs_all * rms_scale(inputs_all) * gain_one).astype(BF)
    qkv_all = dot(first_all, qkv_full).astype(BF)
    seg_row, seg_col = segment_ids.reshape(1, group_len), segment_ids.reshape(group_len, 1)
    attn_sum, lse = attn_fwd(pos, qkv_all, seg_row, seg_col, rows)
    attended = attn_sum.astype(BF)
    inputs = tokens.astype(F32)
    residual = inputs + dot(attended, proj_full)
    scale_two = rms_scale(residual)
    second = (residual * scale_two * gain_two).astype(BF)
    mem_query = dot(second, query_full).astype(BF)
    gate_pre = dot(second, gate_full)
    mixed_grad = dot(out_cotangent, output_full, NT)
    sig = jax.nn.sigmoid(gate_pre)
    gate_act = gate_pre * sig
    memory_grad = (mixed_grad * gate_act).astype(BF)
    key_table = keys_full.reshape(MHEADS * 2, NK, HALF)
    half_scores = jnp.einsum(
        "tcf,cnf->tcn",
        mem_query.reshape(rows, MHEADS * 2, HALF),
        key_table,
        preferred_element_type=F32,
    ).reshape(rows, MHEADS * 2 * NK)
    flat_picks = picks.reshape(rows, MHEADS * TOPK)
    pick_weights, weights_low = pick_fwd(half_scores, flat_picks)

    sent = gather(jnp.concatenate([memory_grad, weights_low], axis=1), ALL)
    if linked:
        part, spread = owner_call(
            arrived, sent, memory_values, flat_bits, lambda s: s % 2 * 16 + s // 2 % 4 * 4 + s // 8
        )
        back = return_rows(part, rows)
    else:
        part, spread = owner_call(arrived, sent, memory_values, flat_bits, lambda s: s)
        back = lax.psum_scatter(part, "grp", scatter_dimension=0, tiled=True)
        back = lax.psum_scatter(back, "mem", scatter_dimension=0, tiled=True)
    values_grad = jnp.einsum(
        "hkl,kd->hld", spread, sent[:, :width], preferred_element_type=F32
    ).reshape(local_rows, width)

    memory_out = back[:, :width].astype(F32)
    weight_grad = back[:, width:].astype(F32)
    mixed = (memory_out * gate_act).astype(BF)
    block_out = (residual + dot(mixed, output_full)).astype(BF)
    gate_grad = (mixed_grad * memory_out * (sig * (1.0 + gate_pre * (1.0 - sig)))).astype(BF)
    half_grad = pick_bwd(pick_weights, weight_grad, flat_picks)
    half_cube = half_grad.reshape(rows, MHEADS * 2, NK)
    query_grad = (
        jnp.einsum("tcn,cnf->tcf", half_cube, key_table, preferred_element_type=F32)
        .astype(BF)
        .reshape(rows, MHEADS * 2 * HALF)
    )
    second_grad = dot(gate_grad, gate_full, NT) + dot(query_grad, query_full, NT)
    resid_from_norm, gain_two_grad = rms_back(residual, scale_two, gain_two, second_grad)
    resid_grad = out_cotangent.astype(F32) + resid_from_norm
    resid_low = resid_grad.astype(BF)
    attn_grad = dot(resid_low, proj_full, NT).astype(BF)
    delta = jnp.sum(
        (attn_grad.astype(F32) * attn_sum).reshape(rows, HEADS, HDIM), axis=-1
    )
    stats = jnp.concatenate([lse[:, :HEADS], delta], axis=1)
    stats_high = lax.reduce_precision(stats, 8, 7)
    stats_low = stats - stats_high
    shared = gather(
        jnp.concatenate(
            [
                resid_low,
                stats_high.astype(BF),
                stats_low.astype(BF),
                jnp.zeros((rows, LANES - 4 * HEADS), BF),
            ],
            axis=1,
        )
    )
    stats_all = shared[:, width : width + 2 * HEADS].astype(F32) + shared[
        :, width + 2 * HEADS : width + 4 * HEADS
    ].astype(F32)
    attn_grad_all = dot(shared[:, :width], proj_full, NT).astype(BF)
    qkv_rows = attn_bwd(pos, qkv_all, attn_grad_all, stats_all, seg_row, seg_col, rows)
    scale_one = rms_scale(inputs)
    first_low = (inputs * scale_one * gain_one).astype(BF)
    first_grad = dot(qkv_rows, qkv_full, NT)
    input_from_norm, gain_one_grad = rms_back(inputs, scale_one, gain_one, first_grad)
    tokens_grad = resid_grad + input_from_norm

    if linked:
        factors = jnp.concatenate(
            [
                mixed,
                second,
                attended,
                first_low,
                out_cotangent,
                gate_grad,
                resid_low,
                half_grad,
                qkv_rows,
                mem_query,
            ],
            axis=1,
        )
        sums = jnp.stack([gain_one_grad, gain_two_grad])
        sums_high = lax.reduce_precision(sums, 8, 7)
        gain_rows = jnp.stack([sums_high, sums - sums_high], axis=1).reshape(4, width)
        gain_rows = jnp.concatenate([gain_rows.astype(BF), jnp.zeros((12, width), BF)])
        reduced = reduce_grads(factors, gain_rows).astype(F32)
        out_share = reduced[:, G_OUT : G_OUT + width]
        gate_share = reduced[:, G_GATE : G_GATE + width]
        proj_share = reduced[:, G_PROJ : G_PROJ + width]
        qkv_share = reduced[:, G_QKV : G_QKV + 3 * width]
        keys_share = (
            reduced[:, G_KEYS : G_KEYS + 2 * HALF]
            .reshape(4, 32, 2, HALF)
            .transpose(0, 2, 1, 3)
            .reshape(half_keys.shape)
        )
        query_share = jnp.einsum(
            "rcn,cnf->rcf",
            reduced[:, G_HALF : G_HALF + KEYS].astype(BF).reshape(rows, MHEADS * 2, NK),
            key_table,
            preferred_element_type=F32,
        ).reshape(rows, QUERIES)
        gain_sums = reduced[:, G_GAIN : G_GAIN + 2].T
    else:
        keys_grad = jnp.einsum(
            "tcn,tcf->cnf",
            half_cube,
            mem_query.reshape(rows, MHEADS * 2, HALF),
            preferred_element_type=F32,
        ).reshape(KEYS, HALF)
        partials = (
            dot(mixed, out_cotangent, TN),
            dot(second, gate_grad, TN),
            keys_grad,
            dot(second, query_grad, TN),
            dot(attended, resid_low, TN),
            dot(first_low, qkv_rows, TN),
        )
        shares = [
            lax.psum_scatter(x.astype(BF), "mem", scatter_dimension=0, tiled=True)
            for x in partials
        ]
        shares = lax.psum(tuple(shares), "grp")
        gain_sums = lax.psum(jnp.stack([gain_one_grad, gain_two_grad]), ALL)
        gain_sums = lax.dynamic_slice_in_dim(
            gain_sums, position * attn_gain.shape[0], attn_gain.shape[0], axis=1
        )
        out_share, gate_share, keys_share, query_share, proj_share, qkv_share = (
            x.astype(F32) for x in shares
        )
    return (
        block_out,
        tokens_grad,
        gain_sums[0],
        qkv_share,
        proj_share,
        gain_sums[1],
        query_share,
        keys_share,
        values_grad,
        gate_share,
        out_share,
    )


def solution(mesh):
    placed = (
        P(ALL, None),
        P("grp"),
        P(ALL, None, None),
        P("mem"),
        P("mem", None),
        P("mem", None),
        P("mem"),
        P("mem", None),
        P("mem", None),
        P(ALL, None),
        P("mem", None),
        P("mem", None),
        P(ALL, None),
    )
    return jax.shard_map(
        per_device,
        mesh=mesh,
        in_specs=placed,
        out_specs=(
            P(ALL, None),
            P(ALL, None),
            P("mem"),
            P("mem", None),
            P("mem", None),
            P("mem"),
            P("mem", None),
            P("mem", None),
            P(ALL, None),
            P("mem", None),
            P("mem", None),
        ),
        check_vma=False,
    )
```

```python
import functools

import jax
import jax.numpy as jnp
from jax import lax
from jax.experimental import pallas as pl
from jax.experimental.pallas import tpu as pltpu
from jax.sharding import PartitionSpec as P

HEADS = 16
HDIM = 64
MHEADS = 4
NK = 256
HALF = 512
TOPK = 32
EPS = 1e-05
LANES = 128
ALL = ("grp", "mem")
BF = jnp.bfloat16
F32 = jnp.float32
NEG = -1e30


def dot(left, right, dims=((1,), (0,))):
    return lax.dot_general(left, right, (dims, ((), ())), preferred_element_type=F32)


NT = ((1,), (1,))
TN = ((0,), (0,))


def iota(shape, dim):
    return lax.broadcasted_iota(jnp.int32, shape, dim)


def lane_halves(rows):
    first = iota((rows, LANES), 1) < HDIM
    return first


def half_masks():
    lane = iota((1, LANES), 1)
    return ((lane < HDIM).astype(BF), (lane >= HDIM).astype(BF))


def attn_fwd_kernel(rows, win, pos_ref, q_ref, k_ref, v_ref, qseg_ref, kseg_ref, out_ref, lse_ref):
    pair = pl.program_id(0)
    row0 = pos_ref[0] * rows
    start = pl.multiple_of(jnp.maximum(row0 + rows - win, 0), LANES)
    keys = k_ref[pl.ds(start, win), :]
    values = v_ref[pl.ds(start, win), :]
    key_pos = start + iota((rows, win), 1)
    query_pos = row0 + iota((rows, win), 0)
    allowed = (key_pos <= query_pos) & (kseg_ref[:, pl.ds(start, win)] == qseg_ref[...])
    lane = iota((rows, LANES), 1)
    masks = half_masks()
    outs = []
    lse = jnp.where(pair == 0, jnp.zeros((rows, LANES), F32), lse_ref[...])
    for half in range(2):
        scores = dot(q_ref[...] * masks[half], keys, NT) * 0.125
        scores = jnp.where(allowed, scores, NEG)
        top = jnp.max(scores, axis=1, keepdims=True)
        weights = jnp.exp(scores - top)
        total = jnp.sum(weights, axis=1, keepdims=True)
        probs = weights * (1.0 / total)
        outs.append(dot(probs.astype(BF), values))
        lse = jnp.where(lane == pair * 2 + half, top + jnp.log(total), lse)
    out_ref[...] = jnp.where(lane < HDIM, outs[0], outs[1])
    lse_ref[...] = lse


def attn_fwd(pos, qkv, seg_row, seg_col, rows):
    group_len, width = qkv.shape[0], qkv.shape[1] // 3
    pairs = width // LANES
    win = min(group_len, group_len // 2 + rows)
    return pl.pallas_call(
        functools.partial(attn_fwd_kernel, rows, win),
        grid_spec=pltpu.PrefetchScalarGridSpec(
            num_scalar_prefetch=1,
            grid=(pairs,),
            in_specs=[
                pl.BlockSpec((rows, LANES), lambda h, p: (p[0], h)),
                pl.BlockSpec((group_len, LANES), lambda h, p: (0, pairs + h)),
                pl.BlockSpec((group_len, LANES), lambda h, p: (0, 2 * pairs + h)),
                pl.BlockSpec((rows, 1), lambda h, p: (p[0], 0)),
                pl.BlockSpec((1, group_len), lambda h, p: (0, 0)),
            ],
            out_specs=[
                pl.BlockSpec((rows, LANES), lambda h, p: (0, h)),
                pl.BlockSpec((rows, LANES), lambda h, p: (0, 0)),
            ],
        ),
        out_shape=[
            jax.ShapeDtypeStruct((rows, width), F32),
            jax.ShapeDtypeStruct((rows, LANES), F32),
        ],
        cost_estimate=pl.CostEstimate(
            flops=4 * rows * win * width,
            bytes_accessed=group_len * width * 4,
            transcendentals=rows * win * HEADS,
        ),
        name="attn_fwd",
    )(pos, qkv, qkv, qkv, seg_col, seg_row)


def attn_bwd_kernel(
    rows, win, pairs, pos_ref, q_ref, k_ref, v_ref, da_ref, stat_ref, segc_ref, segr_ref, out_ref
):
    pair = pl.program_id(0)
    group_len = k_ref.shape[0]
    row0 = pl.multiple_of(pos_ref[0] * rows, LANES)
    start = pl.multiple_of(jnp.maximum(row0 + rows - win, 0), LANES)
    qstart = pl.multiple_of(jnp.minimum(row0, group_len - win), LANES)
    own, back, ahead = pl.ds(row0, rows), pl.ds(start, win), pl.ds(qstart, win)
    masks = half_masks()
    lane = iota((rows, LANES), 1)

    def stat(where, index, count):
        table = stat_ref[where, :]
        return jnp.sum(
            jnp.where(iota((count, table.shape[1]), 1) == index, table, 0.0),
            axis=1,
            keepdims=True,
        )

    allowed = (start + iota((rows, win), 1) <= row0 + iota((rows, win), 0)) & (
        segr_ref[:, back] == segc_ref[own, :]
    )
    allowed_two = (row0 + iota((win, rows), 1) <= qstart + iota((win, rows), 0)) & (
        segr_ref[:, own] == segc_ref[ahead, :]
    )
    dqs, dks, dvs = [], [], []
    for half in range(2):
        head = pair * 2 + half
        lse, delta = stat(own, head, rows), stat(own, HEADS + head, rows)
        keys = k_ref[back, :]
        scores = dot(q_ref[own, :] * masks[half], keys, NT) * 0.125
        probs = jnp.exp(jnp.where(allowed, scores - lse, NEG))
        dprobs = dot(da_ref[own, :] * masks[half], v_ref[back, :], NT)
        grads = (probs * (dprobs - delta)).astype(BF)
        dqs.append(dot(grads, keys))
        lse, delta = stat(ahead, head, win), stat(ahead, HEADS + head, win)
        queries, douts = q_ref[ahead, :], da_ref[ahead, :]
        scores = dot(queries * masks[half], k_ref[own, :], NT) * 0.125
        probs = jnp.exp(jnp.where(allowed_two, scores - lse, NEG))
        dprobs = dot(douts * masks[half], v_ref[own, :], NT)
        grads = (probs * (dprobs - delta)).astype(BF)
        dks.append(dot(grads, queries, TN))
        dvs.append(dot(probs.astype(BF), douts, TN))
    width = pairs * LANES
    for i, (parts, scale) in enumerate(((dqs, 0.125), (dks, 0.125), (dvs, 1.0))):
        column = pl.multiple_of(i * width + pair * LANES, LANES)
        out_ref[:, pl.ds(column, LANES)] = (
            jnp.where(lane < HDIM, parts[0], parts[1]) * scale
        ).astype(BF)


def attn_bwd(pos, qkv, douts, stats, seg_row, seg_col, rows):
    group_len, width = douts.shape
    pairs = width // LANES
    win = min(group_len, group_len // 2 + rows)
    return pl.pallas_call(
        functools.partial(attn_bwd_kernel, rows, win, pairs),
        grid_spec=pltpu.PrefetchScalarGridSpec(
            num_scalar_prefetch=1,
            grid=(pairs,),
            in_specs=[
                pl.BlockSpec((group_len, LANES), lambda h, p: (0, h)),
                pl.BlockSpec((group_len, LANES), lambda h, p: (0, pairs + h)),
                pl.BlockSpec((group_len, LANES), lambda h, p: (0, 2 * pairs + h)),
                pl.BlockSpec((group_len, LANES), lambda h, p: (0, h)),
                pl.BlockSpec(stats.shape, lambda h, p: (0, 0)),
                pl.BlockSpec((group_len, 1), lambda h, p: (0, 0)),
                pl.BlockSpec((1, group_len), lambda h, p: (0, 0)),
            ],
            out_specs=pl.BlockSpec((rows, 3 * width), lambda h, p: (0, 0)),
        ),
        out_shape=jax.ShapeDtypeStruct((rows, 3 * width), BF),
        cost_estimate=pl.CostEstimate(
            flops=14 * rows * win * width,
            bytes_accessed=group_len * width * 8,
            transcendentals=2 * rows * win * HEADS,
        ),
        name="attn_bwd",
    )(pos, qkv, qkv, qkv, douts, stats, seg_col, seg_row)


def by_head(lane, reduce, fill, values):
    spread = jnp.zeros_like(values)
    for c in range(MHEADS):
        inside = lane // TOPK == c
        spread = jnp.where(
            inside, reduce(jnp.where(inside, values, fill), axis=1, keepdims=True), spread
        )
    return spread


def pick_fwd_kernel(scores_ref, picks_ref, weight_ref, low_ref):
    rows = picks_ref.shape[0]
    lane = iota((rows, LANES), 1)
    picks = picks_ref[...]
    index = (picks // NK, picks % NK)
    total = jnp.zeros((rows, LANES), F32)
    for c in range(MHEADS):
        both = jnp.zeros((rows, LANES), F32)
        for e in range(2):
            base = (c * 2 + e) * NK
            for part in range(NK // LANES):
                table = scores_ref[:, base + part * LANES : base + (part + 1) * LANES]
                found = jnp.take_along_axis(table, index[e] % LANES, axis=1)
                both = both + jnp.where(index[e] // LANES == part, found, 0.0)
        total = jnp.where(lane // TOPK == c, both, total)
    top = by_head(lane, jnp.max, NEG, total)
    weights = jnp.exp(total - top)
    weights = weights / by_head(lane, jnp.sum, 0.0, weights)
    weight_ref[...] = weights
    low_ref[...] = weights.astype(BF)


def pick_fwd(half_scores, picks):
    rows = picks.shape[0]
    return pl.pallas_call(
        pick_fwd_kernel,
        out_shape=[
            jax.ShapeDtypeStruct((rows, LANES), F32),
            jax.ShapeDtypeStruct((rows, LANES), BF),
        ],
        name="pick_fwd",
    )(half_scores, picks)


def pick_bwd_kernel(weight_ref, grad_ref, picks_ref, out_ref):
    rows = picks_ref.shape[0]
    lane = iota((rows, LANES), 1)
    weights, grads, picks = weight_ref[...], grad_ref[...], picks_ref[...]
    score = (weights * (grads - by_head(lane, jnp.sum, 0.0, weights * grads))).astype(BF)
    score = score.astype(F32)
    index = (picks // NK, picks % NK)
    key = iota((rows, NK), 1)
    for c in range(MHEADS):
        totals = [jnp.zeros((rows, NK), F32) for _ in range(2)]
        for j in range(TOPK):
            column = slice(c * TOPK + j, c * TOPK + j + 1)
            for e in range(2):
                totals[e] = totals[e] + jnp.where(
                    key == index[e][:, column], score[:, column], 0.0
                )
        for e in range(2):
            base = (c * 2 + e) * NK
            out_ref[:, base : base + NK] = totals[e].astype(BF)


def pick_bwd(weights, grads, picks):
    rows = picks.shape[0]
    block = 32
    spec = pl.BlockSpec((block, LANES), lambda i: (i, 0))
    return pl.pallas_call(
        pick_bwd_kernel,
        grid=(rows // block,),
        in_specs=[spec, spec, spec],
        out_specs=pl.BlockSpec((block, MHEADS * 2 * NK), lambda i: (i, 0)),
        out_shape=jax.ShapeDtypeStruct((rows, MHEADS * 2 * NK), BF),
        name="pick_bwd",
    )(weights, grads, picks)


def owner_kernel(
    his, flat_bits, local_rows, keys_ref, sent_ref, values_ref, part_ref, spread_ref
):
    rows = part_ref.shape[0]
    width = values_ref.shape[1]
    slots = keys_ref.shape[-1]
    low_rows = local_rows // his
    key = keys_ref[0]
    flat = key & ((1 << flat_bits) - 1)
    dummy = ((key >> flat_bits) & 1) == 1
    row = (key >> (flat_bits + 1)) % local_rows
    token = flat // LANES
    pick = flat % LANES
    token = jnp.where(dummy, -1, token)
    block = jnp.where(dummy, -1, (row // low_rows) * rows + token)
    low_row = row % low_rows
    grad = sent_ref[:, :width]
    weights = sent_ref[:, width:]
    is_token = iota((rows, slots), 0) == token
    is_pick = iota((LANES, slots), 0) == pick
    token_hot = is_token.astype(F32).astype(BF)
    found = dot(weights, token_hot, TN)
    weight = jnp.sum(jnp.where(is_pick, found, 0.0), axis=0, keepdims=True)
    is_block = iota((his * rows, slots), 0) == block
    is_low = iota((low_rows, slots), 0) == low_row
    low_hot = is_low.astype(F32).astype(BF)
    spread = dot(jnp.where(is_block, weight, 0.0).astype(BF), low_hot, NT).astype(BF)
    total = jnp.zeros((rows, width), F32)
    products = []
    for h in range(his):
        table = values_ref[h * low_rows : (h + 1) * low_rows, :]
        piece = spread[h * rows : (h + 1) * rows, :]
        spread_ref[h] = piece
        total = total + dot(piece, table)
        products.append(dot(grad, table, NT).astype(BF))
    picked = dot(jnp.concatenate(products, axis=0), is_block.astype(F32).astype(BF), TN)
    picked = jnp.sum(jnp.where(is_low, picked, 0.0), axis=0, keepdims=True)
    part_ref[:, :width] = total.astype(BF)
    part_ref[:, width:] = dot(
        jnp.where(is_token, picked, 0.0).astype(BF), is_pick.astype(F32).astype(BF), NT
    ).astype(BF)


def owner_call(keys, sent, values, flat_bits):
    owners, slots = keys.shape
    rows = sent.shape[0] // owners
    local_rows, width = values.shape
    his = 4
    low_rows = local_rows // his
    return pl.pallas_call(
        functools.partial(owner_kernel, his, flat_bits, local_rows),
        grid=(owners,),
        in_specs=[
            pl.BlockSpec((1, 1, slots), lambda s: (s, 0, 0)),
            pl.BlockSpec((rows, width + LANES), lambda s: (s, 0)),
            pl.BlockSpec((local_rows, width), lambda s: (0, 0)),
        ],
        out_specs=[
            pl.BlockSpec((rows, width + LANES), lambda s: (s, 0)),
            pl.BlockSpec((his, rows, low_rows), lambda s: (0, s, 0)),
        ],
        out_shape=[
            jax.ShapeDtypeStruct((owners * rows, width + LANES), BF),
            jax.ShapeDtypeStruct((his, owners * rows, low_rows), BF),
        ],
        compiler_params=pltpu.CompilerParams(vmem_limit_bytes=48 * 1024 * 1024),
        cost_estimate=pl.CostEstimate(
            flops=2 * owners * rows * local_rows * (2 * slots + 2 * width),
            bytes_accessed=owners * rows * (2 * width + local_rows) * 2,
            transcendentals=0,
        ),
        name="owner",
    )(keys.reshape(owners, 1, slots), sent, values)


def route(picks, owners, local_rows, capacity, flat_bits):
    total = picks.size
    rows_of = picks.reshape(total)
    flat = jnp.arange(total, dtype=jnp.int32)
    each = jnp.arange(owners, dtype=jnp.int32)
    counts = jnp.sum((rows_of[:, None] // local_rows == each[None, :]).astype(jnp.int32), axis=0)
    ends = jnp.cumsum(capacity - counts)
    spares = owners * capacity - total
    spare_owner = jnp.sum(
        (jnp.arange(spares, dtype=jnp.int32)[:, None] >= ends[None, :]).astype(jnp.int32), axis=1
    )
    real = (rows_of << (flat_bits + 1)) + flat
    spare = ((spare_owner * local_rows + local_rows - 1) << (flat_bits + 1)) + (1 << flat_bits)
    keys = lax.sort(jnp.concatenate([real, spare]))
    return keys.reshape(owners, capacity)


MESH = pl.DeviceIdType.MESH


def places():
    g, m = lax.axis_index("grp"), lax.axis_index("mem")
    across = g + 1 - 2 * (g % 2)
    along = (g + 2) % 4
    sibling = m + 1 - 2 * (m % 2)
    return g, m, across, along, sibling


def enter(peers):
    barrier = pltpu.get_barrier_semaphore()
    for peer in peers:
        pl.semaphore_signal(barrier, inc=1, device_id=peer, device_id_type=MESH)
    pl.semaphore_wait(barrier, len(peers))


def push(src, dst, send, recv, peer):
    copy = pltpu.make_async_remote_copy(
        src_ref=src, dst_ref=dst, send_sem=send, recv_sem=recv, device_id=peer, device_id_type=MESH
    )
    copy.start()
    return copy


def reduce_planes(held, ready, x1, y1, x2, y2, zin, send, recv):
    g, m, across, along, _ = places()
    diagonal = 3 - g
    half = held.shape[2] // 2
    low, high = pl.ds(0, half), pl.ds(half, half)
    to_x, to_y = (across, m), (along, m)
    sent, ones, twos, threes = [], [], [], []
    for k in range(4):
        ready(k)
        a = push(held.at[k, diagonal, low], x1.at[k], send.at[0, k], recv.at[0, k], to_x)
        b = push(held.at[k, diagonal, high], y1.at[k], send.at[1, k], recv.at[1, k], to_y)
        ones.append((a, b))
    for k in range(4):
        a, b = ones[k]
        a.wait_recv()
        b.wait_recv()
        held[k, along, low] = held[k, along, low] + x1[k]
        held[k, across, high] = held[k, across, high] + y1[k]
        a = push(held.at[k, across], x2.at[k], send.at[2, k], recv.at[2, k], to_x)
        b = push(held.at[k, along], y2.at[k], send.at[3, k], recv.at[3, k], to_y)
        twos.append((a, b))
    total = None
    for k in range(4):
        a, b = twos[k]
        a.wait_recv()
        b.wait_recv()
        total = held[k, g].astype(F32) + x2[k].astype(F32) + y2[k].astype(F32)
        if k < 3:
            held[k, g] = total.astype(BF)
            peer = (g, (m + 2 * (3 - k)) % 8)
            threes.append(push(held.at[k, g], zin.at[k], send.at[4, k], recv.at[4, k], peer))
    for k in range(3):
        threes[k].wait_recv()
        total = total + zin[k].astype(F32)
    for pair in ones + twos:
        sent.extend(pair)
    for copy in sent + threes:
        copy.wait_send()
    return total


def plane_peers():
    g, m, across, along, sibling = places()
    return [(across, m), (along, m), (g, sibling)] + [(g, (m + 2 * d) % 8) for d in (1, 2, 3)]


def plane_scratch(rows, columns):
    return [
        pltpu.VMEM((4, rows // 2, columns), BF),
        pltpu.VMEM((4, rows // 2, columns), BF),
        pltpu.VMEM((4, rows, columns), BF),
        pltpu.VMEM((4, rows, columns), BF),
        pltpu.VMEM((3, rows, columns), BF),
    ]


def memory_kernel(
    flat_bits,
    payload_ref,
    keys_ref,
    picks_ref,
    values_ref,
    out_ref,
    spread_ref,
    sent_ref,
    sent,
    parts,
    sibs,
    x1,
    y1,
    x2,
    y2,
    zin,
    held,
    spread,
    own_sem,
    spread_sem,
    sent_sem,
    send,
    recv,
):
    g, m, across, along, sibling = places()
    core, z = m % 2, m // 2
    to_x, to_y, to_s = (across, m), (along, m), (g, sibling)
    rows, columns = payload_ref.shape
    width = columns - LANES
    local_rows = values_ref.shape[0]
    slots = keys_ref.shape[1]
    his = spread.shape[1]
    low_rows = local_rows // his
    low, high = pl.ds(0, rows // 2), pl.ds(rows // 2, rows // 2)
    enter(plane_peers())

    def copy(kind, index, src, dst, peer):
        return pltpu.make_async_remote_copy(
            src_ref=src,
            dst_ref=dst,
            send_sem=send.at[kind, index],
            recv_sem=recv.at[kind, index],
            device_id=peer,
            device_id_type=MESH,
        )

    def mine(i):
        return payload_ref if i == 0 else sent.at[i, core]

    def to_sibling(i):
        return copy(0, i, mine(i), sent.at[i, core], to_s)

    def plane_x(k):
        return copy(1, k, mine(4 * k), sent.at[4 * k + 1, core], to_x)

    def plane_y(k):
        return copy(2, k, mine(4 * k), sent.at[4 * k + 2, core], to_y)

    def line(k):
        return copy(3, k, payload_ref, sent.at[4 * k, core], (g, (m + 2 * k) % 8))

    def corner_y(k):
        return copy(4, k, sent.at[4 * k + 1, core, low], sent.at[4 * k + 3, core, low], to_y)

    def corner_x(k):
        return copy(5, k, sent.at[4 * k + 2, core, high], sent.at[4 * k + 3, core, high], to_x)

    def part_sibling(i):
        return copy(6, i, parts.at[i, 1 - core], sibs.at[i], to_s)

    def one_x(k):
        return copy(7, k, parts.at[4 * k + 3, core, low], x1.at[k], to_x)

    def one_y(k):
        return copy(8, k, parts.at[4 * k + 3, core, high], y1.at[k], to_y)

    def two_x(k):
        return copy(9, k, parts.at[4 * k + 1, core], x2.at[k], to_x)

    def two_y(k):
        return copy(10, k, parts.at[4 * k + 2, core], y2.at[k], to_y)

    def three(k):
        return copy(11, k, parts.at[4 * k, core], zin.at[k - 1], (g, (m + 8 - 2 * k) % 8))

    def from_line(k):
        line(k).wait_recv()
        plane_x(k).start()
        plane_y(k).start()
        to_sibling(4 * k).start()

    def from_plane(k):
        plane_x(k).wait_recv()
        corner_y(k).start()
        to_sibling(4 * k + 1).start()
        plane_y(k).wait_recv()
        corner_x(k).start()
        to_sibling(4 * k + 2).start()

    def from_corner(k):
        corner_x(k).wait_recv()
        corner_y(k).wait_recv()
        to_sibling(4 * k + 3).start()

    def pair_sum(k):
        for i in (4 * k + 3, 4 * k + 1, 4 * k + 2, 4 * k):
            part_sibling(i).wait_recv()
            parts[i, core] = parts[i, core] + sibs[i]
            if i == 4 * k + 3:
                one_x(k).start()
                one_y(k).start()

    def corner_sum(k):
        one_x(k).wait_recv()
        parts[4 * k + 2, core, low] = parts[4 * k + 2, core, low] + x1[k]
        two_y(k).start()
        one_y(k).wait_recv()
        parts[4 * k + 1, core, high] = parts[4 * k + 1, core, high] + y1[k]
        two_x(k).start()

    def plane_sum(k):
        two_x(k).wait_recv()
        two_y(k).wait_recv()
        total = parts[4 * k, core].astype(F32) + x2[k].astype(F32) + y2[k].astype(F32)
        if k == 0:
            held[...] = total
        else:
            parts[4 * k, core] = total.astype(BF)
            three(k).start()

    own = pltpu.make_async_copy(payload_ref, sent.at[0, core], own_sem)
    own.start()
    to_sibling(0).start()
    plane_x(0).start()
    plane_y(0).start()
    for k in (1, 2, 3):
        line(k).start()
    own.wait()

    tasks = {
        1: [lambda: from_plane(0)],
        2: [lambda: from_line(1)],
        3: [lambda: from_corner(0), lambda: from_line(2)],
        4: [lambda: from_line(3), lambda: pair_sum(0)],
        5: [lambda: from_plane(1)],
        6: [lambda: corner_sum(0)],
        7: [lambda: from_corner(1)],
        8: [lambda: from_plane(2), lambda: pair_sum(1)],
        9: [lambda: plane_sum(0)],
        10: [lambda: from_corner(2), lambda: corner_sum(1)],
        11: [lambda: from_plane(3)],
        12: [lambda: pair_sum(2), lambda: plane_sum(1)],
        13: [lambda: from_corner(3)],
        14: [lambda: corner_sum(2)],
    }

    def spread_copy(i, buffer):
        return pltpu.make_async_copy(
            spread.at[buffer],
            spread_ref.at[:, pl.ds(pl.multiple_of(i * 2 * rows, 2 * rows), 2 * rows), :],
            spread_sem.at[buffer],
        )

    def step(i, _):
        for when, todo in tasks.items():

            @pl.when(i == when)
            def _():
                for task in todo:
                    task()

        copy(0, i, sent.at[i, core], sent.at[i, 1 - core], to_s).wait_recv()
        pltpu.make_async_copy(sent.at[i], sent_ref.at[i], sent_sem.at[i]).start()
        buffer = i % 2
        pl.when(i >= 2)(lambda: spread_copy(i - 2, buffer).wait())
        k, j = i // 4, i % 4
        grp = (g // 2 + j // 2) % 2 * 2 + (g % 2 + j % 2) % 2
        base = grp * 8 + (z + 4 - k) % 4 * 2
        local = picks_ref[pl.ds(pl.multiple_of(base * rows, 2 * rows), 2 * rows), :]
        local = local - (g * 8 + m) * local_rows
        lane, tile = local % LANES, local // LANES
        for c in range(2):
            key = keys_ref[pl.ds(base + c, 1), :]
            flat = key & ((1 << flat_bits) - 1)
            dummy = ((key >> flat_bits) & 1) == 1
            row = (key >> (flat_bits + 1)) % local_rows
            token = jnp.where(dummy, -1, flat // LANES)
            block = jnp.where(dummy, -1, (row // low_rows) * rows + token)
            is_token = iota((rows, slots), 0) == token
            is_pick = iota((LANES, slots), 0) == flat % LANES
            weights = sent[i, c, :, width:]
            found = dot(weights, is_token.astype(F32).astype(BF), TN)
            weight = jnp.sum(jnp.where(is_pick, found, 0.0), axis=0, keepdims=True)
            is_block = iota((his * rows, slots), 0) == block
            is_low = iota((low_rows, slots), 0) == row % low_rows
            piece = dot(
                jnp.where(is_block, weight, 0.0).astype(BF), is_low.astype(F32).astype(BF), NT
            ).astype(BF)
            for h in range(his):
                spread[buffer, h, c * rows : (c + 1) * rows, :] = piece[h * rows : (h + 1) * rows]
        grads = sent[i, :, :, :width].reshape(2 * rows, width)
        total = jnp.zeros((2 * rows, width), F32)
        picked = jnp.zeros((2 * rows, LANES), F32)
        for h in range(his):
            table = values_ref[h * low_rows : (h + 1) * low_rows, :]
            total = total + dot(spread[buffer, h], table)
            products = dot(grads, table, NT)
            for b in range(low_rows // LANES):
                found = jnp.take_along_axis(
                    products[:, b * LANES : (b + 1) * LANES], lane, axis=1
                )
                picked = jnp.where(tile == h * (low_rows // LANES) + b, found, picked)
        parts[i, :, :, :width] = total.astype(BF).reshape(2, rows, width)
        parts[i, :, :, width:] = picked.astype(BF).reshape(2, rows, LANES)
        part_sibling(i).start()
        spread_copy(i, buffer).start()
        return 0

    lax.fori_loop(0, 16, step, 0)
    plane_sum(2)
    pair_sum(3)
    corner_sum(3)
    plane_sum(3)
    total = held[...]
    for k in (1, 2, 3):
        three(k).wait_recv()
        total = total + zin[k - 1].astype(F32)
    out_ref[...] = total
    for k in range(4):
        todo = [plane_x(k), plane_y(k), corner_x(k), corner_y(k)]
        todo += [one_x(k), one_y(k), two_x(k), two_y(k)]
        if k:
            todo += [line(k), three(k)]
        for j in range(4):
            todo += [to_sibling(4 * k + j), part_sibling(4 * k + j)]
        for item in todo:
            item.wait_send()
    for i in (14, 15):
        spread_copy(i, i % 2).wait()
    for i in range(16):
        pltpu.make_async_copy(sent.at[i], sent_ref.at[i], sent_sem.at[i]).wait()


def memory_call(payload, keys, picks, values, flat_bits):
    rows, columns = payload.shape
    local_rows = values.shape[0]
    his = 4
    half = (4, rows // 2, columns)
    full = (4, rows, columns)
    vmem = pl.BlockSpec(memory_space=pltpu.VMEM)
    hbm = pl.BlockSpec(memory_space=pl.ANY)
    return pl.pallas_call(
        functools.partial(memory_kernel, flat_bits),
        in_specs=[hbm, vmem, vmem, vmem],
        out_specs=[vmem, hbm, hbm],
        out_shape=[
            jax.ShapeDtypeStruct((rows, columns), F32),
            jax.ShapeDtypeStruct((his, 32 * rows, local_rows // his), BF),
            jax.ShapeDtypeStruct((16, 2, rows, columns), BF),
        ],
        scratch_shapes=[
            pltpu.VMEM((16, 2, rows, columns), BF),
            pltpu.VMEM((16, 2, rows, columns), BF),
            pltpu.VMEM((16, rows, columns), BF),
            pltpu.VMEM(half, BF),
            pltpu.VMEM(half, BF),
            pltpu.VMEM(full, BF),
            pltpu.VMEM(full, BF),
            pltpu.VMEM((3, rows, columns), BF),
            pltpu.VMEM((rows, columns), F32),
            pltpu.VMEM((2, his, 2 * rows, local_rows // his), BF),
            pltpu.SemaphoreType.DMA,
            pltpu.SemaphoreType.DMA((2,)),
            pltpu.SemaphoreType.DMA((16,)),
            pltpu.SemaphoreType.DMA((12, 16)),
            pltpu.SemaphoreType.DMA((12, 16)),
        ],
        compiler_params=pltpu.CompilerParams(
            collective_id=1, has_side_effects=True, vmem_limit_bytes=60 * 1024 * 1024
        ),
        name="memory",
    )(payload, keys, picks, values)


def gather_kernel(pieces, count, *refs):
    sources, targets = refs[:count], refs[count : 2 * count]
    local_sem, send, recv = refs[2 * count :]
    g, m, across, along, sibling = places()
    z = m // 2
    to_x, to_y, to_s = (across, m), (along, m), (g, sibling)
    enter(plane_peers())
    total = range(len(pieces))
    ways = [(sign, hop) for hop in (1, 2, 3) for sign in (1, -1)]

    def view(piece, owner, quarter=None, part=None):
        array, first, columns, _ = pieces[piece]
        ref = targets[array]
        size = ref.shape[0] // 8
        start = owner * size
        if quarter is not None:
            size = size // 4
            start = start + quarter * size
        if part is not None:
            size = size // 2
            start = start + part * size
        return ref.at[pl.ds(start, size), pl.ds(first, columns)]

    def copy(piece, index, block, peer, src=None):
        return pltpu.make_async_remote_copy(
            src_ref=block if src is None else src,
            dst_ref=block,
            send_sem=send.at[piece, index],
            recv_sem=recv.at[piece, index],
            device_id=peer,
            device_id_type=MESH,
        )

    def line(p, way, owner, src=None):
        block = view(p, owner, g if pieces[p][3] else None)
        peer = (g, (m + 8 + 2 * ways[way][0]) % 8)
        return copy(p, way, block, peer, src)

    def has(way, hop=None):
        sign, distance = ways[way]
        distance = distance if hop is None else hop
        return z >= distance if sign > 0 else z + distance <= 3

    def more(way):
        return z <= 2 if ways[way][0] > 0 else z >= 1

    def origin(way):
        sign, distance = ways[way]
        return (m + 8 - 2 * sign * distance) % 8

    def planes(p, way):
        block = view(p, origin(way), g)
        return copy(p, 6 + way, block, to_x), copy(p, 12 + way, block, to_y)

    def corners(p, way):
        owner = origin(way)
        return (
            copy(p, 18 + way, view(p, owner, across, 0), to_y),
            copy(p, 24 + way, view(p, owner, along, 1), to_x),
        )

    def core(p, way):
        return copy(p, 30 + way, view(p, origin(way)), to_s)

    def first(p):
        array, start, columns, shared = pieces[p]
        ref = sources[array]
        whole = ref.at[:, pl.ds(start, columns)]
        src = whole
        if shared:
            quarter = ref.shape[0] // 4
            src = ref.at[pl.ds(g * quarter, quarter), pl.ds(start, columns)]
        return (
            [line(p, way, m, src) for way in (0, 1)],
            pltpu.make_async_copy(whole, view(p, m), local_sem.at[p]),
            copy(p, 36, view(p, m), to_s, whole),
        )

    for p in total:
        out, near, side = first(p)
        for way in (0, 1):
            pl.when(more(way))(out[way].start)
        near.start()
        side.start()

    def arrive(p, hop):
        for way in (2 * hop - 2, 2 * hop - 1):

            @pl.when(has(way))
            def _():
                line(p, way, origin(way)).wait_recv()
                if hop < 3:
                    pl.when(more(way))(line(p, way + 2, origin(way)).start)
                if pieces[p][3]:
                    for item in planes(p, way):
                        item.start()
                else:
                    core(p, way).start()

    def turn(p, hop):
        for way in (2 * hop - 2, 2 * hop - 1):

            @pl.when(has(way))
            def _():
                for item, after in zip(planes(p, way), corners(p, way), strict=True):
                    item.wait_recv()
                    after.start()

    def cross(p, hop):
        for way in (2 * hop - 2, 2 * hop - 1):

            @pl.when(has(way))
            def _():
                for item in corners(p, way):
                    item.wait_recv()
                core(p, way).start()

    shared = [p for p in total if pieces[p][3]]
    for hop in range(1, 6):
        for p in total:
            if hop <= 3:
                arrive(p, hop)
            if p in shared and 1 <= hop - 1 <= 3:
                turn(p, hop - 1)
            if p in shared and 1 <= hop - 2 <= 3:
                cross(p, hop - 2)
    for p in total:
        out, near, side = first(p)
        near.wait()
        side.wait()
        for way in (0, 1):
            pl.when(more(way))(out[way].wait_send)
        for way in range(6):

            @pl.when(has(way))
            def _():
                core(p, way).wait()
                if ways[way][1] < 3:
                    pl.when(more(way))(line(p, way + 2, origin(way)).wait_send)
                if pieces[p][3]:
                    for item in planes(p, way) + corners(p, way):
                        item.wait_send()


def gather_weights(arrays, chunk, own_count):
    pieces = []
    for i, x in enumerate(arrays):
        columns = x.shape[1]
        for first in range(0, columns, chunk):
            pieces.append((i, first, min(chunk, columns - first), i >= own_count))
    count = len(arrays)
    return pl.pallas_call(
        functools.partial(gather_kernel, tuple(pieces), count),
        in_specs=[pl.BlockSpec(memory_space=pl.ANY)] * count,
        out_specs=[pl.BlockSpec(memory_space=pl.ANY)] * count,
        out_shape=[jax.ShapeDtypeStruct((8 * x.shape[0], x.shape[1]), x.dtype) for x in arrays],
        scratch_shapes=[
            pltpu.SemaphoreType.DMA((len(pieces),)),
            pltpu.SemaphoreType.DMA((len(pieces), 37)),
            pltpu.SemaphoreType.DMA((len(pieces), 37)),
        ],
        compiler_params=pltpu.CompilerParams(collective_id=3, has_side_effects=True),
        name="gather_weights",
    )(*arrays)


WIDTH = HEADS * HDIM
KEYS = MHEADS * 2 * NK
QUERIES = MHEADS * 2 * HALF
F_MIXED, F_SECOND, F_ATTENDED, F_FIRST, F_COT, F_GATE, F_RESID = (i * WIDTH for i in range(7))
F_HALF = 7 * WIDTH
F_QKV = F_HALF + KEYS
F_QUERY = F_QKV + 3 * WIDTH
F_ALL = F_QUERY + QUERIES
G_OUT, G_GATE, G_PROJ, G_HALF = 0, WIDTH, 2 * WIDTH, 3 * WIDTH
G_QKV = G_HALF + KEYS
G_KEYS = G_QKV + 3 * WIDTH
G_GAIN = G_KEYS + 2 * HALF
G_ALL = G_GAIN + LANES
PRODUCTS = (
    (F_MIXED, F_COT, WIDTH, G_OUT),
    (F_SECOND, F_GATE, WIDTH, G_GATE),
    (F_ATTENDED, F_RESID, WIDTH, G_PROJ),
    (F_SECOND, F_HALF, KEYS, G_HALF),
    (F_FIRST, F_QKV, 3 * WIDTH, G_QKV),
)


def grads_kernel(
    fact_ref, gain_ref, out_ref, fact, gains, held, x1, y1, x2, y2, zin, quarter, local_sem, send, recv
):
    g, m, across, along, sibling = places()
    core, z = m % 2, m // 2
    rows = fact_ref.shape[0]
    enter(plane_peers())
    copies = []
    for i, (src, dst, count) in enumerate(((fact_ref, fact, rows), (gain_ref, gains, 16))):
        near = pltpu.make_async_copy(src, dst.at[pl.ds(0, count)], local_sem.at[i])
        near.start()
        far = push(
            src, dst.at[pl.ds(count, count)], send.at[5, i], recv.at[5, i], (g, sibling)
        )
        copies.append((near, far))
    for near, far in copies:
        near.wait()
        far.wait_recv()
    row = iota((32, LANES), 0) % 16
    column = iota((32, LANES), 1)
    select = ((row < 4) & (row // 2 == column)).astype(F32).astype(BF)
    chunk = WIDTH

    def ready(k):
        block = (z + 3 - k) % 4 * 2 + core

        def store(value, at):
            for i in range(4):
                held[k, i, :, at : at + value.shape[1]] = value[i * 32 : (i + 1) * 32].astype(BF)

        for left, right, count, at in PRODUCTS:
            lhs = fact[:, pl.ds(pl.multiple_of(left + block * LANES, LANES), LANES)]
            for j in range(0, count, chunk):
                store(dot(lhs, fact[:, right + j : right + j + chunk], TN), at + j)
        lhs = fact[:, pl.ds(pl.multiple_of(F_HALF + block * NK, LANES), NK)]
        rhs = fact[:, pl.ds(pl.multiple_of(F_QUERY + block * HALF, LANES), HALF)]
        value = dot(lhs, rhs, TN)
        for i in range(4):
            for h in range(2):
                first = i * 64 + h * 32
                held[k, i, :, G_KEYS + h * HALF : G_KEYS + (h + 1) * HALF] = value[
                    first : first + 32
                ].astype(BF)
        lhs = gains[:, pl.ds(pl.multiple_of(block * LANES, LANES), LANES)]
        store(dot(lhs, select, TN), G_GAIN)

    total = reduce_planes(held, ready, x1, y1, x2, y2, zin, send, recv)
    quarter[g] = total.astype(BF)
    to_x, to_y = (across, m), (along, m)
    low, high = pl.ds(0, 16), pl.ds(16, 16)
    a = push(quarter.at[g], quarter.at[g], send.at[6, 0], recv.at[6, 0], to_x)
    b = push(quarter.at[g], quarter.at[g], send.at[6, 1], recv.at[6, 1], to_y)
    a.wait_recv()
    c = push(quarter.at[across, low], quarter.at[across, low], send.at[6, 2], recv.at[6, 2], to_y)
    b.wait_recv()
    d = push(quarter.at[along, high], quarter.at[along, high], send.at[6, 3], recv.at[6, 3], to_x)
    c.wait_recv()
    d.wait_recv()
    for copy in (a, b, c, d):
        copy.wait_send()
    for _, far in copies:
        far.wait_send()
    out_ref[...] = quarter[...]


def reduce_grads(factors, gains):
    rows = factors.shape[0]
    return pl.pallas_call(
        grads_kernel,
        in_specs=[pl.BlockSpec(memory_space=pl.ANY)] * 2,
        out_specs=pl.BlockSpec(memory_space=pltpu.VMEM),
        out_shape=jax.ShapeDtypeStruct((4, 32, G_ALL), BF),
        scratch_shapes=[
            pltpu.VMEM((2 * rows, F_ALL), BF),
            pltpu.VMEM((32, WIDTH), BF),
            pltpu.VMEM((4, 4, 32, G_ALL), BF),
            *plane_scratch(32, G_ALL),
            pltpu.VMEM((4, 32, G_ALL), BF),
            pltpu.SemaphoreType.DMA((2,)),
            pltpu.SemaphoreType.DMA((7, 4)),
            pltpu.SemaphoreType.DMA((7, 4)),
        ],
        compiler_params=pltpu.CompilerParams(
            collective_id=2, has_side_effects=True, vmem_limit_bytes=56 * 1024 * 1024
        ),
        name="reduce_grads",
    )(factors, gains).reshape(4 * 32, G_ALL)


def rms_scale(values):
    return lax.rsqrt(jnp.mean(values * values, axis=-1, keepdims=True) + EPS)


def rms_back(values, scale, gain, grad):
    scaled = grad * gain
    inner = jnp.mean(values * scaled, axis=-1, keepdims=True)
    gain_grad = jnp.sum(grad * values * scale, axis=0)
    return scale * scaled - values * (scale * scale * scale * inner), gain_grad


def per_device(
    tokens,
    segment_ids,
    picks,
    attn_gain,
    qkv_weight,
    attn_proj,
    mem_gain,
    query_weight,
    half_keys,
    memory_values,
    gate_weight,
    out_weight,
    out_cotangent,
):
    rows, width = tokens.shape
    owners = lax.axis_size("grp") * lax.axis_size("mem")
    local_rows = memory_values.shape[0]
    total_picks = rows * MHEADS * TOPK
    flat_bits = (total_picks - 1).bit_length()
    capacity = 2 * total_picks // owners
    group_len = segment_ids.shape[0]
    linked = (lax.axis_size("grp"), lax.axis_size("mem"), rows) == (4, 8, LANES)
    position = lax.axis_index("mem").astype(jnp.int32)
    pos = position.reshape(1)

    def gather(x, axes="mem"):
        return lax.all_gather(x, axes, axis=0, tiled=True)

    flat_picks = picks.reshape(rows, MHEADS * TOPK)
    if linked:
        picks_all = gather(flat_picks, ALL)
        gain_block = jnp.concatenate(
            [attn_gain[None], mem_gain[None], jnp.zeros((14, LANES), BF)]
        )
        (
            tokens_all,
            gains,
            qkv_full,
            proj_full,
            keys_full,
            query_full,
            gate_full,
            output_full,
        ) = gather_weights(
            (
                tokens,
                gain_block,
                qkv_weight,
                attn_proj,
                half_keys,
                query_weight,
                gate_weight,
                out_weight,
            ),
            2 * width,
            2,
        )
        gains = gains.reshape(8, 16, LANES)[:, :2].transpose(1, 0, 2).reshape(2, width)
    else:
        gains = lax.all_gather(jnp.stack([attn_gain, mem_gain]), "mem", axis=1, tiled=True)
        tokens_all = gather(tokens)
        qkv_full = gather(qkv_weight)
        proj_full = gather(attn_proj)
        query_full = gather(query_weight)
        keys_full = gather(half_keys)
        gate_full = gather(gate_weight)
        output_full = gather(out_weight)
    gains = gains.astype(F32)
    gain_one, gain_two = gains[0:1], gains[1:2]

    requests = route(picks, owners, local_rows, capacity, flat_bits)
    arrived = lax.all_to_all(requests, ALL, split_axis=0, concat_axis=0, tiled=True)

    inputs_all = tokens_all.astype(F32)
    first_all = (inputs_all * rms_scale(inputs_all) * gain_one).astype(BF)
    qkv_all = dot(first_all, qkv_full).astype(BF)
    seg_row, seg_col = segment_ids.reshape(1, group_len), segment_ids.reshape(group_len, 1)
    attn_sum, lse = attn_fwd(pos, qkv_all, seg_row, seg_col, rows)
    attended = attn_sum.astype(BF)
    inputs = tokens.astype(F32)
    residual = inputs + dot(attended, proj_full)
    scale_two = rms_scale(residual)
    second = (residual * scale_two * gain_two).astype(BF)
    mem_query = dot(second, query_full).astype(BF)
    gate_pre = dot(second, gate_full)
    mixed_grad = dot(out_cotangent, output_full, NT)
    sig = jax.nn.sigmoid(gate_pre)
    gate_act = gate_pre * sig
    memory_grad = (mixed_grad * gate_act).astype(BF)
    key_table = keys_full.reshape(MHEADS * 2, NK, HALF)
    half_scores = jnp.einsum(
        "tcf,cnf->tcn",
        mem_query.reshape(rows, MHEADS * 2, HALF),
        key_table,
        preferred_element_type=F32,
    ).reshape(rows, MHEADS * 2 * NK)
    pick_weights, weights_low = pick_fwd(half_scores, flat_picks)

    payload = jnp.concatenate([memory_grad, weights_low], axis=1)
    if linked:
        back, spread, sent = memory_call(payload, arrived, picks_all, memory_values, flat_bits)
        sent = sent.reshape(owners * rows, width + LANES)
    else:
        sent = gather(payload, ALL)
        part, spread = owner_call(arrived, sent, memory_values, flat_bits)
        back = lax.psum_scatter(part, "grp", scatter_dimension=0, tiled=True)
        back = lax.psum_scatter(back, "mem", scatter_dimension=0, tiled=True)
    values_grad = jnp.einsum(
        "hkl,kd->hld", spread, sent[:, :width], preferred_element_type=F32
    ).reshape(local_rows, width)

    memory_out = back[:, :width].astype(F32)
    weight_grad = back[:, width:].astype(F32)
    mixed = (memory_out * gate_act).astype(BF)
    block_out = (residual + dot(mixed, output_full)).astype(BF)
    gate_grad = (mixed_grad * memory_out * (sig * (1.0 + gate_pre * (1.0 - sig)))).astype(BF)
    half_grad = pick_bwd(pick_weights, weight_grad, flat_picks)
    half_cube = half_grad.reshape(rows, MHEADS * 2, NK)
    query_grad = (
        jnp.einsum("tcn,cnf->tcf", half_cube, key_table, preferred_element_type=F32)
        .astype(BF)
        .reshape(rows, MHEADS * 2 * HALF)
    )
    second_grad = dot(gate_grad, gate_full, NT) + dot(query_grad, query_full, NT)
    resid_from_norm, gain_two_grad = rms_back(residual, scale_two, gain_two, second_grad)
    resid_grad = out_cotangent.astype(F32) + resid_from_norm
    resid_low = resid_grad.astype(BF)
    attn_grad = dot(resid_low, proj_full, NT).astype(BF)
    delta = jnp.sum(
        (attn_grad.astype(F32) * attn_sum).reshape(rows, HEADS, HDIM), axis=-1
    )
    stats = jnp.concatenate([lse[:, :HEADS], delta], axis=1)
    stats_high = lax.reduce_precision(stats, 8, 7)
    stats_low = stats - stats_high
    shared = gather(
        jnp.concatenate(
            [
                resid_low,
                stats_high.astype(BF),
                stats_low.astype(BF),
                jnp.zeros((rows, LANES - 4 * HEADS), BF),
            ],
            axis=1,
        )
    )
    stats_all = shared[:, width : width + 2 * HEADS].astype(F32) + shared[
        :, width + 2 * HEADS : width + 4 * HEADS
    ].astype(F32)
    attn_grad_all = dot(shared[:, :width], proj_full, NT).astype(BF)
    qkv_rows = attn_bwd(pos, qkv_all, attn_grad_all, stats_all, seg_row, seg_col, rows)
    scale_one = rms_scale(inputs)
    first_low = (inputs * scale_one * gain_one).astype(BF)
    first_grad = dot(qkv_rows, qkv_full, NT)
    input_from_norm, gain_one_grad = rms_back(inputs, scale_one, gain_one, first_grad)
    tokens_grad = resid_grad + input_from_norm

    if linked:
        factors = jnp.concatenate(
            [
                mixed,
                second,
                attended,
                first_low,
                out_cotangent,
                gate_grad,
                resid_low,
                half_grad,
                qkv_rows,
                mem_query,
            ],
            axis=1,
        )
        sums = jnp.stack([gain_one_grad, gain_two_grad])
        sums_high = lax.reduce_precision(sums, 8, 7)
        gain_rows = jnp.stack([sums_high, sums - sums_high], axis=1).reshape(4, width)
        gain_rows = jnp.concatenate([gain_rows.astype(BF), jnp.zeros((12, width), BF)])
        reduced = reduce_grads(factors, gain_rows).astype(F32)
        out_share = reduced[:, G_OUT : G_OUT + width]
        gate_share = reduced[:, G_GATE : G_GATE + width]
        proj_share = reduced[:, G_PROJ : G_PROJ + width]
        qkv_share = reduced[:, G_QKV : G_QKV + 3 * width]
        keys_share = (
            reduced[:, G_KEYS : G_KEYS + 2 * HALF]
            .reshape(4, 32, 2, HALF)
            .transpose(0, 2, 1, 3)
            .reshape(half_keys.shape)
        )
        query_share = jnp.einsum(
            "rcn,cnf->rcf",
            reduced[:, G_HALF : G_HALF + KEYS].astype(BF).reshape(rows, MHEADS * 2, NK),
            key_table,
            preferred_element_type=F32,
        ).reshape(rows, QUERIES)
        gain_sums = reduced[:, G_GAIN : G_GAIN + 2].T
    else:
        keys_grad = jnp.einsum(
            "tcn,tcf->cnf",
            half_cube,
            mem_query.reshape(rows, MHEADS * 2, HALF),
            preferred_element_type=F32,
        ).reshape(KEYS, HALF)
        partials = (
            dot(mixed, out_cotangent, TN),
            dot(second, gate_grad, TN),
            keys_grad,
            dot(second, query_grad, TN),
            dot(attended, resid_low, TN),
            dot(first_low, qkv_rows, TN),
        )
        shares = [
            lax.psum_scatter(x.astype(BF), "mem", scatter_dimension=0, tiled=True)
            for x in partials
        ]
        shares = lax.psum(tuple(shares), "grp")
        gain_sums = lax.psum(jnp.stack([gain_one_grad, gain_two_grad]), ALL)
        gain_sums = lax.dynamic_slice_in_dim(
            gain_sums, position * attn_gain.shape[0], attn_gain.shape[0], axis=1
        )
        out_share, gate_share, keys_share, query_share, proj_share, qkv_share = (
            x.astype(F32) for x in shares
        )
    return (
        block_out,
        tokens_grad,
        gain_sums[0],
        qkv_share,
        proj_share,
        gain_sums[1],
        query_share,
        keys_share,
        values_grad,
        gate_share,
        out_share,
    )


def solution(mesh):
    placed = (
        P(ALL, None),
        P("grp"),
        P(ALL, None, None),
        P("mem"),
        P("mem", None),
        P("mem", None),
        P("mem"),
        P("mem", None),
        P("mem", None),
        P(ALL, None),
        P("mem", None),
        P("mem", None),
        P(ALL, None),
    )
    return jax.shard_map(
        per_device,
        mesh=mesh,
        in_specs=placed,
        out_specs=(
            P(ALL, None),
            P(ALL, None),
            P("mem"),
            P("mem", None),
            P("mem", None),
            P("mem"),
            P("mem", None),
            P("mem", None),
            P(ALL, None),
            P("mem", None),
            P("mem", None),
        ),
        check_vma=False,
    )
```

```python
import functools

import jax
import jax.numpy as jnp
from jax import lax
from jax.experimental import pallas as pl
from jax.experimental.pallas import tpu as pltpu
from jax.sharding import PartitionSpec as P

HEADS = 16
HDIM = 64
MHEADS = 4
NK = 256
HALF = 512
TOPK = 32
EPS = 1e-05
LANES = 128
ALL = ("grp", "mem")
BF = jnp.bfloat16
F32 = jnp.float32
NEG = -1e30


def dot(left, right, dims=((1,), (0,))):
    return lax.dot_general(left, right, (dims, ((), ())), preferred_element_type=F32)


NT = ((1,), (1,))
TN = ((0,), (0,))


def iota(shape, dim):
    return lax.broadcasted_iota(jnp.int32, shape, dim)


def lane_halves(rows):
    first = iota((rows, LANES), 1) < HDIM
    return first


def half_masks():
    lane = iota((1, LANES), 1)
    return ((lane < HDIM).astype(BF), (lane >= HDIM).astype(BF))


def attn_fwd_kernel(rows, win, pos_ref, q_ref, k_ref, v_ref, qseg_ref, kseg_ref, out_ref, lse_ref):
    pair = pl.program_id(0)
    row0 = pos_ref[0] * rows
    start = pl.multiple_of(jnp.maximum(row0 + rows - win, 0), LANES)
    keys = k_ref[pl.ds(start, win), :]
    values = v_ref[pl.ds(start, win), :]
    key_pos = start + iota((rows, win), 1)
    query_pos = row0 + iota((rows, win), 0)
    allowed = (key_pos <= query_pos) & (kseg_ref[:, pl.ds(start, win)] == qseg_ref[...])
    lane = iota((rows, LANES), 1)
    masks = half_masks()
    outs = []
    lse = jnp.where(pair == 0, jnp.zeros((rows, LANES), F32), lse_ref[...])
    for half in range(2):
        scores = dot(q_ref[...] * masks[half], keys, NT) * 0.125
        scores = jnp.where(allowed, scores, NEG)
        top = jnp.max(scores, axis=1, keepdims=True)
        weights = jnp.exp(scores - top)
        total = jnp.sum(weights, axis=1, keepdims=True)
        probs = weights * (1.0 / total)
        outs.append(dot(probs.astype(BF), values))
        lse = jnp.where(lane == pair * 2 + half, top + jnp.log(total), lse)
    out_ref[...] = jnp.where(lane < HDIM, outs[0], outs[1])
    lse_ref[...] = lse


def attn_fwd(pos, qkv, seg_row, seg_col, rows):
    group_len, width = qkv.shape[0], qkv.shape[1] // 3
    pairs = width // LANES
    win = min(group_len, group_len // 2 + rows)
    return pl.pallas_call(
        functools.partial(attn_fwd_kernel, rows, win),
        grid_spec=pltpu.PrefetchScalarGridSpec(
            num_scalar_prefetch=1,
            grid=(pairs,),
            in_specs=[
                pl.BlockSpec((rows, LANES), lambda h, p: (p[0], h)),
                pl.BlockSpec((group_len, LANES), lambda h, p: (0, pairs + h)),
                pl.BlockSpec((group_len, LANES), lambda h, p: (0, 2 * pairs + h)),
                pl.BlockSpec((rows, 1), lambda h, p: (p[0], 0)),
                pl.BlockSpec((1, group_len), lambda h, p: (0, 0)),
            ],
            out_specs=[
                pl.BlockSpec((rows, LANES), lambda h, p: (0, h)),
                pl.BlockSpec((rows, LANES), lambda h, p: (0, 0)),
            ],
        ),
        out_shape=[
            jax.ShapeDtypeStruct((rows, width), F32),
            jax.ShapeDtypeStruct((rows, LANES), F32),
        ],
        cost_estimate=pl.CostEstimate(
            flops=4 * rows * win * width,
            bytes_accessed=group_len * width * 4,
            transcendentals=rows * win * HEADS,
        ),
        name="attn_fwd",
    )(pos, qkv, qkv, qkv, seg_col, seg_row)


def attn_bwd_pair(rows, win, pair, position, group_len, load, stat_ref, segc_ref, segr_ref):
    row0 = pl.multiple_of(position * rows, LANES)
    start = pl.multiple_of(jnp.maximum(row0 + rows - win, 0), LANES)
    qstart = pl.multiple_of(jnp.minimum(row0, group_len - win), LANES)
    own, back, ahead = pl.ds(row0, rows), pl.ds(start, win), pl.ds(qstart, win)
    masks = half_masks()
    lane = iota((rows, LANES), 1)

    def stat(where, index, count):
        table = stat_ref[where, :]
        return jnp.sum(
            jnp.where(iota((count, table.shape[1]), 1) == index, table, 0.0),
            axis=1,
            keepdims=True,
        )

    allowed = (start + iota((rows, win), 1) <= row0 + iota((rows, win), 0)) & (
        segr_ref[:, back] == segc_ref[own, :]
    )
    allowed_two = (row0 + iota((win, rows), 1) <= qstart + iota((win, rows), 0)) & (
        segr_ref[:, own] == segc_ref[ahead, :]
    )
    dqs, dks, dvs = [], [], []
    for half in range(2):
        head = pair * 2 + half
        lse, delta = stat(own, head, rows), stat(own, HEADS + head, rows)
        keys = load(1, back)
        scores = dot(load(0, own) * masks[half], keys, NT) * 0.125
        probs = jnp.exp(jnp.where(allowed, scores - lse, NEG))
        dprobs = dot(load(3, own) * masks[half], load(2, back), NT)
        grads = (probs * (dprobs - delta)).astype(BF)
        dqs.append(dot(grads, keys))
        lse, delta = stat(ahead, head, win), stat(ahead, HEADS + head, win)
        queries, douts = load(0, ahead), load(3, ahead)
        scores = dot(queries * masks[half], load(1, own), NT) * 0.125
        probs = jnp.exp(jnp.where(allowed_two, scores - lse, NEG))
        dprobs = dot(douts * masks[half], load(2, own), NT)
        grads = (probs * (dprobs - delta)).astype(BF)
        dks.append(dot(grads, queries, TN))
        dvs.append(dot(probs.astype(BF), douts, TN))
    return [
        (jnp.where(lane < HDIM, parts[0], parts[1]) * scale).astype(BF)
        for parts, scale in ((dqs, 0.125), (dks, 0.125), (dvs, 1.0))
    ]


def attn_bwd_kernel(
    rows, win, pairs, pos_ref, q_ref, k_ref, v_ref, da_ref, stat_ref, segc_ref, segr_ref, out_ref
):
    pair = pl.program_id(0)
    refs = (q_ref, k_ref, v_ref, da_ref)
    grads = attn_bwd_pair(
        rows,
        win,
        pair,
        pos_ref[0],
        k_ref.shape[0],
        lambda which, where: refs[which][where, :],
        stat_ref,
        segc_ref,
        segr_ref,
    )
    for i, value in enumerate(grads):
        column = pl.multiple_of((i * pairs + pair) * LANES, LANES)
        out_ref[:, pl.ds(column, LANES)] = value


def attn_bwd(pos, qkv, douts, stats, seg_row, seg_col, rows):
    group_len, width = douts.shape
    pairs = width // LANES
    win = min(group_len, group_len // 2 + rows)
    return pl.pallas_call(
        functools.partial(attn_bwd_kernel, rows, win, pairs),
        grid_spec=pltpu.PrefetchScalarGridSpec(
            num_scalar_prefetch=1,
            grid=(pairs,),
            in_specs=[
                pl.BlockSpec((group_len, LANES), lambda h, p: (0, h)),
                pl.BlockSpec((group_len, LANES), lambda h, p: (0, pairs + h)),
                pl.BlockSpec((group_len, LANES), lambda h, p: (0, 2 * pairs + h)),
                pl.BlockSpec((group_len, LANES), lambda h, p: (0, h)),
                pl.BlockSpec(stats.shape, lambda h, p: (0, 0)),
                pl.BlockSpec((group_len, 1), lambda h, p: (0, 0)),
                pl.BlockSpec((1, group_len), lambda h, p: (0, 0)),
            ],
            out_specs=pl.BlockSpec((rows, 3 * width), lambda h, p: (0, 0)),
        ),
        out_shape=jax.ShapeDtypeStruct((rows, 3 * width), BF),
        cost_estimate=pl.CostEstimate(
            flops=14 * rows * win * width,
            bytes_accessed=group_len * width * 8,
            transcendentals=2 * rows * win * HEADS,
        ),
        name="attn_bwd",
    )(pos, qkv, qkv, qkv, douts, stats, seg_col, seg_row)


def by_head(lane, reduce, fill, values):
    spread = jnp.zeros_like(values)
    for c in range(MHEADS):
        inside = lane // TOPK == c
        spread = jnp.where(
            inside, reduce(jnp.where(inside, values, fill), axis=1, keepdims=True), spread
        )
    return spread


def pick_fwd_kernel(scores_ref, picks_ref, weight_ref, low_ref):
    rows = picks_ref.shape[0]
    lane = iota((rows, LANES), 1)
    picks = picks_ref[...]
    index = (picks // NK, picks % NK)
    total = jnp.zeros((rows, LANES), F32)
    for c in range(MHEADS):
        both = jnp.zeros((rows, LANES), F32)
        for e in range(2):
            base = (c * 2 + e) * NK
            for part in range(NK // LANES):
                table = scores_ref[:, base + part * LANES : base + (part + 1) * LANES]
                found = jnp.take_along_axis(table, index[e] % LANES, axis=1)
                both = both + jnp.where(index[e] // LANES == part, found, 0.0)
        total = jnp.where(lane // TOPK == c, both, total)
    top = by_head(lane, jnp.max, NEG, total)
    weights = jnp.exp(total - top)
    weights = weights / by_head(lane, jnp.sum, 0.0, weights)
    weight_ref[...] = weights
    low_ref[...] = weights.astype(BF)


def pick_fwd(half_scores, picks):
    rows = picks.shape[0]
    return pl.pallas_call(
        pick_fwd_kernel,
        out_shape=[
            jax.ShapeDtypeStruct((rows, LANES), F32),
            jax.ShapeDtypeStruct((rows, LANES), BF),
        ],
        name="pick_fwd",
    )(half_scores, picks)


def pick_bwd_kernel(weight_ref, grad_ref, picks_ref, out_ref, score_t, first_t, second_t):
    rows = picks_ref.shape[0]
    lane = iota((rows, LANES), 1)
    weights, grads = weight_ref[...], grad_ref[...]
    score = (weights * (grads - by_head(lane, jnp.sum, 0.0, weights * grads))).astype(BF)
    score_t[...] = score.astype(F32).T
    picks_t = picks_ref[...].T
    first_t[...] = picks_t // NK
    second_t[...] = picks_t % NK
    key = iota((NK, rows), 0)

    def head(c, _):
        first = jnp.zeros((NK, rows), F32)
        second = jnp.zeros((NK, rows), F32)
        for j in range(TOPK):
            at = pl.ds(c * TOPK + j, 1)
            value = score_t[at, :]
            first = first + jnp.where(key == first_t[at, :], value, 0.0)
            second = second + jnp.where(key == second_t[at, :], value, 0.0)
        for e, total in enumerate((first, second)):
            base = pl.multiple_of((c * 2 + e) * NK, LANES)
            out_ref[:, pl.ds(base, NK)] = total.T.astype(BF)
        return 0

    lax.fori_loop(0, MHEADS, head, 0)


def pick_bwd(weights, grads, picks):
    rows = picks.shape[0]
    return pl.pallas_call(
        pick_bwd_kernel,
        out_shape=jax.ShapeDtypeStruct((rows, MHEADS * 2 * NK), BF),
        scratch_shapes=[
            pltpu.VMEM((LANES, rows), F32),
            pltpu.VMEM((LANES, rows), jnp.int32),
            pltpu.VMEM((LANES, rows), jnp.int32),
        ],
        name="pick_bwd",
    )(weights, grads, picks)


def owner_kernel(
    his, flat_bits, local_rows, keys_ref, sent_ref, values_ref, part_ref, spread_ref
):
    rows = part_ref.shape[0]
    width = values_ref.shape[1]
    slots = keys_ref.shape[-1]
    low_rows = local_rows // his
    key = keys_ref[0]
    flat = key & ((1 << flat_bits) - 1)
    dummy = ((key >> flat_bits) & 1) == 1
    row = (key >> (flat_bits + 1)) % local_rows
    token = flat // LANES
    pick = flat % LANES
    token = jnp.where(dummy, -1, token)
    block = jnp.where(dummy, -1, (row // low_rows) * rows + token)
    low_row = row % low_rows
    grad = sent_ref[:, :width]
    weights = sent_ref[:, width:]
    is_token = iota((rows, slots), 0) == token
    is_pick = iota((LANES, slots), 0) == pick
    token_hot = is_token.astype(F32).astype(BF)
    found = dot(weights, token_hot, TN)
    weight = jnp.sum(jnp.where(is_pick, found, 0.0), axis=0, keepdims=True)
    is_block = iota((his * rows, slots), 0) == block
    is_low = iota((low_rows, slots), 0) == low_row
    low_hot = is_low.astype(F32).astype(BF)
    spread = dot(jnp.where(is_block, weight, 0.0).astype(BF), low_hot, NT).astype(BF)
    total = jnp.zeros((rows, width), F32)
    products = []
    for h in range(his):
        table = values_ref[h * low_rows : (h + 1) * low_rows, :]
        piece = spread[h * rows : (h + 1) * rows, :]
        spread_ref[h] = piece
        total = total + dot(piece, table)
        products.append(dot(grad, table, NT).astype(BF))
    picked = dot(jnp.concatenate(products, axis=0), is_block.astype(F32).astype(BF), TN)
    picked = jnp.sum(jnp.where(is_low, picked, 0.0), axis=0, keepdims=True)
    part_ref[:, :width] = total.astype(BF)
    part_ref[:, width:] = dot(
        jnp.where(is_token, picked, 0.0).astype(BF), is_pick.astype(F32).astype(BF), NT
    ).astype(BF)


def owner_call(keys, sent, values, flat_bits):
    owners, slots = keys.shape
    rows = sent.shape[0] // owners
    local_rows, width = values.shape
    his = 4
    low_rows = local_rows // his
    return pl.pallas_call(
        functools.partial(owner_kernel, his, flat_bits, local_rows),
        grid=(owners,),
        in_specs=[
            pl.BlockSpec((1, 1, slots), lambda s: (s, 0, 0)),
            pl.BlockSpec((rows, width + LANES), lambda s: (s, 0)),
            pl.BlockSpec((local_rows, width), lambda s: (0, 0)),
        ],
        out_specs=[
            pl.BlockSpec((rows, width + LANES), lambda s: (s, 0)),
            pl.BlockSpec((his, rows, low_rows), lambda s: (0, s, 0)),
        ],
        out_shape=[
            jax.ShapeDtypeStruct((owners * rows, width + LANES), BF),
            jax.ShapeDtypeStruct((his, owners * rows, low_rows), BF),
        ],
        compiler_params=pltpu.CompilerParams(vmem_limit_bytes=48 * 1024 * 1024),
        cost_estimate=pl.CostEstimate(
            flops=2 * owners * rows * local_rows * (2 * slots + 2 * width),
            bytes_accessed=owners * rows * (2 * width + local_rows) * 2,
            transcendentals=0,
        ),
        name="owner",
    )(keys.reshape(owners, 1, slots), sent, values)


def route(picks, owners, local_rows, capacity, flat_bits):
    total = picks.size
    rows_of = picks.reshape(total)
    flat = jnp.arange(total, dtype=jnp.int32)
    each = jnp.arange(owners, dtype=jnp.int32)
    counts = jnp.sum((rows_of[:, None] // local_rows == each[None, :]).astype(jnp.int32), axis=0)
    ends = jnp.cumsum(capacity - counts)
    spares = owners * capacity - total
    spare_owner = jnp.sum(
        (jnp.arange(spares, dtype=jnp.int32)[:, None] >= ends[None, :]).astype(jnp.int32), axis=1
    )
    real = (rows_of << (flat_bits + 1)) + flat
    spare = ((spare_owner * local_rows + local_rows - 1) << (flat_bits + 1)) + (1 << flat_bits)
    keys = lax.sort(jnp.concatenate([real, spare]), is_stable=False)
    return keys.reshape(owners, capacity)


MESH = pl.DeviceIdType.MESH


def places():
    g, m = lax.axis_index("grp"), lax.axis_index("mem")
    across = g + 1 - 2 * (g % 2)
    along = (g + 2) % 4
    sibling = m + 1 - 2 * (m % 2)
    return g, m, across, along, sibling


def enter(peers):
    barrier = pltpu.get_barrier_semaphore()
    for peer in peers:
        pl.semaphore_signal(barrier, inc=1, device_id=peer, device_id_type=MESH)
    pl.semaphore_wait(barrier, len(peers))


def push(src, dst, send, recv, peer):
    copy = pltpu.make_async_remote_copy(
        src_ref=src, dst_ref=dst, send_sem=send, recv_sem=recv, device_id=peer, device_id_type=MESH
    )
    copy.start()
    return copy


def plane_tasks(held, x1, y1, x2, y2, zin, send, recv):
    g, m, across, along, _ = places()
    diagonal = 3 - g
    half = held.shape[2] // 2
    low, high = pl.ds(0, half), pl.ds(half, half)
    to_x, to_y = (across, m), (along, m)
    ones, twos, threes, totals = {}, {}, {}, {}

    def first(k):
        ones[k] = (
            push(held.at[k, diagonal, low], x1.at[k], send.at[0, k], recv.at[0, k], to_x),
            push(held.at[k, diagonal, high], y1.at[k], send.at[1, k], recv.at[1, k], to_y),
        )

    def corner(k):
        for copy in ones[k]:
            copy.wait_recv()
        held[k, along, low] = held[k, along, low] + x1[k]
        held[k, across, high] = held[k, across, high] + y1[k]
        twos[k] = (
            push(held.at[k, across], x2.at[k], send.at[2, k], recv.at[2, k], to_x),
            push(held.at[k, along], y2.at[k], send.at[3, k], recv.at[3, k], to_y),
        )

    def plane(k):
        for copy in twos[k]:
            copy.wait_recv()
        total = held[k, g].astype(F32) + x2[k].astype(F32) + y2[k].astype(F32)
        if k == 3:
            totals[k] = total
        else:
            held[k, g] = total.astype(BF)
            peer = (g, (m + 2 * (3 - k)) % 8)
            threes[k] = push(held.at[k, g], zin.at[k], send.at[4, k], recv.at[4, k], peer)

    def last():
        total = totals[3]
        for k in range(3):
            threes[k].wait_recv()
            total = total + zin[k].astype(F32)
        for k in range(4):
            for copy in ones[k] + twos[k]:
                copy.wait_send()
            if k < 3:
                threes[k].wait_send()
        return total

    return first, corner, plane, last


def plane_peers():
    g, m, across, along, sibling = places()
    return [(across, m), (along, m), (g, sibling)] + [(g, (m + 2 * d) % 8) for d in (1, 2, 3)]


def plane_scratch(rows, columns):
    return [
        pltpu.VMEM((4, rows // 2, columns), BF),
        pltpu.VMEM((4, rows // 2, columns), BF),
        pltpu.VMEM((4, rows, columns), BF),
        pltpu.VMEM((4, rows, columns), BF),
        pltpu.VMEM((3, rows, columns), BF),
    ]


def memory_kernel(
    flat_bits,
    payload_ref,
    keys_ref,
    values_ref,
    out_ref,
    grad_ref,
    sent,
    parts,
    sibs,
    x1,
    y1,
    x2,
    y2,
    zin,
    held,
    spread,
    table,
    own_sem,
    table_sem,
    send,
    recv,
):
    g, m, across, along, sibling = places()
    core, z = m % 2, m // 2
    to_x, to_y, to_s = (across, m), (along, m), (g, sibling)
    rows, columns = payload_ref.shape
    width = columns - LANES
    local_rows = values_ref.shape[0]
    slots = keys_ref.shape[1]
    his = spread.shape[0]
    low_rows = local_rows // his
    low, high = pl.ds(0, rows // 2), pl.ds(rows // 2, rows // 2)
    enter(plane_peers())

    def copy(kind, index, src, dst, peer):
        return pltpu.make_async_remote_copy(
            src_ref=src,
            dst_ref=dst,
            send_sem=send.at[kind, index],
            recv_sem=recv.at[kind, index],
            device_id=peer,
            device_id_type=MESH,
        )

    def mine(i):
        return payload_ref if i == 0 else sent.at[i, core]

    def to_sibling(i):
        return copy(0, i, mine(i), sent.at[i, core], to_s)

    def plane_x(k):
        return copy(1, k, mine(4 * k), sent.at[4 * k + 1, core], to_x)

    def plane_y(k):
        return copy(2, k, mine(4 * k), sent.at[4 * k + 2, core], to_y)

    def line(k):
        return copy(3, k, payload_ref, sent.at[4 * k, core], (g, (m + 2 * k) % 8))

    def corner_y(k):
        return copy(4, k, sent.at[4 * k + 1, core, low], sent.at[4 * k + 3, core, low], to_y)

    def corner_x(k):
        return copy(5, k, sent.at[4 * k + 2, core, high], sent.at[4 * k + 3, core, high], to_x)

    def part_sibling(i):
        return copy(6, i, parts.at[i, 1 - core], sibs.at[i], to_s)

    def one_x(k):
        return copy(7, k, parts.at[4 * k + 3, core, low], x1.at[k], to_x)

    def one_y(k):
        return copy(8, k, parts.at[4 * k + 3, core, high], y1.at[k], to_y)

    def two_x(k):
        return copy(9, k, parts.at[4 * k + 1, core], x2.at[k], to_x)

    def two_y(k):
        return copy(10, k, parts.at[4 * k + 2, core], y2.at[k], to_y)

    def three(k):
        return copy(11, k, parts.at[4 * k, core], zin.at[k - 1], (g, (m + 8 - 2 * k) % 8))

    def from_line(k):
        line(k).wait_recv()
        plane_x(k).start()
        plane_y(k).start()
        to_sibling(4 * k).start()

    def from_plane(k):
        plane_x(k).wait_recv()
        corner_y(k).start()
        to_sibling(4 * k + 1).start()
        plane_y(k).wait_recv()
        corner_x(k).start()
        to_sibling(4 * k + 2).start()

    def from_corner(k):
        corner_x(k).wait_recv()
        corner_y(k).wait_recv()
        to_sibling(4 * k + 3).start()

    def pair_sum(k):
        for i in (4 * k + 3, 4 * k + 1, 4 * k + 2, 4 * k):
            part_sibling(i).wait_recv()
            parts[i, core] = parts[i, core] + sibs[i]
            if i == 4 * k + 3:
                one_x(k).start()
                one_y(k).start()

    def corner_sum(k):
        one_x(k).wait_recv()
        parts[4 * k + 2, core, low] = parts[4 * k + 2, core, low] + x1[k]
        two_y(k).start()
        one_y(k).wait_recv()
        parts[4 * k + 1, core, high] = parts[4 * k + 1, core, high] + y1[k]
        two_x(k).start()

    def plane_sum(k):
        two_x(k).wait_recv()
        two_y(k).wait_recv()
        total = parts[4 * k, core].astype(F32) + x2[k].astype(F32) + y2[k].astype(F32)
        if k == 0:
            held[...] = total
        else:
            parts[4 * k, core] = total.astype(BF)
            three(k).start()

    own = pltpu.make_async_copy(payload_ref, sent.at[0, core], own_sem)
    own.start()
    to_sibling(0).start()
    plane_x(0).start()
    plane_y(0).start()
    for k in (1, 2, 3):
        line(k).start()
    own.wait()

    tasks = {
        1: [lambda: from_plane(0)],
        2: [lambda: from_line(1)],
        3: [lambda: from_corner(0), lambda: from_line(2)],
        4: [lambda: from_line(3), lambda: pair_sum(0)],
        5: [lambda: from_plane(1)],
        6: [lambda: corner_sum(0)],
        7: [lambda: from_corner(1)],
        8: [lambda: from_plane(2), lambda: pair_sum(1)],
        9: [lambda: plane_sum(0)],
        10: [lambda: from_corner(2), lambda: corner_sum(1)],
        11: [lambda: from_plane(3)],
        12: [lambda: pair_sum(2), lambda: plane_sum(1)],
        13: [lambda: from_corner(3)],
        14: [lambda: corner_sum(2)],
    }

    def step(i, _):
        for when, todo in tasks.items():

            @pl.when(i == when)
            def _():
                for task in todo:
                    task()

        copy(0, i, sent.at[i, core], sent.at[i, 1 - core], to_s).wait_recv()
        k, j = i // 4, i % 4
        grp = (g // 2 + j // 2) % 2 * 2 + (g % 2 + j % 2) % 2
        base = grp * 8 + (z + 4 - k) % 4 * 2
        lanes, tiles = [], []
        for c in range(2):
            key = keys_ref[pl.ds(base + c, 1), :]
            flat = key & ((1 << flat_bits) - 1)
            dummy = ((key >> flat_bits) & 1) == 1
            row = (key >> (flat_bits + 1)) % local_rows
            token = jnp.where(dummy, -1, flat // LANES)
            block = jnp.where(dummy, -1, (row // low_rows) * rows + token)
            is_token = iota((rows, slots), 0) == token
            is_pick = iota((LANES, slots), 0) == flat % LANES
            place = jnp.concatenate(
                [
                    jnp.where(is_token, (row % LANES).astype(F32), 0.0).astype(BF),
                    jnp.where(is_token, (row // LANES + 1).astype(F32), 0.0).astype(BF),
                ],
                axis=0,
            )
            place = dot(place, is_pick.astype(F32).astype(BF), NT).astype(jnp.int32)
            lanes.append(place[:rows])
            tiles.append(place[rows:] - 1)
            weights = sent[i, c, :, width:]
            found = dot(weights, is_token.astype(F32).astype(BF), TN)
            weight = jnp.sum(jnp.where(is_pick, found, 0.0), axis=0, keepdims=True)
            is_block = iota((his * rows, slots), 0) == block
            is_low = iota((low_rows, slots), 0) == row % low_rows
            piece = dot(
                jnp.where(is_block, weight, 0.0).astype(BF), is_low.astype(F32).astype(BF), NT
            ).astype(BF)
            for h in range(his):
                spread[h, 2 * i + c] = piece[h * rows : (h + 1) * rows]
        lane, tile = jnp.concatenate(lanes, axis=0), jnp.concatenate(tiles, axis=0)
        grads = sent[i, :, :, :width].reshape(2 * rows, width)
        total = jnp.zeros((2 * rows, width), F32)
        picked = jnp.zeros((2 * rows, LANES), F32)
        for h in range(his):
            table = values_ref[h * low_rows : (h + 1) * low_rows, :]
            piece = spread[h, pl.ds(2 * i, 2)].reshape(2 * rows, low_rows)
            total = total + dot(piece, table)
            products = dot(grads, table, NT)
            for b in range(low_rows // LANES):
                found = jnp.take_along_axis(
                    products[:, b * LANES : (b + 1) * LANES], lane, axis=1
                )
                picked = jnp.where(tile == h * (low_rows // LANES) + b, found, picked)
        parts[i, :, :, :width] = total.astype(BF).reshape(2, rows, width)
        parts[i, :, :, width:] = picked.astype(BF).reshape(2, rows, LANES)
        part_sibling(i).start()
        return 0

    def table_copy(h):
        return pltpu.make_async_copy(table.at[h % 2], grad_ref.at[h], table_sem.at[h % 2])

    def table_grad(h):
        if h >= 2:
            table_copy(h - 2).wait()

        def some(n, _):
            grads = sent[pl.ds(4 * n, 4), :, :, :width].reshape(8 * rows, width)
            piece = spread[h, pl.ds(8 * n, 8)].reshape(8 * rows, low_rows)
            table[h % 2] = jnp.where(n == 0, 0.0, table[h % 2]) + dot(piece, grads, TN)
            return 0

        lax.fori_loop(0, 4, some, 0)
        table_copy(h).start()

    lax.fori_loop(0, 16, step, 0)
    plane_sum(2)
    pair_sum(3)
    table_grad(0)
    corner_sum(3)
    table_grad(1)
    plane_sum(3)
    table_grad(2)
    table_grad(3)
    total = held[...]
    for k in (1, 2, 3):
        three(k).wait_recv()
        total = total + zin[k - 1].astype(F32)
    out_ref[...] = total
    for k in range(4):
        todo = [plane_x(k), plane_y(k), corner_x(k), corner_y(k)]
        todo += [one_x(k), one_y(k), two_x(k), two_y(k)]
        if k:
            todo += [line(k), three(k)]
        for j in range(4):
            todo += [to_sibling(4 * k + j), part_sibling(4 * k + j)]
        for item in todo:
            item.wait_send()
    table_copy(2).wait()
    table_copy(3).wait()


def memory_call(payload, keys, values, flat_bits):
    rows, columns = payload.shape
    local_rows = values.shape[0]
    his = 4
    half = (4, rows // 2, columns)
    full = (4, rows, columns)
    vmem = pl.BlockSpec(memory_space=pltpu.VMEM)
    hbm = pl.BlockSpec(memory_space=pl.ANY)
    return pl.pallas_call(
        functools.partial(memory_kernel, flat_bits),
        in_specs=[hbm, vmem, vmem],
        out_specs=[vmem, hbm],
        out_shape=[
            jax.ShapeDtypeStruct((rows, columns), F32),
            jax.ShapeDtypeStruct((his, local_rows // his, columns - LANES), F32),
        ],
        scratch_shapes=[
            pltpu.VMEM((16, 2, rows, columns), BF),
            pltpu.VMEM((16, 2, rows, columns), BF),
            pltpu.VMEM((16, rows, columns), BF),
            pltpu.VMEM(half, BF),
            pltpu.VMEM(half, BF),
            pltpu.VMEM(full, BF),
            pltpu.VMEM(full, BF),
            pltpu.VMEM((3, rows, columns), BF),
            pltpu.VMEM((rows, columns), F32),
            pltpu.VMEM((his, 32, rows, local_rows // his), BF),
            pltpu.VMEM((2, local_rows // his, columns - LANES), F32),
            pltpu.SemaphoreType.DMA,
            pltpu.SemaphoreType.DMA((2,)),
            pltpu.SemaphoreType.DMA((12, 16)),
            pltpu.SemaphoreType.DMA((12, 16)),
        ],
        compiler_params=pltpu.CompilerParams(
            collective_id=1, has_side_effects=True, vmem_limit_bytes=63 * 1024 * 1024
        ),
        name="memory",
    )(payload, keys, values)


def gather_kernel(pieces, count, *refs):
    sources, targets = refs[:count], refs[count : 2 * count]
    local_sem, send, recv = refs[2 * count :]
    g, m, across, along, sibling = places()
    z = m // 2
    to_x, to_y, to_s = (across, m), (along, m), (g, sibling)
    enter(plane_peers())
    total = range(len(pieces))
    ways = [(sign, hop) for hop in (1, 2, 3) for sign in (1, -1)]

    def view(piece, owner, quarter=None, part=None):
        array, first, columns, _ = pieces[piece]
        ref = targets[array]
        size = ref.shape[0] // 8
        start = owner * size
        if quarter is not None:
            size = size // 4
            start = start + quarter * size
        if part is not None:
            size = size // 2
            start = start + part * size
        return ref.at[pl.ds(start, size), pl.ds(first, columns)]

    def copy(piece, index, block, peer, src=None):
        return pltpu.make_async_remote_copy(
            src_ref=block if src is None else src,
            dst_ref=block,
            send_sem=send.at[piece, index],
            recv_sem=recv.at[piece, index],
            device_id=peer,
            device_id_type=MESH,
        )

    def line(p, way, owner, src=None):
        block = view(p, owner, g if pieces[p][3] else None)
        peer = (g, (m + 8 + 2 * ways[way][0]) % 8)
        return copy(p, way, block, peer, src)

    def has(way, hop=None):
        sign, distance = ways[way]
        distance = distance if hop is None else hop
        return z >= distance if sign > 0 else z + distance <= 3

    def more(way):
        return z <= 2 if ways[way][0] > 0 else z >= 1

    def origin(way):
        sign, distance = ways[way]
        return (m + 8 - 2 * sign * distance) % 8

    def planes(p, way):
        block = view(p, origin(way), g)
        return copy(p, 6 + way, block, to_x), copy(p, 12 + way, block, to_y)

    def corners(p, way):
        owner = origin(way)
        return (
            copy(p, 18 + way, view(p, owner, across, 0), to_y),
            copy(p, 24 + way, view(p, owner, along, 1), to_x),
        )

    def core(p, way):
        return copy(p, 30 + way, view(p, origin(way)), to_s)

    def first(p):
        array, start, columns, shared = pieces[p]
        ref = sources[array]
        whole = ref.at[:, pl.ds(start, columns)]
        src = whole
        if shared:
            quarter = ref.shape[0] // 4
            src = ref.at[pl.ds(g * quarter, quarter), pl.ds(start, columns)]
        return (
            [line(p, way, m, src) for way in (0, 1)],
            pltpu.make_async_copy(whole, view(p, m), local_sem.at[p]),
            copy(p, 36, view(p, m), to_s, whole),
        )

    for p in total:
        out, near, side = first(p)
        for way in (0, 1):
            pl.when(more(way))(out[way].start)
        near.start()
        side.start()

    def arrive(p, hop):
        for way in (2 * hop - 2, 2 * hop - 1):

            @pl.when(has(way))
            def _():
                line(p, way, origin(way)).wait_recv()
                if hop < 3:
                    pl.when(more(way))(line(p, way + 2, origin(way)).start)
                if pieces[p][3]:
                    for item in planes(p, way):
                        item.start()
                else:
                    core(p, way).start()

    def turn(p, hop):
        for way in (2 * hop - 2, 2 * hop - 1):

            @pl.when(has(way))
            def _():
                for item, after in zip(planes(p, way), corners(p, way), strict=True):
                    item.wait_recv()
                    after.start()

    def cross(p, hop):
        for way in (2 * hop - 2, 2 * hop - 1):

            @pl.when(has(way))
            def _():
                for item in corners(p, way):
                    item.wait_recv()
                core(p, way).start()

    shared = [p for p in total if pieces[p][3]]
    for hop in range(1, 6):
        for p in total:
            if hop <= 3:
                arrive(p, hop)
            if p in shared and 1 <= hop - 1 <= 3:
                turn(p, hop - 1)
            if p in shared and 1 <= hop - 2 <= 3:
                cross(p, hop - 2)
    for p in total:
        out, near, side = first(p)
        near.wait()
        side.wait()
        for way in (0, 1):
            pl.when(more(way))(out[way].wait_send)
        for way in range(6):

            @pl.when(has(way))
            def _():
                core(p, way).wait()
                if ways[way][1] < 3:
                    pl.when(more(way))(line(p, way + 2, origin(way)).wait_send)
                if pieces[p][3]:
                    for item in planes(p, way) + corners(p, way):
                        item.wait_send()


def gather_weights(arrays, chunk, own_count):
    pieces = []
    for i, x in enumerate(arrays):
        columns = x.shape[1]
        for first in range(0, columns, chunk):
            pieces.append((i, first, min(chunk, columns - first), i >= own_count))
    count = len(arrays)
    return pl.pallas_call(
        functools.partial(gather_kernel, tuple(pieces), count),
        in_specs=[pl.BlockSpec(memory_space=pl.ANY)] * count,
        out_specs=[pl.BlockSpec(memory_space=pl.ANY)] * count,
        out_shape=[jax.ShapeDtypeStruct((8 * x.shape[0], x.shape[1]), x.dtype) for x in arrays],
        scratch_shapes=[
            pltpu.SemaphoreType.DMA((len(pieces),)),
            pltpu.SemaphoreType.DMA((len(pieces), 37)),
            pltpu.SemaphoreType.DMA((len(pieces), 37)),
        ],
        compiler_params=pltpu.CompilerParams(collective_id=3, has_side_effects=True),
        name="gather_weights",
    )(*arrays)


WIDTH = HEADS * HDIM
KEYS = MHEADS * 2 * NK
QUERIES = MHEADS * 2 * HALF
EARLY = (WIDTH,) * 6 + (KEYS, QUERIES)
EARLY_PRODUCTS = (
    (0, 3 * WIDTH, WIDTH, 0),
    (WIDTH, 4 * WIDTH, WIDTH, WIDTH),
    (2 * WIDTH, 5 * WIDTH, WIDTH, 2 * WIDTH),
    (WIDTH, 6 * WIDTH, KEYS, 3 * WIDTH),
)
E_OUT, E_GATE, E_PROJ, E_HALF = 0, WIDTH, 2 * WIDTH, 3 * WIDTH
E_KEYS = E_HALF + KEYS
E_ALL = E_KEYS + 2 * HALF
LATE = (WIDTH, 3 * WIDTH)
LATE_PRODUCTS = ((0, WIDTH, 3 * WIDTH, 0),)
L_GAIN = 3 * WIDTH
L_ALL = L_GAIN + LANES


def share_factors(moves, local_sem, send, recv):
    g, _, _, _, sibling = places()
    copies = []
    for i, (src, dst, at, columns) in enumerate(moves):
        count = src.shape[0]
        where = pl.ds(at, columns)
        far = push(
            src, dst.at[pl.ds(count, count), where], send.at[5, i], recv.at[5, i], (g, sibling)
        )
        near = pltpu.make_async_copy(src, dst.at[pl.ds(0, count), where], local_sem.at[i])
        near.start()
        copies.append((near, far))
    return copies


def factor_moves(refs, widths, fact):
    moves, at = [], 0
    for ref, columns in zip(refs, widths, strict=True):
        moves.append((ref, fact, at, columns))
        at += columns
    return moves


def store_blocks(held, k, value, at):
    for i in range(4):
        held[k, i, :, at : at + value.shape[1]] = value[i * 32 : (i + 1) * 32].astype(BF)


def block_of(k):
    m = lax.axis_index("mem")
    return (m // 2 + 3 - k) % 4 * 2 + m % 2


def products_of(k, fact, held, products):
    block = block_of(k)
    for left, right, count, at in products:
        lhs = fact[:, pl.ds(pl.multiple_of(left + block * LANES, LANES), LANES)]
        for j in range(0, count, WIDTH):
            store_blocks(held, k, dot(lhs, fact[:, right + j : right + j + WIDTH], TN), at + j)


def spread_quarters(total, quarter, send, recv):
    g, m, across, along, _ = places()
    quarter[g] = total.astype(BF)
    to_x, to_y = (across, m), (along, m)
    low, high = pl.ds(0, 16), pl.ds(16, 16)
    a = push(quarter.at[g], quarter.at[g], send.at[6, 0], recv.at[6, 0], to_x)
    b = push(quarter.at[g], quarter.at[g], send.at[6, 1], recv.at[6, 1], to_y)
    a.wait_recv()
    c = push(quarter.at[across, low], quarter.at[across, low], send.at[6, 2], recv.at[6, 2], to_y)
    b.wait_recv()
    d = push(quarter.at[along, high], quarter.at[along, high], send.at[6, 3], recv.at[6, 3], to_x)
    c.wait_recv()
    d.wait_recv()
    for copy in (a, b, c, d):
        copy.wait_send()


def late_kernel(
    first_ref, rows_ref, gain_ref, out_ref, fact, gains, held, x1, y1, x2, y2, zin, quarter, *sems
):
    local_sem, send, recv = sems
    enter(plane_peers())
    moves = factor_moves((first_ref, rows_ref), LATE, fact)
    copies = share_factors([*moves, (gain_ref, gains, 0, WIDTH)], local_sem, send, recv)
    first, corner, plane, last = plane_tasks(held, x1, y1, x2, y2, zin, send, recv)
    for near, far in copies:
        near.wait()
        far.wait_recv()
    row = iota((32, LANES), 0) % 16
    column = iota((32, LANES), 1)
    select = ((row < 4) & (row // 2 == column)).astype(F32).astype(BF)
    for k in range(4):
        products_of(k, fact, held, LATE_PRODUCTS)
        lhs = gains[:, pl.ds(pl.multiple_of(block_of(k) * LANES, LANES), LANES)]
        store_blocks(held, k, dot(lhs, select, TN), L_GAIN)
        first(k)
    for k in range(4):
        corner(k)
    for k in range(4):
        plane(k)
    spread_quarters(last(), quarter, send, recv)
    for _, far in copies:
        far.wait_send()
    out_ref[...] = quarter[...]


def reduce_late(first, qkv_rows, gains):
    rows = first.shape[0]
    return pl.pallas_call(
        late_kernel,
        in_specs=[pl.BlockSpec(memory_space=pl.ANY)] * 3,
        out_specs=pl.BlockSpec(memory_space=pltpu.VMEM),
        out_shape=jax.ShapeDtypeStruct((4, 32, L_ALL), BF),
        scratch_shapes=[
            pltpu.VMEM((2 * rows, sum(LATE)), BF),
            pltpu.VMEM((32, WIDTH), BF),
            pltpu.VMEM((4, 4, 32, L_ALL), BF),
            *plane_scratch(32, L_ALL),
            pltpu.VMEM((4, 32, L_ALL), BF),
            pltpu.SemaphoreType.DMA((3,)),
            pltpu.SemaphoreType.DMA((7, 4)),
            pltpu.SemaphoreType.DMA((7, 4)),
        ],
        compiler_params=pltpu.CompilerParams(
            collective_id=2, has_side_effects=True, vmem_limit_bytes=40 * 1024 * 1024
        ),
        name="reduce_late",
    )(first, qkv_rows, gains).reshape(4 * 32, L_ALL)


def back_kernel(rows, win, *refs):
    fact_refs, refs = refs[: len(EARLY)], refs[len(EARLY) :]
    shared_ref, qkv_ref, proj_ref, segc_ref, segr_ref, out_ref, rows_ref = refs[:7]
    fact, held, x1, y1, x2, y2, zin, quarter, shared, douts, stats = refs[7:18]
    local_sem, send, recv = refs[18:]
    g, m, _, _, sibling = places()
    to_s = (g, sibling)
    pairs = WIDTH // LANES
    enter(plane_peers())

    def part(owner):
        return shared.at[pl.ds(pl.multiple_of(owner * rows, LANES), rows)]

    def move(index, src, owner, peer):
        return pltpu.make_async_remote_copy(
            src_ref=src,
            dst_ref=part(owner),
            send_sem=send.at[7, index],
            recv_sem=recv.at[7, index],
            device_id=peer,
            device_id_type=MESH,
        )

    def origin(d):
        return (m + 8 - 2 * d) % 8

    lines = [move(d, shared_ref, m, (g, (m + 2 * d) % 8)) for d in (1, 2, 3)]
    side = move(0, shared_ref, m, to_s)
    forward = [move(3 + d, part(origin(d)), origin(d), to_s) for d in (1, 2, 3)]
    own = pltpu.make_async_copy(shared_ref, part(m), local_sem.at[len(EARLY)])
    for copy in lines:
        copy.start()
    side.start()
    own.start()
    copies = share_factors(factor_moves(fact_refs, EARLY, fact), local_sem, send, recv)
    first, corner, plane, last = plane_tasks(held, x1, y1, x2, y2, zin, send, recv)
    for near, far in copies:
        near.wait()
        far.wait_recv()
    for k in range(4):
        products_of(k, fact, held, EARLY_PRODUCTS)
        block = block_of(k)
        lhs = fact[:, pl.ds(pl.multiple_of(6 * WIDTH + block * NK, LANES), NK)]
        at = 6 * WIDTH + KEYS
        rhs = fact[:, pl.ds(pl.multiple_of(at + block * HALF, LANES), HALF)]
        value = dot(lhs, rhs, TN)
        for i in range(4):
            for h in range(2):
                row = i * 64 + h * 32
                held[k, i, :, E_KEYS + h * HALF : E_KEYS + (h + 1) * HALF] = value[
                    row : row + 32
                ].astype(BF)
        first(k)
    corner(0)
    for copy, after in zip(lines, forward, strict=True):
        copy.wait_recv()
        after.start()
    corner(1)
    own.wait()
    side.wait_recv()
    for copy in forward:
        copy.wait_recv()
    corner(2)
    for i in range(0, shared.shape[0], 2 * rows):
        where = slice(i, i + 2 * rows)
        douts[where, :] = dot(shared[where, :WIDTH], proj_ref[...], NT).astype(BF)
        stats[where, :] = shared[where, WIDTH : WIDTH + 2 * HEADS].astype(F32) + shared[
            where, WIDTH + 2 * HEADS : WIDTH + 4 * HEADS
        ].astype(F32)
    corner(3)

    def load_of(pair):
        def load(which, where):
            ref, base = (douts, 0) if which == 3 else (qkv_ref, which * pairs)
            return ref[where, pl.ds(pl.multiple_of((base + pair) * LANES, LANES), LANES)]

        return load

    def attend(pair, _):
        grads = attn_bwd_pair(
            rows, win, pair, m, shared.shape[0], load_of(pair), stats, segc_ref, segr_ref
        )
        for i, value in enumerate(grads):
            column = pl.multiple_of((i * pairs + pair) * LANES, LANES)
            rows_ref[:, pl.ds(column, LANES)] = value
        return 0

    for k in range(4):
        lax.fori_loop(2 * k, 2 * k + 2, attend, 0)
        plane(k)
    spread_quarters(last(), quarter, send, recv)
    for _, far in copies:
        far.wait_send()
    for copy in [*lines, side, *forward]:
        copy.wait_send()
    out_ref[...] = quarter[...]


def reduce_back(factors, shared, qkv, proj, seg_col, seg_row):
    rows = factors[0].shape[0]
    group_len = qkv.shape[0]
    win = min(group_len, group_len // 2 + rows)
    hbm = pl.BlockSpec(memory_space=pl.ANY)
    vmem = pl.BlockSpec(memory_space=pltpu.VMEM)
    count = len(EARLY)
    sums, qkv_rows = pl.pallas_call(
        functools.partial(back_kernel, rows, win),
        in_specs=[hbm] * (count + 1) + [vmem] * 4,
        out_specs=[vmem, vmem],
        out_shape=[
            jax.ShapeDtypeStruct((4, 32, E_ALL), BF),
            jax.ShapeDtypeStruct((rows, 3 * WIDTH), BF),
        ],
        scratch_shapes=[
            pltpu.VMEM((2 * rows, sum(EARLY)), BF),
            pltpu.VMEM((4, 4, 32, E_ALL), BF),
            *plane_scratch(32, E_ALL),
            pltpu.VMEM((4, 32, E_ALL), BF),
            pltpu.VMEM((group_len, WIDTH + LANES), BF),
            pltpu.VMEM((group_len, WIDTH), BF),
            pltpu.VMEM((group_len, 2 * HEADS), F32),
            pltpu.SemaphoreType.DMA((count + 1,)),
            pltpu.SemaphoreType.DMA((8, count)),
            pltpu.SemaphoreType.DMA((8, count)),
        ],
        compiler_params=pltpu.CompilerParams(
            collective_id=4, has_side_effects=True, vmem_limit_bytes=56 * 1024 * 1024
        ),
        name="reduce_back",
    )(*factors, shared, qkv, proj, seg_col, seg_row)
    return sums.reshape(4 * 32, E_ALL), qkv_rows


def finish_kernel(
    early_ref, late_ref, keys_ref, table_ref, out, gate, proj, qkv, query, half, gains, whole, sem
):
    copy = pltpu.make_async_copy(table_ref, whole, sem)
    copy.start()
    for ref, first in ((out, E_OUT), (gate, E_GATE), (proj, E_PROJ)):
        ref[...] = early_ref[:, first : first + WIDTH].astype(F32)
    qkv[...] = late_ref[:, : 3 * WIDTH].astype(F32)
    for c in range(MHEADS * 2):
        table = keys_ref[c * NK : (c + 1) * NK, :]
        query[:, c * HALF : (c + 1) * HALF] = dot(
            early_ref[:, E_HALF + c * NK : E_HALF + (c + 1) * NK], table
        )
    for i in range(4):
        for h in range(2):
            first = i * 64 + h * 32
            half[first : first + 32, :] = early_ref[
                i * 32 : (i + 1) * 32, E_KEYS + h * HALF : E_KEYS + (h + 1) * HALF
            ].astype(F32)
    gains[...] = late_ref[:, L_GAIN:].astype(F32).T[:8]
    copy.wait()


def finish(early, late, keys, table):
    rows = early.shape[0]
    shapes = [(rows, WIDTH)] * 3 + [(rows, 3 * WIDTH), (rows, QUERIES), (2 * rows, HALF)]
    shapes.append((8, LANES))
    vmem, hbm = pl.BlockSpec(memory_space=pltpu.VMEM), pl.BlockSpec(memory_space=pl.ANY)
    return pl.pallas_call(
        finish_kernel,
        in_specs=[vmem, vmem, vmem, hbm],
        out_specs=[vmem] * len(shapes) + [hbm],
        out_shape=[jax.ShapeDtypeStruct(shape, F32) for shape in [*shapes, table.shape]],
        scratch_shapes=[pltpu.SemaphoreType.DMA],
        compiler_params=pltpu.CompilerParams(vmem_limit_bytes=40 * 1024 * 1024),
        name="finish",
    )(early, late, keys, table)


def rms_scale(values):
    return lax.rsqrt(jnp.mean(values * values, axis=-1, keepdims=True) + EPS)


def rms_back(values, scale, gain, grad):
    scaled = grad * gain
    inner = jnp.mean(values * scaled, axis=-1, keepdims=True)
    gain_grad = jnp.sum(grad * values * scale, axis=0)
    return scale * scaled - values * (scale * scale * scale * inner), gain_grad


def per_device(
    tokens,
    segment_ids,
    picks,
    attn_gain,
    qkv_weight,
    attn_proj,
    mem_gain,
    query_weight,
    half_keys,
    memory_values,
    gate_weight,
    out_weight,
    out_cotangent,
):
    rows, width = tokens.shape
    owners = lax.axis_size("grp") * lax.axis_size("mem")
    local_rows = memory_values.shape[0]
    total_picks = rows * MHEADS * TOPK
    flat_bits = (total_picks - 1).bit_length()
    capacity = 2 * total_picks // owners
    group_len = segment_ids.shape[0]
    linked = (lax.axis_size("grp"), lax.axis_size("mem"), rows) == (4, 8, LANES)
    position = lax.axis_index("mem").astype(jnp.int32)
    pos = position.reshape(1)

    def gather(x, axes="mem"):
        return lax.all_gather(x, axes, axis=0, tiled=True)

    flat_picks = picks.reshape(rows, MHEADS * TOPK)
    if linked:
        gain_block = jnp.concatenate(
            [attn_gain[None], mem_gain[None], jnp.zeros((14, LANES), BF)]
        )
        (
            tokens_all,
            gains,
            qkv_full,
            proj_full,
            keys_full,
            query_full,
            gate_full,
            output_full,
        ) = gather_weights(
            (
                tokens,
                gain_block,
                qkv_weight,
                attn_proj,
                half_keys,
                query_weight,
                gate_weight,
                out_weight,
            ),
            2 * width,
            2,
        )
        gains = gains.reshape(8, 16, LANES)[:, :2].transpose(1, 0, 2).reshape(2, width)
    else:
        gains = lax.all_gather(jnp.stack([attn_gain, mem_gain]), "mem", axis=1, tiled=True)
        tokens_all = gather(tokens)
        qkv_full = gather(qkv_weight)
        proj_full = gather(attn_proj)
        query_full = gather(query_weight)
        keys_full = gather(half_keys)
        gate_full = gather(gate_weight)
        output_full = gather(out_weight)
    gains = gains.astype(F32)
    gain_one, gain_two = gains[0:1], gains[1:2]

    requests = route(picks, owners, local_rows, capacity, flat_bits)
    arrived = lax.all_to_all(requests, ALL, split_axis=0, concat_axis=0, tiled=True)

    inputs_all = tokens_all.astype(F32)
    first_all = (inputs_all * rms_scale(inputs_all) * gain_one).astype(BF)
    qkv_all = dot(first_all, qkv_full).astype(BF)
    seg_row, seg_col = segment_ids.reshape(1, group_len), segment_ids.reshape(group_len, 1)
    attn_sum, lse = attn_fwd(pos, qkv_all, seg_row, seg_col, rows)
    attended = attn_sum.astype(BF)
    inputs = tokens.astype(F32)
    residual = inputs + dot(attended, proj_full)
    scale_two = rms_scale(residual)
    second = (residual * scale_two * gain_two).astype(BF)
    mem_query = dot(second, query_full).astype(BF)
    gate_pre = dot(second, gate_full)
    mixed_grad = dot(out_cotangent, output_full, NT)
    sig = jax.nn.sigmoid(gate_pre)
    gate_act = gate_pre * sig
    memory_grad = (mixed_grad * gate_act).astype(BF)
    key_table = keys_full.reshape(MHEADS * 2, NK, HALF)
    half_scores = jnp.einsum(
        "tcf,cnf->tcn",
        mem_query.reshape(rows, MHEADS * 2, HALF),
        key_table,
        preferred_element_type=F32,
    ).reshape(rows, MHEADS * 2 * NK)
    pick_weights, weights_low = pick_fwd(half_scores, flat_picks)

    payload = jnp.concatenate([memory_grad, weights_low], axis=1)
    if linked:
        back, values_grad = memory_call(payload, arrived, memory_values, flat_bits)
    else:
        sent = gather(payload, ALL)
        part, spread = owner_call(arrived, sent, memory_values, flat_bits)
        back = lax.psum_scatter(part, "grp", scatter_dimension=0, tiled=True)
        back = lax.psum_scatter(back, "mem", scatter_dimension=0, tiled=True)
        values_grad = jnp.einsum(
            "hkl,kd->hld", spread, sent[:, :width], preferred_element_type=F32
        )
    values_grad = values_grad.reshape(local_rows, width)

    memory_out = back[:, :width].astype(F32)
    weight_grad = back[:, width:].astype(F32)
    mixed = (memory_out * gate_act).astype(BF)
    block_out = (residual + dot(mixed, output_full)).astype(BF)
    gate_grad = (mixed_grad * memory_out * (sig * (1.0 + gate_pre * (1.0 - sig)))).astype(BF)
    half_grad = pick_bwd(pick_weights, weight_grad, flat_picks)
    half_cube = half_grad.reshape(rows, MHEADS * 2, NK)
    query_grad = (
        jnp.einsum("tcn,cnf->tcf", half_cube, key_table, preferred_element_type=F32)
        .astype(BF)
        .reshape(rows, MHEADS * 2 * HALF)
    )
    second_grad = dot(gate_grad, gate_full, NT) + dot(query_grad, query_full, NT)
    resid_from_norm, gain_two_grad = rms_back(residual, scale_two, gain_two, second_grad)
    resid_grad = out_cotangent.astype(F32) + resid_from_norm
    resid_low = resid_grad.astype(BF)
    attn_grad = dot(resid_low, proj_full, NT).astype(BF)
    heads = (iota((width, HEADS), 0) // HDIM == iota((width, HEADS), 1)).astype(F32)
    delta = jnp.dot(
        attn_grad.astype(F32) * attn_sum,
        heads,
        precision=lax.Precision.HIGHEST,
        preferred_element_type=F32,
    )
    stats = jnp.concatenate([lse[:, :HEADS], delta], axis=1)
    stats_high = lax.reduce_precision(stats, 8, 7)
    stats_low = stats - stats_high
    shared = jnp.concatenate(
        [
            resid_low,
            stats_high.astype(BF),
            stats_low.astype(BF),
            jnp.zeros((rows, LANES - 4 * HEADS), BF),
        ],
        axis=1,
    )
    if linked:
        early = (
            mixed,
            second,
            attended,
            out_cotangent,
            gate_grad,
            resid_low,
            half_grad,
            mem_query,
        )
        early, qkv_rows = reduce_back(early, shared, qkv_all, proj_full, seg_col, seg_row)
    else:
        shared = gather(shared)
        stats_all = shared[:, width : width + 2 * HEADS].astype(F32) + shared[
            :, width + 2 * HEADS : width + 4 * HEADS
        ].astype(F32)
        attn_grad_all = dot(shared[:, :width], proj_full, NT).astype(BF)
        qkv_rows = attn_bwd(pos, qkv_all, attn_grad_all, stats_all, seg_row, seg_col, rows)
    scale_one = rms_scale(inputs)
    first_low = (inputs * scale_one * gain_one).astype(BF)
    first_grad = dot(qkv_rows, qkv_full, NT)
    input_from_norm, gain_one_grad = rms_back(inputs, scale_one, gain_one, first_grad)
    tokens_grad = resid_grad + input_from_norm

    if linked:
        sums = jnp.stack([gain_one_grad, gain_two_grad])
        sums_high = lax.reduce_precision(sums, 8, 7)
        gain_rows = jnp.stack([sums_high, sums - sums_high], axis=1).reshape(4, width)
        gain_rows = jnp.concatenate([gain_rows.astype(BF), jnp.zeros((12, width), BF)])
        late = reduce_late(first_low, qkv_rows, gain_rows)
        (
            out_share,
            gate_share,
            proj_share,
            qkv_share,
            query_share,
            keys_share,
            gain_sums,
            values_grad,
        ) = finish(early, late, keys_full, values_grad)
    else:
        keys_grad = jnp.einsum(
            "tcn,tcf->cnf",
            half_cube,
            mem_query.reshape(rows, MHEADS * 2, HALF),
            preferred_element_type=F32,
        ).reshape(KEYS, HALF)
        partials = (
            dot(mixed, out_cotangent, TN),
            dot(second, gate_grad, TN),
            keys_grad,
            dot(second, query_grad, TN),
            dot(attended, resid_low, TN),
            dot(first_low, qkv_rows, TN),
        )
        shares = [
            lax.psum_scatter(x.astype(BF), "mem", scatter_dimension=0, tiled=True)
            for x in partials
        ]
        shares = lax.psum(tuple(shares), "grp")
        gain_sums = lax.psum(jnp.stack([gain_one_grad, gain_two_grad]), ALL)
        gain_sums = lax.dynamic_slice_in_dim(
            gain_sums, position * attn_gain.shape[0], attn_gain.shape[0], axis=1
        )
        out_share, gate_share, keys_share, query_share, proj_share, qkv_share = (
            x.astype(F32) for x in shares
        )
    return (
        block_out,
        tokens_grad,
        gain_sums[0],
        qkv_share,
        proj_share,
        gain_sums[1],
        query_share,
        keys_share,
        values_grad,
        gate_share,
        out_share,
    )


def solution(mesh):
    placed = (
        P(ALL, None),
        P("grp"),
        P(ALL, None, None),
        P("mem"),
        P("mem", None),
        P("mem", None),
        P("mem"),
        P("mem", None),
        P("mem", None),
        P(ALL, None),
        P("mem", None),
        P("mem", None),
        P(ALL, None),
    )
    return jax.shard_map(
        per_device,
        mesh=mesh,
        in_specs=placed,
        out_specs=(
            P(ALL, None),
            P(ALL, None),
            P("mem"),
            P("mem", None),
            P("mem", None),
            P("mem"),
            P("mem", None),
            P("mem", None),
            P(ALL, None),
            P("mem", None),
            P("mem", None),
        ),
        check_vma=False,
    )
```

```python
import functools

import jax
import jax.numpy as jnp
from jax import lax
from jax.experimental import pallas as pl
from jax.experimental.pallas import tpu as pltpu
from jax.sharding import PartitionSpec as P

HEADS = 16
HDIM = 64
MHEADS = 4
NK = 256
HALF = 512
TOPK = 32
EPS = 1e-05
LANES = 128
ALL = ("grp", "mem")
BF = jnp.bfloat16
F32 = jnp.float32
NEG = -1e30


def dot(left, right, dims=((1,), (0,))):
    return lax.dot_general(left, right, (dims, ((), ())), preferred_element_type=F32)


NT = ((1,), (1,))
TN = ((0,), (0,))


def iota(shape, dim):
    return lax.broadcasted_iota(jnp.int32, shape, dim)


def lane_halves(rows):
    first = iota((rows, LANES), 1) < HDIM
    return first


def half_masks():
    lane = iota((1, LANES), 1)
    return ((lane < HDIM).astype(BF), (lane >= HDIM).astype(BF))


def attn_fwd_pair(rows, win, pair, position, query, load, qseg_ref, kseg_ref, lse):
    row0 = position * rows
    start = pl.multiple_of(jnp.maximum(row0 + rows - win, 0), LANES)
    keys, values = load(1, pl.ds(start, win)), load(2, pl.ds(start, win))
    key_pos = start + iota((rows, win), 1)
    query_pos = row0 + iota((rows, win), 0)
    allowed = (key_pos <= query_pos) & (kseg_ref[:, pl.ds(start, win)] == qseg_ref[...])
    lane = iota((rows, LANES), 1)
    masks = half_masks()
    outs = []
    for half in range(2):
        scores = dot(query * masks[half], keys, NT) * 0.125
        scores = jnp.where(allowed, scores, NEG)
        top = jnp.max(scores, axis=1, keepdims=True)
        weights = jnp.exp(scores - top)
        total = jnp.sum(weights, axis=1, keepdims=True)
        probs = weights * (1.0 / total)
        outs.append(dot(probs.astype(BF), values))
        lse = jnp.where(lane == pair * 2 + half, top + jnp.log(total), lse)
    return jnp.where(lane < HDIM, outs[0], outs[1]), lse


def attn_fwd_kernel(rows, win, pos_ref, q_ref, k_ref, v_ref, qseg_ref, kseg_ref, out_ref, lse_ref):
    pair = pl.program_id(0)
    refs = (q_ref, k_ref, v_ref)
    lse = jnp.where(pair == 0, jnp.zeros((rows, LANES), F32), lse_ref[...])
    out_ref[...], lse_ref[...] = attn_fwd_pair(
        rows,
        win,
        pair,
        pos_ref[0],
        q_ref[...],
        lambda which, where: refs[which][where, :],
        qseg_ref,
        kseg_ref,
        lse,
    )


def attn_fwd(pos, qkv, seg_row, seg_col, rows):
    group_len, width = qkv.shape[0], qkv.shape[1] // 3
    pairs = width // LANES
    win = min(group_len, group_len // 2 + rows)
    return pl.pallas_call(
        functools.partial(attn_fwd_kernel, rows, win),
        grid_spec=pltpu.PrefetchScalarGridSpec(
            num_scalar_prefetch=1,
            grid=(pairs,),
            in_specs=[
                pl.BlockSpec((rows, LANES), lambda h, p: (p[0], h)),
                pl.BlockSpec((group_len, LANES), lambda h, p: (0, pairs + h)),
                pl.BlockSpec((group_len, LANES), lambda h, p: (0, 2 * pairs + h)),
                pl.BlockSpec((rows, 1), lambda h, p: (p[0], 0)),
                pl.BlockSpec((1, group_len), lambda h, p: (0, 0)),
            ],
            out_specs=[
                pl.BlockSpec((rows, LANES), lambda h, p: (0, h)),
                pl.BlockSpec((rows, LANES), lambda h, p: (0, 0)),
            ],
        ),
        out_shape=[
            jax.ShapeDtypeStruct((rows, width), F32),
            jax.ShapeDtypeStruct((rows, LANES), F32),
        ],
        cost_estimate=pl.CostEstimate(
            flops=4 * rows * win * width,
            bytes_accessed=group_len * width * 4,
            transcendentals=rows * win * HEADS,
        ),
        name="attn_fwd",
    )(pos, qkv, qkv, qkv, seg_col, seg_row)


def attn_bwd_pair(rows, win, pair, position, group_len, load, stat_ref, segc_ref, segr_ref):
    row0 = pl.multiple_of(position * rows, LANES)
    start = pl.multiple_of(jnp.maximum(row0 + rows - win, 0), LANES)
    qstart = pl.multiple_of(jnp.minimum(row0, group_len - win), LANES)
    own, back, ahead = pl.ds(row0, rows), pl.ds(start, win), pl.ds(qstart, win)
    masks = half_masks()
    lane = iota((rows, LANES), 1)

    def stat(where, index, count):
        table = stat_ref[where, :]
        return jnp.sum(
            jnp.where(iota((count, table.shape[1]), 1) == index, table, 0.0),
            axis=1,
            keepdims=True,
        )

    allowed = (start + iota((rows, win), 1) <= row0 + iota((rows, win), 0)) & (
        segr_ref[:, back] == segc_ref[own, :]
    )
    allowed_two = (row0 + iota((win, rows), 1) <= qstart + iota((win, rows), 0)) & (
        segr_ref[:, own] == segc_ref[ahead, :]
    )
    dqs, dks, dvs = [], [], []
    for half in range(2):
        head = pair * 2 + half
        lse, delta = stat(own, head, rows), stat(own, HEADS + head, rows)
        keys = load(1, back)
        scores = dot(load(0, own) * masks[half], keys, NT) * 0.125
        probs = jnp.exp(jnp.where(allowed, scores - lse, NEG))
        dprobs = dot(load(3, own) * masks[half], load(2, back), NT)
        grads = (probs * (dprobs - delta)).astype(BF)
        dqs.append(dot(grads, keys))
        lse, delta = stat(ahead, head, win), stat(ahead, HEADS + head, win)
        queries, douts = load(0, ahead), load(3, ahead)
        scores = dot(queries * masks[half], load(1, own), NT) * 0.125
        probs = jnp.exp(jnp.where(allowed_two, scores - lse, NEG))
        dprobs = dot(douts * masks[half], load(2, own), NT)
        grads = (probs * (dprobs - delta)).astype(BF)
        dks.append(dot(grads, queries, TN))
        dvs.append(dot(probs.astype(BF), douts, TN))
    return [
        (jnp.where(lane < HDIM, parts[0], parts[1]) * scale).astype(BF)
        for parts, scale in ((dqs, 0.125), (dks, 0.125), (dvs, 1.0))
    ]


def attn_bwd_kernel(
    rows, win, pairs, pos_ref, q_ref, k_ref, v_ref, da_ref, stat_ref, segc_ref, segr_ref, out_ref
):
    pair = pl.program_id(0)
    refs = (q_ref, k_ref, v_ref, da_ref)
    grads = attn_bwd_pair(
        rows,
        win,
        pair,
        pos_ref[0],
        k_ref.shape[0],
        lambda which, where: refs[which][where, :],
        stat_ref,
        segc_ref,
        segr_ref,
    )
    for i, value in enumerate(grads):
        column = pl.multiple_of((i * pairs + pair) * LANES, LANES)
        out_ref[:, pl.ds(column, LANES)] = value


def attn_bwd(pos, qkv, douts, stats, seg_row, seg_col, rows):
    group_len, width = douts.shape
    pairs = width // LANES
    win = min(group_len, group_len // 2 + rows)
    return pl.pallas_call(
        functools.partial(attn_bwd_kernel, rows, win, pairs),
        grid_spec=pltpu.PrefetchScalarGridSpec(
            num_scalar_prefetch=1,
            grid=(pairs,),
            in_specs=[
                pl.BlockSpec((group_len, LANES), lambda h, p: (0, h)),
                pl.BlockSpec((group_len, LANES), lambda h, p: (0, pairs + h)),
                pl.BlockSpec((group_len, LANES), lambda h, p: (0, 2 * pairs + h)),
                pl.BlockSpec((group_len, LANES), lambda h, p: (0, h)),
                pl.BlockSpec(stats.shape, lambda h, p: (0, 0)),
                pl.BlockSpec((group_len, 1), lambda h, p: (0, 0)),
                pl.BlockSpec((1, group_len), lambda h, p: (0, 0)),
            ],
            out_specs=pl.BlockSpec((rows, 3 * width), lambda h, p: (0, 0)),
        ),
        out_shape=jax.ShapeDtypeStruct((rows, 3 * width), BF),
        cost_estimate=pl.CostEstimate(
            flops=14 * rows * win * width,
            bytes_accessed=group_len * width * 8,
            transcendentals=2 * rows * win * HEADS,
        ),
        name="attn_bwd",
    )(pos, qkv, qkv, qkv, douts, stats, seg_col, seg_row)


def by_head(lane, reduce, fill, values):
    spread = jnp.zeros_like(values)
    for c in range(MHEADS):
        inside = lane // TOPK == c
        spread = jnp.where(
            inside, reduce(jnp.where(inside, values, fill), axis=1, keepdims=True), spread
        )
    return spread


def pick_fwd_kernel(scores_ref, picks_ref, weight_ref, low_ref):
    rows = picks_ref.shape[0]
    lane = iota((rows, LANES), 1)
    picks = picks_ref[...]
    index = (picks // NK, picks % NK)
    total = jnp.zeros((rows, LANES), F32)
    for c in range(MHEADS):
        both = jnp.zeros((rows, LANES), F32)
        for e in range(2):
            base = (c * 2 + e) * NK
            for part in range(NK // LANES):
                table = scores_ref[:, base + part * LANES : base + (part + 1) * LANES]
                found = jnp.take_along_axis(table, index[e] % LANES, axis=1)
                both = both + jnp.where(index[e] // LANES == part, found, 0.0)
        total = jnp.where(lane // TOPK == c, both, total)
    top = by_head(lane, jnp.max, NEG, total)
    weights = jnp.exp(total - top)
    weights = weights / by_head(lane, jnp.sum, 0.0, weights)
    weight_ref[...] = weights
    low_ref[...] = weights.astype(BF)


def pick_fwd(half_scores, picks):
    rows = picks.shape[0]
    return pl.pallas_call(
        pick_fwd_kernel,
        out_shape=[
            jax.ShapeDtypeStruct((rows, LANES), F32),
            jax.ShapeDtypeStruct((rows, LANES), BF),
        ],
        name="pick_fwd",
    )(half_scores, picks)


def pick_bwd_kernel(
    weight_ref,
    grad_ref,
    picks_ref,
    table_ref,
    out_ref,
    whole_ref,
    score_t,
    first_t,
    second_t,
    stage,
    in_sem,
    out_sem,
):
    block = table_ref.shape[0] // MHEADS

    def part(c):
        return pl.ds(pl.multiple_of(c * block, block), block)

    def fetch(c):
        return pltpu.make_async_copy(table_ref.at[part(c)], stage.at[c], in_sem.at[c])

    def put(c):
        return pltpu.make_async_copy(stage.at[c], whole_ref.at[part(c)], out_sem.at[c])

    for c in range(MHEADS):
        fetch(c).start()
    rows = picks_ref.shape[0]
    lane = iota((rows, LANES), 1)
    weights, grads = weight_ref[...], grad_ref[...]
    score = (weights * (grads - by_head(lane, jnp.sum, 0.0, weights * grads))).astype(BF)
    score_t[...] = score.astype(F32).T
    picks_t = picks_ref[...].T
    first_t[...] = picks_t // NK
    second_t[...] = picks_t % NK
    key = iota((NK, rows), 0)

    def head(c, _):
        first = jnp.zeros((NK, rows), F32)
        second = jnp.zeros((NK, rows), F32)
        for j in range(TOPK):
            at = pl.ds(c * TOPK + j, 1)
            value = score_t[at, :]
            first = first + jnp.where(key == first_t[at, :], value, 0.0)
            second = second + jnp.where(key == second_t[at, :], value, 0.0)
        for e, total in enumerate((first, second)):
            base = pl.multiple_of((c * 2 + e) * NK, LANES)
            out_ref[:, pl.ds(base, NK)] = total.T.astype(BF)
        fetch(c).wait()
        put(c).start()
        return 0

    lax.fori_loop(0, MHEADS, head, 0)
    for c in range(MHEADS):
        put(c).wait()


def pick_bwd(weights, grads, picks, table):
    rows = picks.shape[0]
    last = grads.shape[1] // LANES - 1
    spec = pl.BlockSpec((rows, LANES), lambda i: (0, 0))
    hbm = pl.BlockSpec(memory_space=pltpu.HBM)
    return pl.pallas_call(
        pick_bwd_kernel,
        grid=(1,),
        in_specs=[spec, pl.BlockSpec((rows, LANES), lambda i: (0, last)), spec, hbm],
        out_specs=[pl.BlockSpec((rows, MHEADS * 2 * NK), lambda i: (0, 0)), hbm],
        out_shape=[
            jax.ShapeDtypeStruct((rows, MHEADS * 2 * NK), BF),
            jax.ShapeDtypeStruct(table.shape, table.dtype),
        ],
        scratch_shapes=[
            pltpu.VMEM((LANES, rows), F32),
            pltpu.VMEM((LANES, rows), jnp.int32),
            pltpu.VMEM((LANES, rows), jnp.int32),
            pltpu.VMEM((MHEADS, table.shape[0] // MHEADS, table.shape[1]), table.dtype),
            pltpu.SemaphoreType.DMA((MHEADS,)),
            pltpu.SemaphoreType.DMA((MHEADS,)),
        ],
        compiler_params=pltpu.CompilerParams(vmem_limit_bytes=40 * 1024 * 1024),
        name="pick_bwd",
    )(weights, grads, picks, table)


def owner_kernel(
    his, flat_bits, local_rows, keys_ref, sent_ref, values_ref, part_ref, spread_ref
):
    rows = part_ref.shape[0]
    width = values_ref.shape[1]
    slots = keys_ref.shape[-1]
    low_rows = local_rows // his
    key = keys_ref[0]
    flat = key & ((1 << flat_bits) - 1)
    dummy = ((key >> flat_bits) & 1) == 1
    row = (key >> (flat_bits + 1)) % local_rows
    token = flat // LANES
    pick = flat % LANES
    token = jnp.where(dummy, -1, token)
    block = jnp.where(dummy, -1, (row // low_rows) * rows + token)
    low_row = row % low_rows
    grad = sent_ref[:, :width]
    weights = sent_ref[:, width:]
    is_token = iota((rows, slots), 0) == token
    is_pick = iota((LANES, slots), 0) == pick
    token_hot = is_token.astype(F32).astype(BF)
    found = dot(weights, token_hot, TN)
    weight = jnp.sum(jnp.where(is_pick, found, 0.0), axis=0, keepdims=True)
    is_block = iota((his * rows, slots), 0) == block
    is_low = iota((low_rows, slots), 0) == low_row
    low_hot = is_low.astype(F32).astype(BF)
    spread = dot(jnp.where(is_block, weight, 0.0).astype(BF), low_hot, NT).astype(BF)
    total = jnp.zeros((rows, width), F32)
    products = []
    for h in range(his):
        table = values_ref[h * low_rows : (h + 1) * low_rows, :]
        piece = spread[h * rows : (h + 1) * rows, :]
        spread_ref[h] = piece
        total = total + dot(piece, table)
        products.append(dot(grad, table, NT).astype(BF))
    picked = dot(jnp.concatenate(products, axis=0), is_block.astype(F32).astype(BF), TN)
    picked = jnp.sum(jnp.where(is_low, picked, 0.0), axis=0, keepdims=True)
    part_ref[:, :width] = total.astype(BF)
    part_ref[:, width:] = dot(
        jnp.where(is_token, picked, 0.0).astype(BF), is_pick.astype(F32).astype(BF), NT
    ).astype(BF)


def owner_call(keys, sent, values, flat_bits):
    owners, slots = keys.shape
    rows = sent.shape[0] // owners
    local_rows, width = values.shape
    his = 4
    low_rows = local_rows // his
    return pl.pallas_call(
        functools.partial(owner_kernel, his, flat_bits, local_rows),
        grid=(owners,),
        in_specs=[
            pl.BlockSpec((1, 1, slots), lambda s: (s, 0, 0)),
            pl.BlockSpec((rows, width + LANES), lambda s: (s, 0)),
            pl.BlockSpec((local_rows, width), lambda s: (0, 0)),
        ],
        out_specs=[
            pl.BlockSpec((rows, width + LANES), lambda s: (s, 0)),
            pl.BlockSpec((his, rows, low_rows), lambda s: (0, s, 0)),
        ],
        out_shape=[
            jax.ShapeDtypeStruct((owners * rows, width + LANES), BF),
            jax.ShapeDtypeStruct((his, owners * rows, low_rows), BF),
        ],
        compiler_params=pltpu.CompilerParams(vmem_limit_bytes=48 * 1024 * 1024),
        cost_estimate=pl.CostEstimate(
            flops=2 * owners * rows * local_rows * (2 * slots + 2 * width),
            bytes_accessed=owners * rows * (2 * width + local_rows) * 2,
            transcendentals=0,
        ),
        name="owner",
    )(keys.reshape(owners, 1, slots), sent, values)


def route(picks, owners, local_rows, capacity, flat_bits):
    total = picks.size
    rows_of = picks.reshape(total)
    flat = jnp.arange(total, dtype=jnp.int32)
    each = jnp.arange(owners, dtype=jnp.int32)
    counts = jnp.sum((rows_of[:, None] // local_rows == each[None, :]).astype(jnp.int32), axis=0)
    ends = jnp.cumsum(capacity - counts)
    spares = owners * capacity - total
    spare_owner = jnp.sum(
        (jnp.arange(spares, dtype=jnp.int32)[:, None] >= ends[None, :]).astype(jnp.int32), axis=1
    )
    real = (rows_of << (flat_bits + 1)) + flat
    spare = ((spare_owner * local_rows + local_rows - 1) << (flat_bits + 1)) + (1 << flat_bits)
    keys = lax.sort(jnp.concatenate([real, spare]), is_stable=False)
    return keys.reshape(owners, capacity)


MESH = pl.DeviceIdType.MESH


def places():
    g, m = lax.axis_index("grp"), lax.axis_index("mem")
    across = g + 1 - 2 * (g % 2)
    along = (g + 2) % 4
    sibling = m + 1 - 2 * (m % 2)
    return g, m, across, along, sibling


def enter(peers):
    barrier = pltpu.get_barrier_semaphore()
    for peer in peers:
        pl.semaphore_signal(barrier, inc=1, device_id=peer, device_id_type=MESH)
    pl.semaphore_wait(barrier, len(peers))


def push(src, dst, send, recv, peer):
    copy = pltpu.make_async_remote_copy(
        src_ref=src, dst_ref=dst, send_sem=send, recv_sem=recv, device_id=peer, device_id_type=MESH
    )
    copy.start()
    return copy


def plane_tasks(held, x1, y1, x2, y2, zin, send, recv):
    g, m, across, along, _ = places()
    diagonal = 3 - g
    half = held.shape[2] // 2
    low, high = pl.ds(0, half), pl.ds(half, half)
    to_x, to_y = (across, m), (along, m)

    def copy(kind, k, src, dst, peer):
        return pltpu.make_async_remote_copy(
            src_ref=src,
            dst_ref=dst,
            send_sem=send.at[kind, k],
            recv_sem=recv.at[kind, k],
            device_id=peer,
            device_id_type=MESH,
        )

    def ones(k):
        return (
            copy(0, k, held.at[k, diagonal, low], x1.at[k], to_x),
            copy(1, k, held.at[k, diagonal, high], y1.at[k], to_y),
        )

    def twos(k):
        return (
            copy(2, k, held.at[k, across], x2.at[k], to_x),
            copy(3, k, held.at[k, along], y2.at[k], to_y),
        )

    def three(k):
        return copy(4, k, held.at[k, g], zin.at[k], (g, (m + 2 * (3 - k)) % 8))

    def first(k):
        for item in ones(k):
            item.start()

    def corner(k):
        for item in ones(k):
            item.wait_recv()
        held[k, along, low] = held[k, along, low] + x1[k]
        held[k, across, high] = held[k, across, high] + y1[k]
        for item in twos(k):
            item.start()

    def total_of(k):
        for item in twos(k):
            item.wait_recv()
        return held[k, g].astype(F32) + x2[k].astype(F32) + y2[k].astype(F32)

    def plane(k):
        held[k, g] = total_of(k).astype(BF)
        three(k).start()

    def last():
        total = total_of(3)
        for k in range(3):
            three(k).wait_recv()
            total = total + zin[k].astype(F32)
        for k in range(4):
            for item in ones(k) + twos(k):
                item.wait_send()
            if k < 3:
                three(k).wait_send()
        return total

    return first, corner, plane, last


def plane_peers():
    g, m, across, along, sibling = places()
    return [(across, m), (along, m), (g, sibling)] + [(g, (m + 2 * d) % 8) for d in (1, 2, 3)]


def plane_scratch(rows, columns):
    return [
        pltpu.VMEM((4, rows // 2, columns), BF),
        pltpu.VMEM((4, rows // 2, columns), BF),
        pltpu.VMEM((4, rows, columns), BF),
        pltpu.VMEM((4, rows, columns), BF),
        pltpu.VMEM((3, rows, columns), BF),
    ]


def memory_kernel(
    flat_bits,
    payload_ref,
    keys_ref,
    values_ref,
    out_ref,
    grad_ref,
    sent,
    parts,
    sibs,
    x1,
    y1,
    x2,
    y2,
    zin,
    held,
    spread,
    table,
    own_sem,
    table_sem,
    send,
    recv,
):
    g, m, across, along, sibling = places()
    core, z = m % 2, m // 2
    to_x, to_y, to_s = (across, m), (along, m), (g, sibling)
    rows, columns = payload_ref.shape
    width = columns - LANES
    local_rows = values_ref.shape[0]
    slots = keys_ref.shape[1]
    his = spread.shape[0]
    low_rows = local_rows // his
    low, high = pl.ds(0, rows // 2), pl.ds(rows // 2, rows // 2)
    enter(plane_peers())

    def copy(kind, index, src, dst, peer):
        return pltpu.make_async_remote_copy(
            src_ref=src,
            dst_ref=dst,
            send_sem=send.at[kind, index],
            recv_sem=recv.at[kind, index],
            device_id=peer,
            device_id_type=MESH,
        )

    def mine(i):
        return payload_ref if i == 0 else sent.at[i, core]

    def to_sibling(i):
        return copy(0, i, mine(i), sent.at[i, core], to_s)

    def plane_x(k):
        return copy(1, k, mine(4 * k), sent.at[4 * k + 1, core], to_x)

    def plane_y(k):
        return copy(2, k, mine(4 * k), sent.at[4 * k + 2, core], to_y)

    def line(k):
        return copy(3, k, payload_ref, sent.at[4 * k, core], (g, (m + 2 * k) % 8))

    def corner_y(k):
        return copy(4, k, sent.at[4 * k + 1, core, low], sent.at[4 * k + 3, core, low], to_y)

    def corner_x(k):
        return copy(5, k, sent.at[4 * k + 2, core, high], sent.at[4 * k + 3, core, high], to_x)

    def part_sibling(i):
        return copy(6, i, parts.at[i, 1 - core], sibs.at[i], to_s)

    def one_x(k):
        return copy(7, k, parts.at[4 * k + 3, core, low], x1.at[k], to_x)

    def one_y(k):
        return copy(8, k, parts.at[4 * k + 3, core, high], y1.at[k], to_y)

    def two_x(k):
        return copy(9, k, parts.at[4 * k + 1, core], x2.at[k], to_x)

    def two_y(k):
        return copy(10, k, parts.at[4 * k + 2, core], y2.at[k], to_y)

    def three(k):
        return copy(11, k, parts.at[4 * k, core], zin.at[k - 1], (g, (m + 8 - 2 * k) % 8))

    def from_line(k):
        line(k).wait_recv()
        plane_x(k).start()
        plane_y(k).start()
        to_sibling(4 * k).start()

    def from_plane(k):
        plane_x(k).wait_recv()
        corner_y(k).start()
        to_sibling(4 * k + 1).start()
        plane_y(k).wait_recv()
        corner_x(k).start()
        to_sibling(4 * k + 2).start()

    def from_corner(k):
        corner_x(k).wait_recv()
        corner_y(k).wait_recv()
        to_sibling(4 * k + 3).start()

    def pair_sum(k):
        for i in (4 * k + 3, 4 * k + 1, 4 * k + 2, 4 * k):
            part_sibling(i).wait_recv()
            parts[i, core] = parts[i, core] + sibs[i]
            if i == 4 * k + 3:
                one_x(k).start()
                one_y(k).start()

    def corner_sum(k):
        one_x(k).wait_recv()
        parts[4 * k + 2, core, low] = parts[4 * k + 2, core, low] + x1[k]
        two_y(k).start()
        one_y(k).wait_recv()
        parts[4 * k + 1, core, high] = parts[4 * k + 1, core, high] + y1[k]
        two_x(k).start()

    def plane_sum(k):
        two_x(k).wait_recv()
        two_y(k).wait_recv()
        total = parts[4 * k, core].astype(F32) + x2[k].astype(F32) + y2[k].astype(F32)
        if k == 0:
            held[...] = total
        else:
            parts[4 * k, core] = total.astype(BF)
            three(k).start()

    own = pltpu.make_async_copy(payload_ref, sent.at[0, core], own_sem)
    own.start()
    to_sibling(0).start()
    plane_x(0).start()
    plane_y(0).start()
    for k in (1, 2, 3):
        line(k).start()
    own.wait()

    tasks = {
        1: [lambda: from_plane(0)],
        2: [lambda: from_line(1)],
        3: [lambda: from_corner(0), lambda: from_line(2)],
        4: [lambda: from_line(3), lambda: pair_sum(0)],
        5: [lambda: from_plane(1)],
        6: [lambda: corner_sum(0)],
        7: [lambda: from_corner(1)],
        8: [lambda: from_plane(2), lambda: pair_sum(1)],
        9: [lambda: plane_sum(0)],
        10: [lambda: from_corner(2), lambda: corner_sum(1)],
        11: [lambda: from_plane(3)],
        12: [lambda: pair_sum(2), lambda: plane_sum(1)],
        13: [lambda: from_corner(3)],
        14: [lambda: corner_sum(2)],
    }

    def step(i, _):
        for when, todo in tasks.items():

            @pl.when(i == when)
            def _():
                for task in todo:
                    task()

        copy(0, i, sent.at[i, core], sent.at[i, 1 - core], to_s).wait_recv()
        k, j = i // 4, i % 4
        grp = (g // 2 + j // 2) % 2 * 2 + (g % 2 + j % 2) % 2
        base = grp * 8 + (z + 4 - k) % 4 * 2
        lanes, tiles = [], []
        for c in range(2):
            key = keys_ref[pl.ds(base + c, 1), :]
            flat = key & ((1 << flat_bits) - 1)
            dummy = ((key >> flat_bits) & 1) == 1
            row = (key >> (flat_bits + 1)) % local_rows
            token = jnp.where(dummy, -1, flat // LANES)
            block = jnp.where(dummy, -1, (row // low_rows) * rows + token)
            is_token = iota((rows, slots), 0) == token
            is_pick = iota((LANES, slots), 0) == flat % LANES
            place = jnp.concatenate(
                [
                    jnp.where(is_token, (row % LANES).astype(F32), 0.0).astype(BF),
                    jnp.where(is_token, (row // LANES + 1).astype(F32), 0.0).astype(BF),
                ],
                axis=0,
            )
            place = dot(place, is_pick.astype(F32).astype(BF), NT).astype(jnp.int32)
            lanes.append(place[:rows])
            tiles.append(place[rows:] - 1)
            weights = sent[i, c, :, width:]
            found = dot(weights, is_token.astype(F32).astype(BF), TN)
            weight = jnp.sum(jnp.where(is_pick, found, 0.0), axis=0, keepdims=True)
            is_block = iota((his * rows, slots), 0) == block
            is_low = iota((low_rows, slots), 0) == row % low_rows
            piece = dot(
                jnp.where(is_block, weight, 0.0).astype(BF), is_low.astype(F32).astype(BF), NT
            ).astype(BF)
            for h in range(his):
                spread[h, 2 * i + c] = piece[h * rows : (h + 1) * rows]
        lane, tile = jnp.concatenate(lanes, axis=0), jnp.concatenate(tiles, axis=0)
        grads = sent[i, :, :, :width].reshape(2 * rows, width)
        total = jnp.zeros((2 * rows, width), F32)
        picked = jnp.zeros((2 * rows, LANES), F32)
        for h in range(his):
            table = values_ref[h * low_rows : (h + 1) * low_rows, :]
            piece = spread[h, pl.ds(2 * i, 2)].reshape(2 * rows, low_rows)
            total = total + dot(piece, table)
            products = dot(grads, table, NT)
            for b in range(low_rows // LANES):
                found = jnp.take_along_axis(
                    products[:, b * LANES : (b + 1) * LANES], lane, axis=1
                )
                picked = jnp.where(tile == h * (low_rows // LANES) + b, found, picked)
        parts[i, :, :, :width] = total.astype(BF).reshape(2, rows, width)
        parts[i, :, :, width:] = picked.astype(BF).reshape(2, rows, LANES)
        part_sibling(i).start()
        return 0

    def table_copy(h):
        return pltpu.make_async_copy(table.at[h % 2], grad_ref.at[h], table_sem.at[h % 2])

    def table_grad(h):
        if h >= 2:
            table_copy(h - 2).wait()

        def some(n, _):
            grads = sent[pl.ds(4 * n, 4), :, :, :width].reshape(8 * rows, width)
            piece = spread[h, pl.ds(8 * n, 8)].reshape(8 * rows, low_rows)
            table[h % 2] = jnp.where(n == 0, 0.0, table[h % 2]) + dot(piece, grads, TN)
            return 0

        lax.fori_loop(0, 4, some, 0)
        table_copy(h).start()

    lax.fori_loop(0, 16, step, 0)
    plane_sum(2)
    pair_sum(3)
    table_grad(0)
    corner_sum(3)
    table_grad(1)
    plane_sum(3)
    table_grad(2)
    table_grad(3)
    total = held[...]
    for k in (1, 2, 3):
        three(k).wait_recv()
        total = total + zin[k - 1].astype(F32)
    out_ref[...] = total
    for k in range(4):
        todo = [plane_x(k), plane_y(k), corner_x(k), corner_y(k)]
        todo += [one_x(k), one_y(k), two_x(k), two_y(k)]
        if k:
            todo += [line(k), three(k)]
        for j in range(4):
            todo += [to_sibling(4 * k + j), part_sibling(4 * k + j)]
        for item in todo:
            item.wait_send()
    table_copy(2).wait()
    table_copy(3).wait()


def memory_call(payload, keys, values, flat_bits):
    rows, columns = payload.shape
    local_rows = values.shape[0]
    his = 4
    half = (4, rows // 2, columns)
    full = (4, rows, columns)
    vmem = pl.BlockSpec(memory_space=pltpu.VMEM)
    hbm = pl.BlockSpec(memory_space=pl.ANY)
    return pl.pallas_call(
        functools.partial(memory_kernel, flat_bits),
        in_specs=[hbm, vmem, vmem],
        out_specs=[vmem, hbm],
        out_shape=[
            jax.ShapeDtypeStruct((rows, columns), F32),
            jax.ShapeDtypeStruct((his, local_rows // his, columns - LANES), F32),
        ],
        scratch_shapes=[
            pltpu.VMEM((16, 2, rows, columns), BF),
            pltpu.VMEM((16, 2, rows, columns), BF),
            pltpu.VMEM((16, rows, columns), BF),
            pltpu.VMEM(half, BF),
            pltpu.VMEM(half, BF),
            pltpu.VMEM(full, BF),
            pltpu.VMEM(full, BF),
            pltpu.VMEM((3, rows, columns), BF),
            pltpu.VMEM((rows, columns), F32),
            pltpu.VMEM((his, 32, rows, local_rows // his), BF),
            pltpu.VMEM((2, local_rows // his, columns - LANES), F32),
            pltpu.SemaphoreType.DMA,
            pltpu.SemaphoreType.DMA((2,)),
            pltpu.SemaphoreType.DMA((12, 16)),
            pltpu.SemaphoreType.DMA((12, 16)),
        ],
        compiler_params=pltpu.CompilerParams(
            collective_id=1, has_side_effects=True, vmem_limit_bytes=63 * 1024 * 1024
        ),
        name="memory",
    )(payload, keys, values)


def gather_tasks(pieces, sources, targets, local_sem, send, recv):
    g, m, across, along, sibling = places()
    z = m // 2
    to_x, to_y, to_s = (across, m), (along, m), (g, sibling)
    total = range(len(pieces))
    ways = [(sign, hop) for hop in (1, 2, 3) for sign in (1, -1)]
    shared = [p for p in total if pieces[p][3]]

    def view(piece, owner, quarter=None, part=None):
        array, first, columns, _ = pieces[piece]
        ref = targets[array]
        size = ref.shape[0] // 8
        start = owner * size
        if quarter is not None:
            size = size // 4
            start = start + quarter * size
        if part is not None:
            size = size // 2
            start = start + part * size
        return ref.at[pl.ds(start, size), pl.ds(first, columns)]

    def copy(piece, index, block, peer, src=None):
        return pltpu.make_async_remote_copy(
            src_ref=block if src is None else src,
            dst_ref=block,
            send_sem=send.at[piece, index],
            recv_sem=recv.at[piece, index],
            device_id=peer,
            device_id_type=MESH,
        )

    def line(p, way, owner, src=None):
        block = view(p, owner, g if pieces[p][3] else None)
        peer = (g, (m + 8 + 2 * ways[way][0]) % 8)
        return copy(p, way, block, peer, src)

    def has(way):
        sign, distance = ways[way]
        return z >= distance if sign > 0 else z + distance <= 3

    def more(way):
        return z <= 2 if ways[way][0] > 0 else z >= 1

    def origin(way):
        sign, distance = ways[way]
        return (m + 8 - 2 * sign * distance) % 8

    def planes(p, way):
        block = view(p, origin(way), g)
        return copy(p, 6 + way, block, to_x), copy(p, 12 + way, block, to_y)

    def corners(p, way):
        owner = origin(way)
        return (
            copy(p, 18 + way, view(p, owner, across, 0), to_y),
            copy(p, 24 + way, view(p, owner, along, 1), to_x),
        )

    def core(p, way):
        return copy(p, 30 + way, view(p, origin(way)), to_s)

    def first(p):
        array, start, columns, is_shared = pieces[p]
        ref = sources[array]
        whole = ref.at[:, pl.ds(start, columns)]
        src = whole
        if is_shared:
            quarter = ref.shape[0] // 4
            src = ref.at[pl.ds(g * quarter, quarter), pl.ds(start, columns)]
        return (
            [line(p, way, m, src) for way in (0, 1)],
            pltpu.make_async_copy(whole, view(p, m), local_sem.at[p]),
            copy(p, 36, view(p, m), to_s, whole),
        )

    def begin():
        for p in total:
            for way in (0, 1):
                pl.when(more(way))(first(p)[0][way].start)
        for p in total:
            _, near, side = first(p)
            near.start()
            side.start()

    def level(hop):
        return (2 * hop - 2, 2 * hop - 1)

    def arrive(hop):
        for p in total:
            for way in level(hop):

                @pl.when(has(way))
                def _():
                    line(p, way, origin(way)).wait_recv()
                    if hop < 3:
                        pl.when(more(way))(line(p, way + 2, origin(way)).start)

        for p in total:
            for way in level(hop):

                @pl.when(has(way))
                def _():
                    for item in planes(p, way) if p in shared else [core(p, way)]:
                        item.start()

    def turn(hop):
        for p in shared:
            for way in level(hop):

                @pl.when(has(way))
                def _():
                    for item, after in zip(planes(p, way), corners(p, way), strict=True):
                        item.wait_recv()
                        after.start()

    def cross(hop):
        for p in shared:
            for way in level(hop):

                @pl.when(has(way))
                def _():
                    for item in corners(p, way):
                        item.wait_recv()
                    core(p, way).start()

    def end():
        for p in total:
            out, near, side = first(p)
            near.wait()
            side.wait()
            for way in (0, 1):
                pl.when(more(way))(out[way].wait_send)
            for way in range(6):

                @pl.when(has(way))
                def _():
                    core(p, way).wait()
                    if ways[way][1] < 3:
                        pl.when(more(way))(line(p, way + 2, origin(way)).wait_send)
                    if p in shared:
                        for item in planes(p, way) + corners(p, way):
                            item.wait_send()

    return begin, arrive, turn, cross, end


def pieces_of(arrays, chunk, own_count):
    pieces = []
    for i, x in enumerate(arrays):
        columns = x.shape[1]
        for first in range(0, columns, chunk):
            pieces.append((i, first, min(chunk, columns - first), i >= own_count))
    return tuple(pieces)


def gathered(arrays):
    return [jax.ShapeDtypeStruct((8 * x.shape[0], x.shape[1]), x.dtype) for x in arrays]


def gather_sems(pieces):
    return [
        pltpu.SemaphoreType.DMA((len(pieces),)),
        pltpu.SemaphoreType.DMA((len(pieces), 37)),
        pltpu.SemaphoreType.DMA((len(pieces), 37)),
    ]


def gather_kernel(pieces, count, *refs):
    enter(plane_peers())
    begin, arrive, turn, cross, end = gather_tasks(
        pieces, refs[:count], refs[count : 2 * count], *refs[2 * count :]
    )
    begin()
    arrive(1)
    arrive(2)
    turn(1)
    arrive(3)
    turn(2)
    cross(1)
    turn(3)
    cross(2)
    cross(3)
    end()


def gather_first(arrays, chunk, own_count):
    pieces = pieces_of(arrays, chunk, own_count)
    count = len(arrays)
    return pl.pallas_call(
        functools.partial(gather_kernel, pieces, count),
        in_specs=[pl.BlockSpec(memory_space=pltpu.VMEM)] * count,
        out_specs=[pl.BlockSpec(memory_space=pl.ANY)] * count,
        out_shape=gathered(arrays),
        scratch_shapes=gather_sems(pieces),
        compiler_params=pltpu.CompilerParams(collective_id=3, has_side_effects=True),
        name="gather_first",
    )(*arrays)


def gather_attend_kernel(pieces, count, rows, win, *refs):
    sources, refs = refs[:count], refs[count:]
    tokens_ref, gain_ref, weight_ref, segc_ref, segr_ref = refs[:5]
    targets, refs = refs[5 : 5 + count], refs[5 + count :]
    qkv_ref, out_ref, lse_ref, first_ref = refs[:4]
    m = lax.axis_index("mem")
    group_len, width = tokens_ref.shape
    pairs = width // LANES
    enter(plane_peers())
    begin, arrive, turn, cross, end = gather_tasks(pieces, sources, targets, *refs[4:])

    def normalize():
        block = 2 * rows

        def some(i, _):
            where = pl.ds(pl.multiple_of(i * block, block), block)
            values = tokens_ref[where, :].astype(F32)
            first_ref[where, :] = (values * rms_scale(values) * gain_ref[...]).astype(BF)
            return 0

        lax.fori_loop(0, group_len // block, some, 0)

    def project(i, _):
        where = pl.ds(pl.multiple_of(i * 3 * LANES, LANES), 3 * LANES)
        qkv_ref[:, where] = dot(first_ref[...], weight_ref[:, where]).astype(BF)

        @pl.when(i == 2)
        def _():
            arrive(1)

        @pl.when(i == 6)
        def _():
            arrive(2)

        return 0

    def load_of(pair):
        def load(which, where):
            column = pl.multiple_of((which * pairs + pair) * LANES, LANES)
            return qkv_ref[where, pl.ds(column, LANES)]

        return load

    own = pl.ds(pl.multiple_of(m * rows, LANES), rows)

    def attend(pair, _):
        load = load_of(pair)
        value, lse_ref[...] = attn_fwd_pair(
            rows, win, pair, m, load(0, own), load, segc_ref.at[own], segr_ref, lse_ref[...]
        )
        out_ref[:, pl.ds(pl.multiple_of(pair * LANES, LANES), LANES)] = value

        @pl.when(pair == 0)
        def _():
            turn(1)

        @pl.when(pair == 3)
        def _():
            arrive(3)

        @pl.when(pair == 5)
        def _():
            turn(2)
            cross(1)

        return 0

    lse_ref[...] = jnp.zeros_like(lse_ref)
    begin()
    normalize()
    lax.fori_loop(0, 8, project, 0)
    lax.fori_loop(0, 8, attend, 0)
    turn(3)
    cross(2)
    cross(3)
    end()


def gather_attend(arrays, chunk, tokens, gain, weight, seg_col, seg_row, rows):
    pieces = pieces_of(arrays, chunk, 0)
    count = len(arrays)
    group_len, width = tokens.shape
    win = min(group_len, group_len // 2 + rows)
    vmem, hbm = pl.BlockSpec(memory_space=pltpu.VMEM), pl.BlockSpec(memory_space=pl.ANY)
    return pl.pallas_call(
        functools.partial(gather_attend_kernel, pieces, count, rows, win),
        in_specs=[vmem] * (count + 5),
        out_specs=[hbm] * count + [vmem] * 3,
        out_shape=[
            *gathered(arrays),
            jax.ShapeDtypeStruct((group_len, 3 * width), BF),
            jax.ShapeDtypeStruct((rows, width), F32),
            jax.ShapeDtypeStruct((rows, LANES), F32),
        ],
        scratch_shapes=[pltpu.VMEM((group_len, width), BF), *gather_sems(pieces)],
        compiler_params=pltpu.CompilerParams(
            collective_id=5, has_side_effects=True, vmem_limit_bytes=48 * 1024 * 1024
        ),
        name="gather_attend",
    )(*arrays, tokens, gain, weight, seg_col, seg_row)


WIDTH = HEADS * HDIM
KEYS = MHEADS * 2 * NK
QUERIES = MHEADS * 2 * HALF
EARLY = (WIDTH,) * 6 + (KEYS,)
EARLY_PRODUCTS = (
    (0, 3 * WIDTH, WIDTH, 0),
    (WIDTH, 4 * WIDTH, WIDTH, WIDTH),
    (2 * WIDTH, 5 * WIDTH, WIDTH, 2 * WIDTH),
    (WIDTH, 6 * WIDTH, KEYS, 3 * WIDTH),
)
E_OUT, E_GATE, E_PROJ, E_HALF = 0, WIDTH, 2 * WIDTH, 3 * WIDTH
E_ALL = E_HALF + KEYS
LATE = (WIDTH, 3 * WIDTH)
LATE_PRODUCTS = ((0, WIDTH, 3 * WIDTH, 0),)
L_GAIN = 3 * WIDTH
L_ALL = L_GAIN + LANES


def share_factors(moves, local_sem, send, recv):
    g, _, _, _, sibling = places()
    copies = []
    for i, (src, dst, at, columns) in enumerate(moves):
        count = src.shape[0]
        where = pl.ds(at, columns)
        far = push(
            src, dst.at[pl.ds(count, count), where], send.at[5, i], recv.at[5, i], (g, sibling)
        )
        near = pltpu.make_async_copy(src, dst.at[pl.ds(0, count), where], local_sem.at[i])
        near.start()
        copies.append((near, far))
    return copies


def factor_moves(refs, widths, fact):
    moves, at = [], 0
    for ref, columns in zip(refs, widths, strict=True):
        moves.append((ref, fact, at, columns))
        at += columns
    return moves


def store_blocks(held, k, value, at):
    for i in range(4):
        held[k, i, :, at : at + value.shape[1]] = value[i * 32 : (i + 1) * 32].astype(BF)


def block_of(k):
    m = lax.axis_index("mem")
    return (m // 2 + 3 - k) % 4 * 2 + m % 2


def products_of(k, fact, held, products):
    block = block_of(k)
    for left, right, count, at in products:
        lhs = fact[:, pl.ds(pl.multiple_of(left + block * LANES, LANES), LANES)]
        for j in range(0, count, WIDTH):
            store_blocks(held, k, dot(lhs, fact[:, right + j : right + j + WIDTH], TN), at + j)


def spread_quarters(total, quarter, send, recv):
    g, m, across, along, _ = places()
    quarter[g] = total.astype(BF)
    to_x, to_y = (across, m), (along, m)
    low, high = pl.ds(0, 16), pl.ds(16, 16)
    a = push(quarter.at[g], quarter.at[g], send.at[6, 0], recv.at[6, 0], to_x)
    b = push(quarter.at[g], quarter.at[g], send.at[6, 1], recv.at[6, 1], to_y)
    a.wait_recv()
    c = push(quarter.at[across, low], quarter.at[across, low], send.at[6, 2], recv.at[6, 2], to_y)
    b.wait_recv()
    d = push(quarter.at[along, high], quarter.at[along, high], send.at[6, 3], recv.at[6, 3], to_x)
    c.wait_recv()
    d.wait_recv()
    for copy in (a, b, c, d):
        copy.wait_send()


def late_kernel(
    first_ref,
    rows_ref,
    gain_ref,
    half_ref,
    query_ref,
    out_ref,
    keys_ref,
    fact,
    gains,
    wide,
    held,
    x1,
    y1,
    x2,
    y2,
    zin,
    quarter,
    tables,
    arrived,
    local_sem,
    send,
    recv,
):
    g, m, _, _, _ = places()
    core, z = m % 2, m // 2
    enter(plane_peers())
    moves = factor_moves((first_ref, rows_ref), LATE, fact)
    moves.append((gain_ref, gains, 0, WIDTH))
    moves += factor_moves((half_ref, query_ref), (KEYS, QUERIES), wide)
    copies = share_factors(moves, local_sem, send, recv)
    first, corner, plane, last = plane_tasks(held, x1, y1, x2, y2, zin, send, recv)
    for near, far in copies[:3]:
        near.wait()
        far.wait_recv()
    row = iota((32, LANES), 0) % 16
    column = iota((32, LANES), 1)
    select = ((row < 4) & (row // 2 == column)).astype(F32).astype(BF)

    def table(d):
        block = (z + d) % 4 * 2 + core
        lhs = wide[:, pl.ds(pl.multiple_of(block * NK, LANES), NK)]
        rhs = wide[:, pl.ds(pl.multiple_of(KEYS + block * HALF, LANES), HALF)]
        return dot(lhs, rhs, TN)

    def line(k):
        return pltpu.make_async_remote_copy(
            src_ref=tables.at[k],
            dst_ref=arrived.at[k],
            send_sem=send.at[7, k],
            recv_sem=recv.at[7, k],
            device_id=(g, (m + 2 * (k + 1)) % 8),
            device_id_type=MESH,
        )

    def ready(k, _):
        products_of(k, fact, held, LATE_PRODUCTS)
        lhs = gains[:, pl.ds(pl.multiple_of(block_of(k) * LANES, LANES), LANES)]
        store_blocks(held, k, dot(lhs, select, TN), L_GAIN)
        first(k)
        return 0

    lax.fori_loop(0, 4, ready, 0)
    for near, far in copies[3:]:
        near.wait()
        far.wait_recv()

    def send_table(k, _):
        tables[k] = table(k + 1).astype(BF)
        line(k).start()
        return 0

    lax.fori_loop(0, 3, send_table, 0)
    keys_ref[...] = table(0)
    for k in range(4):
        corner(k)
    for k in range(3):
        plane(k)
    spread_quarters(last(), quarter, send, recv)
    for k in range(3):
        line(k).wait_recv()
        keys_ref[...] += arrived[k].astype(F32)
        line(k).wait_send()
    for _, far in copies:
        far.wait_send()
    out_ref[...] = quarter[...]


def reduce_late(first, qkv_rows, gains, half, query):
    rows = first.shape[0]
    vmem = pl.BlockSpec(memory_space=pltpu.VMEM)
    sums, keys = pl.pallas_call(
        late_kernel,
        in_specs=[pl.BlockSpec(memory_space=pl.ANY)] * 5,
        out_specs=[vmem, vmem],
        out_shape=[
            jax.ShapeDtypeStruct((4, 32, L_ALL), BF),
            jax.ShapeDtypeStruct((NK, HALF), F32),
        ],
        scratch_shapes=[
            pltpu.VMEM((2 * rows, sum(LATE)), BF),
            pltpu.VMEM((32, WIDTH), BF),
            pltpu.VMEM((2 * rows, KEYS + QUERIES), BF),
            pltpu.VMEM((4, 4, 32, L_ALL), BF),
            *plane_scratch(32, L_ALL),
            pltpu.VMEM((4, 32, L_ALL), BF),
            pltpu.VMEM((3, NK, HALF), BF),
            pltpu.VMEM((3, NK, HALF), BF),
            pltpu.SemaphoreType.DMA((5,)),
            pltpu.SemaphoreType.DMA((8, 5)),
            pltpu.SemaphoreType.DMA((8, 5)),
        ],
        compiler_params=pltpu.CompilerParams(
            collective_id=2, has_side_effects=True, vmem_limit_bytes=48 * 1024 * 1024
        ),
        name="reduce_late",
    )(first, qkv_rows, gains, half, query)
    return sums.reshape(4 * 32, L_ALL), keys


def back_kernel(rows, win, *refs):
    fact_refs, refs = refs[: len(EARLY)], refs[len(EARLY) :]
    shared_ref, qkv_ref, proj_ref, segc_ref, segr_ref, out_ref, rows_ref = refs[:7]
    fact, held, x1, y1, x2, y2, zin, quarter, shared, douts, stats = refs[7:18]
    local_sem, send, recv = refs[18:]
    g, m, _, _, sibling = places()
    to_s = (g, sibling)
    pairs = WIDTH // LANES
    enter(plane_peers())

    def part(owner):
        return shared.at[pl.ds(pl.multiple_of(owner * rows, LANES), rows)]

    def move(index, src, owner, peer):
        return pltpu.make_async_remote_copy(
            src_ref=src,
            dst_ref=part(owner),
            send_sem=send.at[7, index],
            recv_sem=recv.at[7, index],
            device_id=peer,
            device_id_type=MESH,
        )

    def origin(d):
        return (m + 8 - 2 * d) % 8

    lines = [move(d, shared_ref, m, (g, (m + 2 * d) % 8)) for d in (1, 2, 3)]
    side = move(0, shared_ref, m, to_s)
    forward = [move(3 + d, part(origin(d)), origin(d), to_s) for d in (1, 2, 3)]
    own = pltpu.make_async_copy(shared_ref, part(m), local_sem.at[len(EARLY)])
    for copy in lines:
        copy.start()
    side.start()
    own.start()
    copies = share_factors(factor_moves(fact_refs, EARLY, fact), local_sem, send, recv)
    first, corner, plane, last = plane_tasks(held, x1, y1, x2, y2, zin, send, recv)
    for near, far in copies:
        near.wait()
        far.wait_recv()

    def ready(k, _):
        products_of(k, fact, held, EARLY_PRODUCTS)
        first(k)
        return 0

    lax.fori_loop(0, 4, ready, 0)
    corner(0)
    for copy, after in zip(lines, forward, strict=True):
        copy.wait_recv()
        after.start()
    corner(1)
    own.wait()
    side.wait_recv()
    for copy in forward:
        copy.wait_recv()
    corner(2)
    def project(i, _):
        where = pl.ds(pl.multiple_of(i * 2 * rows, 2 * rows), 2 * rows)
        douts[where, :] = dot(shared[where, :WIDTH], proj_ref[...], NT).astype(BF)
        stats[where, :] = shared[where, WIDTH : WIDTH + 2 * HEADS].astype(F32) + shared[
            where, WIDTH + 2 * HEADS : WIDTH + 4 * HEADS
        ].astype(F32)
        return 0

    lax.fori_loop(0, shared.shape[0] // (2 * rows), project, 0)
    corner(3)

    def load_of(pair):
        def load(which, where):
            ref, base = (douts, 0) if which == 3 else (qkv_ref, which * pairs)
            return ref[where, pl.ds(pl.multiple_of((base + pair) * LANES, LANES), LANES)]

        return load

    def attend(pair, _):
        grads = attn_bwd_pair(
            rows, win, pair, m, shared.shape[0], load_of(pair), stats, segc_ref, segr_ref
        )
        for i, value in enumerate(grads):
            column = pl.multiple_of((i * pairs + pair) * LANES, LANES)
            rows_ref[:, pl.ds(column, LANES)] = value
        for k in range(3):
            pl.when(pair == 2 * k + 1)(functools.partial(plane, k))
        return 0

    lax.fori_loop(0, pairs, attend, 0)
    spread_quarters(last(), quarter, send, recv)
    for _, far in copies:
        far.wait_send()
    for copy in [*lines, side, *forward]:
        copy.wait_send()
    out_ref[...] = quarter[...]


def reduce_back(factors, shared, qkv, proj, seg_col, seg_row):
    rows = factors[0].shape[0]
    group_len = qkv.shape[0]
    win = min(group_len, group_len // 2 + rows)
    hbm = pl.BlockSpec(memory_space=pl.ANY)
    vmem = pl.BlockSpec(memory_space=pltpu.VMEM)
    count = len(EARLY)
    sums, qkv_rows = pl.pallas_call(
        functools.partial(back_kernel, rows, win),
        in_specs=[hbm] * (count + 1) + [vmem] * 4,
        out_specs=[vmem, vmem],
        out_shape=[
            jax.ShapeDtypeStruct((4, 32, E_ALL), BF),
            jax.ShapeDtypeStruct((rows, 3 * WIDTH), BF),
        ],
        scratch_shapes=[
            pltpu.VMEM((2 * rows, sum(EARLY)), BF),
            pltpu.VMEM((4, 4, 32, E_ALL), BF),
            *plane_scratch(32, E_ALL),
            pltpu.VMEM((4, 32, E_ALL), BF),
            pltpu.VMEM((group_len, WIDTH + LANES), BF),
            pltpu.VMEM((group_len, WIDTH), BF),
            pltpu.VMEM((group_len, 2 * HEADS), F32),
            pltpu.SemaphoreType.DMA((count + 1,)),
            pltpu.SemaphoreType.DMA((8, count)),
            pltpu.SemaphoreType.DMA((8, count)),
        ],
        compiler_params=pltpu.CompilerParams(
            collective_id=4, has_side_effects=True, vmem_limit_bytes=56 * 1024 * 1024
        ),
        name="reduce_back",
    )(*factors, shared, qkv, proj, seg_col, seg_row)
    return sums.reshape(4 * 32, E_ALL), qkv_rows


def fold_kernel(query_ref, keys_ref, out_ref):
    for c in range(MHEADS * 2):
        out_ref[:, c * NK : (c + 1) * NK] = dot(
            query_ref[:, c * HALF : (c + 1) * HALF], keys_ref[c * NK : (c + 1) * NK, :], NT
        ).astype(BF)


def fold(query, keys):
    return pl.pallas_call(
        fold_kernel, out_shape=jax.ShapeDtypeStruct((query.shape[0], KEYS), BF), name="fold"
    )(query, keys)


def finish_kernel(
    early_ref, late_ref, keys_ref, out, gate, proj, qkv, query, gains
):
    for ref, first in ((out, E_OUT), (gate, E_GATE), (proj, E_PROJ)):
        ref[...] = early_ref[:, first : first + WIDTH].astype(F32)
    qkv[...] = late_ref[:, : 3 * WIDTH].astype(F32)
    for c in range(MHEADS * 2):
        table = keys_ref[c * NK : (c + 1) * NK, :]
        query[:, c * HALF : (c + 1) * HALF] = dot(
            early_ref[:, E_HALF + c * NK : E_HALF + (c + 1) * NK], table
        )
    gains[...] = late_ref[:, L_GAIN:].astype(F32).T[:8]


def finish(early, late, keys):
    rows = early.shape[0]
    shapes = [(rows, WIDTH)] * 3 + [(rows, 3 * WIDTH), (rows, QUERIES)]
    shapes.append((8, LANES))
    return pl.pallas_call(
        finish_kernel,
        out_shape=[jax.ShapeDtypeStruct(shape, F32) for shape in shapes],
        compiler_params=pltpu.CompilerParams(vmem_limit_bytes=40 * 1024 * 1024),
        name="finish",
    )(early, late, keys)


def rms_scale(values):
    return lax.rsqrt(jnp.mean(values * values, axis=-1, keepdims=True) + EPS)


def rms_back(values, scale, gain, grad):
    scaled = grad * gain
    inner = jnp.mean(values * scaled, axis=-1, keepdims=True)
    gain_grad = jnp.sum(grad * values * scale, axis=0)
    return scale * scaled - values * (scale * scale * scale * inner), gain_grad


def per_device(
    tokens,
    segment_ids,
    picks,
    attn_gain,
    qkv_weight,
    attn_proj,
    mem_gain,
    query_weight,
    half_keys,
    memory_values,
    gate_weight,
    out_weight,
    out_cotangent,
):
    rows, width = tokens.shape
    owners = lax.axis_size("grp") * lax.axis_size("mem")
    local_rows = memory_values.shape[0]
    total_picks = rows * MHEADS * TOPK
    flat_bits = (total_picks - 1).bit_length()
    capacity = 2 * total_picks // owners
    group_len = segment_ids.shape[0]
    linked = (lax.axis_size("grp"), lax.axis_size("mem"), rows) == (4, 8, LANES)
    position = lax.axis_index("mem").astype(jnp.int32)
    pos = position.reshape(1)

    def gather(x, axes="mem"):
        return lax.all_gather(x, axes, axis=0, tiled=True)

    flat_picks = picks.reshape(rows, MHEADS * TOPK)
    if linked:
        gain_block = jnp.concatenate(
            [attn_gain[None], mem_gain[None], jnp.zeros((14, LANES), BF)]
        )
        tokens_all, gains, qkv_full, keys_full = gather_first(
            (tokens, gain_block, qkv_weight, half_keys), 3 * width // 2, 2
        )
        gains = gains.reshape(8, 16, LANES)[:, :2].transpose(1, 0, 2).reshape(2, width)
    else:
        gains = lax.all_gather(jnp.stack([attn_gain, mem_gain]), "mem", axis=1, tiled=True)
        tokens_all = gather(tokens)
        qkv_full = gather(qkv_weight)
        proj_full = gather(attn_proj)
        query_full = gather(query_weight)
        keys_full = gather(half_keys)
        gate_full = gather(gate_weight)
        output_full = gather(out_weight)
    gains = gains.astype(F32)
    gain_one, gain_two = gains[0:1], gains[1:2]
    seg_row, seg_col = segment_ids.reshape(1, group_len), segment_ids.reshape(group_len, 1)

    requests = route(picks, owners, local_rows, capacity, flat_bits)
    arrived = lax.all_to_all(requests, ALL, split_axis=0, concat_axis=0, tiled=True)

    if linked:
        folded = fold(query_weight, keys_full)
        proj_full, folded_full, gate_full, output_full, qkv_all, attn_sum, lse = gather_attend(
            (attn_proj, folded, gate_weight, out_weight),
            width,
            tokens_all,
            gain_one,
            qkv_full,
            seg_col,
            seg_row,
            rows,
        )
    else:
        inputs_all = tokens_all.astype(F32)
        first_all = (inputs_all * rms_scale(inputs_all) * gain_one).astype(BF)
        qkv_all = dot(first_all, qkv_full).astype(BF)
        attn_sum, lse = attn_fwd(pos, qkv_all, seg_row, seg_col, rows)
    attended = attn_sum.astype(BF)
    inputs = tokens.astype(F32)
    residual = inputs + dot(attended, proj_full)
    scale_two = rms_scale(residual)
    second = (residual * scale_two * gain_two).astype(BF)
    gate_pre = dot(second, gate_full)
    mixed_grad = dot(out_cotangent, output_full, NT)
    sig = jax.nn.sigmoid(gate_pre)
    gate_act = gate_pre * sig
    memory_grad = (mixed_grad * gate_act).astype(BF)
    if linked:
        half_scores = dot(second, folded_full)
    else:
        mem_query = dot(second, query_full).astype(BF)
        key_table = keys_full.reshape(MHEADS * 2, NK, HALF)
        half_scores = jnp.einsum(
            "tcf,cnf->tcn",
            mem_query.reshape(rows, MHEADS * 2, HALF),
            key_table,
            preferred_element_type=F32,
        ).reshape(rows, KEYS)
    pick_weights, weights_low = pick_fwd(half_scores, flat_picks)

    payload = jnp.concatenate([memory_grad, weights_low], axis=1)
    if linked:
        back, values_grad = memory_call(payload, arrived, memory_values, flat_bits)
    else:
        sent = gather(payload, ALL)
        part, spread = owner_call(arrived, sent, memory_values, flat_bits)
        back = lax.psum_scatter(part, "grp", scatter_dimension=0, tiled=True)
        back = lax.psum_scatter(back, "mem", scatter_dimension=0, tiled=True)
        values_grad = jnp.einsum(
            "hkl,kd->hld", spread, sent[:, :width], preferred_element_type=F32
        )
    values_grad = values_grad.reshape(local_rows, width)

    memory_out = back[:, :width].astype(F32)
    mixed = (memory_out * gate_act).astype(BF)
    block_out = (residual + dot(mixed, output_full)).astype(BF)
    gate_grad = (mixed_grad * memory_out * (sig * (1.0 + gate_pre * (1.0 - sig)))).astype(BF)
    half_grad, values_grad = pick_bwd(
        pick_weights, back.astype(F32), flat_picks, values_grad
    )
    if linked:
        second_grad = dot(gate_grad, gate_full, NT) + dot(half_grad, folded_full, NT)
    else:
        half_cube = half_grad.reshape(rows, MHEADS * 2, NK)
        query_grad = (
            jnp.einsum("tcn,cnf->tcf", half_cube, key_table, preferred_element_type=F32)
            .astype(BF)
            .reshape(rows, QUERIES)
        )
        second_grad = dot(gate_grad, gate_full, NT) + dot(query_grad, query_full, NT)
    resid_from_norm, gain_two_grad = rms_back(residual, scale_two, gain_two, second_grad)
    resid_grad = out_cotangent.astype(F32) + resid_from_norm
    resid_low = resid_grad.astype(BF)
    attn_grad = dot(resid_low, proj_full, NT).astype(BF)
    heads = (iota((width, HEADS), 0) // HDIM == iota((width, HEADS), 1)).astype(F32)
    delta = jnp.dot(
        attn_grad.astype(F32) * attn_sum,
        heads,
        precision=lax.Precision.HIGHEST,
        preferred_element_type=F32,
    )
    stats = jnp.concatenate([lse[:, :HEADS], delta], axis=1)
    stats_high = lax.reduce_precision(stats, 8, 7)
    stats_low = stats - stats_high
    shared = jnp.concatenate(
        [
            resid_low,
            stats_high.astype(BF),
            stats_low.astype(BF),
            jnp.zeros((rows, LANES - 4 * HEADS), BF),
        ],
        axis=1,
    )
    if linked:
        early = (
            mixed,
            second,
            attended,
            out_cotangent,
            gate_grad,
            resid_low,
            half_grad,
        )
        early, qkv_rows = reduce_back(early, shared, qkv_all, proj_full, seg_col, seg_row)
    else:
        shared = gather(shared)
        stats_all = shared[:, width : width + 2 * HEADS].astype(F32) + shared[
            :, width + 2 * HEADS : width + 4 * HEADS
        ].astype(F32)
        attn_grad_all = dot(shared[:, :width], proj_full, NT).astype(BF)
        qkv_rows = attn_bwd(pos, qkv_all, attn_grad_all, stats_all, seg_row, seg_col, rows)
    scale_one = rms_scale(inputs)
    first_low = (inputs * scale_one * gain_one).astype(BF)
    first_grad = dot(qkv_rows, qkv_full, NT)
    input_from_norm, gain_one_grad = rms_back(inputs, scale_one, gain_one, first_grad)
    tokens_grad = resid_grad + input_from_norm

    if linked:
        sums = jnp.stack([gain_one_grad, gain_two_grad])
        sums_high = lax.reduce_precision(sums, 8, 7)
        gain_rows = jnp.stack([sums_high, sums - sums_high], axis=1).reshape(4, width)
        gain_rows = jnp.concatenate([gain_rows.astype(BF), jnp.zeros((12, width), BF)])
        late, keys_share = reduce_late(
            first_low, qkv_rows, gain_rows, early[:, E_HALF:], query_weight
        )
        (
            out_share,
            gate_share,
            proj_share,
            qkv_share,
            query_share,
            gain_sums,
        ) = finish(early, late, keys_full)
    else:
        keys_grad = jnp.einsum(
            "tcn,tcf->cnf",
            half_cube,
            mem_query.reshape(rows, MHEADS * 2, HALF),
            preferred_element_type=F32,
        ).reshape(KEYS, HALF)
        partials = (
            dot(mixed, out_cotangent, TN),
            dot(second, gate_grad, TN),
            keys_grad,
            dot(second, query_grad, TN),
            dot(attended, resid_low, TN),
            dot(first_low, qkv_rows, TN),
        )
        shares = [
            lax.psum_scatter(x.astype(BF), "mem", scatter_dimension=0, tiled=True)
            for x in partials
        ]
        shares = lax.psum(tuple(shares), "grp")
        gain_sums = lax.psum(jnp.stack([gain_one_grad, gain_two_grad]), ALL)
        gain_sums = lax.dynamic_slice_in_dim(
            gain_sums, position * attn_gain.shape[0], attn_gain.shape[0], axis=1
        )
        out_share, gate_share, keys_share, query_share, proj_share, qkv_share = (
            x.astype(F32) for x in shares
        )
    return (
        block_out,
        tokens_grad,
        gain_sums[0],
        qkv_share,
        proj_share,
        gain_sums[1],
        query_share,
        keys_share,
        values_grad,
        gate_share,
        out_share,
    )


def solution(mesh):
    placed = (
        P(ALL, None),
        P("grp"),
        P(ALL, None, None),
        P("mem"),
        P("mem", None),
        P("mem", None),
        P("mem"),
        P("mem", None),
        P("mem", None),
        P(ALL, None),
        P("mem", None),
        P("mem", None),
        P(ALL, None),
    )
    return jax.shard_map(
        per_device,
        mesh=mesh,
        in_specs=placed,
        out_specs=(
            P(ALL, None),
            P(ALL, None),
            P("mem"),
            P("mem", None),
            P("mem", None),
            P("mem"),
            P("mem", None),
            P("mem", None),
            P(ALL, None),
            P("mem", None),
            P("mem", None),
        ),
        check_vma=False,
    )
```

```python
import functools

import jax
import jax.numpy as jnp
from jax import lax
from jax.experimental import pallas as pl
from jax.experimental.pallas import tpu as pltpu
from jax.sharding import PartitionSpec as P

HEADS = 16
HDIM = 64
MHEADS = 4
NK = 256
HALF = 512
TOPK = 32
EPS = 1e-05
LANES = 128
ALL = ("grp", "mem")
BF = jnp.bfloat16
F32 = jnp.float32
NEG = -1e30


def dot(left, right, dims=((1,), (0,))):
    return lax.dot_general(left, right, (dims, ((), ())), preferred_element_type=F32)


NT = ((1,), (1,))
TN = ((0,), (0,))


def iota(shape, dim):
    return lax.broadcasted_iota(jnp.int32, shape, dim)


def lane_halves(rows):
    first = iota((rows, LANES), 1) < HDIM
    return first


def half_masks():
    lane = iota((1, LANES), 1)
    return ((lane < HDIM).astype(BF), (lane >= HDIM).astype(BF))


def attn_fwd_pair(rows, win, pair, position, query, load, qseg_ref, kseg_ref, lse):
    row0 = position * rows
    start = pl.multiple_of(jnp.maximum(row0 + rows - win, 0), LANES)
    keys, values = load(1, pl.ds(start, win)), load(2, pl.ds(start, win))
    key_pos = start + iota((rows, win), 1)
    query_pos = row0 + iota((rows, win), 0)
    allowed = (key_pos <= query_pos) & (kseg_ref[:, pl.ds(start, win)] == qseg_ref[...])
    lane = iota((rows, LANES), 1)
    masks = half_masks()
    outs = []
    for half in range(2):
        scores = dot(query * masks[half], keys, NT) * 0.125
        scores = jnp.where(allowed, scores, NEG)
        top = jnp.max(scores, axis=1, keepdims=True)
        weights = jnp.exp(scores - top)
        total = jnp.sum(weights, axis=1, keepdims=True)
        probs = weights * (1.0 / total)
        outs.append(dot(probs.astype(BF), values))
        lse = jnp.where(lane == pair * 2 + half, top + jnp.log(total), lse)
    return jnp.where(lane < HDIM, outs[0], outs[1]), lse


def attn_fwd_kernel(rows, win, pos_ref, q_ref, k_ref, v_ref, qseg_ref, kseg_ref, out_ref, lse_ref):
    pair = pl.program_id(0)
    refs = (q_ref, k_ref, v_ref)
    lse = jnp.where(pair == 0, jnp.zeros((rows, LANES), F32), lse_ref[...])
    out_ref[...], lse_ref[...] = attn_fwd_pair(
        rows,
        win,
        pair,
        pos_ref[0],
        q_ref[...],
        lambda which, where: refs[which][where, :],
        qseg_ref,
        kseg_ref,
        lse,
    )


def attn_fwd(pos, qkv, seg_row, seg_col, rows):
    group_len, width = qkv.shape[0], qkv.shape[1] // 3
    pairs = width // LANES
    win = min(group_len, group_len // 2 + rows)
    return pl.pallas_call(
        functools.partial(attn_fwd_kernel, rows, win),
        grid_spec=pltpu.PrefetchScalarGridSpec(
            num_scalar_prefetch=1,
            grid=(pairs,),
            in_specs=[
                pl.BlockSpec((rows, LANES), lambda h, p: (p[0], h)),
                pl.BlockSpec((group_len, LANES), lambda h, p: (0, pairs + h)),
                pl.BlockSpec((group_len, LANES), lambda h, p: (0, 2 * pairs + h)),
                pl.BlockSpec((rows, 1), lambda h, p: (p[0], 0)),
                pl.BlockSpec((1, group_len), lambda h, p: (0, 0)),
            ],
            out_specs=[
                pl.BlockSpec((rows, LANES), lambda h, p: (0, h)),
                pl.BlockSpec((rows, LANES), lambda h, p: (0, 0)),
            ],
        ),
        out_shape=[
            jax.ShapeDtypeStruct((rows, width), F32),
            jax.ShapeDtypeStruct((rows, LANES), F32),
        ],
        cost_estimate=pl.CostEstimate(
            flops=4 * rows * win * width,
            bytes_accessed=group_len * width * 4,
            transcendentals=rows * win * HEADS,
        ),
        name="attn_fwd",
    )(pos, qkv, qkv, qkv, seg_col, seg_row)


def attn_bwd_pair(rows, win, pair, position, group_len, load, stat_ref, segc_ref, segr_ref):
    row0 = pl.multiple_of(position * rows, LANES)
    start = pl.multiple_of(jnp.maximum(row0 + rows - win, 0), LANES)
    qstart = pl.multiple_of(jnp.minimum(row0, group_len - win), LANES)
    own, back, ahead = pl.ds(row0, rows), pl.ds(start, win), pl.ds(qstart, win)
    masks = half_masks()
    lane = iota((rows, LANES), 1)

    def stat(where, index, count):
        table = stat_ref[where, :]
        return jnp.sum(
            jnp.where(iota((count, table.shape[1]), 1) == index, table, 0.0),
            axis=1,
            keepdims=True,
        )

    allowed = (start + iota((rows, win), 1) <= row0 + iota((rows, win), 0)) & (
        segr_ref[:, back] == segc_ref[own, :]
    )
    allowed_two = (row0 + iota((win, rows), 1) <= qstart + iota((win, rows), 0)) & (
        segr_ref[:, own] == segc_ref[ahead, :]
    )
    dqs, dks, dvs = [], [], []
    for half in range(2):
        head = pair * 2 + half
        lse, delta = stat(own, head, rows), stat(own, HEADS + head, rows)
        keys = load(1, back)
        scores = dot(load(0, own) * masks[half], keys, NT) * 0.125
        probs = jnp.exp(jnp.where(allowed, scores - lse, NEG))
        dprobs = dot(load(3, own) * masks[half], load(2, back), NT)
        grads = (probs * (dprobs - delta)).astype(BF)
        dqs.append(dot(grads, keys))
        lse, delta = stat(ahead, head, win), stat(ahead, HEADS + head, win)
        queries, douts = load(0, ahead), load(3, ahead)
        scores = dot(queries * masks[half], load(1, own), NT) * 0.125
        probs = jnp.exp(jnp.where(allowed_two, scores - lse, NEG))
        dprobs = dot(douts * masks[half], load(2, own), NT)
        grads = (probs * (dprobs - delta)).astype(BF)
        dks.append(dot(grads, queries, TN))
        dvs.append(dot(probs.astype(BF), douts, TN))
    return [
        (jnp.where(lane < HDIM, parts[0], parts[1]) * scale).astype(BF)
        for parts, scale in ((dqs, 0.125), (dks, 0.125), (dvs, 1.0))
    ]


def attn_bwd_kernel(
    rows, win, pairs, pos_ref, q_ref, k_ref, v_ref, da_ref, stat_ref, segc_ref, segr_ref, out_ref
):
    pair = pl.program_id(0)
    refs = (q_ref, k_ref, v_ref, da_ref)
    grads = attn_bwd_pair(
        rows,
        win,
        pair,
        pos_ref[0],
        k_ref.shape[0],
        lambda which, where: refs[which][where, :],
        stat_ref,
        segc_ref,
        segr_ref,
    )
    for i, value in enumerate(grads):
        column = pl.multiple_of((i * pairs + pair) * LANES, LANES)
        out_ref[:, pl.ds(column, LANES)] = value


def attn_bwd(pos, qkv, douts, stats, seg_row, seg_col, rows):
    group_len, width = douts.shape
    pairs = width // LANES
    win = min(group_len, group_len // 2 + rows)
    return pl.pallas_call(
        functools.partial(attn_bwd_kernel, rows, win, pairs),
        grid_spec=pltpu.PrefetchScalarGridSpec(
            num_scalar_prefetch=1,
            grid=(pairs,),
            in_specs=[
                pl.BlockSpec((group_len, LANES), lambda h, p: (0, h)),
                pl.BlockSpec((group_len, LANES), lambda h, p: (0, pairs + h)),
                pl.BlockSpec((group_len, LANES), lambda h, p: (0, 2 * pairs + h)),
                pl.BlockSpec((group_len, LANES), lambda h, p: (0, h)),
                pl.BlockSpec(stats.shape, lambda h, p: (0, 0)),
                pl.BlockSpec((group_len, 1), lambda h, p: (0, 0)),
                pl.BlockSpec((1, group_len), lambda h, p: (0, 0)),
            ],
            out_specs=pl.BlockSpec((rows, 3 * width), lambda h, p: (0, 0)),
        ),
        out_shape=jax.ShapeDtypeStruct((rows, 3 * width), BF),
        cost_estimate=pl.CostEstimate(
            flops=14 * rows * win * width,
            bytes_accessed=group_len * width * 8,
            transcendentals=2 * rows * win * HEADS,
        ),
        name="attn_bwd",
    )(pos, qkv, qkv, qkv, douts, stats, seg_col, seg_row)


def by_head(lane, reduce, fill, values):
    spread = jnp.zeros_like(values)
    for c in range(MHEADS):
        inside = lane // TOPK == c
        spread = jnp.where(
            inside, reduce(jnp.where(inside, values, fill), axis=1, keepdims=True), spread
        )
    return spread


def pick_fwd_kernel(scores_ref, picks_ref, weight_ref, low_ref):
    rows = picks_ref.shape[0]
    lane = iota((rows, LANES), 1)
    picks = picks_ref[...]
    index = (picks // NK, picks % NK)
    total = jnp.zeros((rows, LANES), F32)
    for c in range(MHEADS):
        both = jnp.zeros((rows, LANES), F32)
        for e in range(2):
            base = (c * 2 + e) * NK
            for part in range(NK // LANES):
                table = scores_ref[:, base + part * LANES : base + (part + 1) * LANES]
                found = jnp.take_along_axis(table, index[e] % LANES, axis=1)
                both = both + jnp.where(index[e] // LANES == part, found, 0.0)
        total = jnp.where(lane // TOPK == c, both, total)
    top = by_head(lane, jnp.max, NEG, total)
    weights = jnp.exp(total - top)
    weights = weights / by_head(lane, jnp.sum, 0.0, weights)
    weight_ref[...] = weights
    low_ref[...] = weights.astype(BF)


def pick_fwd(half_scores, picks):
    rows = picks.shape[0]
    return pl.pallas_call(
        pick_fwd_kernel,
        out_shape=[
            jax.ShapeDtypeStruct((rows, LANES), F32),
            jax.ShapeDtypeStruct((rows, LANES), BF),
        ],
        name="pick_fwd",
    )(half_scores, picks)


def pick_bwd_kernel(
    weight_ref,
    grad_ref,
    picks_ref,
    table_ref,
    out_ref,
    whole_ref,
    score_t,
    first_t,
    second_t,
    stage,
    in_sem,
    out_sem,
):
    block = table_ref.shape[0] // MHEADS

    def part(c):
        return pl.ds(pl.multiple_of(c * block, block), block)

    def fetch(c):
        return pltpu.make_async_copy(table_ref.at[part(c)], stage.at[c], in_sem.at[c])

    def put(c):
        return pltpu.make_async_copy(stage.at[c], whole_ref.at[part(c)], out_sem.at[c])

    for c in range(MHEADS):
        fetch(c).start()
    rows = picks_ref.shape[0]
    lane = iota((rows, LANES), 1)
    weights, grads = weight_ref[...], grad_ref[...]
    score = (weights * (grads - by_head(lane, jnp.sum, 0.0, weights * grads))).astype(BF)
    score_t[...] = score.astype(F32).T
    picks_t = picks_ref[...].T
    first_t[...] = picks_t // NK
    second_t[...] = picks_t % NK
    key = iota((NK, rows), 0)

    def head(c, _):
        first = jnp.zeros((NK, rows), F32)
        second = jnp.zeros((NK, rows), F32)
        for j in range(TOPK):
            at = pl.ds(c * TOPK + j, 1)
            value = score_t[at, :]
            first = first + jnp.where(key == first_t[at, :], value, 0.0)
            second = second + jnp.where(key == second_t[at, :], value, 0.0)
        for e, total in enumerate((first, second)):
            base = pl.multiple_of((c * 2 + e) * NK, LANES)
            out_ref[:, pl.ds(base, NK)] = total.T.astype(BF)
        fetch(c).wait()
        put(c).start()
        return 0

    lax.fori_loop(0, MHEADS, head, 0)
    for c in range(MHEADS):
        put(c).wait()


def pick_bwd(weights, grads, picks, table):
    rows = picks.shape[0]
    last = grads.shape[1] // LANES - 1
    spec = pl.BlockSpec((rows, LANES), lambda i: (0, 0))
    hbm = pl.BlockSpec(memory_space=pltpu.HBM)
    return pl.pallas_call(
        pick_bwd_kernel,
        grid=(1,),
        in_specs=[spec, pl.BlockSpec((rows, LANES), lambda i: (0, last)), spec, hbm],
        out_specs=[pl.BlockSpec((rows, MHEADS * 2 * NK), lambda i: (0, 0)), hbm],
        out_shape=[
            jax.ShapeDtypeStruct((rows, MHEADS * 2 * NK), BF),
            jax.ShapeDtypeStruct(table.shape, table.dtype),
        ],
        scratch_shapes=[
            pltpu.VMEM((LANES, rows), F32),
            pltpu.VMEM((LANES, rows), jnp.int32),
            pltpu.VMEM((LANES, rows), jnp.int32),
            pltpu.VMEM((MHEADS, table.shape[0] // MHEADS, table.shape[1]), table.dtype),
            pltpu.SemaphoreType.DMA((MHEADS,)),
            pltpu.SemaphoreType.DMA((MHEADS,)),
        ],
        compiler_params=pltpu.CompilerParams(vmem_limit_bytes=40 * 1024 * 1024),
        name="pick_bwd",
    )(weights, grads, picks, table)


def owner_kernel(
    his, flat_bits, local_rows, keys_ref, sent_ref, values_ref, part_ref, spread_ref
):
    rows = part_ref.shape[0]
    width = values_ref.shape[1]
    slots = keys_ref.shape[-1]
    low_rows = local_rows // his
    key = keys_ref[0]
    flat = key & ((1 << flat_bits) - 1)
    dummy = ((key >> flat_bits) & 1) == 1
    row = (key >> (flat_bits + 1)) % local_rows
    token = flat // LANES
    pick = flat % LANES
    token = jnp.where(dummy, -1, token)
    block = jnp.where(dummy, -1, (row // low_rows) * rows + token)
    low_row = row % low_rows
    grad = sent_ref[:, :width]
    weights = sent_ref[:, width:]
    is_token = iota((rows, slots), 0) == token
    is_pick = iota((LANES, slots), 0) == pick
    token_hot = is_token.astype(F32).astype(BF)
    found = dot(weights, token_hot, TN)
    weight = jnp.sum(jnp.where(is_pick, found, 0.0), axis=0, keepdims=True)
    is_block = iota((his * rows, slots), 0) == block
    is_low = iota((low_rows, slots), 0) == low_row
    low_hot = is_low.astype(F32).astype(BF)
    spread = dot(jnp.where(is_block, weight, 0.0).astype(BF), low_hot, NT).astype(BF)
    total = jnp.zeros((rows, width), F32)
    products = []
    for h in range(his):
        table = values_ref[h * low_rows : (h + 1) * low_rows, :]
        piece = spread[h * rows : (h + 1) * rows, :]
        spread_ref[h] = piece
        total = total + dot(piece, table)
        products.append(dot(grad, table, NT).astype(BF))
    picked = dot(jnp.concatenate(products, axis=0), is_block.astype(F32).astype(BF), TN)
    picked = jnp.sum(jnp.where(is_low, picked, 0.0), axis=0, keepdims=True)
    part_ref[:, :width] = total.astype(BF)
    part_ref[:, width:] = dot(
        jnp.where(is_token, picked, 0.0).astype(BF), is_pick.astype(F32).astype(BF), NT
    ).astype(BF)


def owner_call(keys, sent, values, flat_bits):
    owners, slots = keys.shape
    rows = sent.shape[0] // owners
    local_rows, width = values.shape
    his = 4
    low_rows = local_rows // his
    return pl.pallas_call(
        functools.partial(owner_kernel, his, flat_bits, local_rows),
        grid=(owners,),
        in_specs=[
            pl.BlockSpec((1, 1, slots), lambda s: (s, 0, 0)),
            pl.BlockSpec((rows, width + LANES), lambda s: (s, 0)),
            pl.BlockSpec((local_rows, width), lambda s: (0, 0)),
        ],
        out_specs=[
            pl.BlockSpec((rows, width + LANES), lambda s: (s, 0)),
            pl.BlockSpec((his, rows, low_rows), lambda s: (0, s, 0)),
        ],
        out_shape=[
            jax.ShapeDtypeStruct((owners * rows, width + LANES), BF),
            jax.ShapeDtypeStruct((his, owners * rows, low_rows), BF),
        ],
        compiler_params=pltpu.CompilerParams(vmem_limit_bytes=48 * 1024 * 1024),
        cost_estimate=pl.CostEstimate(
            flops=2 * owners * rows * local_rows * (2 * slots + 2 * width),
            bytes_accessed=owners * rows * (2 * width + local_rows) * 2,
            transcendentals=0,
        ),
        name="owner",
    )(keys.reshape(owners, 1, slots), sent, values)


def route(picks, owners, local_rows, capacity, flat_bits):
    total = picks.size
    rows_of = picks.reshape(total)
    flat = jnp.arange(total, dtype=jnp.int32)
    each = jnp.arange(owners, dtype=jnp.int32)
    counts = jnp.sum((rows_of[:, None] // local_rows == each[None, :]).astype(jnp.int32), axis=0)
    ends = jnp.cumsum(capacity - counts)
    spares = owners * capacity - total
    spare_owner = jnp.sum(
        (jnp.arange(spares, dtype=jnp.int32)[:, None] >= ends[None, :]).astype(jnp.int32), axis=1
    )
    real = (rows_of << (flat_bits + 1)) + flat
    spare = ((spare_owner * local_rows + local_rows - 1) << (flat_bits + 1)) + (1 << flat_bits)
    keys = lax.sort(jnp.concatenate([real, spare]), is_stable=False)
    return keys.reshape(owners, capacity)


MESH = pl.DeviceIdType.MESH


def places():
    g, m = lax.axis_index("grp"), lax.axis_index("mem")
    across = g + 1 - 2 * (g % 2)
    along = (g + 2) % 4
    sibling = m + 1 - 2 * (m % 2)
    return g, m, across, along, sibling


def enter(peers):
    barrier = pltpu.get_barrier_semaphore()
    for peer in peers:
        pl.semaphore_signal(barrier, inc=1, device_id=peer, device_id_type=MESH)
    pl.semaphore_wait(barrier, len(peers))


def push(src, dst, send, recv, peer):
    copy = pltpu.make_async_remote_copy(
        src_ref=src, dst_ref=dst, send_sem=send, recv_sem=recv, device_id=peer, device_id_type=MESH
    )
    copy.start()
    return copy


def plane_tasks(held, x1, y1, x2, y2, zin, send, recv):
    g, m, across, along, _ = places()
    diagonal = 3 - g
    half = held.shape[2] // 2
    low, high = pl.ds(0, half), pl.ds(half, half)
    to_x, to_y = (across, m), (along, m)

    def copy(kind, k, src, dst, peer):
        return pltpu.make_async_remote_copy(
            src_ref=src,
            dst_ref=dst,
            send_sem=send.at[kind, k],
            recv_sem=recv.at[kind, k],
            device_id=peer,
            device_id_type=MESH,
        )

    def ones(k):
        return (
            copy(0, k, held.at[k, diagonal, low], x1.at[k], to_x),
            copy(1, k, held.at[k, diagonal, high], y1.at[k], to_y),
        )

    def twos(k):
        return (
            copy(2, k, held.at[k, across], x2.at[k], to_x),
            copy(3, k, held.at[k, along], y2.at[k], to_y),
        )

    def three(k):
        return copy(4, k, held.at[k, g], zin.at[k], (g, (m + 2 * (3 - k)) % 8))

    def first(k):
        for item in ones(k):
            item.start()

    def corner(k):
        for item in ones(k):
            item.wait_recv()
        held[k, along, low] = held[k, along, low] + x1[k]
        held[k, across, high] = held[k, across, high] + y1[k]
        for item in twos(k):
            item.start()

    def total_of(k):
        for item in twos(k):
            item.wait_recv()
        return held[k, g].astype(F32) + x2[k].astype(F32) + y2[k].astype(F32)

    def plane(k):
        held[k, g] = total_of(k).astype(BF)
        three(k).start()

    def last():
        total = total_of(3)
        for k in range(3):
            three(k).wait_recv()
            total = total + zin[k].astype(F32)
        for k in range(4):
            for item in ones(k) + twos(k):
                item.wait_send()
            if k < 3:
                three(k).wait_send()
        return total

    return first, corner, plane, last


def plane_peers():
    g, m, across, along, sibling = places()
    return [(across, m), (along, m), (g, sibling)] + [(g, (m + 2 * d) % 8) for d in (1, 2, 3)]


def plane_scratch(rows, columns):
    return [
        pltpu.VMEM((4, rows // 2, columns), BF),
        pltpu.VMEM((4, rows // 2, columns), BF),
        pltpu.VMEM((4, rows, columns), BF),
        pltpu.VMEM((4, rows, columns), BF),
        pltpu.VMEM((3, rows, columns), BF),
    ]


def memory_kernel(
    flat_bits,
    payload_ref,
    keys_ref,
    values_ref,
    out_ref,
    grad_ref,
    sent,
    parts,
    sibs,
    x1,
    y1,
    x2,
    y2,
    zin,
    held,
    spread,
    table,
    own_sem,
    table_sem,
    send,
    recv,
):
    g, m, across, along, sibling = places()
    core, z = m % 2, m // 2
    to_x, to_y, to_s = (across, m), (along, m), (g, sibling)
    rows, columns = payload_ref.shape
    width = columns - LANES
    local_rows = values_ref.shape[0]
    slots = keys_ref.shape[1]
    his = spread.shape[0]
    low_rows = local_rows // his
    low, high = pl.ds(0, rows // 2), pl.ds(rows // 2, rows // 2)
    enter(plane_peers())

    def copy(kind, index, src, dst, peer):
        return pltpu.make_async_remote_copy(
            src_ref=src,
            dst_ref=dst,
            send_sem=send.at[kind, index],
            recv_sem=recv.at[kind, index],
            device_id=peer,
            device_id_type=MESH,
        )

    def mine(i):
        return payload_ref if i == 0 else sent.at[i, core]

    def to_sibling(i):
        return copy(0, i, mine(i), sent.at[i, core], to_s)

    def plane_x(k):
        return copy(1, k, mine(4 * k), sent.at[4 * k + 1, core], to_x)

    def plane_y(k):
        return copy(2, k, mine(4 * k), sent.at[4 * k + 2, core], to_y)

    def line(k):
        return copy(3, k, payload_ref, sent.at[4 * k, core], (g, (m + 2 * k) % 8))

    def corner_y(k):
        return copy(4, k, sent.at[4 * k + 1, core, low], sent.at[4 * k + 3, core, low], to_y)

    def corner_x(k):
        return copy(5, k, sent.at[4 * k + 2, core, high], sent.at[4 * k + 3, core, high], to_x)

    def part_sibling(i):
        return copy(6, i, parts.at[i, 1 - core], sibs.at[i], to_s)

    def one_x(k):
        return copy(7, k, parts.at[4 * k + 3, core, low], x1.at[k], to_x)

    def one_y(k):
        return copy(8, k, parts.at[4 * k + 3, core, high], y1.at[k], to_y)

    def two_x(k):
        return copy(9, k, parts.at[4 * k + 1, core], x2.at[k], to_x)

    def two_y(k):
        return copy(10, k, parts.at[4 * k + 2, core], y2.at[k], to_y)

    def three(k):
        return copy(11, k, parts.at[4 * k, core], zin.at[k - 1], (g, (m + 8 - 2 * k) % 8))

    def from_line(k):
        line(k).wait_recv()
        plane_x(k).start()
        plane_y(k).start()
        to_sibling(4 * k).start()

    def from_plane(k):
        plane_x(k).wait_recv()
        corner_y(k).start()
        to_sibling(4 * k + 1).start()
        plane_y(k).wait_recv()
        corner_x(k).start()
        to_sibling(4 * k + 2).start()

    def from_corner(k):
        corner_x(k).wait_recv()
        corner_y(k).wait_recv()
        to_sibling(4 * k + 3).start()

    def pair_sum(k):
        for i in (4 * k + 3, 4 * k + 1, 4 * k + 2, 4 * k):
            part_sibling(i).wait_recv()
            parts[i, core] = parts[i, core] + sibs[i]
            if i == 4 * k + 3:
                one_x(k).start()
                one_y(k).start()

    def corner_sum(k):
        one_x(k).wait_recv()
        parts[4 * k + 2, core, low] = parts[4 * k + 2, core, low] + x1[k]
        two_y(k).start()
        one_y(k).wait_recv()
        parts[4 * k + 1, core, high] = parts[4 * k + 1, core, high] + y1[k]
        two_x(k).start()

    def plane_sum(k):
        two_x(k).wait_recv()
        two_y(k).wait_recv()
        total = parts[4 * k, core].astype(F32) + x2[k].astype(F32) + y2[k].astype(F32)
        if k == 0:
            held[...] = total
        else:
            parts[4 * k, core] = total.astype(BF)
            three(k).start()

    own = pltpu.make_async_copy(payload_ref, sent.at[0, core], own_sem)
    own.start()
    to_sibling(0).start()
    plane_x(0).start()
    plane_y(0).start()
    for k in (1, 2, 3):
        line(k).start()
    own.wait()

    tasks = {
        1: [lambda: from_plane(0)],
        2: [lambda: from_line(1)],
        3: [lambda: from_corner(0), lambda: from_line(2)],
        4: [lambda: from_line(3), lambda: pair_sum(0)],
        5: [lambda: from_plane(1)],
        6: [lambda: corner_sum(0)],
        7: [lambda: from_corner(1)],
        8: [lambda: from_plane(2), lambda: pair_sum(1)],
        9: [lambda: plane_sum(0)],
        10: [lambda: from_corner(2), lambda: corner_sum(1)],
        11: [lambda: from_plane(3)],
        12: [lambda: pair_sum(2), lambda: plane_sum(1)],
        13: [lambda: from_corner(3)],
        14: [lambda: corner_sum(2)],
    }

    def step(i, _):
        for when, todo in tasks.items():

            @pl.when(i == when)
            def _():
                for task in todo:
                    task()

        copy(0, i, sent.at[i, core], sent.at[i, 1 - core], to_s).wait_recv()
        k, j = i // 4, i % 4
        grp = (g // 2 + j // 2) % 2 * 2 + (g % 2 + j % 2) % 2
        base = grp * 8 + (z + 4 - k) % 4 * 2
        lanes, tiles = [], []
        for c in range(2):
            key = keys_ref[pl.ds(base + c, 1), :]
            flat = key & ((1 << flat_bits) - 1)
            dummy = ((key >> flat_bits) & 1) == 1
            row = (key >> (flat_bits + 1)) % local_rows
            token = jnp.where(dummy, -1, flat // LANES)
            block = jnp.where(dummy, -1, (row // low_rows) * rows + token)
            is_token = iota((rows, slots), 0) == token
            is_pick = iota((LANES, slots), 0) == flat % LANES
            place = jnp.concatenate(
                [
                    jnp.where(is_token, (row % LANES).astype(F32), 0.0).astype(BF),
                    jnp.where(is_token, (row // LANES + 1).astype(F32), 0.0).astype(BF),
                ],
                axis=0,
            )
            place = dot(place, is_pick.astype(F32).astype(BF), NT).astype(jnp.int32)
            lanes.append(place[:rows])
            tiles.append(place[rows:] - 1)
            weights = sent[i, c, :, width:]
            found = dot(weights, is_token.astype(F32).astype(BF), TN)
            weight = jnp.sum(jnp.where(is_pick, found, 0.0), axis=0, keepdims=True)
            is_block = iota((his * rows, slots), 0) == block
            is_low = iota((low_rows, slots), 0) == row % low_rows
            piece = dot(
                jnp.where(is_block, weight, 0.0).astype(BF), is_low.astype(F32).astype(BF), NT
            ).astype(BF)
            for h in range(his):
                spread[h, 2 * i + c] = piece[h * rows : (h + 1) * rows]
        lane, tile = jnp.concatenate(lanes, axis=0), jnp.concatenate(tiles, axis=0)
        grads = sent[i, :, :, :width].reshape(2 * rows, width)
        total = jnp.zeros((2 * rows, width), F32)
        picked = jnp.zeros((2 * rows, LANES), F32)
        for h in range(his):
            table = values_ref[h * low_rows : (h + 1) * low_rows, :]
            piece = spread[h, pl.ds(2 * i, 2)].reshape(2 * rows, low_rows)
            total = total + dot(piece, table)
            products = dot(grads, table, NT)
            for b in range(low_rows // LANES):
                found = jnp.take_along_axis(
                    products[:, b * LANES : (b + 1) * LANES], lane, axis=1
                )
                picked = jnp.where(tile == h * (low_rows // LANES) + b, found, picked)
        parts[i, :, :, :width] = total.astype(BF).reshape(2, rows, width)
        parts[i, :, :, width:] = picked.astype(BF).reshape(2, rows, LANES)
        part_sibling(i).start()
        return 0

    def table_copy(h):
        return pltpu.make_async_copy(table.at[h % 2], grad_ref.at[h], table_sem.at[h % 2])

    def table_grad(h):
        if h >= 2:
            table_copy(h - 2).wait()

        def some(n, _):
            grads = sent[pl.ds(4 * n, 4), :, :, :width].reshape(8 * rows, width)
            piece = spread[h, pl.ds(8 * n, 8)].reshape(8 * rows, low_rows)
            table[h % 2] = jnp.where(n == 0, 0.0, table[h % 2]) + dot(piece, grads, TN)
            return 0

        lax.fori_loop(0, 4, some, 0)
        table_copy(h).start()

    lax.fori_loop(0, 16, step, 0)
    plane_sum(2)
    pair_sum(3)
    table_grad(0)
    corner_sum(3)
    table_grad(1)
    plane_sum(3)
    table_grad(2)
    table_grad(3)
    total = held[...]
    for k in (1, 2, 3):
        three(k).wait_recv()
        total = total + zin[k - 1].astype(F32)
    out_ref[...] = total
    for k in range(4):
        todo = [plane_x(k), plane_y(k), corner_x(k), corner_y(k)]
        todo += [one_x(k), one_y(k), two_x(k), two_y(k)]
        if k:
            todo += [line(k), three(k)]
        for j in range(4):
            todo += [to_sibling(4 * k + j), part_sibling(4 * k + j)]
        for item in todo:
            item.wait_send()
    table_copy(2).wait()
    table_copy(3).wait()


def memory_call(payload, keys, values, flat_bits):
    rows, columns = payload.shape
    local_rows = values.shape[0]
    his = 4
    half = (4, rows // 2, columns)
    full = (4, rows, columns)
    vmem = pl.BlockSpec(memory_space=pltpu.VMEM)
    hbm = pl.BlockSpec(memory_space=pl.ANY)
    return pl.pallas_call(
        functools.partial(memory_kernel, flat_bits),
        in_specs=[hbm, vmem, vmem],
        out_specs=[vmem, hbm],
        out_shape=[
            jax.ShapeDtypeStruct((rows, columns), F32),
            jax.ShapeDtypeStruct((his, local_rows // his, columns - LANES), F32),
        ],
        scratch_shapes=[
            pltpu.VMEM((16, 2, rows, columns), BF),
            pltpu.VMEM((16, 2, rows, columns), BF),
            pltpu.VMEM((16, rows, columns), BF),
            pltpu.VMEM(half, BF),
            pltpu.VMEM(half, BF),
            pltpu.VMEM(full, BF),
            pltpu.VMEM(full, BF),
            pltpu.VMEM((3, rows, columns), BF),
            pltpu.VMEM((rows, columns), F32),
            pltpu.VMEM((his, 32, rows, local_rows // his), BF),
            pltpu.VMEM((2, local_rows // his, columns - LANES), F32),
            pltpu.SemaphoreType.DMA,
            pltpu.SemaphoreType.DMA((2,)),
            pltpu.SemaphoreType.DMA((12, 16)),
            pltpu.SemaphoreType.DMA((12, 16)),
        ],
        compiler_params=pltpu.CompilerParams(
            collective_id=1, has_side_effects=True, vmem_limit_bytes=63 * 1024 * 1024
        ),
        name="memory",
    )(payload, keys, values)


def gather_tasks(pieces, sources, targets, local_sem, send, recv):
    g, m, across, along, sibling = places()
    z = m // 2
    to_x, to_y, to_s = (across, m), (along, m), (g, sibling)
    total = range(len(pieces))
    ways = [(sign, hop) for hop in (1, 2, 3) for sign in (1, -1)]
    shared = [p for p in total if pieces[p][3]]

    def view(piece, owner, quarter=None, part=None):
        array, first, columns, _ = pieces[piece]
        ref = targets[array]
        size = ref.shape[0] // 8
        start = owner * size
        if quarter is not None:
            size = size // 4
            start = start + quarter * size
        if part is not None:
            size = size // 2
            start = start + part * size
        return ref.at[pl.ds(start, size), pl.ds(first, columns)]

    def copy(piece, index, block, peer, src=None):
        return pltpu.make_async_remote_copy(
            src_ref=block if src is None else src,
            dst_ref=block,
            send_sem=send.at[piece, index],
            recv_sem=recv.at[piece, index],
            device_id=peer,
            device_id_type=MESH,
        )

    def line(p, way, owner, src=None):
        block = view(p, owner, g if pieces[p][3] else None)
        peer = (g, (m + 8 + 2 * ways[way][0]) % 8)
        return copy(p, way, block, peer, src)

    def has(way):
        sign, distance = ways[way]
        return z >= distance if sign > 0 else z + distance <= 3

    def more(way):
        return z <= 2 if ways[way][0] > 0 else z >= 1

    def origin(way):
        sign, distance = ways[way]
        return (m + 8 - 2 * sign * distance) % 8

    def planes(p, way):
        block = view(p, origin(way), g)
        return copy(p, 6 + way, block, to_x), copy(p, 12 + way, block, to_y)

    def corners(p, way):
        owner = origin(way)
        return (
            copy(p, 18 + way, view(p, owner, across, 0), to_y),
            copy(p, 24 + way, view(p, owner, along, 1), to_x),
        )

    def core(p, way):
        return copy(p, 30 + way, view(p, origin(way)), to_s)

    def first(p):
        array, start, columns, is_shared = pieces[p]
        ref = sources[array]
        whole = ref.at[:, pl.ds(start, columns)]
        src = whole
        if is_shared:
            quarter = ref.shape[0] // 4
            src = ref.at[pl.ds(g * quarter, quarter), pl.ds(start, columns)]
        return (
            [line(p, way, m, src) for way in (0, 1)],
            pltpu.make_async_copy(whole, view(p, m), local_sem.at[p]),
            copy(p, 36, view(p, m), to_s, whole),
        )

    def begin():
        for p in total:
            for way in (0, 1):
                pl.when(more(way))(first(p)[0][way].start)
        for p in total:
            _, near, side = first(p)
            near.start()
            side.start()

    def level(hop):
        return (2 * hop - 2, 2 * hop - 1)

    def arrive(hop):
        for p in total:
            for way in level(hop):

                @pl.when(has(way))
                def _():
                    line(p, way, origin(way)).wait_recv()
                    if hop < 3:
                        pl.when(more(way))(line(p, way + 2, origin(way)).start)

        for p in total:
            for way in level(hop):

                @pl.when(has(way))
                def _():
                    for item in planes(p, way) if p in shared else [core(p, way)]:
                        item.start()

    def turn(hop):
        for p in shared:
            for way in level(hop):

                @pl.when(has(way))
                def _():
                    for item, after in zip(planes(p, way), corners(p, way), strict=True):
                        item.wait_recv()
                        after.start()

    def cross(hop):
        for p in shared:
            for way in level(hop):

                @pl.when(has(way))
                def _():
                    for item in corners(p, way):
                        item.wait_recv()
                    core(p, way).start()

    def receive():
        for p in total:
            _, near, side = first(p)
            near.wait()
            side.wait_recv()
            for way in range(6):

                @pl.when(has(way))
                def _():
                    core(p, way).wait_recv()

    def drain():
        for p in total:
            out, _, side = first(p)
            side.wait_send()
            for way in (0, 1):
                pl.when(more(way))(out[way].wait_send)
            for way in range(6):

                @pl.when(has(way))
                def _():
                    core(p, way).wait_send()
                    if ways[way][1] < 3:
                        pl.when(more(way))(line(p, way + 2, origin(way)).wait_send)
                    if p in shared:
                        for item in planes(p, way) + corners(p, way):
                            item.wait_send()

    return begin, arrive, turn, cross, receive, drain


def pieces_of(arrays, chunk, own_count):
    pieces = []
    for i, x in enumerate(arrays):
        columns = x.shape[1]
        for first in range(0, columns, chunk):
            pieces.append((i, first, min(chunk, columns - first), i >= own_count))
    return tuple(pieces)


def gathered(arrays):
    return [jax.ShapeDtypeStruct((8 * x.shape[0], x.shape[1]), x.dtype) for x in arrays]


def gather_sems(pieces):
    return [
        pltpu.SemaphoreType.DMA((len(pieces),)),
        pltpu.SemaphoreType.DMA((len(pieces), 37)),
        pltpu.SemaphoreType.DMA((len(pieces), 37)),
    ]


def gather_kernel(sets, rows, win, *refs):
    sources, refs = refs[:7], refs[7:]
    query_ref, segc_ref, segr_ref = refs[:3]
    targets, refs = refs[3:9], refs[9:]
    qkv_ref, out_ref, lse_ref, gains = refs[:4]
    tokens, gain_row, normal, folded = refs[4:8]
    sems = refs[8:]
    keys_src, qkv_src, proj_src, gate_src, head_src, tokens_src, gain_src = sources
    keys_full, weight_full, proj_full, gate_full, head_full, folded_full = targets
    m = lax.axis_index("mem")
    group_len, width = tokens.shape
    pairs = width // LANES
    enter(plane_peers())
    k_set, a_set, c_set, b_set = (
        gather_tasks(pieces, src, dst, *sems[3 * i : 3 * i + 3])
        for i, (pieces, src, dst) in enumerate(
            zip(
                sets,
                (
                    [keys_src],
                    [tokens_src, gain_src, qkv_src],
                    [folded],
                    [proj_src, gate_src, head_src],
                ),
                (
                    [keys_full],
                    [tokens, gains, weight_full],
                    [folded_full],
                    [proj_full, gate_full, head_full],
                ),
                strict=True,
            )
        )
    )
    begin, arrive, turn, cross, receive, drain = range(6)

    def go(which, task, *hop):
        which[task](*hop)

    def fold():
        for c in range(MHEADS * 2):
            folded[:, c * NK : (c + 1) * NK] = dot(
                query_ref[:, c * HALF : (c + 1) * HALF], keys_full[c * NK : (c + 1) * NK, :], NT
            ).astype(BF)

    def normalize():
        for i in range(8):
            gain_row[:, i * LANES : (i + 1) * LANES] = gains[i * 16 : i * 16 + 1, :].astype(F32)
        block = 2 * rows

        def some(i, _):
            where = pl.ds(pl.multiple_of(i * block, block), block)
            values = tokens[where, :].astype(F32)
            normal[where, :] = (values * rms_scale(values) * gain_row[...]).astype(BF)
            return 0

        lax.fori_loop(0, group_len // block, some, 0)

    def project(i, _):
        where = pl.ds(pl.multiple_of(i * 3 * LANES, LANES), 3 * LANES)
        qkv_ref[:, where] = dot(normal[...], weight_full[:, where]).astype(BF)
        during(i, PROJECT_TASKS)
        return 0

    def load_of(pair):
        def load(which, where):
            column = pl.multiple_of((which * pairs + pair) * LANES, LANES)
            return qkv_ref[where, pl.ds(column, LANES)]

        return load

    own = pl.ds(pl.multiple_of(m * rows, LANES), rows)

    def attend(pair, _):
        load = load_of(pair)
        value, lse_ref[...] = attn_fwd_pair(
            rows, win, pair, m, load(0, own), load, segc_ref.at[own], segr_ref, lse_ref[...]
        )
        out_ref[:, pl.ds(pl.multiple_of(pair * LANES, LANES), LANES)] = value
        during(pair, ATTEND_TASKS)
        return 0

    def during(i, tasks):
        for when, todo in tasks.items():

            @pl.when(i == when)
            def _():
                for which, task, hop in todo:
                    go(which, task, hop)

    PROJECT_TASKS = {
        0: [(c_set, turn, 1), (b_set, arrive, 2)],
        2: [(b_set, turn, 1), (c_set, arrive, 3)],
        4: [(c_set, turn, 2), (b_set, arrive, 3)],
        6: [(b_set, turn, 2), (c_set, cross, 1)],
    }
    ATTEND_TASKS = {
        0: [(c_set, turn, 3), (b_set, cross, 1)],
        2: [(b_set, turn, 3), (c_set, cross, 2)],
        3: [(b_set, cross, 2)],
        4: [(c_set, cross, 3)],
        5: [(b_set, cross, 3)],
    }
    lse_ref[...] = jnp.zeros_like(lse_ref)
    go(k_set, begin)
    go(a_set, begin)
    go(k_set, arrive, 1)
    go(k_set, arrive, 2)
    go(a_set, arrive, 1)
    go(k_set, turn, 1)
    go(k_set, arrive, 3)
    go(k_set, turn, 2)
    go(k_set, cross, 1)
    go(k_set, turn, 3)
    go(k_set, cross, 2)
    go(a_set, arrive, 2)
    go(k_set, cross, 3)
    go(a_set, turn, 1)
    go(k_set, receive)
    fold()
    go(c_set, begin)
    go(b_set, begin)
    go(a_set, arrive, 3)
    go(a_set, turn, 2)
    go(a_set, cross, 1)
    go(c_set, arrive, 1)
    go(a_set, turn, 3)
    go(b_set, arrive, 1)
    go(a_set, cross, 2)
    go(a_set, cross, 3)
    go(c_set, arrive, 2)
    go(a_set, receive)
    normalize()
    lax.fori_loop(0, 8, project, 0)
    lax.fori_loop(0, 8, attend, 0)
    go(c_set, receive)
    go(b_set, receive)
    for one in (k_set, a_set, c_set, b_set):
        go(one, drain)


def gather_weights(keys, qkv, proj, gate, head, tokens, gains, query, seg_col, seg_row, rows):
    sets = (
        pieces_of([keys], WIDTH, 0),
        pieces_of([tokens, gains, qkv], 3 * WIDTH, 2),
        pieces_of([jax.ShapeDtypeStruct((query.shape[0], KEYS), BF)], KEYS, 0),
        pieces_of([proj, gate, head], WIDTH, 0),
    )
    group_len = seg_col.shape[0]
    width = tokens.shape[1]
    win = min(group_len, group_len // 2 + rows)
    vmem, hbm = pl.BlockSpec(memory_space=pltpu.VMEM), pl.BlockSpec(memory_space=pl.ANY)
    sems = []
    for pieces in sets:
        sems += gather_sems(pieces)
    return pl.pallas_call(
        functools.partial(gather_kernel, sets, rows, win),
        in_specs=[vmem] * 10,
        out_specs=[vmem, vmem, hbm, hbm, hbm, hbm, vmem, vmem, vmem, vmem],
        out_shape=[
            *gathered([keys, qkv, proj, gate, head]),
            jax.ShapeDtypeStruct((8 * query.shape[0], KEYS), BF),
            jax.ShapeDtypeStruct((group_len, 3 * width), BF),
            jax.ShapeDtypeStruct((rows, width), F32),
            jax.ShapeDtypeStruct((rows, LANES), F32),
            *gathered([gains]),
        ],
        scratch_shapes=[
            pltpu.VMEM((group_len, width), BF),
            pltpu.VMEM((1, width), F32),
            pltpu.VMEM((group_len, width), BF),
            pltpu.VMEM((query.shape[0], KEYS), BF),
            *sems,
        ],
        compiler_params=pltpu.CompilerParams(
            collective_id=3, has_side_effects=True, vmem_limit_bytes=56 * 1024 * 1024
        ),
        name="gather_weights",
    )(keys, qkv, proj, gate, head, tokens, gains, query, seg_col, seg_row)


WIDTH = HEADS * HDIM
KEYS = MHEADS * 2 * NK
QUERIES = MHEADS * 2 * HALF
EARLY = (WIDTH,) * 6 + (KEYS,)
EARLY_PRODUCTS = (
    (0, 3 * WIDTH, WIDTH, 0),
    (WIDTH, 4 * WIDTH, WIDTH, WIDTH),
    (2 * WIDTH, 5 * WIDTH, WIDTH, 2 * WIDTH),
    (WIDTH, 6 * WIDTH, KEYS, 3 * WIDTH),
)
E_OUT, E_GATE, E_PROJ, E_HALF = 0, WIDTH, 2 * WIDTH, 3 * WIDTH
E_ALL = E_HALF + KEYS
LATE = (WIDTH, 3 * WIDTH)
LATE_PRODUCTS = ((0, WIDTH, 3 * WIDTH, 0),)
L_GAIN = 3 * WIDTH
L_ALL = L_GAIN + LANES


def share_factors(moves, local_sem, send, recv):
    g, _, _, _, sibling = places()
    copies = []
    for i, (src, dst, at, columns) in enumerate(moves):
        count = src.shape[0]
        where = pl.ds(at, columns)
        far = push(
            src, dst.at[pl.ds(count, count), where], send.at[5, i], recv.at[5, i], (g, sibling)
        )
        near = pltpu.make_async_copy(src, dst.at[pl.ds(0, count), where], local_sem.at[i])
        near.start()
        copies.append((near, far))
    return copies


def factor_moves(refs, widths, fact):
    moves, at = [], 0
    for ref, columns in zip(refs, widths, strict=True):
        moves.append((ref, fact, at, columns))
        at += columns
    return moves


def store_blocks(held, k, value, at):
    for i in range(4):
        held[k, i, :, at : at + value.shape[1]] = value[i * 32 : (i + 1) * 32].astype(BF)


def block_of(k):
    m = lax.axis_index("mem")
    return (m // 2 + 3 - k) % 4 * 2 + m % 2


def products_of(k, fact, held, products):
    block = block_of(k)
    for left, right, count, at in products:
        lhs = fact[:, pl.ds(pl.multiple_of(left + block * LANES, LANES), LANES)]
        for j in range(0, count, WIDTH):
            store_blocks(held, k, dot(lhs, fact[:, right + j : right + j + WIDTH], TN), at + j)


def spread_quarters(total, quarter, send, recv):
    g, m, across, along, _ = places()
    quarter[g] = total.astype(BF)
    to_x, to_y = (across, m), (along, m)
    low, high = pl.ds(0, 16), pl.ds(16, 16)
    a = push(quarter.at[g], quarter.at[g], send.at[6, 0], recv.at[6, 0], to_x)
    b = push(quarter.at[g], quarter.at[g], send.at[6, 1], recv.at[6, 1], to_y)
    a.wait_recv()
    c = push(quarter.at[across, low], quarter.at[across, low], send.at[6, 2], recv.at[6, 2], to_y)
    b.wait_recv()
    d = push(quarter.at[along, high], quarter.at[along, high], send.at[6, 3], recv.at[6, 3], to_x)
    c.wait_recv()
    d.wait_recv()
    for copy in (a, b, c, d):
        copy.wait_send()


def late_kernel(
    first_ref,
    rows_ref,
    gain_ref,
    half_ref,
    query_ref,
    out_ref,
    keys_ref,
    fact,
    gains,
    wide,
    held,
    x1,
    y1,
    x2,
    y2,
    zin,
    quarter,
    tables,
    arrived,
    local_sem,
    send,
    recv,
):
    g, m, _, _, _ = places()
    core, z = m % 2, m // 2
    enter(plane_peers())
    moves = factor_moves((first_ref, rows_ref), LATE, fact)
    moves.append((gain_ref, gains, 0, WIDTH))
    moves += factor_moves((half_ref, query_ref), (KEYS, QUERIES), wide)
    copies = share_factors(moves, local_sem, send, recv)
    first, corner, plane, last = plane_tasks(held, x1, y1, x2, y2, zin, send, recv)
    for near, far in copies[:3]:
        near.wait()
        far.wait_recv()
    row = iota((32, LANES), 0) % 16
    column = iota((32, LANES), 1)
    select = ((row < 4) & (row // 2 == column)).astype(F32).astype(BF)

    def table(d):
        block = (z + d) % 4 * 2 + core
        lhs = wide[:, pl.ds(pl.multiple_of(block * NK, LANES), NK)]
        rhs = wide[:, pl.ds(pl.multiple_of(KEYS + block * HALF, LANES), HALF)]
        return dot(lhs, rhs, TN)

    def line(k):
        return pltpu.make_async_remote_copy(
            src_ref=tables.at[k],
            dst_ref=arrived.at[k],
            send_sem=send.at[7, k],
            recv_sem=recv.at[7, k],
            device_id=(g, (m + 2 * (k + 1)) % 8),
            device_id_type=MESH,
        )

    def ready(k, _):
        products_of(k, fact, held, LATE_PRODUCTS)
        lhs = gains[:, pl.ds(pl.multiple_of(block_of(k) * LANES, LANES), LANES)]
        store_blocks(held, k, dot(lhs, select, TN), L_GAIN)
        first(k)
        return 0

    lax.fori_loop(0, 4, ready, 0)
    for near, far in copies[3:]:
        near.wait()
        far.wait_recv()

    def send_table(k, _):
        tables[k] = table(k + 1).astype(BF)
        line(k).start()
        return 0

    lax.fori_loop(0, 3, send_table, 0)
    keys_ref[...] = table(0)
    for k in range(4):
        corner(k)
    for k in range(3):
        plane(k)
    spread_quarters(last(), quarter, send, recv)
    for k in range(3):
        line(k).wait_recv()
        keys_ref[...] += arrived[k].astype(F32)
        line(k).wait_send()
    for _, far in copies:
        far.wait_send()
    out_ref[...] = quarter[...]


def reduce_late(first, qkv_rows, gains, half, query):
    rows = first.shape[0]
    vmem = pl.BlockSpec(memory_space=pltpu.VMEM)
    sums, keys = pl.pallas_call(
        late_kernel,
        in_specs=[pl.BlockSpec(memory_space=pl.ANY)] * 5,
        out_specs=[vmem, vmem],
        out_shape=[
            jax.ShapeDtypeStruct((4, 32, L_ALL), BF),
            jax.ShapeDtypeStruct((NK, HALF), F32),
        ],
        scratch_shapes=[
            pltpu.VMEM((2 * rows, sum(LATE)), BF),
            pltpu.VMEM((32, WIDTH), BF),
            pltpu.VMEM((2 * rows, KEYS + QUERIES), BF),
            pltpu.VMEM((4, 4, 32, L_ALL), BF),
            *plane_scratch(32, L_ALL),
            pltpu.VMEM((4, 32, L_ALL), BF),
            pltpu.VMEM((3, NK, HALF), BF),
            pltpu.VMEM((3, NK, HALF), BF),
            pltpu.SemaphoreType.DMA((5,)),
            pltpu.SemaphoreType.DMA((8, 5)),
            pltpu.SemaphoreType.DMA((8, 5)),
        ],
        compiler_params=pltpu.CompilerParams(
            collective_id=2, has_side_effects=True, vmem_limit_bytes=48 * 1024 * 1024
        ),
        name="reduce_late",
    )(first, qkv_rows, gains, half, query)
    return sums.reshape(4 * 32, L_ALL), keys


def back_kernel(rows, win, *refs):
    fact_refs, refs = refs[: len(EARLY)], refs[len(EARLY) :]
    shared_ref, qkv_ref, proj_ref, segc_ref, segr_ref, out_ref, rows_ref = refs[:7]
    fact, held, x1, y1, x2, y2, zin, quarter, shared, douts, stats = refs[7:18]
    local_sem, send, recv = refs[18:]
    g, m, _, _, sibling = places()
    to_s = (g, sibling)
    pairs = WIDTH // LANES
    enter(plane_peers())

    def part(owner):
        return shared.at[pl.ds(pl.multiple_of(owner * rows, LANES), rows)]

    def move(index, src, owner, peer):
        return pltpu.make_async_remote_copy(
            src_ref=src,
            dst_ref=part(owner),
            send_sem=send.at[7, index],
            recv_sem=recv.at[7, index],
            device_id=peer,
            device_id_type=MESH,
        )

    def origin(d):
        return (m + 8 - 2 * d) % 8

    lines = [move(d, shared_ref, m, (g, (m + 2 * d) % 8)) for d in (1, 2, 3)]
    side = move(0, shared_ref, m, to_s)
    forward = [move(3 + d, part(origin(d)), origin(d), to_s) for d in (1, 2, 3)]
    own = pltpu.make_async_copy(shared_ref, part(m), local_sem.at[len(EARLY)])
    for copy in lines:
        copy.start()
    side.start()
    own.start()
    copies = share_factors(factor_moves(fact_refs, EARLY, fact), local_sem, send, recv)
    first, corner, plane, last = plane_tasks(held, x1, y1, x2, y2, zin, send, recv)
    for near, far in copies:
        near.wait()
        far.wait_recv()

    def ready(k, _):
        products_of(k, fact, held, EARLY_PRODUCTS)
        first(k)
        return 0

    lax.fori_loop(0, 4, ready, 0)
    corner(0)
    for copy, after in zip(lines, forward, strict=True):
        copy.wait_recv()
        after.start()
    corner(1)
    own.wait()
    side.wait_recv()
    for copy in forward:
        copy.wait_recv()
    corner(2)
    def project(i, _):
        where = pl.ds(pl.multiple_of(i * 2 * rows, 2 * rows), 2 * rows)
        douts[where, :] = dot(shared[where, :WIDTH], proj_ref[...], NT).astype(BF)
        stats[where, :] = shared[where, WIDTH : WIDTH + 2 * HEADS].astype(F32) + shared[
            where, WIDTH + 2 * HEADS : WIDTH + 4 * HEADS
        ].astype(F32)
        return 0

    lax.fori_loop(0, shared.shape[0] // (2 * rows), project, 0)
    corner(3)

    def load_of(pair):
        def load(which, where):
            ref, base = (douts, 0) if which == 3 else (qkv_ref, which * pairs)
            return ref[where, pl.ds(pl.multiple_of((base + pair) * LANES, LANES), LANES)]

        return load

    def attend(pair, _):
        grads = attn_bwd_pair(
            rows, win, pair, m, shared.shape[0], load_of(pair), stats, segc_ref, segr_ref
        )
        for i, value in enumerate(grads):
            column = pl.multiple_of((i * pairs + pair) * LANES, LANES)
            rows_ref[:, pl.ds(column, LANES)] = value
        for k in range(3):
            pl.when(pair == 2 * k + 1)(functools.partial(plane, k))
        return 0

    lax.fori_loop(0, pairs, attend, 0)
    spread_quarters(last(), quarter, send, recv)
    for _, far in copies:
        far.wait_send()
    for copy in [*lines, side, *forward]:
        copy.wait_send()
    out_ref[...] = quarter[...]


def reduce_back(factors, shared, qkv, proj, seg_col, seg_row):
    rows = factors[0].shape[0]
    group_len = qkv.shape[0]
    win = min(group_len, group_len // 2 + rows)
    hbm = pl.BlockSpec(memory_space=pl.ANY)
    vmem = pl.BlockSpec(memory_space=pltpu.VMEM)
    count = len(EARLY)
    sums, qkv_rows = pl.pallas_call(
        functools.partial(back_kernel, rows, win),
        in_specs=[hbm] * (count + 1) + [vmem] * 4,
        out_specs=[vmem, vmem],
        out_shape=[
            jax.ShapeDtypeStruct((4, 32, E_ALL), BF),
            jax.ShapeDtypeStruct((rows, 3 * WIDTH), BF),
        ],
        scratch_shapes=[
            pltpu.VMEM((2 * rows, sum(EARLY)), BF),
            pltpu.VMEM((4, 4, 32, E_ALL), BF),
            *plane_scratch(32, E_ALL),
            pltpu.VMEM((4, 32, E_ALL), BF),
            pltpu.VMEM((group_len, WIDTH + LANES), BF),
            pltpu.VMEM((group_len, WIDTH), BF),
            pltpu.VMEM((group_len, 2 * HEADS), F32),
            pltpu.SemaphoreType.DMA((count + 1,)),
            pltpu.SemaphoreType.DMA((8, count)),
            pltpu.SemaphoreType.DMA((8, count)),
        ],
        compiler_params=pltpu.CompilerParams(
            collective_id=4, has_side_effects=True, vmem_limit_bytes=56 * 1024 * 1024
        ),
        name="reduce_back",
    )(*factors, shared, qkv, proj, seg_col, seg_row)
    return sums.reshape(4 * 32, E_ALL), qkv_rows


def finish_kernel(
    early_ref, late_ref, keys_ref, out, gate, proj, qkv, query, gains
):
    for ref, first in ((out, E_OUT), (gate, E_GATE), (proj, E_PROJ)):
        ref[...] = early_ref[:, first : first + WIDTH].astype(F32)
    qkv[...] = late_ref[:, : 3 * WIDTH].astype(F32)
    for c in range(MHEADS * 2):
        table = keys_ref[c * NK : (c + 1) * NK, :]
        query[:, c * HALF : (c + 1) * HALF] = dot(
            early_ref[:, E_HALF + c * NK : E_HALF + (c + 1) * NK], table
        )
    gains[...] = late_ref[:, L_GAIN:].astype(F32).T[:8]


def finish(early, late, keys):
    rows = early.shape[0]
    shapes = [(rows, WIDTH)] * 3 + [(rows, 3 * WIDTH), (rows, QUERIES)]
    shapes.append((8, LANES))
    return pl.pallas_call(
        finish_kernel,
        out_shape=[jax.ShapeDtypeStruct(shape, F32) for shape in shapes],
        compiler_params=pltpu.CompilerParams(vmem_limit_bytes=40 * 1024 * 1024),
        name="finish",
    )(early, late, keys)


def rms_scale(values):
    return lax.rsqrt(jnp.mean(values * values, axis=-1, keepdims=True) + EPS)


def rms_back(values, scale, gain, grad):
    scaled = grad * gain
    inner = jnp.mean(values * scaled, axis=-1, keepdims=True)
    gain_grad = jnp.sum(grad * values * scale, axis=0)
    return scale * scaled - values * (scale * scale * scale * inner), gain_grad


def per_device(
    tokens,
    segment_ids,
    picks,
    attn_gain,
    qkv_weight,
    attn_proj,
    mem_gain,
    query_weight,
    half_keys,
    memory_values,
    gate_weight,
    out_weight,
    out_cotangent,
):
    rows, width = tokens.shape
    owners = lax.axis_size("grp") * lax.axis_size("mem")
    local_rows = memory_values.shape[0]
    total_picks = rows * MHEADS * TOPK
    flat_bits = (total_picks - 1).bit_length()
    capacity = 2 * total_picks // owners
    group_len = segment_ids.shape[0]
    linked = (lax.axis_size("grp"), lax.axis_size("mem"), rows) == (4, 8, LANES)
    position = lax.axis_index("mem").astype(jnp.int32)
    pos = position.reshape(1)

    def gather(x, axes="mem"):
        return lax.all_gather(x, axes, axis=0, tiled=True)

    flat_picks = picks.reshape(rows, MHEADS * TOPK)
    if linked:
        gain_block = jnp.concatenate(
            [attn_gain[None], mem_gain[None], jnp.zeros((14, LANES), BF)]
        )
    else:
        gains = lax.all_gather(jnp.stack([attn_gain, mem_gain]), "mem", axis=1, tiled=True)
        tokens_all = gather(tokens)
        qkv_full = gather(qkv_weight)
        proj_full = gather(attn_proj)
        query_full = gather(query_weight)
        keys_full = gather(half_keys)
        gate_full = gather(gate_weight)
        output_full = gather(out_weight)
        gains = gains.astype(F32)
        gain_one, gain_two = gains[0:1], gains[1:2]
    seg_row, seg_col = segment_ids.reshape(1, group_len), segment_ids.reshape(group_len, 1)

    requests = route(picks, owners, local_rows, capacity, flat_bits)
    arrived = lax.all_to_all(requests, ALL, split_axis=0, concat_axis=0, tiled=True)

    if linked:
        (
            keys_full,
            qkv_full,
            proj_full,
            gate_full,
            output_full,
            folded_full,
            qkv_all,
            attn_sum,
            lse,
            gains,
        ) = gather_weights(
            half_keys,
            qkv_weight,
            attn_proj,
            gate_weight,
            out_weight,
            tokens,
            gain_block,
            query_weight,
            seg_col,
            seg_row,
            rows,
        )
        gains = gains.reshape(8, 16, LANES)[:, :2].transpose(1, 0, 2).reshape(2, width)
        gains = gains.astype(F32)
        gain_one, gain_two = gains[0:1], gains[1:2]
    else:
        inputs_all = tokens_all.astype(F32)
        first_all = (inputs_all * rms_scale(inputs_all) * gain_one).astype(BF)
        qkv_all = dot(first_all, qkv_full).astype(BF)
        attn_sum, lse = attn_fwd(pos, qkv_all, seg_row, seg_col, rows)
    attended = attn_sum.astype(BF)
    inputs = tokens.astype(F32)
    residual = inputs + dot(attended, proj_full)
    scale_two = rms_scale(residual)
    second = (residual * scale_two * gain_two).astype(BF)
    gate_pre = dot(second, gate_full)
    mixed_grad = dot(out_cotangent, output_full, NT)
    sig = jax.nn.sigmoid(gate_pre)
    gate_act = gate_pre * sig
    memory_grad = (mixed_grad * gate_act).astype(BF)
    if linked:
        half_scores = dot(second, folded_full)
    else:
        mem_query = dot(second, query_full).astype(BF)
        key_table = keys_full.reshape(MHEADS * 2, NK, HALF)
        half_scores = jnp.einsum(
            "tcf,cnf->tcn",
            mem_query.reshape(rows, MHEADS * 2, HALF),
            key_table,
            preferred_element_type=F32,
        ).reshape(rows, KEYS)
    pick_weights, weights_low = pick_fwd(half_scores, flat_picks)

    payload = jnp.concatenate([memory_grad, weights_low], axis=1)
    if linked:
        back, values_grad = memory_call(payload, arrived, memory_values, flat_bits)
    else:
        sent = gather(payload, ALL)
        part, spread = owner_call(arrived, sent, memory_values, flat_bits)
        back = lax.psum_scatter(part, "grp", scatter_dimension=0, tiled=True)
        back = lax.psum_scatter(back, "mem", scatter_dimension=0, tiled=True)
        values_grad = jnp.einsum(
            "hkl,kd->hld", spread, sent[:, :width], preferred_element_type=F32
        )
    values_grad = values_grad.reshape(local_rows, width)

    memory_out = back[:, :width].astype(F32)
    mixed = (memory_out * gate_act).astype(BF)
    block_out = (residual + dot(mixed, output_full)).astype(BF)
    gate_grad = (mixed_grad * memory_out * (sig * (1.0 + gate_pre * (1.0 - sig)))).astype(BF)
    half_grad, values_grad = pick_bwd(
        pick_weights, back.astype(F32), flat_picks, values_grad
    )
    if linked:
        second_grad = dot(gate_grad, gate_full, NT) + dot(half_grad, folded_full, NT)
    else:
        half_cube = half_grad.reshape(rows, MHEADS * 2, NK)
        query_grad = (
            jnp.einsum("tcn,cnf->tcf", half_cube, key_table, preferred_element_type=F32)
            .astype(BF)
            .reshape(rows, QUERIES)
        )
        second_grad = dot(gate_grad, gate_full, NT) + dot(query_grad, query_full, NT)
    resid_from_norm, gain_two_grad = rms_back(residual, scale_two, gain_two, second_grad)
    resid_grad = out_cotangent.astype(F32) + resid_from_norm
    resid_low = resid_grad.astype(BF)
    attn_grad = dot(resid_low, proj_full, NT).astype(BF)
    heads = (iota((width, HEADS), 0) // HDIM == iota((width, HEADS), 1)).astype(F32)
    delta = jnp.dot(
        attn_grad.astype(F32) * attn_sum,
        heads,
        precision=lax.Precision.HIGHEST,
        preferred_element_type=F32,
    )
    stats = jnp.concatenate([lse[:, :HEADS], delta], axis=1)
    stats_high = lax.reduce_precision(stats, 8, 7)
    stats_low = stats - stats_high
    shared = jnp.concatenate(
        [
            resid_low,
            stats_high.astype(BF),
            stats_low.astype(BF),
            jnp.zeros((rows, LANES - 4 * HEADS), BF),
        ],
        axis=1,
    )
    if linked:
        early = (
            mixed,
            second,
            attended,
            out_cotangent,
            gate_grad,
            resid_low,
            half_grad,
        )
        early, qkv_rows = reduce_back(early, shared, qkv_all, proj_full, seg_col, seg_row)
    else:
        shared = gather(shared)
        stats_all = shared[:, width : width + 2 * HEADS].astype(F32) + shared[
            :, width + 2 * HEADS : width + 4 * HEADS
        ].astype(F32)
        attn_grad_all = dot(shared[:, :width], proj_full, NT).astype(BF)
        qkv_rows = attn_bwd(pos, qkv_all, attn_grad_all, stats_all, seg_row, seg_col, rows)
    scale_one = rms_scale(inputs)
    first_low = (inputs * scale_one * gain_one).astype(BF)
    first_grad = dot(qkv_rows, qkv_full, NT)
    input_from_norm, gain_one_grad = rms_back(inputs, scale_one, gain_one, first_grad)
    tokens_grad = resid_grad + input_from_norm

    if linked:
        sums = jnp.stack([gain_one_grad, gain_two_grad])
        sums_high = lax.reduce_precision(sums, 8, 7)
        gain_rows = jnp.stack([sums_high, sums - sums_high], axis=1).reshape(4, width)
        gain_rows = jnp.concatenate([gain_rows.astype(BF), jnp.zeros((12, width), BF)])
        late, keys_share = reduce_late(
            first_low, qkv_rows, gain_rows, early[:, E_HALF:], query_weight
        )
        (
            out_share,
            gate_share,
            proj_share,
            qkv_share,
            query_share,
            gain_sums,
        ) = finish(early, late, keys_full)
    else:
        keys_grad = jnp.einsum(
            "tcn,tcf->cnf",
            half_cube,
            mem_query.reshape(rows, MHEADS * 2, HALF),
            preferred_element_type=F32,
        ).reshape(KEYS, HALF)
        partials = (
            dot(mixed, out_cotangent, TN),
            dot(second, gate_grad, TN),
            keys_grad,
            dot(second, query_grad, TN),
            dot(attended, resid_low, TN),
            dot(first_low, qkv_rows, TN),
        )
        shares = [
            lax.psum_scatter(x.astype(BF), "mem", scatter_dimension=0, tiled=True)
            for x in partials
        ]
        shares = lax.psum(tuple(shares), "grp")
        gain_sums = lax.psum(jnp.stack([gain_one_grad, gain_two_grad]), ALL)
        gain_sums = lax.dynamic_slice_in_dim(
            gain_sums, position * attn_gain.shape[0], attn_gain.shape[0], axis=1
        )
        out_share, gate_share, keys_share, query_share, proj_share, qkv_share = (
            x.astype(F32) for x in shares
        )
    return (
        block_out,
        tokens_grad,
        gain_sums[0],
        qkv_share,
        proj_share,
        gain_sums[1],
        query_share,
        keys_share,
        values_grad,
        gate_share,
        out_share,
    )


def solution(mesh):
    placed = (
        P(ALL, None),
        P("grp"),
        P(ALL, None, None),
        P("mem"),
        P("mem", None),
        P("mem", None),
        P("mem"),
        P("mem", None),
        P("mem", None),
        P(ALL, None),
        P("mem", None),
        P("mem", None),
        P(ALL, None),
    )
    return jax.shard_map(
        per_device,
        mesh=mesh,
        in_specs=placed,
        out_specs=(
            P(ALL, None),
            P(ALL, None),
            P("mem"),
            P("mem", None),
            P("mem", None),
            P("mem"),
            P("mem", None),
            P("mem", None),
            P(ALL, None),
            P("mem", None),
            P("mem", None),
        ),
        check_vma=False,
    )
```

```python
import functools

import jax
import jax.numpy as jnp
from jax import lax
from jax.experimental import pallas as pl
from jax.experimental.pallas import tpu as pltpu
from jax.sharding import PartitionSpec as P

HEADS = 16
HDIM = 64
MHEADS = 4
NK = 256
HALF = 512
TOPK = 32
EPS = 1e-05
LANES = 128
ALL = ("grp", "mem")
BF = jnp.bfloat16
F32 = jnp.float32
NEG = -1e30


def dot(left, right, dims=((1,), (0,))):
    return lax.dot_general(left, right, (dims, ((), ())), preferred_element_type=F32)


NT = ((1,), (1,))
TN = ((0,), (0,))


def iota(shape, dim):
    return lax.broadcasted_iota(jnp.int32, shape, dim)


def lane_halves(rows):
    first = iota((rows, LANES), 1) < HDIM
    return first


def half_masks():
    lane = iota((1, LANES), 1)
    return ((lane < HDIM).astype(BF), (lane >= HDIM).astype(BF))


def attn_fwd_pair(rows, win, pair, position, query, load, qseg_ref, kseg_ref, lse):
    row0 = position * rows
    start = pl.multiple_of(jnp.maximum(row0 + rows - win, 0), LANES)
    keys, values = load(1, pl.ds(start, win)), load(2, pl.ds(start, win))
    key_pos = start + iota((rows, win), 1)
    query_pos = row0 + iota((rows, win), 0)
    allowed = (key_pos <= query_pos) & (kseg_ref[:, pl.ds(start, win)] == qseg_ref[...])
    lane = iota((rows, LANES), 1)
    masks = half_masks()
    outs = []
    for half in range(2):
        scores = dot(query * masks[half], keys, NT) * 0.125
        scores = jnp.where(allowed, scores, NEG)
        top = jnp.max(scores, axis=1, keepdims=True)
        weights = jnp.exp(scores - top)
        total = jnp.sum(weights, axis=1, keepdims=True)
        probs = weights * (1.0 / total)
        outs.append(dot(probs.astype(BF), values))
        lse = jnp.where(lane == pair * 2 + half, top + jnp.log(total), lse)
    return jnp.where(lane < HDIM, outs[0], outs[1]), lse


def attn_fwd_kernel(rows, win, pos_ref, q_ref, k_ref, v_ref, qseg_ref, kseg_ref, out_ref, lse_ref):
    pair = pl.program_id(0)
    refs = (q_ref, k_ref, v_ref)
    lse = jnp.where(pair == 0, jnp.zeros((rows, LANES), F32), lse_ref[...])
    out_ref[...], lse_ref[...] = attn_fwd_pair(
        rows,
        win,
        pair,
        pos_ref[0],
        q_ref[...],
        lambda which, where: refs[which][where, :],
        qseg_ref,
        kseg_ref,
        lse,
    )


def attn_fwd(pos, qkv, seg_row, seg_col, rows):
    group_len, width = qkv.shape[0], qkv.shape[1] // 3
    pairs = width // LANES
    win = min(group_len, group_len // 2 + rows)
    return pl.pallas_call(
        functools.partial(attn_fwd_kernel, rows, win),
        grid_spec=pltpu.PrefetchScalarGridSpec(
            num_scalar_prefetch=1,
            grid=(pairs,),
            in_specs=[
                pl.BlockSpec((rows, LANES), lambda h, p: (p[0], h)),
                pl.BlockSpec((group_len, LANES), lambda h, p: (0, pairs + h)),
                pl.BlockSpec((group_len, LANES), lambda h, p: (0, 2 * pairs + h)),
                pl.BlockSpec((rows, 1), lambda h, p: (p[0], 0)),
                pl.BlockSpec((1, group_len), lambda h, p: (0, 0)),
            ],
            out_specs=[
                pl.BlockSpec((rows, LANES), lambda h, p: (0, h)),
                pl.BlockSpec((rows, LANES), lambda h, p: (0, 0)),
            ],
        ),
        out_shape=[
            jax.ShapeDtypeStruct((rows, width), F32),
            jax.ShapeDtypeStruct((rows, LANES), F32),
        ],
        cost_estimate=pl.CostEstimate(
            flops=4 * rows * win * width,
            bytes_accessed=group_len * width * 4,
            transcendentals=rows * win * HEADS,
        ),
        name="attn_fwd",
    )(pos, qkv, qkv, qkv, seg_col, seg_row)


def attn_bwd_pair(rows, win, pair, position, group_len, load, stat_ref, segc_ref, segr_ref):
    row0 = pl.multiple_of(position * rows, LANES)
    start = pl.multiple_of(jnp.maximum(row0 + rows - win, 0), LANES)
    qstart = pl.multiple_of(jnp.minimum(row0, group_len - win), LANES)
    own, back, ahead = pl.ds(row0, rows), pl.ds(start, win), pl.ds(qstart, win)
    masks = half_masks()
    lane = iota((rows, LANES), 1)

    def stat(where, index, count):
        table = stat_ref[where, :]
        return jnp.sum(
            jnp.where(iota((count, table.shape[1]), 1) == index, table, 0.0),
            axis=1,
            keepdims=True,
        )

    allowed = (start + iota((rows, win), 1) <= row0 + iota((rows, win), 0)) & (
        segr_ref[:, back] == segc_ref[own, :]
    )
    allowed_two = (row0 + iota((win, rows), 1) <= qstart + iota((win, rows), 0)) & (
        segr_ref[:, own] == segc_ref[ahead, :]
    )
    dqs, dks, dvs = [], [], []
    for half in range(2):
        head = pair * 2 + half
        lse, delta = stat(own, head, rows), stat(own, HEADS + head, rows)
        keys = load(1, back)
        scores = dot(load(0, own) * masks[half], keys, NT) * 0.125
        probs = jnp.exp(jnp.where(allowed, scores - lse, NEG))
        dprobs = dot(load(3, own) * masks[half], load(2, back), NT)
        grads = (probs * (dprobs - delta)).astype(BF)
        dqs.append(dot(grads, keys))
        lse, delta = stat(ahead, head, win), stat(ahead, HEADS + head, win)
        queries, douts = load(0, ahead), load(3, ahead)
        scores = dot(queries * masks[half], load(1, own), NT) * 0.125
        probs = jnp.exp(jnp.where(allowed_two, scores - lse, NEG))
        dprobs = dot(douts * masks[half], load(2, own), NT)
        grads = (probs * (dprobs - delta)).astype(BF)
        dks.append(dot(grads, queries, TN))
        dvs.append(dot(probs.astype(BF), douts, TN))
    return [
        (jnp.where(lane < HDIM, parts[0], parts[1]) * scale).astype(BF)
        for parts, scale in ((dqs, 0.125), (dks, 0.125), (dvs, 1.0))
    ]


def attn_bwd_kernel(
    rows, win, pairs, pos_ref, q_ref, k_ref, v_ref, da_ref, stat_ref, segc_ref, segr_ref, out_ref
):
    pair = pl.program_id(0)
    refs = (q_ref, k_ref, v_ref, da_ref)
    grads = attn_bwd_pair(
        rows,
        win,
        pair,
        pos_ref[0],
        k_ref.shape[0],
        lambda which, where: refs[which][where, :],
        stat_ref,
        segc_ref,
        segr_ref,
    )
    for i, value in enumerate(grads):
        column = pl.multiple_of((i * pairs + pair) * LANES, LANES)
        out_ref[:, pl.ds(column, LANES)] = value


def attn_bwd(pos, qkv, douts, stats, seg_row, seg_col, rows):
    group_len, width = douts.shape
    pairs = width // LANES
    win = min(group_len, group_len // 2 + rows)
    return pl.pallas_call(
        functools.partial(attn_bwd_kernel, rows, win, pairs),
        grid_spec=pltpu.PrefetchScalarGridSpec(
            num_scalar_prefetch=1,
            grid=(pairs,),
            in_specs=[
                pl.BlockSpec((group_len, LANES), lambda h, p: (0, h)),
                pl.BlockSpec((group_len, LANES), lambda h, p: (0, pairs + h)),
                pl.BlockSpec((group_len, LANES), lambda h, p: (0, 2 * pairs + h)),
                pl.BlockSpec((group_len, LANES), lambda h, p: (0, h)),
                pl.BlockSpec(stats.shape, lambda h, p: (0, 0)),
                pl.BlockSpec((group_len, 1), lambda h, p: (0, 0)),
                pl.BlockSpec((1, group_len), lambda h, p: (0, 0)),
            ],
            out_specs=pl.BlockSpec((rows, 3 * width), lambda h, p: (0, 0)),
        ),
        out_shape=jax.ShapeDtypeStruct((rows, 3 * width), BF),
        cost_estimate=pl.CostEstimate(
            flops=14 * rows * win * width,
            bytes_accessed=group_len * width * 8,
            transcendentals=2 * rows * win * HEADS,
        ),
        name="attn_bwd",
    )(pos, qkv, qkv, qkv, douts, stats, seg_col, seg_row)


def by_head(lane, reduce, fill, values):
    spread = jnp.zeros_like(values)
    for c in range(MHEADS):
        inside = lane // TOPK == c
        spread = jnp.where(
            inside, reduce(jnp.where(inside, values, fill), axis=1, keepdims=True), spread
        )
    return spread


def pick_fwd_kernel(scores_ref, picks_ref, weight_ref, low_ref):
    rows = picks_ref.shape[0]
    lane = iota((rows, LANES), 1)
    picks = picks_ref[...]
    index = (picks // NK, picks % NK)
    total = jnp.zeros((rows, LANES), F32)
    for c in range(MHEADS):
        both = jnp.zeros((rows, LANES), F32)
        for e in range(2):
            base = (c * 2 + e) * NK
            for part in range(NK // LANES):
                table = scores_ref[:, base + part * LANES : base + (part + 1) * LANES]
                found = jnp.take_along_axis(table, index[e] % LANES, axis=1)
                both = both + jnp.where(index[e] // LANES == part, found, 0.0)
        total = jnp.where(lane // TOPK == c, both, total)
    top = by_head(lane, jnp.max, NEG, total)
    weights = jnp.exp(total - top)
    weights = weights / by_head(lane, jnp.sum, 0.0, weights)
    weight_ref[...] = weights
    low_ref[...] = weights.astype(BF)


def pick_fwd(half_scores, picks):
    rows = picks.shape[0]
    return pl.pallas_call(
        pick_fwd_kernel,
        out_shape=[
            jax.ShapeDtypeStruct((rows, LANES), F32),
            jax.ShapeDtypeStruct((rows, LANES), BF),
        ],
        name="pick_fwd",
    )(half_scores, picks)


def pick_bwd_kernel(
    weight_ref,
    grad_ref,
    picks_ref,
    table_ref,
    out_ref,
    whole_ref,
    score_t,
    first_t,
    second_t,
    stage,
    in_sem,
    out_sem,
):
    block = table_ref.shape[0] // MHEADS

    def part(c):
        return pl.ds(pl.multiple_of(c * block, block), block)

    def fetch(c):
        return pltpu.make_async_copy(table_ref.at[part(c)], stage.at[c], in_sem.at[c])

    def put(c):
        return pltpu.make_async_copy(stage.at[c], whole_ref.at[part(c)], out_sem.at[c])

    for c in range(MHEADS):
        fetch(c).start()
    rows = picks_ref.shape[0]
    lane = iota((rows, LANES), 1)
    weights, grads = weight_ref[...], grad_ref[...]
    score = (weights * (grads - by_head(lane, jnp.sum, 0.0, weights * grads))).astype(BF)
    score_t[...] = score.astype(F32).T
    picks_t = picks_ref[...].T
    first_t[...] = picks_t // NK
    second_t[...] = picks_t % NK
    key = iota((NK, rows), 0)

    def head(c, _):
        first = jnp.zeros((NK, rows), F32)
        second = jnp.zeros((NK, rows), F32)
        for j in range(TOPK):
            at = pl.ds(c * TOPK + j, 1)
            value = score_t[at, :]
            first = first + jnp.where(key == first_t[at, :], value, 0.0)
            second = second + jnp.where(key == second_t[at, :], value, 0.0)
        for e, total in enumerate((first, second)):
            base = pl.multiple_of((c * 2 + e) * NK, LANES)
            out_ref[:, pl.ds(base, NK)] = total.T.astype(BF)
        fetch(c).wait()
        put(c).start()
        return 0

    lax.fori_loop(0, MHEADS, head, 0)
    for c in range(MHEADS):
        put(c).wait()


def pick_bwd(weights, grads, picks, table):
    rows = picks.shape[0]
    last = grads.shape[1] // LANES - 1
    spec = pl.BlockSpec((rows, LANES), lambda i: (0, 0))
    hbm = pl.BlockSpec(memory_space=pltpu.HBM)
    return pl.pallas_call(
        pick_bwd_kernel,
        grid=(1,),
        in_specs=[spec, pl.BlockSpec((rows, LANES), lambda i: (0, last)), spec, hbm],
        out_specs=[pl.BlockSpec((rows, MHEADS * 2 * NK), lambda i: (0, 0)), hbm],
        out_shape=[
            jax.ShapeDtypeStruct((rows, MHEADS * 2 * NK), BF),
            jax.ShapeDtypeStruct(table.shape, table.dtype),
        ],
        scratch_shapes=[
            pltpu.VMEM((LANES, rows), F32),
            pltpu.VMEM((LANES, rows), jnp.int32),
            pltpu.VMEM((LANES, rows), jnp.int32),
            pltpu.VMEM((MHEADS, table.shape[0] // MHEADS, table.shape[1]), table.dtype),
            pltpu.SemaphoreType.DMA((MHEADS,)),
            pltpu.SemaphoreType.DMA((MHEADS,)),
        ],
        compiler_params=pltpu.CompilerParams(vmem_limit_bytes=40 * 1024 * 1024),
        name="pick_bwd",
    )(weights, grads, picks, table)


def owner_kernel(
    his, flat_bits, local_rows, keys_ref, sent_ref, values_ref, part_ref, spread_ref
):
    rows = part_ref.shape[0]
    width = values_ref.shape[1]
    slots = keys_ref.shape[-1]
    low_rows = local_rows // his
    key = keys_ref[0]
    flat = key & ((1 << flat_bits) - 1)
    dummy = ((key >> flat_bits) & 1) == 1
    row = (key >> (flat_bits + 1)) % local_rows
    token = flat // LANES
    pick = flat % LANES
    token = jnp.where(dummy, -1, token)
    block = jnp.where(dummy, -1, (row // low_rows) * rows + token)
    low_row = row % low_rows
    grad = sent_ref[:, :width]
    weights = sent_ref[:, width:]
    is_token = iota((rows, slots), 0) == token
    is_pick = iota((LANES, slots), 0) == pick
    token_hot = is_token.astype(F32).astype(BF)
    found = dot(weights, token_hot, TN)
    weight = jnp.sum(jnp.where(is_pick, found, 0.0), axis=0, keepdims=True)
    is_block = iota((his * rows, slots), 0) == block
    is_low = iota((low_rows, slots), 0) == low_row
    low_hot = is_low.astype(F32).astype(BF)
    spread = dot(jnp.where(is_block, weight, 0.0).astype(BF), low_hot, NT).astype(BF)
    total = jnp.zeros((rows, width), F32)
    products = []
    for h in range(his):
        table = values_ref[h * low_rows : (h + 1) * low_rows, :]
        piece = spread[h * rows : (h + 1) * rows, :]
        spread_ref[h] = piece
        total = total + dot(piece, table)
        products.append(dot(grad, table, NT).astype(BF))
    picked = dot(jnp.concatenate(products, axis=0), is_block.astype(F32).astype(BF), TN)
    picked = jnp.sum(jnp.where(is_low, picked, 0.0), axis=0, keepdims=True)
    part_ref[:, :width] = total.astype(BF)
    part_ref[:, width:] = dot(
        jnp.where(is_token, picked, 0.0).astype(BF), is_pick.astype(F32).astype(BF), NT
    ).astype(BF)


def owner_call(keys, sent, values, flat_bits):
    owners, slots = keys.shape
    rows = sent.shape[0] // owners
    local_rows, width = values.shape
    his = 4
    low_rows = local_rows // his
    return pl.pallas_call(
        functools.partial(owner_kernel, his, flat_bits, local_rows),
        grid=(owners,),
        in_specs=[
            pl.BlockSpec((1, 1, slots), lambda s: (s, 0, 0)),
            pl.BlockSpec((rows, width + LANES), lambda s: (s, 0)),
            pl.BlockSpec((local_rows, width), lambda s: (0, 0)),
        ],
        out_specs=[
            pl.BlockSpec((rows, width + LANES), lambda s: (s, 0)),
            pl.BlockSpec((his, rows, low_rows), lambda s: (0, s, 0)),
        ],
        out_shape=[
            jax.ShapeDtypeStruct((owners * rows, width + LANES), BF),
            jax.ShapeDtypeStruct((his, owners * rows, low_rows), BF),
        ],
        compiler_params=pltpu.CompilerParams(vmem_limit_bytes=48 * 1024 * 1024),
        cost_estimate=pl.CostEstimate(
            flops=2 * owners * rows * local_rows * (2 * slots + 2 * width),
            bytes_accessed=owners * rows * (2 * width + local_rows) * 2,
            transcendentals=0,
        ),
        name="owner",
    )(keys.reshape(owners, 1, slots), sent, values)


def route(picks, owners, local_rows, capacity, flat_bits):
    total = picks.size
    rows_of = picks.reshape(total)
    flat = jnp.arange(total, dtype=jnp.int32)
    each = jnp.arange(owners, dtype=jnp.int32)
    counts = jnp.sum((rows_of[:, None] // local_rows == each[None, :]).astype(jnp.int32), axis=0)
    ends = jnp.cumsum(capacity - counts)
    spares = owners * capacity - total
    spare_owner = jnp.sum(
        (jnp.arange(spares, dtype=jnp.int32)[:, None] >= ends[None, :]).astype(jnp.int32), axis=1
    )
    real = (rows_of << (flat_bits + 1)) + flat
    spare = ((spare_owner * local_rows + local_rows - 1) << (flat_bits + 1)) + (1 << flat_bits)
    keys = lax.sort(jnp.concatenate([real, spare]), is_stable=False)
    return keys.reshape(owners, capacity)


MESH = pl.DeviceIdType.MESH


def places():
    g, m = lax.axis_index("grp"), lax.axis_index("mem")
    across = g + 1 - 2 * (g % 2)
    along = (g + 2) % 4
    sibling = m + 1 - 2 * (m % 2)
    return g, m, across, along, sibling


def enter(peers):
    barrier = pltpu.get_barrier_semaphore()
    for peer in peers:
        pl.semaphore_signal(barrier, inc=1, device_id=peer, device_id_type=MESH)
    pl.semaphore_wait(barrier, len(peers))


def push(src, dst, send, recv, peer):
    copy = pltpu.make_async_remote_copy(
        src_ref=src, dst_ref=dst, send_sem=send, recv_sem=recv, device_id=peer, device_id_type=MESH
    )
    copy.start()
    return copy


def plane_tasks(held, x1, y1, x2, y2, zin, send, recv):
    g, m, across, along, _ = places()
    diagonal = 3 - g
    half = held.shape[2] // 2
    low, high = pl.ds(0, half), pl.ds(half, half)
    to_x, to_y = (across, m), (along, m)

    def copy(kind, k, src, dst, peer):
        return pltpu.make_async_remote_copy(
            src_ref=src,
            dst_ref=dst,
            send_sem=send.at[kind, k],
            recv_sem=recv.at[kind, k],
            device_id=peer,
            device_id_type=MESH,
        )

    def ones(k):
        return (
            copy(0, k, held.at[k, diagonal, low], x1.at[k], to_x),
            copy(1, k, held.at[k, diagonal, high], y1.at[k], to_y),
        )

    def twos(k):
        return (
            copy(2, k, held.at[k, across], x2.at[k], to_x),
            copy(3, k, held.at[k, along], y2.at[k], to_y),
        )

    def three(k):
        return copy(4, k, held.at[k, g], zin.at[k], (g, (m + 2 * (3 - k)) % 8))

    def first(k):
        for item in ones(k):
            item.start()

    def corner(k):
        for item in ones(k):
            item.wait_recv()
        held[k, along, low] = held[k, along, low] + x1[k]
        held[k, across, high] = held[k, across, high] + y1[k]
        for item in twos(k):
            item.start()

    def total_of(k):
        for item in twos(k):
            item.wait_recv()
        return held[k, g].astype(F32) + x2[k].astype(F32) + y2[k].astype(F32)

    def plane(k):
        held[k, g] = total_of(k).astype(BF)
        three(k).start()

    def last():
        total = total_of(3)
        for k in range(3):
            three(k).wait_recv()
            total = total + zin[k].astype(F32)
        for k in range(4):
            for item in ones(k) + twos(k):
                item.wait_send()
            if k < 3:
                three(k).wait_send()
        return total

    return first, corner, plane, last


def plane_peers():
    g, m, across, along, sibling = places()
    return [(across, m), (along, m), (g, sibling)] + [(g, (m + 2 * d) % 8) for d in (1, 2, 3)]


def plane_scratch(rows, columns):
    return [
        pltpu.VMEM((4, rows // 2, columns), BF),
        pltpu.VMEM((4, rows // 2, columns), BF),
        pltpu.VMEM((4, rows, columns), BF),
        pltpu.VMEM((4, rows, columns), BF),
        pltpu.VMEM((3, rows, columns), BF),
    ]


def memory_kernel(
    flat_bits,
    payload_ref,
    keys_ref,
    values_ref,
    out_ref,
    grad_ref,
    sent,
    parts,
    sibs,
    x1,
    y1,
    x2,
    y2,
    zin,
    held,
    spread,
    table,
    own_sem,
    table_sem,
    send,
    recv,
):
    g, m, across, along, sibling = places()
    core, z = m % 2, m // 2
    to_x, to_y, to_s = (across, m), (along, m), (g, sibling)
    rows, columns = payload_ref.shape
    width = columns - LANES
    local_rows = values_ref.shape[0]
    slots = keys_ref.shape[1]
    his = spread.shape[0]
    low_rows = local_rows // his
    low, high = pl.ds(0, rows // 2), pl.ds(rows // 2, rows // 2)
    enter(plane_peers())

    def copy(kind, index, src, dst, peer):
        return pltpu.make_async_remote_copy(
            src_ref=src,
            dst_ref=dst,
            send_sem=send.at[kind, index],
            recv_sem=recv.at[kind, index],
            device_id=peer,
            device_id_type=MESH,
        )

    def mine(i):
        return payload_ref if i == 0 else sent.at[i, core]

    def to_sibling(i):
        return copy(0, i, mine(i), sent.at[i, core], to_s)

    def plane_x(k):
        return copy(1, k, mine(4 * k), sent.at[4 * k + 1, core], to_x)

    def plane_y(k):
        return copy(2, k, mine(4 * k), sent.at[4 * k + 2, core], to_y)

    def line(k):
        return copy(3, k, payload_ref, sent.at[4 * k, core], (g, (m + 2 * k) % 8))

    def corner_y(k):
        return copy(4, k, sent.at[4 * k + 1, core, low], sent.at[4 * k + 3, core, low], to_y)

    def corner_x(k):
        return copy(5, k, sent.at[4 * k + 2, core, high], sent.at[4 * k + 3, core, high], to_x)

    def part_sibling(i):
        return copy(6, i, parts.at[i, 1 - core], sibs.at[i], to_s)

    def one_x(k):
        return copy(7, k, parts.at[4 * k + 3, core, low], x1.at[k], to_x)

    def one_y(k):
        return copy(8, k, parts.at[4 * k + 3, core, high], y1.at[k], to_y)

    def two_x(k):
        return copy(9, k, parts.at[4 * k + 1, core], x2.at[k], to_x)

    def two_y(k):
        return copy(10, k, parts.at[4 * k + 2, core], y2.at[k], to_y)

    def three(k):
        return copy(11, k, parts.at[4 * k, core], zin.at[k - 1], (g, (m + 8 - 2 * k) % 8))

    def from_line(k):
        line(k).wait_recv()
        plane_x(k).start()
        plane_y(k).start()
        to_sibling(4 * k).start()

    def from_plane(k):
        plane_x(k).wait_recv()
        corner_y(k).start()
        to_sibling(4 * k + 1).start()
        plane_y(k).wait_recv()
        corner_x(k).start()
        to_sibling(4 * k + 2).start()

    def from_corner(k):
        corner_x(k).wait_recv()
        corner_y(k).wait_recv()
        to_sibling(4 * k + 3).start()

    def pair_sum(k):
        for i in (4 * k + 3, 4 * k + 1, 4 * k + 2, 4 * k):
            part_sibling(i).wait_recv()
            parts[i, core] = parts[i, core] + sibs[i]
            if i == 4 * k + 3:
                one_x(k).start()
                one_y(k).start()

    def corner_sum(k):
        one_x(k).wait_recv()
        parts[4 * k + 2, core, low] = parts[4 * k + 2, core, low] + x1[k]
        two_y(k).start()
        one_y(k).wait_recv()
        parts[4 * k + 1, core, high] = parts[4 * k + 1, core, high] + y1[k]
        two_x(k).start()

    def plane_sum(k):
        two_x(k).wait_recv()
        two_y(k).wait_recv()
        total = parts[4 * k, core].astype(F32) + x2[k].astype(F32) + y2[k].astype(F32)
        if k == 0:
            held[...] = total
        else:
            parts[4 * k, core] = total.astype(BF)
            three(k).start()

    own = pltpu.make_async_copy(payload_ref, sent.at[0, core], own_sem)
    own.start()
    to_sibling(0).start()
    plane_x(0).start()
    plane_y(0).start()
    for k in (1, 2, 3):
        line(k).start()
    own.wait()

    tasks = {
        1: [lambda: from_plane(0)],
        2: [lambda: from_line(1)],
        3: [lambda: from_corner(0), lambda: from_line(2)],
        4: [lambda: from_line(3), lambda: pair_sum(0)],
        5: [lambda: from_plane(1)],
        6: [lambda: corner_sum(0)],
        7: [lambda: from_corner(1)],
        8: [lambda: from_plane(2), lambda: pair_sum(1)],
        9: [lambda: plane_sum(0)],
        10: [lambda: from_corner(2), lambda: corner_sum(1)],
        11: [lambda: from_plane(3)],
        12: [lambda: pair_sum(2), lambda: plane_sum(1)],
        13: [lambda: from_corner(3)],
        14: [lambda: corner_sum(2)],
    }

    def step(i, _):
        for when, todo in tasks.items():

            @pl.when(i == when)
            def _():
                for task in todo:
                    task()

        copy(0, i, sent.at[i, core], sent.at[i, 1 - core], to_s).wait_recv()
        k, j = i // 4, i % 4
        grp = (g // 2 + j // 2) % 2 * 2 + (g % 2 + j % 2) % 2
        base = grp * 8 + (z + 4 - k) % 4 * 2
        lanes, tiles = [], []
        for c in range(2):
            key = keys_ref[pl.ds(base + c, 1), :]
            flat = key & ((1 << flat_bits) - 1)
            dummy = ((key >> flat_bits) & 1) == 1
            row = (key >> (flat_bits + 1)) % local_rows
            token = jnp.where(dummy, -1, flat // LANES)
            block = jnp.where(dummy, -1, (row // low_rows) * rows + token)
            is_token = iota((rows, slots), 0) == token
            is_pick = iota((LANES, slots), 0) == flat % LANES
            place = jnp.concatenate(
                [
                    jnp.where(is_token, (row % LANES).astype(F32), 0.0).astype(BF),
                    jnp.where(is_token, (row // LANES + 1).astype(F32), 0.0).astype(BF),
                ],
                axis=0,
            )
            place = dot(place, is_pick.astype(F32).astype(BF), NT).astype(jnp.int32)
            lanes.append(place[:rows])
            tiles.append(place[rows:] - 1)
            weights = sent[i, c, :, width:]
            found = dot(weights, is_token.astype(F32).astype(BF), TN)
            weight = jnp.sum(jnp.where(is_pick, found, 0.0), axis=0, keepdims=True)
            is_block = iota((his * rows, slots), 0) == block
            is_low = iota((low_rows, slots), 0) == row % low_rows
            piece = dot(
                jnp.where(is_block, weight, 0.0).astype(BF), is_low.astype(F32).astype(BF), NT
            ).astype(BF)
            for h in range(his):
                spread[h, 2 * i + c] = piece[h * rows : (h + 1) * rows]
        lane, tile = jnp.concatenate(lanes, axis=0), jnp.concatenate(tiles, axis=0)
        grads = sent[i, :, :, :width].reshape(2 * rows, width)
        total = jnp.zeros((2 * rows, width), F32)
        picked = jnp.zeros((2 * rows, LANES), F32)
        for h in range(his):
            table = values_ref[h * low_rows : (h + 1) * low_rows, :]
            piece = spread[h, pl.ds(2 * i, 2)].reshape(2 * rows, low_rows)
            total = total + dot(piece, table)
            products = dot(grads, table, NT)
            for b in range(low_rows // LANES):
                found = jnp.take_along_axis(
                    products[:, b * LANES : (b + 1) * LANES], lane, axis=1
                )
                picked = jnp.where(tile == h * (low_rows // LANES) + b, found, picked)
        parts[i, :, :, :width] = total.astype(BF).reshape(2, rows, width)
        parts[i, :, :, width:] = picked.astype(BF).reshape(2, rows, LANES)
        part_sibling(i).start()
        return 0

    def table_copy(h):
        return pltpu.make_async_copy(table.at[h % 2], grad_ref.at[h], table_sem.at[h % 2])

    def table_grad(h):
        if h >= 2:
            table_copy(h - 2).wait()

        def some(n, _):
            grads = sent[pl.ds(4 * n, 4), :, :, :width].reshape(8 * rows, width)
            piece = spread[h, pl.ds(8 * n, 8)].reshape(8 * rows, low_rows)
            table[h % 2] = jnp.where(n == 0, 0.0, table[h % 2]) + dot(piece, grads, TN)
            return 0

        lax.fori_loop(0, 4, some, 0)
        table_copy(h).start()

    lax.fori_loop(0, 16, step, 0)
    plane_sum(2)
    pair_sum(3)
    table_grad(0)
    corner_sum(3)
    table_grad(1)
    plane_sum(3)
    table_grad(2)
    table_grad(3)
    total = held[...]
    for k in (1, 2, 3):
        three(k).wait_recv()
        total = total + zin[k - 1].astype(F32)
    out_ref[...] = total
    for k in range(4):
        todo = [plane_x(k), plane_y(k), corner_x(k), corner_y(k)]
        todo += [one_x(k), one_y(k), two_x(k), two_y(k)]
        if k:
            todo += [line(k), three(k)]
        for j in range(4):
            todo += [to_sibling(4 * k + j), part_sibling(4 * k + j)]
        for item in todo:
            item.wait_send()
    table_copy(2).wait()
    table_copy(3).wait()


def memory_call(payload, keys, values, flat_bits):
    rows, columns = payload.shape
    local_rows = values.shape[0]
    his = 4
    half = (4, rows // 2, columns)
    full = (4, rows, columns)
    vmem = pl.BlockSpec(memory_space=pltpu.VMEM)
    hbm = pl.BlockSpec(memory_space=pl.ANY)
    return pl.pallas_call(
        functools.partial(memory_kernel, flat_bits),
        in_specs=[hbm, vmem, vmem],
        out_specs=[vmem, hbm],
        out_shape=[
            jax.ShapeDtypeStruct((rows, columns), F32),
            jax.ShapeDtypeStruct((his, local_rows // his, columns - LANES), F32),
        ],
        scratch_shapes=[
            pltpu.VMEM((16, 2, rows, columns), BF),
            pltpu.VMEM((16, 2, rows, columns), BF),
            pltpu.VMEM((16, rows, columns), BF),
            pltpu.VMEM(half, BF),
            pltpu.VMEM(half, BF),
            pltpu.VMEM(full, BF),
            pltpu.VMEM(full, BF),
            pltpu.VMEM((3, rows, columns), BF),
            pltpu.VMEM((rows, columns), F32),
            pltpu.VMEM((his, 32, rows, local_rows // his), BF),
            pltpu.VMEM((2, local_rows // his, columns - LANES), F32),
            pltpu.SemaphoreType.DMA,
            pltpu.SemaphoreType.DMA((2,)),
            pltpu.SemaphoreType.DMA((12, 16)),
            pltpu.SemaphoreType.DMA((12, 16)),
        ],
        compiler_params=pltpu.CompilerParams(
            collective_id=1, has_side_effects=True, vmem_limit_bytes=63 * 1024 * 1024
        ),
        name="memory",
    )(payload, keys, values)


def gather_tasks(pieces, sources, targets, local_sem, send, recv):
    g, m, across, along, sibling = places()
    z = m // 2
    to_x, to_y, to_s = (across, m), (along, m), (g, sibling)
    total = range(len(pieces))
    ways = [(sign, hop) for hop in (1, 2, 3) for sign in (1, -1)]
    shared = [p for p in total if pieces[p][3]]

    def view(piece, owner, quarter=None, part=None):
        array, first, columns, _ = pieces[piece]
        ref = targets[array]
        size = ref.shape[0] // 8
        start = owner * size
        if quarter is not None:
            size = size // 4
            start = start + quarter * size
        if part is not None:
            size = size // 2
            start = start + part * size
        return ref.at[pl.ds(start, size), pl.ds(first, columns)]

    def copy(piece, index, block, peer, src=None):
        return pltpu.make_async_remote_copy(
            src_ref=block if src is None else src,
            dst_ref=block,
            send_sem=send.at[piece, index],
            recv_sem=recv.at[piece, index],
            device_id=peer,
            device_id_type=MESH,
        )

    def line(p, way, owner, src=None):
        block = view(p, owner, g if pieces[p][3] else None)
        peer = (g, (m + 8 + 2 * ways[way][0]) % 8)
        return copy(p, way, block, peer, src)

    def has(way):
        sign, distance = ways[way]
        return z >= distance if sign > 0 else z + distance <= 3

    def more(way):
        return z <= 2 if ways[way][0] > 0 else z >= 1

    def origin(way):
        sign, distance = ways[way]
        return (m + 8 - 2 * sign * distance) % 8

    def planes(p, way):
        block = view(p, origin(way), g)
        return copy(p, 6 + way, block, to_x), copy(p, 12 + way, block, to_y)

    def corners(p, way):
        owner = origin(way)
        return (
            copy(p, 18 + way, view(p, owner, across, 0), to_y),
            copy(p, 24 + way, view(p, owner, along, 1), to_x),
        )

    def core(p, way):
        return copy(p, 30 + way, view(p, origin(way)), to_s)

    def first(p):
        array, start, columns, is_shared = pieces[p]
        ref = sources[array]
        whole = ref.at[:, pl.ds(start, columns)]
        src = whole
        if is_shared:
            quarter = ref.shape[0] // 4
            src = ref.at[pl.ds(g * quarter, quarter), pl.ds(start, columns)]
        return (
            [line(p, way, m, src) for way in (0, 1)],
            pltpu.make_async_copy(whole, view(p, m), local_sem.at[p]),
            copy(p, 36, view(p, m), to_s, whole),
        )

    def begin():
        for p in total:
            for way in (0, 1):
                pl.when(more(way))(first(p)[0][way].start)
        for p in total:
            _, near, side = first(p)
            near.start()
            side.start()

    def level(hop):
        return (2 * hop - 2, 2 * hop - 1)

    def arrive(hop):
        for p in total:
            for way in level(hop):

                @pl.when(has(way))
                def _():
                    line(p, way, origin(way)).wait_recv()
                    if hop < 3:
                        pl.when(more(way))(line(p, way + 2, origin(way)).start)

        for p in total:
            for way in level(hop):

                @pl.when(has(way))
                def _():
                    for item in planes(p, way) if p in shared else [core(p, way)]:
                        item.start()

    def turn(hop):
        for p in shared:
            for way in level(hop):

                @pl.when(has(way))
                def _():
                    for item, after in zip(planes(p, way), corners(p, way), strict=True):
                        item.wait_recv()
                        after.start()

    def cross(hop):
        for p in shared:
            for way in level(hop):

                @pl.when(has(way))
                def _():
                    for item in corners(p, way):
                        item.wait_recv()
                    core(p, way).start()

    def receive():
        for p in total:
            _, near, side = first(p)
            near.wait()
            side.wait_recv()
            for way in range(6):

                @pl.when(has(way))
                def _():
                    core(p, way).wait_recv()

    def drain():
        for p in total:
            out, _, side = first(p)
            side.wait_send()
            for way in (0, 1):
                pl.when(more(way))(out[way].wait_send)
            for way in range(6):

                @pl.when(has(way))
                def _():
                    core(p, way).wait_send()
                    if ways[way][1] < 3:
                        pl.when(more(way))(line(p, way + 2, origin(way)).wait_send)
                    if p in shared:
                        for item in planes(p, way) + corners(p, way):
                            item.wait_send()

    return begin, arrive, turn, cross, receive, drain


def pieces_of(arrays, chunk, own_count):
    pieces = []
    for i, x in enumerate(arrays):
        columns = x.shape[1]
        for first in range(0, columns, chunk):
            pieces.append((i, first, min(chunk, columns - first), i >= own_count))
    return tuple(pieces)


def gathered(arrays):
    return [jax.ShapeDtypeStruct((8 * x.shape[0], x.shape[1]), x.dtype) for x in arrays]


def gather_sems(pieces):
    return [
        pltpu.SemaphoreType.DMA((len(pieces),)),
        pltpu.SemaphoreType.DMA((len(pieces), 37)),
        pltpu.SemaphoreType.DMA((len(pieces), 37)),
    ]


def gather_kernel(sets, rows, win, *refs):
    sources, refs = refs[:7], refs[7:]
    query_ref, segc_ref, segr_ref = refs[:3]
    targets, refs = refs[3:9], refs[9:]
    qkv_ref, out_ref, lse_ref, gains = refs[:4]
    tokens, gain_row, normal, folded = refs[4:8]
    sems = refs[8:]
    keys_src, qkv_src, proj_src, gate_src, head_src, tokens_src, gain_src = sources
    keys_full, weight_full, proj_full, gate_full, head_full, folded_full = targets
    m = lax.axis_index("mem")
    group_len, width = tokens.shape
    pairs = width // LANES
    enter(plane_peers())
    k_set, a_set, c_set, b_set = (
        gather_tasks(pieces, src, dst, *sems[3 * i : 3 * i + 3])
        for i, (pieces, src, dst) in enumerate(
            zip(
                sets,
                (
                    [keys_src],
                    [tokens_src, gain_src, qkv_src],
                    [folded],
                    [proj_src, gate_src, head_src],
                ),
                (
                    [keys_full],
                    [tokens, gains, weight_full],
                    [folded_full],
                    [proj_full, gate_full, head_full],
                ),
                strict=True,
            )
        )
    )
    begin, arrive, turn, cross, receive, drain = range(6)

    def go(which, task, *hop):
        which[task](*hop)

    def fold():
        for c in range(MHEADS * 2):
            folded[:, c * NK : (c + 1) * NK] = dot(
                query_ref[:, c * HALF : (c + 1) * HALF], keys_full[c * NK : (c + 1) * NK, :], NT
            ).astype(BF)

    def normalize():
        for i in range(8):
            gain_row[:, i * LANES : (i + 1) * LANES] = gains[i * 16 : i * 16 + 1, :].astype(F32)
        block = 2 * rows

        def some(i, _):
            where = pl.ds(pl.multiple_of(i * block, block), block)
            values = tokens[where, :].astype(F32)
            normal[where, :] = (values * rms_scale(values) * gain_row[...]).astype(BF)
            return 0

        lax.fori_loop(0, group_len // block, some, 0)

    def project(i, _):
        where = pl.ds(pl.multiple_of(i * 3 * LANES, LANES), 3 * LANES)
        qkv_ref[:, where] = dot(normal[...], weight_full[:, where]).astype(BF)
        during(i, PROJECT_TASKS)
        return 0

    def load_of(pair):
        def load(which, where):
            column = pl.multiple_of((which * pairs + pair) * LANES, LANES)
            return qkv_ref[where, pl.ds(column, LANES)]

        return load

    own = pl.ds(pl.multiple_of(m * rows, LANES), rows)

    def attend(pair, _):
        load = load_of(pair)
        value, lse_ref[...] = attn_fwd_pair(
            rows, win, pair, m, load(0, own), load, segc_ref.at[own], segr_ref, lse_ref[...]
        )
        out_ref[:, pl.ds(pl.multiple_of(pair * LANES, LANES), LANES)] = value
        during(pair, ATTEND_TASKS)
        return 0

    def during(i, tasks):
        for when, todo in tasks.items():

            @pl.when(i == when)
            def _():
                for which, task, hop in todo:
                    go(which, task, hop)

    PROJECT_TASKS = {
        0: [(c_set, turn, 1), (b_set, arrive, 2)],
        2: [(b_set, turn, 1), (c_set, arrive, 3)],
        4: [(c_set, turn, 2), (b_set, arrive, 3)],
        6: [(b_set, turn, 2), (c_set, cross, 1)],
    }
    ATTEND_TASKS = {
        0: [(c_set, turn, 3), (b_set, cross, 1)],
        2: [(b_set, turn, 3), (c_set, cross, 2)],
        3: [(b_set, cross, 2)],
        4: [(c_set, cross, 3)],
        5: [(b_set, cross, 3)],
    }
    lse_ref[...] = jnp.zeros_like(lse_ref)
    go(k_set, begin)
    go(a_set, begin)
    go(k_set, arrive, 1)
    go(k_set, arrive, 2)
    go(a_set, arrive, 1)
    go(k_set, turn, 1)
    go(k_set, arrive, 3)
    go(k_set, turn, 2)
    go(k_set, cross, 1)
    go(k_set, turn, 3)
    go(k_set, cross, 2)
    go(a_set, arrive, 2)
    go(k_set, cross, 3)
    go(a_set, turn, 1)
    go(k_set, receive)
    fold()
    go(c_set, begin)
    go(b_set, begin)
    go(a_set, arrive, 3)
    go(a_set, turn, 2)
    go(a_set, cross, 1)
    go(c_set, arrive, 1)
    go(a_set, turn, 3)
    go(b_set, arrive, 1)
    go(a_set, cross, 2)
    go(a_set, cross, 3)
    go(c_set, arrive, 2)
    go(a_set, receive)
    normalize()
    lax.fori_loop(0, 8, project, 0)
    lax.fori_loop(0, 8, attend, 0)
    go(c_set, receive)
    go(b_set, receive)
    for one in (k_set, a_set, c_set, b_set):
        go(one, drain)


def gather_weights(keys, qkv, proj, gate, head, tokens, gains, query, seg_col, seg_row, rows):
    sets = (
        pieces_of([keys], WIDTH, 0),
        pieces_of([tokens, gains, qkv], 3 * WIDTH, 2),
        pieces_of([jax.ShapeDtypeStruct((query.shape[0], KEYS), BF)], KEYS, 0),
        pieces_of([proj, gate, head], WIDTH, 0),
    )
    group_len = seg_col.shape[0]
    width = tokens.shape[1]
    win = min(group_len, group_len // 2 + rows)
    vmem, hbm = pl.BlockSpec(memory_space=pltpu.VMEM), pl.BlockSpec(memory_space=pl.ANY)
    sems = []
    for pieces in sets:
        sems += gather_sems(pieces)
    return pl.pallas_call(
        functools.partial(gather_kernel, sets, rows, win),
        in_specs=[vmem] * 10,
        out_specs=[vmem, vmem, hbm, hbm, hbm, hbm, vmem, vmem, vmem, vmem],
        out_shape=[
            *gathered([keys, qkv, proj, gate, head]),
            jax.ShapeDtypeStruct((8 * query.shape[0], KEYS), BF),
            jax.ShapeDtypeStruct((group_len, 3 * width), BF),
            jax.ShapeDtypeStruct((rows, width), F32),
            jax.ShapeDtypeStruct((rows, LANES), F32),
            *gathered([gains]),
        ],
        scratch_shapes=[
            pltpu.VMEM((group_len, width), BF),
            pltpu.VMEM((1, width), F32),
            pltpu.VMEM((group_len, width), BF),
            pltpu.VMEM((query.shape[0], KEYS), BF),
            *sems,
        ],
        compiler_params=pltpu.CompilerParams(
            collective_id=3, has_side_effects=True, vmem_limit_bytes=56 * 1024 * 1024
        ),
        name="gather_weights",
    )(keys, qkv, proj, gate, head, tokens, gains, query, seg_col, seg_row)


WIDTH = HEADS * HDIM
KEYS = MHEADS * 2 * NK
QUERIES = MHEADS * 2 * HALF
EARLY = (WIDTH,) * 6 + (KEYS,)
EARLY_PRODUCTS = (
    (0, 3 * WIDTH, WIDTH, 0),
    (WIDTH, 4 * WIDTH, WIDTH, WIDTH),
    (2 * WIDTH, 5 * WIDTH, WIDTH, 2 * WIDTH),
    (WIDTH, 6 * WIDTH, KEYS, 3 * WIDTH),
)
E_OUT, E_GATE, E_PROJ, E_HALF = 0, WIDTH, 2 * WIDTH, 3 * WIDTH
E_ALL = E_HALF + KEYS
LATE = (WIDTH, 3 * WIDTH)
LATE_PRODUCTS = ((0, WIDTH, 3 * WIDTH, 0),)
L_GAIN = 3 * WIDTH
L_ALL = L_GAIN + LANES


def share_factors(moves, local_sem, send, recv):
    g, _, _, _, sibling = places()
    copies = []
    for i, (src, dst, at, columns) in enumerate(moves):
        count = src.shape[0]
        where = pl.ds(at, columns)
        far = push(
            src, dst.at[pl.ds(count, count), where], send.at[5, i], recv.at[5, i], (g, sibling)
        )
        near = pltpu.make_async_copy(src, dst.at[pl.ds(0, count), where], local_sem.at[i])
        near.start()
        copies.append((near, far))
    return copies


def factor_moves(refs, widths, fact):
    moves, at = [], 0
    for ref, columns in zip(refs, widths, strict=True):
        moves.append((ref, fact, at, columns))
        at += columns
    return moves


def store_blocks(held, k, value, at):
    for i in range(4):
        held[k, i, :, at : at + value.shape[1]] = value[i * 32 : (i + 1) * 32].astype(BF)


def block_of(k):
    m = lax.axis_index("mem")
    return (m // 2 + 3 - k) % 4 * 2 + m % 2


def products_of(k, fact, held, products):
    block = block_of(k)
    for left, right, count, at in products:
        lhs = fact[:, pl.ds(pl.multiple_of(left + block * LANES, LANES), LANES)]
        for j in range(0, count, WIDTH):
            store_blocks(held, k, dot(lhs, fact[:, right + j : right + j + WIDTH], TN), at + j)


def spread_quarters(total, quarter, kind, send, recv):
    g, m, across, along, _ = places()
    quarter[g] = total.astype(BF)
    half = quarter.shape[1] // 2
    to_x, to_y = (across, m), (along, m)
    low, high = pl.ds(0, half), pl.ds(half, half)

    def go(i, block, peer):
        return push(block, block, send.at[kind, i], recv.at[kind, i], peer)

    a = go(0, quarter.at[g], to_x)
    b = go(1, quarter.at[g], to_y)
    a.wait_recv()
    c = go(2, quarter.at[across, low], to_y)
    b.wait_recv()
    d = go(3, quarter.at[along, high], to_x)
    c.wait_recv()
    d.wait_recv()
    for copy in (a, b, c, d):
        copy.wait_send()


def late_kernel(
    first_ref,
    rows_ref,
    gain_ref,
    half_ref,
    query_ref,
    out_ref,
    keys_ref,
    fact,
    gains,
    wide,
    held,
    x1,
    y1,
    x2,
    y2,
    zin,
    quarter,
    tables,
    arrived,
    spread,
    local_sem,
    send,
    recv,
):
    g, m, _, _, _ = places()
    core, z = m % 2, m // 2
    enter(plane_peers())
    moves = factor_moves((first_ref, rows_ref), LATE, fact)
    moves.append((gain_ref, gains, 0, WIDTH))
    moves += factor_moves((half_ref, query_ref), (KEYS, QUERIES), wide)
    copies = share_factors(moves, local_sem, send, recv)
    first, corner, plane, last = plane_tasks(held, x1, y1, x2, y2, zin, send, recv)
    for near, far in copies[:3]:
        near.wait()
        far.wait_recv()
    row = iota((32, LANES), 0) % 16
    column = iota((32, LANES), 1)
    select = ((row < 4) & (row // 2 == column)).astype(F32).astype(BF)

    def table(d):
        block = (z + d) % 4 * 2 + core
        lhs = wide[:, pl.ds(pl.multiple_of(block * NK, LANES), NK)]
        at = KEYS + block * HALF + g * (HALF // 4)
        return dot(lhs, wide[:, pl.ds(pl.multiple_of(at, LANES), HALF // 4)], TN)

    def line(k):
        return pltpu.make_async_remote_copy(
            src_ref=tables.at[k],
            dst_ref=arrived.at[k],
            send_sem=send.at[7, k],
            recv_sem=recv.at[7, k],
            device_id=(g, (m + 2 * (k + 1)) % 8),
            device_id_type=MESH,
        )

    def ready(k, _):
        products_of(k, fact, held, LATE_PRODUCTS)
        lhs = gains[:, pl.ds(pl.multiple_of(block_of(k) * LANES, LANES), LANES)]
        store_blocks(held, k, dot(lhs, select, TN), L_GAIN)
        first(k)
        return 0

    lax.fori_loop(0, 4, ready, 0)
    for near, far in copies[3:]:
        near.wait()
        far.wait_recv()

    def send_table(k, _):
        tables[k] = table(k + 1).astype(BF)
        line(k).start()
        return 0

    lax.fori_loop(0, 3, send_table, 0)
    keys = table(0)
    for k in range(4):
        corner(k)
    for k in range(3):
        plane(k)
    for k in range(3):
        line(k).wait_recv()
        keys = keys + arrived[k].astype(F32)
        line(k).wait_send()
    spread_quarters(keys, spread, 8, send, recv)
    for i in range(4):
        keys_ref[:, i * (HALF // 4) : (i + 1) * (HALF // 4)] = spread[i].astype(F32)
    spread_quarters(last(), quarter, 6, send, recv)
    for _, far in copies:
        far.wait_send()
    out_ref[...] = quarter[...]


def reduce_late(first, qkv_rows, gains, half, query):
    rows = first.shape[0]
    vmem = pl.BlockSpec(memory_space=pltpu.VMEM)
    sums, keys = pl.pallas_call(
        late_kernel,
        in_specs=[pl.BlockSpec(memory_space=pl.ANY)] * 5,
        out_specs=[vmem, vmem],
        out_shape=[
            jax.ShapeDtypeStruct((4, 32, L_ALL), BF),
            jax.ShapeDtypeStruct((NK, HALF), F32),
        ],
        scratch_shapes=[
            pltpu.VMEM((2 * rows, sum(LATE)), BF),
            pltpu.VMEM((32, WIDTH), BF),
            pltpu.VMEM((2 * rows, KEYS + QUERIES), BF),
            pltpu.VMEM((4, 4, 32, L_ALL), BF),
            *plane_scratch(32, L_ALL),
            pltpu.VMEM((4, 32, L_ALL), BF),
            pltpu.VMEM((3, NK, HALF // 4), BF),
            pltpu.VMEM((3, NK, HALF // 4), BF),
            pltpu.VMEM((4, NK, HALF // 4), BF),
            pltpu.SemaphoreType.DMA((5,)),
            pltpu.SemaphoreType.DMA((9, 5)),
            pltpu.SemaphoreType.DMA((9, 5)),
        ],
        compiler_params=pltpu.CompilerParams(
            collective_id=2, has_side_effects=True, vmem_limit_bytes=48 * 1024 * 1024
        ),
        name="reduce_late",
    )(first, qkv_rows, gains, half, query)
    return sums.reshape(4 * 32, L_ALL), keys


def back_kernel(rows, win, *refs):
    fact_refs, refs = refs[: len(EARLY)], refs[len(EARLY) :]
    shared_ref, qkv_ref, proj_ref, segc_ref, segr_ref, out_ref, rows_ref = refs[:7]
    fact, held, x1, y1, x2, y2, zin, quarter, shared, douts, stats = refs[7:18]
    local_sem, send, recv = refs[18:]
    g, m, _, _, sibling = places()
    to_s = (g, sibling)
    pairs = WIDTH // LANES
    enter(plane_peers())

    def part(owner):
        return shared.at[pl.ds(pl.multiple_of(owner * rows, LANES), rows)]

    def move(index, src, owner, peer):
        return pltpu.make_async_remote_copy(
            src_ref=src,
            dst_ref=part(owner),
            send_sem=send.at[7, index],
            recv_sem=recv.at[7, index],
            device_id=peer,
            device_id_type=MESH,
        )

    def origin(d):
        return (m + 8 - 2 * d) % 8

    lines = [move(d, shared_ref, m, (g, (m + 2 * d) % 8)) for d in (1, 2, 3)]
    side = move(0, shared_ref, m, to_s)
    forward = [move(3 + d, part(origin(d)), origin(d), to_s) for d in (1, 2, 3)]
    own = pltpu.make_async_copy(shared_ref, part(m), local_sem.at[len(EARLY)])
    for copy in lines:
        copy.start()
    side.start()
    own.start()
    copies = share_factors(factor_moves(fact_refs, EARLY, fact), local_sem, send, recv)
    first, corner, plane, last = plane_tasks(held, x1, y1, x2, y2, zin, send, recv)
    for near, far in copies:
        near.wait()
        far.wait_recv()

    def ready(k, _):
        products_of(k, fact, held, EARLY_PRODUCTS)
        first(k)
        return 0

    lax.fori_loop(0, 4, ready, 0)
    corner(0)
    for copy, after in zip(lines, forward, strict=True):
        copy.wait_recv()
        after.start()
    corner(1)
    own.wait()
    side.wait_recv()
    for copy in forward:
        copy.wait_recv()
    corner(2)
    def project(i, _):
        where = pl.ds(pl.multiple_of(i * 2 * rows, 2 * rows), 2 * rows)
        douts[where, :] = dot(shared[where, :WIDTH], proj_ref[...], NT).astype(BF)
        stats[where, :] = shared[where, WIDTH : WIDTH + 2 * HEADS].astype(F32) + shared[
            where, WIDTH + 2 * HEADS : WIDTH + 4 * HEADS
        ].astype(F32)
        return 0

    lax.fori_loop(0, shared.shape[0] // (2 * rows), project, 0)
    corner(3)

    def load_of(pair):
        def load(which, where):
            ref, base = (douts, 0) if which == 3 else (qkv_ref, which * pairs)
            return ref[where, pl.ds(pl.multiple_of((base + pair) * LANES, LANES), LANES)]

        return load

    def attend(pair, _):
        grads = attn_bwd_pair(
            rows, win, pair, m, shared.shape[0], load_of(pair), stats, segc_ref, segr_ref
        )
        for i, value in enumerate(grads):
            column = pl.multiple_of((i * pairs + pair) * LANES, LANES)
            rows_ref[:, pl.ds(column, LANES)] = value
        for k in range(3):
            pl.when(pair == 2 * k + 1)(functools.partial(plane, k))
        return 0

    lax.fori_loop(0, pairs, attend, 0)
    spread_quarters(last(), quarter, 6, send, recv)
    for _, far in copies:
        far.wait_send()
    for copy in [*lines, side, *forward]:
        copy.wait_send()
    out_ref[...] = quarter[...]


def reduce_back(factors, shared, qkv, proj, seg_col, seg_row):
    rows = factors[0].shape[0]
    group_len = qkv.shape[0]
    win = min(group_len, group_len // 2 + rows)
    hbm = pl.BlockSpec(memory_space=pl.ANY)
    vmem = pl.BlockSpec(memory_space=pltpu.VMEM)
    count = len(EARLY)
    sums, qkv_rows = pl.pallas_call(
        functools.partial(back_kernel, rows, win),
        in_specs=[hbm] * (count + 1) + [vmem] * 4,
        out_specs=[vmem, vmem],
        out_shape=[
            jax.ShapeDtypeStruct((4, 32, E_ALL), BF),
            jax.ShapeDtypeStruct((rows, 3 * WIDTH), BF),
        ],
        scratch_shapes=[
            pltpu.VMEM((2 * rows, sum(EARLY)), BF),
            pltpu.VMEM((4, 4, 32, E_ALL), BF),
            *plane_scratch(32, E_ALL),
            pltpu.VMEM((4, 32, E_ALL), BF),
            pltpu.VMEM((group_len, WIDTH + LANES), BF),
            pltpu.VMEM((group_len, WIDTH), BF),
            pltpu.VMEM((group_len, 2 * HEADS), F32),
            pltpu.SemaphoreType.DMA((count + 1,)),
            pltpu.SemaphoreType.DMA((8, count)),
            pltpu.SemaphoreType.DMA((8, count)),
        ],
        compiler_params=pltpu.CompilerParams(
            collective_id=4, has_side_effects=True, vmem_limit_bytes=56 * 1024 * 1024
        ),
        name="reduce_back",
    )(*factors, shared, qkv, proj, seg_col, seg_row)
    return sums.reshape(4 * 32, E_ALL), qkv_rows


def finish_kernel(
    early_ref, late_ref, keys_ref, out, gate, proj, qkv, query, gains
):
    for ref, first in ((out, E_OUT), (gate, E_GATE), (proj, E_PROJ)):
        ref[...] = early_ref[:, first : first + WIDTH].astype(F32)
    qkv[...] = late_ref[:, : 3 * WIDTH].astype(F32)
    for c in range(MHEADS * 2):
        table = keys_ref[c * NK : (c + 1) * NK, :]
        query[:, c * HALF : (c + 1) * HALF] = dot(
            early_ref[:, E_HALF + c * NK : E_HALF + (c + 1) * NK], table
        )
    gains[...] = late_ref[:, L_GAIN:].astype(F32).T[:8]


def finish(early, late, keys):
    rows = early.shape[0]
    shapes = [(rows, WIDTH)] * 3 + [(rows, 3 * WIDTH), (rows, QUERIES)]
    shapes.append((8, LANES))
    return pl.pallas_call(
        finish_kernel,
        out_shape=[jax.ShapeDtypeStruct(shape, F32) for shape in shapes],
        compiler_params=pltpu.CompilerParams(vmem_limit_bytes=40 * 1024 * 1024),
        name="finish",
    )(early, late, keys)


def rms_scale(values):
    return lax.rsqrt(jnp.mean(values * values, axis=-1, keepdims=True) + EPS)


def rms_back(values, scale, gain, grad):
    scaled = grad * gain
    inner = jnp.mean(values * scaled, axis=-1, keepdims=True)
    gain_grad = jnp.sum(grad * values * scale, axis=0)
    return scale * scaled - values * (scale * scale * scale * inner), gain_grad


def per_device(
    tokens,
    segment_ids,
    picks,
    attn_gain,
    qkv_weight,
    attn_proj,
    mem_gain,
    query_weight,
    half_keys,
    memory_values,
    gate_weight,
    out_weight,
    out_cotangent,
):
    rows, width = tokens.shape
    owners = lax.axis_size("grp") * lax.axis_size("mem")
    local_rows = memory_values.shape[0]
    total_picks = rows * MHEADS * TOPK
    flat_bits = (total_picks - 1).bit_length()
    capacity = 2 * total_picks // owners
    group_len = segment_ids.shape[0]
    linked = (lax.axis_size("grp"), lax.axis_size("mem"), rows) == (4, 8, LANES)
    position = lax.axis_index("mem").astype(jnp.int32)
    pos = position.reshape(1)

    def gather(x, axes="mem"):
        return lax.all_gather(x, axes, axis=0, tiled=True)

    flat_picks = picks.reshape(rows, MHEADS * TOPK)
    if linked:
        gain_block = jnp.concatenate(
            [attn_gain[None], mem_gain[None], jnp.zeros((14, LANES), BF)]
        )
    else:
        gains = lax.all_gather(jnp.stack([attn_gain, mem_gain]), "mem", axis=1, tiled=True)
        tokens_all = gather(tokens)
        qkv_full = gather(qkv_weight)
        proj_full = gather(attn_proj)
        query_full = gather(query_weight)
        keys_full = gather(half_keys)
        gate_full = gather(gate_weight)
        output_full = gather(out_weight)
        gains = gains.astype(F32)
        gain_one, gain_two = gains[0:1], gains[1:2]
    seg_row, seg_col = segment_ids.reshape(1, group_len), segment_ids.reshape(group_len, 1)

    requests = route(picks, owners, local_rows, capacity, flat_bits)
    arrived = lax.all_to_all(requests, ALL, split_axis=0, concat_axis=0, tiled=True)

    if linked:
        (
            keys_full,
            qkv_full,
            proj_full,
            gate_full,
            output_full,
            folded_full,
            qkv_all,
            attn_sum,
            lse,
            gains,
        ) = gather_weights(
            half_keys,
            qkv_weight,
            attn_proj,
            gate_weight,
            out_weight,
            tokens,
            gain_block,
            query_weight,
            seg_col,
            seg_row,
            rows,
        )
        gains = gains.reshape(8, 16, LANES)[:, :2].transpose(1, 0, 2).reshape(2, width)
        gains = gains.astype(F32)
        gain_one, gain_two = gains[0:1], gains[1:2]
    else:
        inputs_all = tokens_all.astype(F32)
        first_all = (inputs_all * rms_scale(inputs_all) * gain_one).astype(BF)
        qkv_all = dot(first_all, qkv_full).astype(BF)
        attn_sum, lse = attn_fwd(pos, qkv_all, seg_row, seg_col, rows)
    attended = attn_sum.astype(BF)
    inputs = tokens.astype(F32)
    residual = inputs + dot(attended, proj_full)
    scale_two = rms_scale(residual)
    second = (residual * scale_two * gain_two).astype(BF)
    gate_pre = dot(second, gate_full)
    mixed_grad = dot(out_cotangent, output_full, NT)
    sig = jax.nn.sigmoid(gate_pre)
    gate_act = gate_pre * sig
    memory_grad = (mixed_grad * gate_act).astype(BF)
    if linked:
        half_scores = dot(second, folded_full)
    else:
        mem_query = dot(second, query_full).astype(BF)
        key_table = keys_full.reshape(MHEADS * 2, NK, HALF)
        half_scores = jnp.einsum(
            "tcf,cnf->tcn",
            mem_query.reshape(rows, MHEADS * 2, HALF),
            key_table,
            preferred_element_type=F32,
        ).reshape(rows, KEYS)
    pick_weights, weights_low = pick_fwd(half_scores, flat_picks)

    payload = jnp.concatenate([memory_grad, weights_low], axis=1)
    if linked:
        back, values_grad = memory_call(payload, arrived, memory_values, flat_bits)
    else:
        sent = gather(payload, ALL)
        part, spread = owner_call(arrived, sent, memory_values, flat_bits)
        back = lax.psum_scatter(part, "grp", scatter_dimension=0, tiled=True)
        back = lax.psum_scatter(back, "mem", scatter_dimension=0, tiled=True)
        values_grad = jnp.einsum(
            "hkl,kd->hld", spread, sent[:, :width], preferred_element_type=F32
        )
    values_grad = values_grad.reshape(local_rows, width)

    memory_out = back[:, :width].astype(F32)
    mixed = (memory_out * gate_act).astype(BF)
    block_out = (residual + dot(mixed, output_full)).astype(BF)
    gate_grad = (mixed_grad * memory_out * (sig * (1.0 + gate_pre * (1.0 - sig)))).astype(BF)
    half_grad, values_grad = pick_bwd(
        pick_weights, back.astype(F32), flat_picks, values_grad
    )
    if linked:
        second_grad = dot(gate_grad, gate_full, NT) + dot(half_grad, folded_full, NT)
    else:
        half_cube = half_grad.reshape(rows, MHEADS * 2, NK)
        query_grad = (
            jnp.einsum("tcn,cnf->tcf", half_cube, key_table, preferred_element_type=F32)
            .astype(BF)
            .reshape(rows, QUERIES)
        )
        second_grad = dot(gate_grad, gate_full, NT) + dot(query_grad, query_full, NT)
    resid_from_norm, gain_two_grad = rms_back(residual, scale_two, gain_two, second_grad)
    resid_grad = out_cotangent.astype(F32) + resid_from_norm
    resid_low = resid_grad.astype(BF)
    attn_grad = dot(resid_low, proj_full, NT).astype(BF)
    heads = (iota((width, HEADS), 0) // HDIM == iota((width, HEADS), 1)).astype(F32)
    delta = jnp.dot(
        attn_grad.astype(F32) * attn_sum,
        heads,
        precision=lax.Precision.HIGHEST,
        preferred_element_type=F32,
    )
    stats = jnp.concatenate([lse[:, :HEADS], delta], axis=1)
    stats_high = lax.reduce_precision(stats, 8, 7)
    stats_low = stats - stats_high
    shared = jnp.concatenate(
        [
            resid_low,
            stats_high.astype(BF),
            stats_low.astype(BF),
            jnp.zeros((rows, LANES - 4 * HEADS), BF),
        ],
        axis=1,
    )
    if linked:
        early = (
            mixed,
            second,
            attended,
            out_cotangent,
            gate_grad,
            resid_low,
            half_grad,
        )
        early, qkv_rows = reduce_back(early, shared, qkv_all, proj_full, seg_col, seg_row)
    else:
        shared = gather(shared)
        stats_all = shared[:, width : width + 2 * HEADS].astype(F32) + shared[
            :, width + 2 * HEADS : width + 4 * HEADS
        ].astype(F32)
        attn_grad_all = dot(shared[:, :width], proj_full, NT).astype(BF)
        qkv_rows = attn_bwd(pos, qkv_all, attn_grad_all, stats_all, seg_row, seg_col, rows)
    scale_one = rms_scale(inputs)
    first_low = (inputs * scale_one * gain_one).astype(BF)
    first_grad = dot(qkv_rows, qkv_full, NT)
    input_from_norm, gain_one_grad = rms_back(inputs, scale_one, gain_one, first_grad)
    tokens_grad = resid_grad + input_from_norm

    if linked:
        sums = jnp.stack([gain_one_grad, gain_two_grad])
        sums_high = lax.reduce_precision(sums, 8, 7)
        gain_rows = jnp.stack([sums_high, sums - sums_high], axis=1).reshape(4, width)
        gain_rows = jnp.concatenate([gain_rows.astype(BF), jnp.zeros((12, width), BF)])
        late, keys_share = reduce_late(
            first_low, qkv_rows, gain_rows, early[:, E_HALF:], query_weight
        )
        (
            out_share,
            gate_share,
            proj_share,
            qkv_share,
            query_share,
            gain_sums,
        ) = finish(early, late, keys_full)
    else:
        keys_grad = jnp.einsum(
            "tcn,tcf->cnf",
            half_cube,
            mem_query.reshape(rows, MHEADS * 2, HALF),
            preferred_element_type=F32,
        ).reshape(KEYS, HALF)
        partials = (
            dot(mixed, out_cotangent, TN),
            dot(second, gate_grad, TN),
            keys_grad,
            dot(second, query_grad, TN),
            dot(attended, resid_low, TN),
            dot(first_low, qkv_rows, TN),
        )
        shares = [
            lax.psum_scatter(x.astype(BF), "mem", scatter_dimension=0, tiled=True)
            for x in partials
        ]
        shares = lax.psum(tuple(shares), "grp")
        gain_sums = lax.psum(jnp.stack([gain_one_grad, gain_two_grad]), ALL)
        gain_sums = lax.dynamic_slice_in_dim(
            gain_sums, position * attn_gain.shape[0], attn_gain.shape[0], axis=1
        )
        out_share, gate_share, keys_share, query_share, proj_share, qkv_share = (
            x.astype(F32) for x in shares
        )
    return (
        block_out,
        tokens_grad,
        gain_sums[0],
        qkv_share,
        proj_share,
        gain_sums[1],
        query_share,
        keys_share,
        values_grad,
        gate_share,
        out_share,
    )


def solution(mesh):
    placed = (
        P(ALL, None),
        P("grp"),
        P(ALL, None, None),
        P("mem"),
        P("mem", None),
        P("mem", None),
        P("mem"),
        P("mem", None),
        P("mem", None),
        P(ALL, None),
        P("mem", None),
        P("mem", None),
        P(ALL, None),
    )
    return jax.shard_map(
        per_device,
        mesh=mesh,
        in_specs=placed,
        out_specs=(
            P(ALL, None),
            P(ALL, None),
            P("mem"),
            P("mem", None),
            P("mem", None),
            P("mem"),
            P("mem", None),
            P("mem", None),
            P(ALL, None),
            P("mem", None),
            P("mem", None),
        ),
        check_vma=False,
    )
```

```python
import functools

import jax
import jax.numpy as jnp
from jax import lax
from jax.experimental import pallas as pl
from jax.experimental.pallas import tpu as pltpu
from jax.sharding import PartitionSpec as P

HEADS = 16
HDIM = 64
MHEADS = 4
NK = 256
HALF = 512
TOPK = 32
EPS = 1e-05
LANES = 128
ALL = ("grp", "mem")
BF = jnp.bfloat16
F32 = jnp.float32
NEG = -1e30


def dot(left, right, dims=((1,), (0,))):
    return lax.dot_general(left, right, (dims, ((), ())), preferred_element_type=F32)


NT = ((1,), (1,))
TN = ((0,), (0,))


def iota(shape, dim):
    return lax.broadcasted_iota(jnp.int32, shape, dim)


def lane_halves(rows):
    first = iota((rows, LANES), 1) < HDIM
    return first


def half_masks():
    lane = iota((1, LANES), 1)
    return ((lane < HDIM).astype(BF), (lane >= HDIM).astype(BF))


def attn_fwd_pair(rows, win, pair, position, query, load, qseg_ref, kseg_ref, lse):
    row0 = position * rows
    start = pl.multiple_of(jnp.maximum(row0 + rows - win, 0), LANES)
    keys, values = load(1, pl.ds(start, win)), load(2, pl.ds(start, win))
    key_pos = start + iota((rows, win), 1)
    query_pos = row0 + iota((rows, win), 0)
    allowed = (key_pos <= query_pos) & (kseg_ref[:, pl.ds(start, win)] == qseg_ref[...])
    lane = iota((rows, LANES), 1)
    masks = half_masks()
    outs = []
    for half in range(2):
        scores = dot(query * masks[half], keys, NT) * 0.125
        scores = jnp.where(allowed, scores, NEG)
        top = jnp.max(scores, axis=1, keepdims=True)
        weights = jnp.exp(scores - top)
        total = jnp.sum(weights, axis=1, keepdims=True)
        probs = weights * (1.0 / total)
        outs.append(dot(probs.astype(BF), values))
        lse = jnp.where(lane == pair * 2 + half, top + jnp.log(total), lse)
    return jnp.where(lane < HDIM, outs[0], outs[1]), lse


def attn_fwd_kernel(rows, win, pos_ref, q_ref, k_ref, v_ref, qseg_ref, kseg_ref, out_ref, lse_ref):
    pair = pl.program_id(0)
    refs = (q_ref, k_ref, v_ref)
    lse = jnp.where(pair == 0, jnp.zeros((rows, LANES), F32), lse_ref[...])
    out_ref[...], lse_ref[...] = attn_fwd_pair(
        rows,
        win,
        pair,
        pos_ref[0],
        q_ref[...],
        lambda which, where: refs[which][where, :],
        qseg_ref,
        kseg_ref,
        lse,
    )


def attn_fwd(pos, qkv, seg_row, seg_col, rows):
    group_len, width = qkv.shape[0], qkv.shape[1] // 3
    pairs = width // LANES
    win = min(group_len, group_len // 2 + rows)
    return pl.pallas_call(
        functools.partial(attn_fwd_kernel, rows, win),
        grid_spec=pltpu.PrefetchScalarGridSpec(
            num_scalar_prefetch=1,
            grid=(pairs,),
            in_specs=[
                pl.BlockSpec((rows, LANES), lambda h, p: (p[0], h)),
                pl.BlockSpec((group_len, LANES), lambda h, p: (0, pairs + h)),
                pl.BlockSpec((group_len, LANES), lambda h, p: (0, 2 * pairs + h)),
                pl.BlockSpec((rows, 1), lambda h, p: (p[0], 0)),
                pl.BlockSpec((1, group_len), lambda h, p: (0, 0)),
            ],
            out_specs=[
                pl.BlockSpec((rows, LANES), lambda h, p: (0, h)),
                pl.BlockSpec((rows, LANES), lambda h, p: (0, 0)),
            ],
        ),
        out_shape=[
            jax.ShapeDtypeStruct((rows, width), F32),
            jax.ShapeDtypeStruct((rows, LANES), F32),
        ],
        cost_estimate=pl.CostEstimate(
            flops=4 * rows * win * width,
            bytes_accessed=group_len * width * 4,
            transcendentals=rows * win * HEADS,
        ),
        name="attn_fwd",
    )(pos, qkv, qkv, qkv, seg_col, seg_row)


def attn_bwd_pair(rows, win, pair, position, group_len, load, stat_ref, segc_ref, segr_ref):
    row0 = pl.multiple_of(position * rows, LANES)
    start = pl.multiple_of(jnp.maximum(row0 + rows - win, 0), LANES)
    qstart = pl.multiple_of(jnp.minimum(row0, group_len - win), LANES)
    own, back, ahead = pl.ds(row0, rows), pl.ds(start, win), pl.ds(qstart, win)
    masks = half_masks()
    lane = iota((rows, LANES), 1)

    def stat(where, index, count):
        table = stat_ref[where, :]
        return jnp.sum(
            jnp.where(iota((count, table.shape[1]), 1) == index, table, 0.0),
            axis=1,
            keepdims=True,
        )

    allowed = (start + iota((rows, win), 1) <= row0 + iota((rows, win), 0)) & (
        segr_ref[:, back] == segc_ref[own, :]
    )
    allowed_two = (row0 + iota((win, rows), 1) <= qstart + iota((win, rows), 0)) & (
        segr_ref[:, own] == segc_ref[ahead, :]
    )
    dqs, dks, dvs = [], [], []
    for half in range(2):
        head = pair * 2 + half
        lse, delta = stat(own, head, rows), stat(own, HEADS + head, rows)
        keys = load(1, back)
        scores = dot(load(0, own) * masks[half], keys, NT) * 0.125
        probs = jnp.exp(jnp.where(allowed, scores - lse, NEG))
        dprobs = dot(load(3, own) * masks[half], load(2, back), NT)
        grads = (probs * (dprobs - delta)).astype(BF)
        dqs.append(dot(grads, keys))
        lse, delta = stat(ahead, head, win), stat(ahead, HEADS + head, win)
        queries, douts = load(0, ahead), load(3, ahead)
        scores = dot(queries * masks[half], load(1, own), NT) * 0.125
        probs = jnp.exp(jnp.where(allowed_two, scores - lse, NEG))
        dprobs = dot(douts * masks[half], load(2, own), NT)
        grads = (probs * (dprobs - delta)).astype(BF)
        dks.append(dot(grads, queries, TN))
        dvs.append(dot(probs.astype(BF), douts, TN))
    return [
        (jnp.where(lane < HDIM, parts[0], parts[1]) * scale).astype(BF)
        for parts, scale in ((dqs, 0.125), (dks, 0.125), (dvs, 1.0))
    ]


def attn_bwd_kernel(
    rows, win, pairs, pos_ref, q_ref, k_ref, v_ref, da_ref, stat_ref, segc_ref, segr_ref, out_ref
):
    pair = pl.program_id(0)
    refs = (q_ref, k_ref, v_ref, da_ref)
    grads = attn_bwd_pair(
        rows,
        win,
        pair,
        pos_ref[0],
        k_ref.shape[0],
        lambda which, where: refs[which][where, :],
        stat_ref,
        segc_ref,
        segr_ref,
    )
    for i, value in enumerate(grads):
        column = pl.multiple_of((i * pairs + pair) * LANES, LANES)
        out_ref[:, pl.ds(column, LANES)] = value


def attn_bwd(pos, qkv, douts, stats, seg_row, seg_col, rows):
    group_len, width = douts.shape
    pairs = width // LANES
    win = min(group_len, group_len // 2 + rows)
    return pl.pallas_call(
        functools.partial(attn_bwd_kernel, rows, win, pairs),
        grid_spec=pltpu.PrefetchScalarGridSpec(
            num_scalar_prefetch=1,
            grid=(pairs,),
            in_specs=[
                pl.BlockSpec((group_len, LANES), lambda h, p: (0, h)),
                pl.BlockSpec((group_len, LANES), lambda h, p: (0, pairs + h)),
                pl.BlockSpec((group_len, LANES), lambda h, p: (0, 2 * pairs + h)),
                pl.BlockSpec((group_len, LANES), lambda h, p: (0, h)),
                pl.BlockSpec(stats.shape, lambda h, p: (0, 0)),
                pl.BlockSpec((group_len, 1), lambda h, p: (0, 0)),
                pl.BlockSpec((1, group_len), lambda h, p: (0, 0)),
            ],
            out_specs=pl.BlockSpec((rows, 3 * width), lambda h, p: (0, 0)),
        ),
        out_shape=jax.ShapeDtypeStruct((rows, 3 * width), BF),
        cost_estimate=pl.CostEstimate(
            flops=14 * rows * win * width,
            bytes_accessed=group_len * width * 8,
            transcendentals=2 * rows * win * HEADS,
        ),
        name="attn_bwd",
    )(pos, qkv, qkv, qkv, douts, stats, seg_col, seg_row)


def by_head(lane, reduce, fill, values):
    spread = jnp.zeros_like(values)
    for c in range(MHEADS):
        inside = lane // TOPK == c
        spread = jnp.where(
            inside, reduce(jnp.where(inside, values, fill), axis=1, keepdims=True), spread
        )
    return spread


def pick_fwd_kernel(scores_ref, picks_ref, weight_ref, low_ref):
    rows = picks_ref.shape[0]
    lane = iota((rows, LANES), 1)
    picks = picks_ref[...]
    index = (picks // NK, picks % NK)
    total = jnp.zeros((rows, LANES), F32)
    for c in range(MHEADS):
        both = jnp.zeros((rows, LANES), F32)
        for e in range(2):
            base = (c * 2 + e) * NK
            for part in range(NK // LANES):
                table = scores_ref[:, base + part * LANES : base + (part + 1) * LANES]
                found = jnp.take_along_axis(table, index[e] % LANES, axis=1)
                both = both + jnp.where(index[e] // LANES == part, found, 0.0)
        total = jnp.where(lane // TOPK == c, both, total)
    top = by_head(lane, jnp.max, NEG, total)
    weights = jnp.exp(total - top)
    weights = weights / by_head(lane, jnp.sum, 0.0, weights)
    weight_ref[...] = weights
    low_ref[...] = weights.astype(BF)


def pick_fwd(half_scores, picks):
    rows = picks.shape[0]
    return pl.pallas_call(
        pick_fwd_kernel,
        out_shape=[
            jax.ShapeDtypeStruct((rows, LANES), F32),
            jax.ShapeDtypeStruct((rows, LANES), BF),
        ],
        name="pick_fwd",
    )(half_scores, picks)


def pick_bwd_kernel(
    weight_ref,
    grad_ref,
    picks_ref,
    table_ref,
    out_ref,
    whole_ref,
    score_t,
    first_t,
    second_t,
    stage,
    in_sem,
    out_sem,
):
    block = table_ref.shape[0] // MHEADS

    def part(c):
        return pl.ds(pl.multiple_of(c * block, block), block)

    def fetch(c):
        return pltpu.make_async_copy(table_ref.at[part(c)], stage.at[c], in_sem.at[c])

    def put(c):
        return pltpu.make_async_copy(stage.at[c], whole_ref.at[part(c)], out_sem.at[c])

    for c in range(MHEADS):
        fetch(c).start()
    rows = picks_ref.shape[0]
    lane = iota((rows, LANES), 1)
    weights, grads = weight_ref[...], grad_ref[...]
    score = (weights * (grads - by_head(lane, jnp.sum, 0.0, weights * grads))).astype(BF)
    score_t[...] = score.astype(F32).T
    picks_t = picks_ref[...].T
    first_t[...] = picks_t // NK
    second_t[...] = picks_t % NK
    key = iota((NK, rows), 0)

    def head(c, _):
        first = jnp.zeros((NK, rows), F32)
        second = jnp.zeros((NK, rows), F32)
        for j in range(TOPK):
            at = pl.ds(c * TOPK + j, 1)
            value = score_t[at, :]
            first = first + jnp.where(key == first_t[at, :], value, 0.0)
            second = second + jnp.where(key == second_t[at, :], value, 0.0)
        for e, total in enumerate((first, second)):
            base = pl.multiple_of((c * 2 + e) * NK, LANES)
            out_ref[:, pl.ds(base, NK)] = total.T.astype(BF)
        fetch(c).wait()
        put(c).start()
        return 0

    lax.fori_loop(0, MHEADS, head, 0)
    for c in range(MHEADS):
        put(c).wait()


def pick_bwd(weights, grads, picks, table):
    rows = picks.shape[0]
    last = grads.shape[1] // LANES - 1
    spec = pl.BlockSpec((rows, LANES), lambda i: (0, 0))
    hbm = pl.BlockSpec(memory_space=pltpu.HBM)
    return pl.pallas_call(
        pick_bwd_kernel,
        grid=(1,),
        in_specs=[spec, pl.BlockSpec((rows, LANES), lambda i: (0, last)), spec, hbm],
        out_specs=[pl.BlockSpec((rows, MHEADS * 2 * NK), lambda i: (0, 0)), hbm],
        out_shape=[
            jax.ShapeDtypeStruct((rows, MHEADS * 2 * NK), BF),
            jax.ShapeDtypeStruct(table.shape, table.dtype),
        ],
        scratch_shapes=[
            pltpu.VMEM((LANES, rows), F32),
            pltpu.VMEM((LANES, rows), jnp.int32),
            pltpu.VMEM((LANES, rows), jnp.int32),
            pltpu.VMEM((MHEADS, table.shape[0] // MHEADS, table.shape[1]), table.dtype),
            pltpu.SemaphoreType.DMA((MHEADS,)),
            pltpu.SemaphoreType.DMA((MHEADS,)),
        ],
        compiler_params=pltpu.CompilerParams(vmem_limit_bytes=40 * 1024 * 1024),
        name="pick_bwd",
    )(weights, grads, picks, table)


def owner_kernel(
    his, flat_bits, local_rows, keys_ref, sent_ref, values_ref, part_ref, spread_ref
):
    rows = part_ref.shape[0]
    width = values_ref.shape[1]
    slots = keys_ref.shape[-1]
    low_rows = local_rows // his
    key = keys_ref[0]
    flat = key & ((1 << flat_bits) - 1)
    dummy = ((key >> flat_bits) & 1) == 1
    row = (key >> (flat_bits + 1)) % local_rows
    token = flat // LANES
    pick = flat % LANES
    token = jnp.where(dummy, -1, token)
    block = jnp.where(dummy, -1, (row // low_rows) * rows + token)
    low_row = row % low_rows
    grad = sent_ref[:, :width]
    weights = sent_ref[:, width:]
    is_token = iota((rows, slots), 0) == token
    is_pick = iota((LANES, slots), 0) == pick
    token_hot = is_token.astype(F32).astype(BF)
    found = dot(weights, token_hot, TN)
    weight = jnp.sum(jnp.where(is_pick, found, 0.0), axis=0, keepdims=True)
    is_block = iota((his * rows, slots), 0) == block
    is_low = iota((low_rows, slots), 0) == low_row
    low_hot = is_low.astype(F32).astype(BF)
    spread = dot(jnp.where(is_block, weight, 0.0).astype(BF), low_hot, NT).astype(BF)
    total = jnp.zeros((rows, width), F32)
    products = []
    for h in range(his):
        table = values_ref[h * low_rows : (h + 1) * low_rows, :]
        piece = spread[h * rows : (h + 1) * rows, :]
        spread_ref[h] = piece
        total = total + dot(piece, table)
        products.append(dot(grad, table, NT).astype(BF))
    picked = dot(jnp.concatenate(products, axis=0), is_block.astype(F32).astype(BF), TN)
    picked = jnp.sum(jnp.where(is_low, picked, 0.0), axis=0, keepdims=True)
    part_ref[:, :width] = total.astype(BF)
    part_ref[:, width:] = dot(
        jnp.where(is_token, picked, 0.0).astype(BF), is_pick.astype(F32).astype(BF), NT
    ).astype(BF)


def owner_call(keys, sent, values, flat_bits):
    owners, slots = keys.shape
    rows = sent.shape[0] // owners
    local_rows, width = values.shape
    his = 4
    low_rows = local_rows // his
    return pl.pallas_call(
        functools.partial(owner_kernel, his, flat_bits, local_rows),
        grid=(owners,),
        in_specs=[
            pl.BlockSpec((1, 1, slots), lambda s: (s, 0, 0)),
            pl.BlockSpec((rows, width + LANES), lambda s: (s, 0)),
            pl.BlockSpec((local_rows, width), lambda s: (0, 0)),
        ],
        out_specs=[
            pl.BlockSpec((rows, width + LANES), lambda s: (s, 0)),
            pl.BlockSpec((his, rows, low_rows), lambda s: (0, s, 0)),
        ],
        out_shape=[
            jax.ShapeDtypeStruct((owners * rows, width + LANES), BF),
            jax.ShapeDtypeStruct((his, owners * rows, low_rows), BF),
        ],
        compiler_params=pltpu.CompilerParams(vmem_limit_bytes=48 * 1024 * 1024),
        cost_estimate=pl.CostEstimate(
            flops=2 * owners * rows * local_rows * (2 * slots + 2 * width),
            bytes_accessed=owners * rows * (2 * width + local_rows) * 2,
            transcendentals=0,
        ),
        name="owner",
    )(keys.reshape(owners, 1, slots), sent, values)


def route(picks, owners, local_rows, capacity, flat_bits):
    total = picks.size
    rows_of = picks.reshape(total)
    flat = jnp.arange(total, dtype=jnp.int32)
    each = jnp.arange(owners, dtype=jnp.int32)
    counts = jnp.sum((rows_of[:, None] // local_rows == each[None, :]).astype(jnp.int32), axis=0)
    ends = jnp.cumsum(capacity - counts)
    spares = owners * capacity - total
    spare_owner = jnp.sum(
        (jnp.arange(spares, dtype=jnp.int32)[:, None] >= ends[None, :]).astype(jnp.int32), axis=1
    )
    real = (rows_of << (flat_bits + 1)) + flat
    spare = ((spare_owner * local_rows + local_rows - 1) << (flat_bits + 1)) + (1 << flat_bits)
    keys = lax.sort(jnp.concatenate([real, spare]), is_stable=False)
    return keys.reshape(owners, capacity)


MESH = pl.DeviceIdType.MESH


def places():
    g, m = lax.axis_index("grp"), lax.axis_index("mem")
    across = g + 1 - 2 * (g % 2)
    along = (g + 2) % 4
    sibling = m + 1 - 2 * (m % 2)
    return g, m, across, along, sibling


def enter(peers):
    barrier = pltpu.get_barrier_semaphore()
    for peer in peers:
        pl.semaphore_signal(barrier, inc=1, device_id=peer, device_id_type=MESH)
    pl.semaphore_wait(barrier, len(peers))


def push(src, dst, send, recv, peer):
    copy = pltpu.make_async_remote_copy(
        src_ref=src, dst_ref=dst, send_sem=send, recv_sem=recv, device_id=peer, device_id_type=MESH
    )
    copy.start()
    return copy


def plane_tasks(held, x1, y1, x2, y2, zin, send, recv):
    g, m, across, along, _ = places()
    diagonal = 3 - g
    half = held.shape[2] // 2
    low, high = pl.ds(0, half), pl.ds(half, half)
    to_x, to_y = (across, m), (along, m)

    def copy(kind, k, src, dst, peer):
        return pltpu.make_async_remote_copy(
            src_ref=src,
            dst_ref=dst,
            send_sem=send.at[kind, k],
            recv_sem=recv.at[kind, k],
            device_id=peer,
            device_id_type=MESH,
        )

    def ones(k):
        return (
            copy(0, k, held.at[k, diagonal, low], x1.at[k], to_x),
            copy(1, k, held.at[k, diagonal, high], y1.at[k], to_y),
        )

    def twos(k):
        return (
            copy(2, k, held.at[k, across], x2.at[k], to_x),
            copy(3, k, held.at[k, along], y2.at[k], to_y),
        )

    def three(k):
        return copy(4, k, held.at[k, g], zin.at[k], (g, (m + 2 * (3 - k)) % 8))

    def first(k):
        for item in ones(k):
            item.start()

    def corner(k):
        for item in ones(k):
            item.wait_recv()
        held[k, along, low] = held[k, along, low] + x1[k]
        held[k, across, high] = held[k, across, high] + y1[k]
        for item in twos(k):
            item.start()

    def total_of(k):
        for item in twos(k):
            item.wait_recv()
        return held[k, g].astype(F32) + x2[k].astype(F32) + y2[k].astype(F32)

    def plane(k):
        held[k, g] = total_of(k).astype(BF)
        three(k).start()

    def last():
        total = total_of(3)
        for k in range(3):
            three(k).wait_recv()
            total = total + zin[k].astype(F32)
        for k in range(4):
            for item in ones(k) + twos(k):
                item.wait_send()
            if k < 3:
                three(k).wait_send()
        return total

    return first, corner, plane, last


def plane_peers():
    g, m, across, along, sibling = places()
    return [(across, m), (along, m), (g, sibling)] + [(g, (m + 2 * d) % 8) for d in (1, 2, 3)]


def plane_scratch(rows, columns):
    return [
        pltpu.VMEM((4, rows // 2, columns), BF),
        pltpu.VMEM((4, rows // 2, columns), BF),
        pltpu.VMEM((4, rows, columns), BF),
        pltpu.VMEM((4, rows, columns), BF),
        pltpu.VMEM((3, rows, columns), BF),
    ]


def memory_kernel(
    flat_bits,
    payload_ref,
    keys_ref,
    values_ref,
    out_ref,
    grad_ref,
    sent,
    parts,
    sibs,
    x1,
    y1,
    x2,
    y2,
    zin,
    held,
    spread,
    table,
    own_sem,
    table_sem,
    send,
    recv,
):
    g, m, across, along, sibling = places()
    core, z = m % 2, m // 2
    to_x, to_y, to_s = (across, m), (along, m), (g, sibling)
    rows, columns = payload_ref.shape
    width = columns - LANES
    local_rows = values_ref.shape[0]
    slots = keys_ref.shape[1]
    his = spread.shape[0]
    low_rows = local_rows // his
    low, high = pl.ds(0, rows // 2), pl.ds(rows // 2, rows // 2)
    enter(plane_peers())

    def copy(kind, index, src, dst, peer):
        return pltpu.make_async_remote_copy(
            src_ref=src,
            dst_ref=dst,
            send_sem=send.at[kind, index],
            recv_sem=recv.at[kind, index],
            device_id=peer,
            device_id_type=MESH,
        )

    def mine(i):
        return payload_ref if i == 0 else sent.at[i, core]

    def to_sibling(i):
        return copy(0, i, mine(i), sent.at[i, core], to_s)

    def plane_x(k):
        return copy(1, k, mine(4 * k), sent.at[4 * k + 1, core], to_x)

    def plane_y(k):
        return copy(2, k, mine(4 * k), sent.at[4 * k + 2, core], to_y)

    def line(k):
        return copy(3, k, payload_ref, sent.at[4 * k, core], (g, (m + 2 * k) % 8))

    def corner_y(k):
        return copy(4, k, sent.at[4 * k + 1, core, low], sent.at[4 * k + 3, core, low], to_y)

    def corner_x(k):
        return copy(5, k, sent.at[4 * k + 2, core, high], sent.at[4 * k + 3, core, high], to_x)

    def part_sibling(i):
        return copy(6, i, parts.at[i, 1 - core], sibs.at[i], to_s)

    def one_x(k):
        return copy(7, k, parts.at[4 * k + 3, core, low], x1.at[k], to_x)

    def one_y(k):
        return copy(8, k, parts.at[4 * k + 3, core, high], y1.at[k], to_y)

    def two_x(k):
        return copy(9, k, parts.at[4 * k + 1, core], x2.at[k], to_x)

    def two_y(k):
        return copy(10, k, parts.at[4 * k + 2, core], y2.at[k], to_y)

    def three(k):
        return copy(11, k, parts.at[4 * k, core], zin.at[k - 1], (g, (m + 8 - 2 * k) % 8))

    def from_line(k):
        line(k).wait_recv()
        plane_x(k).start()
        plane_y(k).start()
        to_sibling(4 * k).start()

    def from_plane(k):
        plane_x(k).wait_recv()
        corner_y(k).start()
        to_sibling(4 * k + 1).start()
        plane_y(k).wait_recv()
        corner_x(k).start()
        to_sibling(4 * k + 2).start()

    def from_corner(k):
        corner_x(k).wait_recv()
        corner_y(k).wait_recv()
        to_sibling(4 * k + 3).start()

    def pair_sum(k):
        for i in (4 * k + 3, 4 * k + 1, 4 * k + 2, 4 * k):
            part_sibling(i).wait_recv()
            parts[i, core] = parts[i, core] + sibs[i]
            if i == 4 * k + 3:
                one_x(k).start()
                one_y(k).start()

    def corner_sum(k):
        one_x(k).wait_recv()
        parts[4 * k + 2, core, low] = parts[4 * k + 2, core, low] + x1[k]
        two_y(k).start()
        one_y(k).wait_recv()
        parts[4 * k + 1, core, high] = parts[4 * k + 1, core, high] + y1[k]
        two_x(k).start()

    def plane_sum(k):
        two_x(k).wait_recv()
        two_y(k).wait_recv()
        total = parts[4 * k, core].astype(F32) + x2[k].astype(F32) + y2[k].astype(F32)
        if k == 0:
            held[...] = total
        else:
            parts[4 * k, core] = total.astype(BF)
            three(k).start()

    own = pltpu.make_async_copy(payload_ref, sent.at[0, core], own_sem)
    own.start()
    to_sibling(0).start()
    plane_x(0).start()
    plane_y(0).start()
    for k in (1, 2, 3):
        line(k).start()
    own.wait()

    tasks = {
        1: [lambda: from_plane(0)],
        2: [lambda: from_line(1)],
        3: [lambda: from_corner(0), lambda: from_line(2)],
        4: [lambda: from_line(3), lambda: pair_sum(0), lambda: from_plane(1)],
        6: [lambda: corner_sum(0)],
        7: [lambda: from_corner(1)],
        8: [lambda: from_plane(2), lambda: pair_sum(1)],
        9: [lambda: plane_sum(0)],
        10: [lambda: from_corner(2), lambda: corner_sum(1)],
        11: [lambda: from_plane(3)],
        12: [lambda: pair_sum(2), lambda: plane_sum(1)],
        13: [lambda: from_corner(3)],
        14: [lambda: corner_sum(2)],
    }

    def step(i, _):
        for when, todo in tasks.items():

            @pl.when(i == when)
            def _():
                for task in todo:
                    task()

        copy(0, i, sent.at[i, core], sent.at[i, 1 - core], to_s).wait_recv()
        k, j = i // 4, i % 4
        grp = (g // 2 + j // 2) % 2 * 2 + (g % 2 + j % 2) % 2
        base = grp * 8 + (z + 4 - k) % 4 * 2
        lanes, tiles = [], []
        for c in range(2):
            key = keys_ref[pl.ds(base + c, 1), :]
            flat = key & ((1 << flat_bits) - 1)
            dummy = ((key >> flat_bits) & 1) == 1
            row = (key >> (flat_bits + 1)) % local_rows
            token = jnp.where(dummy, -1, flat // LANES)
            block = jnp.where(dummy, -1, (row // low_rows) * rows + token)
            is_token = iota((rows, slots), 0) == token
            is_pick = iota((LANES, slots), 0) == flat % LANES
            place = jnp.concatenate(
                [
                    jnp.where(is_token, (row % LANES).astype(F32), 0.0).astype(BF),
                    jnp.where(is_token, (row // LANES + 1).astype(F32), 0.0).astype(BF),
                ],
                axis=0,
            )
            place = dot(place, is_pick.astype(F32).astype(BF), NT).astype(jnp.int32)
            lanes.append(place[:rows])
            tiles.append(place[rows:] - 1)
            weights = sent[i, c, :, width:]
            found = dot(weights, is_token.astype(F32).astype(BF), TN)
            weight = jnp.sum(jnp.where(is_pick, found, 0.0), axis=0, keepdims=True)
            is_block = iota((his * rows, slots), 0) == block
            is_low = iota((low_rows, slots), 0) == row % low_rows
            piece = dot(
                jnp.where(is_block, weight, 0.0).astype(BF), is_low.astype(F32).astype(BF), NT
            ).astype(BF)
            for h in range(his):
                spread[h, 2 * i + c] = piece[h * rows : (h + 1) * rows]
        lane, tile = jnp.concatenate(lanes, axis=0), jnp.concatenate(tiles, axis=0)
        grads = sent[i, :, :, :width].reshape(2 * rows, width)
        total = jnp.zeros((2 * rows, width), F32)
        picked = jnp.zeros((2 * rows, LANES), F32)
        for h in range(his):
            table = values_ref[h * low_rows : (h + 1) * low_rows, :]
            piece = spread[h, pl.ds(2 * i, 2)].reshape(2 * rows, low_rows)
            total = total + dot(piece, table)
            products = dot(grads, table, NT)
            for b in range(low_rows // LANES):
                found = jnp.take_along_axis(
                    products[:, b * LANES : (b + 1) * LANES], lane, axis=1
                )
                picked = jnp.where(tile == h * (low_rows // LANES) + b, found, picked)
        parts[i, :, :, :width] = total.astype(BF).reshape(2, rows, width)
        parts[i, :, :, width:] = picked.astype(BF).reshape(2, rows, LANES)
        part_sibling(i).start()
        return 0

    def table_copy(h):
        return pltpu.make_async_copy(table.at[h % 2], grad_ref.at[h], table_sem.at[h % 2])

    def table_grad(h):
        if h >= 2:
            table_copy(h - 2).wait()

        def some(n, _):
            grads = sent[pl.ds(4 * n, 4), :, :, :width].reshape(8 * rows, width)
            piece = spread[h, pl.ds(8 * n, 8)].reshape(8 * rows, low_rows)
            table[h % 2] = jnp.where(n == 0, 0.0, table[h % 2]) + dot(piece, grads, TN)
            return 0

        lax.fori_loop(0, 4, some, 0)
        table_copy(h).start()

    lax.fori_loop(0, 16, step, 0)
    pair_sum(3)
    plane_sum(2)
    table_grad(0)
    corner_sum(3)
    table_grad(1)
    plane_sum(3)
    table_grad(2)
    table_grad(3)
    total = held[...]
    for k in (1, 2, 3):
        three(k).wait_recv()
        total = total + zin[k - 1].astype(F32)
    out_ref[...] = total
    for k in range(4):
        todo = [plane_x(k), plane_y(k), corner_x(k), corner_y(k)]
        todo += [one_x(k), one_y(k), two_x(k), two_y(k)]
        if k:
            todo += [line(k), three(k)]
        for j in range(4):
            todo += [to_sibling(4 * k + j), part_sibling(4 * k + j)]
        for item in todo:
            item.wait_send()
    table_copy(2).wait()
    table_copy(3).wait()


def memory_call(payload, keys, values, flat_bits):
    rows, columns = payload.shape
    local_rows = values.shape[0]
    his = 4
    half = (4, rows // 2, columns)
    full = (4, rows, columns)
    vmem = pl.BlockSpec(memory_space=pltpu.VMEM)
    hbm = pl.BlockSpec(memory_space=pl.ANY)
    return pl.pallas_call(
        functools.partial(memory_kernel, flat_bits),
        in_specs=[hbm, vmem, vmem],
        out_specs=[vmem, hbm],
        out_shape=[
            jax.ShapeDtypeStruct((rows, columns), F32),
            jax.ShapeDtypeStruct((his, local_rows // his, columns - LANES), F32),
        ],
        scratch_shapes=[
            pltpu.VMEM((16, 2, rows, columns), BF),
            pltpu.VMEM((16, 2, rows, columns), BF),
            pltpu.VMEM((16, rows, columns), BF),
            pltpu.VMEM(half, BF),
            pltpu.VMEM(half, BF),
            pltpu.VMEM(full, BF),
            pltpu.VMEM(full, BF),
            pltpu.VMEM((3, rows, columns), BF),
            pltpu.VMEM((rows, columns), F32),
            pltpu.VMEM((his, 32, rows, local_rows // his), BF),
            pltpu.VMEM((2, local_rows // his, columns - LANES), F32),
            pltpu.SemaphoreType.DMA,
            pltpu.SemaphoreType.DMA((2,)),
            pltpu.SemaphoreType.DMA((12, 16)),
            pltpu.SemaphoreType.DMA((12, 16)),
        ],
        compiler_params=pltpu.CompilerParams(
            collective_id=1, has_side_effects=True, vmem_limit_bytes=63 * 1024 * 1024
        ),
        name="memory",
    )(payload, keys, values)


def gather_tasks(pieces, sources, targets, local_sem, send, recv):
    g, m, across, along, sibling = places()
    z = m // 2
    to_x, to_y, to_s = (across, m), (along, m), (g, sibling)
    total = range(len(pieces))
    ways = [(sign, hop) for hop in (1, 2, 3) for sign in (1, -1)]
    shared = [p for p in total if pieces[p][3]]

    def view(piece, owner, quarter=None, part=None):
        array, first, columns, _ = pieces[piece]
        ref = targets[array]
        size = ref.shape[0] // 8
        start = owner * size
        if quarter is not None:
            size = size // 4
            start = start + quarter * size
        if part is not None:
            size = size // 2
            start = start + part * size
        return ref.at[pl.ds(start, size), pl.ds(first, columns)]

    def copy(piece, index, block, peer, src=None):
        return pltpu.make_async_remote_copy(
            src_ref=block if src is None else src,
            dst_ref=block,
            send_sem=send.at[piece, index],
            recv_sem=recv.at[piece, index],
            device_id=peer,
            device_id_type=MESH,
        )

    def line(p, way, owner, src=None):
        block = view(p, owner, g if pieces[p][3] else None)
        peer = (g, (m + 8 + 2 * ways[way][0]) % 8)
        return copy(p, way, block, peer, src)

    def has(way):
        sign, distance = ways[way]
        return z >= distance if sign > 0 else z + distance <= 3

    def more(way):
        return z <= 2 if ways[way][0] > 0 else z >= 1

    def origin(way):
        sign, distance = ways[way]
        return (m + 8 - 2 * sign * distance) % 8

    def planes(p, way):
        block = view(p, origin(way), g)
        return copy(p, 6 + way, block, to_x), copy(p, 12 + way, block, to_y)

    def corners(p, way):
        owner = origin(way)
        return (
            copy(p, 18 + way, view(p, owner, across, 0), to_y),
            copy(p, 24 + way, view(p, owner, along, 1), to_x),
        )

    def core(p, way):
        return copy(p, 30 + way, view(p, origin(way)), to_s)

    def first(p):
        array, start, columns, is_shared = pieces[p]
        ref = sources[array]
        whole = ref.at[:, pl.ds(start, columns)]
        src = whole
        if is_shared:
            quarter = ref.shape[0] // 4
            src = ref.at[pl.ds(g * quarter, quarter), pl.ds(start, columns)]
        return (
            [line(p, way, m, src) for way in (0, 1)],
            pltpu.make_async_copy(whole, view(p, m), local_sem.at[p]),
            copy(p, 36, view(p, m), to_s, whole),
        )

    def begin():
        for p in total:
            for way in (0, 1):
                pl.when(more(way))(first(p)[0][way].start)
        for p in total:
            _, near, side = first(p)
            near.start()
            side.start()

    def level(hop):
        return (2 * hop - 2, 2 * hop - 1)

    def arrive(hop):
        for p in total:
            for way in level(hop):

                @pl.when(has(way))
                def _():
                    line(p, way, origin(way)).wait_recv()
                    if hop < 3:
                        pl.when(more(way))(line(p, way + 2, origin(way)).start)

        for p in total:
            for way in level(hop):

                @pl.when(has(way))
                def _():
                    for item in planes(p, way) if p in shared else [core(p, way)]:
                        item.start()

    def turn(hop):
        for p in shared:
            for way in level(hop):

                @pl.when(has(way))
                def _():
                    for item, after in zip(planes(p, way), corners(p, way), strict=True):
                        item.wait_recv()
                        after.start()

    def cross(hop):
        for p in shared:
            for way in level(hop):

                @pl.when(has(way))
                def _():
                    for item in corners(p, way):
                        item.wait_recv()
                    core(p, way).start()

    def receive():
        for p in total:
            _, near, side = first(p)
            near.wait()
            side.wait_recv()
            for way in range(6):

                @pl.when(has(way))
                def _():
                    core(p, way).wait_recv()

    def drain():
        for p in total:
            out, _, side = first(p)
            side.wait_send()
            for way in (0, 1):
                pl.when(more(way))(out[way].wait_send)
            for way in range(6):

                @pl.when(has(way))
                def _():
                    core(p, way).wait_send()
                    if ways[way][1] < 3:
                        pl.when(more(way))(line(p, way + 2, origin(way)).wait_send)
                    if p in shared:
                        for item in planes(p, way) + corners(p, way):
                            item.wait_send()

    return begin, arrive, turn, cross, receive, drain


def pieces_of(arrays, chunk, own_count):
    pieces = []
    for i, x in enumerate(arrays):
        columns = x.shape[1]
        for first in range(0, columns, chunk):
            pieces.append((i, first, min(chunk, columns - first), i >= own_count))
    return tuple(pieces)


def gathered(arrays):
    return [jax.ShapeDtypeStruct((8 * x.shape[0], x.shape[1]), x.dtype) for x in arrays]


def gather_sems(pieces):
    return [
        pltpu.SemaphoreType.DMA((len(pieces),)),
        pltpu.SemaphoreType.DMA((len(pieces), 37)),
        pltpu.SemaphoreType.DMA((len(pieces), 37)),
    ]


def gather_kernel(sets, rows, win, *refs):
    sources, refs = refs[:7], refs[7:]
    query_ref, segc_ref, segr_ref = refs[:3]
    targets, refs = refs[3:9], refs[9:]
    qkv_ref, out_ref, lse_ref, gains = refs[:4]
    tokens, gain_row, normal, folded = refs[4:8]
    sems = refs[8:]
    keys_src, qkv_src, proj_src, gate_src, head_src, tokens_src, gain_src = sources
    keys_full, weight_full, proj_full, gate_full, head_full, folded_full = targets
    m = lax.axis_index("mem")
    group_len, width = tokens.shape
    pairs = width // LANES
    enter(plane_peers())
    k_set, a_set, c_set, b_set = (
        gather_tasks(pieces, src, dst, *sems[3 * i : 3 * i + 3])
        for i, (pieces, src, dst) in enumerate(
            zip(
                sets,
                (
                    [keys_src],
                    [tokens_src, gain_src, qkv_src],
                    [folded],
                    [proj_src, gate_src, head_src],
                ),
                (
                    [keys_full],
                    [tokens, gains, weight_full],
                    [folded_full],
                    [proj_full, gate_full, head_full],
                ),
                strict=True,
            )
        )
    )
    begin, arrive, turn, cross, receive, drain = range(6)

    def go(which, task, *hop):
        which[task](*hop)

    def fold():
        for c in range(MHEADS * 2):
            folded[:, c * NK : (c + 1) * NK] = dot(
                query_ref[:, c * HALF : (c + 1) * HALF], keys_full[c * NK : (c + 1) * NK, :], NT
            ).astype(BF)

    def normalize():
        for i in range(8):
            gain_row[:, i * LANES : (i + 1) * LANES] = gains[i * 16 : i * 16 + 1, :].astype(F32)
        block = 2 * rows

        def some(i, _):
            where = pl.ds(pl.multiple_of(i * block, block), block)
            values = tokens[where, :].astype(F32)
            normal[where, :] = (values * rms_scale(values) * gain_row[...]).astype(BF)
            return 0

        lax.fori_loop(0, group_len // block, some, 0)

    def project(i, _):
        where = pl.ds(pl.multiple_of(i * 3 * LANES, LANES), 3 * LANES)
        qkv_ref[:, where] = dot(normal[...], weight_full[:, where]).astype(BF)
        during(i, PROJECT_TASKS)
        return 0

    def load_of(pair):
        def load(which, where):
            column = pl.multiple_of((which * pairs + pair) * LANES, LANES)
            return qkv_ref[where, pl.ds(column, LANES)]

        return load

    own = pl.ds(pl.multiple_of(m * rows, LANES), rows)

    def attend(pair, _):
        load = load_of(pair)
        value, lse_ref[...] = attn_fwd_pair(
            rows, win, pair, m, load(0, own), load, segc_ref.at[own], segr_ref, lse_ref[...]
        )
        out_ref[:, pl.ds(pl.multiple_of(pair * LANES, LANES), LANES)] = value
        during(pair, ATTEND_TASKS)
        return 0

    def during(i, tasks):
        for when, todo in tasks.items():

            @pl.when(i == when)
            def _():
                for which, task, hop in todo:
                    go(which, task, hop)

    PROJECT_TASKS = {
        0: [(c_set, turn, 1), (b_set, arrive, 2)],
        2: [(b_set, turn, 1), (c_set, arrive, 3)],
        4: [(c_set, turn, 2), (b_set, arrive, 3)],
        6: [(b_set, turn, 2), (c_set, cross, 1)],
    }
    ATTEND_TASKS = {
        0: [(c_set, turn, 3), (b_set, cross, 1)],
        2: [(b_set, turn, 3), (c_set, cross, 2)],
        3: [(b_set, cross, 2)],
        4: [(c_set, cross, 3)],
        5: [(b_set, cross, 3)],
    }
    lse_ref[...] = jnp.zeros_like(lse_ref)
    go(k_set, begin)
    go(a_set, begin)
    go(k_set, arrive, 1)
    go(k_set, arrive, 2)
    go(a_set, arrive, 1)
    go(k_set, turn, 1)
    go(k_set, arrive, 3)
    go(k_set, turn, 2)
    go(k_set, cross, 1)
    go(k_set, turn, 3)
    go(k_set, cross, 2)
    go(a_set, arrive, 2)
    go(k_set, cross, 3)
    go(a_set, turn, 1)
    go(k_set, receive)
    fold()
    go(c_set, begin)
    go(b_set, begin)
    go(a_set, arrive, 3)
    go(a_set, turn, 2)
    go(a_set, cross, 1)
    go(c_set, arrive, 1)
    go(a_set, turn, 3)
    go(b_set, arrive, 1)
    go(a_set, cross, 2)
    go(a_set, cross, 3)
    go(c_set, arrive, 2)
    go(a_set, receive)
    normalize()
    lax.fori_loop(0, 8, project, 0)
    lax.fori_loop(0, 8, attend, 0)
    go(c_set, receive)
    go(b_set, receive)
    for one in (k_set, a_set, c_set, b_set):
        go(one, drain)


def gather_weights(keys, qkv, proj, gate, head, tokens, gains, query, seg_col, seg_row, rows):
    sets = (
        pieces_of([keys], WIDTH, 0),
        pieces_of([tokens, gains, qkv], 3 * WIDTH, 2),
        pieces_of([jax.ShapeDtypeStruct((query.shape[0], KEYS), BF)], KEYS, 0),
        pieces_of([proj, gate, head], WIDTH, 0),
    )
    group_len = seg_col.shape[0]
    width = tokens.shape[1]
    win = min(group_len, group_len // 2 + rows)
    vmem, hbm = pl.BlockSpec(memory_space=pltpu.VMEM), pl.BlockSpec(memory_space=pl.ANY)
    sems = []
    for pieces in sets:
        sems += gather_sems(pieces)
    return pl.pallas_call(
        functools.partial(gather_kernel, sets, rows, win),
        in_specs=[vmem] * 10,
        out_specs=[vmem, vmem, hbm, hbm, hbm, hbm, vmem, vmem, vmem, vmem],
        out_shape=[
            *gathered([keys, qkv, proj, gate, head]),
            jax.ShapeDtypeStruct((8 * query.shape[0], KEYS), BF),
            jax.ShapeDtypeStruct((group_len, 3 * width), BF),
            jax.ShapeDtypeStruct((rows, width), F32),
            jax.ShapeDtypeStruct((rows, LANES), F32),
            *gathered([gains]),
        ],
        scratch_shapes=[
            pltpu.VMEM((group_len, width), BF),
            pltpu.VMEM((1, width), F32),
            pltpu.VMEM((group_len, width), BF),
            pltpu.VMEM((query.shape[0], KEYS), BF),
            *sems,
        ],
        compiler_params=pltpu.CompilerParams(
            collective_id=3, has_side_effects=True, vmem_limit_bytes=56 * 1024 * 1024
        ),
        name="gather_weights",
    )(keys, qkv, proj, gate, head, tokens, gains, query, seg_col, seg_row)


WIDTH = HEADS * HDIM
KEYS = MHEADS * 2 * NK
QUERIES = MHEADS * 2 * HALF
EARLY = (WIDTH,) * 6 + (KEYS,)
EARLY_PRODUCTS = (
    (0, 3 * WIDTH, WIDTH, 0),
    (WIDTH, 4 * WIDTH, WIDTH, WIDTH),
    (2 * WIDTH, 5 * WIDTH, WIDTH, 2 * WIDTH),
    (WIDTH, 6 * WIDTH, KEYS, 3 * WIDTH),
)
E_OUT, E_GATE, E_PROJ, E_HALF = 0, WIDTH, 2 * WIDTH, 3 * WIDTH
E_ALL = E_HALF + KEYS
LATE = (WIDTH, 3 * WIDTH)
LATE_PRODUCTS = ((0, WIDTH, 3 * WIDTH, 0),)
L_GAIN = 3 * WIDTH
L_ALL = L_GAIN + LANES


def share_factors(moves, local_sem, send, recv):
    g, _, _, _, sibling = places()
    copies = []
    for i, (src, dst, at, columns) in enumerate(moves):
        count = src.shape[0]
        where = pl.ds(at, columns)
        far = push(
            src, dst.at[pl.ds(count, count), where], send.at[5, i], recv.at[5, i], (g, sibling)
        )
        near = pltpu.make_async_copy(src, dst.at[pl.ds(0, count), where], local_sem.at[i])
        near.start()
        copies.append((near, far))
    return copies


def factor_moves(refs, widths, fact):
    moves, at = [], 0
    for ref, columns in zip(refs, widths, strict=True):
        moves.append((ref, fact, at, columns))
        at += columns
    return moves


def store_blocks(held, k, value, at):
    for i in range(4):
        held[k, i, :, at : at + value.shape[1]] = value[i * 32 : (i + 1) * 32].astype(BF)


def block_of(k):
    m = lax.axis_index("mem")
    return (m // 2 + 3 - k) % 4 * 2 + m % 2


def products_of(k, fact, held, products):
    block = block_of(k)
    for left, right, count, at in products:
        lhs = fact[:, pl.ds(pl.multiple_of(left + block * LANES, LANES), LANES)]
        for j in range(0, count, WIDTH):
            store_blocks(held, k, dot(lhs, fact[:, right + j : right + j + WIDTH], TN), at + j)


def spread_quarters(total, quarter, kind, send, recv):
    g, m, across, along, _ = places()
    quarter[g] = total.astype(BF)
    half = quarter.shape[1] // 2
    to_x, to_y = (across, m), (along, m)
    low, high = pl.ds(0, half), pl.ds(half, half)

    def go(i, block, peer):
        return push(block, block, send.at[kind, i], recv.at[kind, i], peer)

    a = go(0, quarter.at[g], to_x)
    b = go(1, quarter.at[g], to_y)
    a.wait_recv()
    c = go(2, quarter.at[across, low], to_y)
    b.wait_recv()
    d = go(3, quarter.at[along, high], to_x)
    c.wait_recv()
    d.wait_recv()
    for copy in (a, b, c, d):
        copy.wait_send()


def late_kernel(
    first_ref,
    rows_ref,
    gain_ref,
    half_ref,
    query_ref,
    out_ref,
    keys_ref,
    fact,
    gains,
    wide,
    held,
    x1,
    y1,
    x2,
    y2,
    zin,
    quarter,
    tables,
    arrived,
    spread,
    local_sem,
    send,
    recv,
):
    g, m, _, _, _ = places()
    core, z = m % 2, m // 2
    enter(plane_peers())
    moves = factor_moves((first_ref, rows_ref), LATE, fact)
    moves.append((gain_ref, gains, 0, WIDTH))
    moves += factor_moves((half_ref, query_ref), (KEYS, QUERIES), wide)
    copies = share_factors(moves, local_sem, send, recv)
    first, corner, plane, last = plane_tasks(held, x1, y1, x2, y2, zin, send, recv)
    for near, far in copies[:3]:
        near.wait()
        far.wait_recv()
    row = iota((32, LANES), 0) % 16
    column = iota((32, LANES), 1)
    select = ((row < 4) & (row // 2 == column)).astype(F32).astype(BF)

    def table(d):
        block = (z + d) % 4 * 2 + core
        lhs = wide[:, pl.ds(pl.multiple_of(block * NK, LANES), NK)]
        at = KEYS + block * HALF + g * (HALF // 4)
        return dot(lhs, wide[:, pl.ds(pl.multiple_of(at, LANES), HALF // 4)], TN)

    def line(k):
        return pltpu.make_async_remote_copy(
            src_ref=tables.at[k],
            dst_ref=arrived.at[k],
            send_sem=send.at[7, k],
            recv_sem=recv.at[7, k],
            device_id=(g, (m + 2 * (k + 1)) % 8),
            device_id_type=MESH,
        )

    def ready(k, _):
        products_of(k, fact, held, LATE_PRODUCTS)
        lhs = gains[:, pl.ds(pl.multiple_of(block_of(k) * LANES, LANES), LANES)]
        store_blocks(held, k, dot(lhs, select, TN), L_GAIN)
        first(k)
        return 0

    lax.fori_loop(0, 4, ready, 0)
    for near, far in copies[3:]:
        near.wait()
        far.wait_recv()

    def send_table(k, _):
        tables[k] = table(k + 1).astype(BF)
        line(k).start()
        return 0

    lax.fori_loop(0, 3, send_table, 0)
    keys = table(0)
    for k in range(4):
        corner(k)
    for k in range(3):
        plane(k)
    for k in range(3):
        line(k).wait_recv()
        keys = keys + arrived[k].astype(F32)
        line(k).wait_send()
    spread_quarters(keys, spread, 8, send, recv)
    for i in range(4):
        keys_ref[:, i * (HALF // 4) : (i + 1) * (HALF // 4)] = spread[i].astype(F32)
    spread_quarters(last(), quarter, 6, send, recv)
    for _, far in copies:
        far.wait_send()
    out_ref[...] = quarter[...]


def reduce_late(first, qkv_rows, gains, half, query):
    rows = first.shape[0]
    vmem = pl.BlockSpec(memory_space=pltpu.VMEM)
    sums, keys = pl.pallas_call(
        late_kernel,
        in_specs=[pl.BlockSpec(memory_space=pl.ANY)] * 5,
        out_specs=[vmem, vmem],
        out_shape=[
            jax.ShapeDtypeStruct((4, 32, L_ALL), BF),
            jax.ShapeDtypeStruct((NK, HALF), F32),
        ],
        scratch_shapes=[
            pltpu.VMEM((2 * rows, sum(LATE)), BF),
            pltpu.VMEM((32, WIDTH), BF),
            pltpu.VMEM((2 * rows, KEYS + QUERIES), BF),
            pltpu.VMEM((4, 4, 32, L_ALL), BF),
            *plane_scratch(32, L_ALL),
            pltpu.VMEM((4, 32, L_ALL), BF),
            pltpu.VMEM((3, NK, HALF // 4), BF),
            pltpu.VMEM((3, NK, HALF // 4), BF),
            pltpu.VMEM((4, NK, HALF // 4), BF),
            pltpu.SemaphoreType.DMA((5,)),
            pltpu.SemaphoreType.DMA((9, 5)),
            pltpu.SemaphoreType.DMA((9, 5)),
        ],
        compiler_params=pltpu.CompilerParams(
            collective_id=2, has_side_effects=True, vmem_limit_bytes=48 * 1024 * 1024
        ),
        name="reduce_late",
    )(first, qkv_rows, gains, half, query)
    return sums.reshape(4 * 32, L_ALL), keys


def back_kernel(rows, win, *refs):
    fact_refs, refs = refs[: len(EARLY)], refs[len(EARLY) :]
    shared_ref, qkv_ref, proj_ref, segc_ref, segr_ref, out_ref, rows_ref = refs[:7]
    fact, held, x1, y1, x2, y2, zin, quarter, shared, douts, stats = refs[7:18]
    local_sem, send, recv = refs[18:]
    g, m, _, _, sibling = places()
    to_s = (g, sibling)
    pairs = WIDTH // LANES
    enter(plane_peers())

    def part(owner):
        return shared.at[pl.ds(pl.multiple_of(owner * rows, LANES), rows)]

    def move(index, src, owner, peer):
        return pltpu.make_async_remote_copy(
            src_ref=src,
            dst_ref=part(owner),
            send_sem=send.at[7, index],
            recv_sem=recv.at[7, index],
            device_id=peer,
            device_id_type=MESH,
        )

    def origin(d):
        return (m + 8 - 2 * d) % 8

    lines = [move(d, shared_ref, m, (g, (m + 2 * d) % 8)) for d in (1, 2, 3)]
    side = move(0, shared_ref, m, to_s)
    forward = [move(3 + d, part(origin(d)), origin(d), to_s) for d in (1, 2, 3)]
    own = pltpu.make_async_copy(shared_ref, part(m), local_sem.at[len(EARLY)])
    for copy in lines:
        copy.start()
    side.start()
    own.start()
    copies = share_factors(factor_moves(fact_refs, EARLY, fact), local_sem, send, recv)
    first, corner, plane, last = plane_tasks(held, x1, y1, x2, y2, zin, send, recv)
    for near, far in copies:
        near.wait()
        far.wait_recv()

    def ready(k, _):
        products_of(k, fact, held, EARLY_PRODUCTS)
        first(k)
        return 0

    lax.fori_loop(0, 4, ready, 0)
    corner(0)
    for copy, after in zip(lines, forward, strict=True):
        copy.wait_recv()
        after.start()
    corner(1)
    own.wait()
    side.wait_recv()
    for copy in forward:
        copy.wait_recv()
    corner(2)
    def project(i, _):
        where = pl.ds(pl.multiple_of(i * 2 * rows, 2 * rows), 2 * rows)
        douts[where, :] = dot(shared[where, :WIDTH], proj_ref[...], NT).astype(BF)
        stats[where, :] = shared[where, WIDTH : WIDTH + 2 * HEADS].astype(F32) + shared[
            where, WIDTH + 2 * HEADS : WIDTH + 4 * HEADS
        ].astype(F32)
        return 0

    lax.fori_loop(0, shared.shape[0] // (2 * rows), project, 0)
    corner(3)

    def load_of(pair):
        def load(which, where):
            ref, base = (douts, 0) if which == 3 else (qkv_ref, which * pairs)
            return ref[where, pl.ds(pl.multiple_of((base + pair) * LANES, LANES), LANES)]

        return load

    def attend(pair, _):
        grads = attn_bwd_pair(
            rows, win, pair, m, shared.shape[0], load_of(pair), stats, segc_ref, segr_ref
        )
        for i, value in enumerate(grads):
            column = pl.multiple_of((i * pairs + pair) * LANES, LANES)
            rows_ref[:, pl.ds(column, LANES)] = value
        for k in range(3):
            pl.when(pair == 2 * k + 1)(functools.partial(plane, k))
        return 0

    lax.fori_loop(0, pairs, attend, 0)
    spread_quarters(last(), quarter, 6, send, recv)
    for _, far in copies:
        far.wait_send()
    for copy in [*lines, side, *forward]:
        copy.wait_send()
    out_ref[...] = quarter[...]


def reduce_back(factors, shared, qkv, proj, seg_col, seg_row):
    rows = factors[0].shape[0]
    group_len = qkv.shape[0]
    win = min(group_len, group_len // 2 + rows)
    hbm = pl.BlockSpec(memory_space=pl.ANY)
    vmem = pl.BlockSpec(memory_space=pltpu.VMEM)
    count = len(EARLY)
    sums, qkv_rows = pl.pallas_call(
        functools.partial(back_kernel, rows, win),
        in_specs=[hbm] * (count + 1) + [vmem] * 4,
        out_specs=[vmem, vmem],
        out_shape=[
            jax.ShapeDtypeStruct((4, 32, E_ALL), BF),
            jax.ShapeDtypeStruct((rows, 3 * WIDTH), BF),
        ],
        scratch_shapes=[
            pltpu.VMEM((2 * rows, sum(EARLY)), BF),
            pltpu.VMEM((4, 4, 32, E_ALL), BF),
            *plane_scratch(32, E_ALL),
            pltpu.VMEM((4, 32, E_ALL), BF),
            pltpu.VMEM((group_len, WIDTH + LANES), BF),
            pltpu.VMEM((group_len, WIDTH), BF),
            pltpu.VMEM((group_len, 2 * HEADS), F32),
            pltpu.SemaphoreType.DMA((count + 1,)),
            pltpu.SemaphoreType.DMA((8, count)),
            pltpu.SemaphoreType.DMA((8, count)),
        ],
        compiler_params=pltpu.CompilerParams(
            collective_id=4, has_side_effects=True, vmem_limit_bytes=56 * 1024 * 1024
        ),
        name="reduce_back",
    )(*factors, shared, qkv, proj, seg_col, seg_row)
    return sums.reshape(4 * 32, E_ALL), qkv_rows


def finish_kernel(
    early_ref, late_ref, keys_ref, out, gate, proj, qkv, query, gains
):
    for ref, first in ((out, E_OUT), (gate, E_GATE), (proj, E_PROJ)):
        ref[...] = early_ref[:, first : first + WIDTH].astype(F32)
    qkv[...] = late_ref[:, : 3 * WIDTH].astype(F32)
    for c in range(MHEADS * 2):
        table = keys_ref[c * NK : (c + 1) * NK, :]
        query[:, c * HALF : (c + 1) * HALF] = dot(
            early_ref[:, E_HALF + c * NK : E_HALF + (c + 1) * NK], table
        )
    gains[...] = late_ref[:, L_GAIN:].astype(F32).T[:8]


def finish(early, late, keys):
    rows = early.shape[0]
    shapes = [(rows, WIDTH)] * 3 + [(rows, 3 * WIDTH), (rows, QUERIES)]
    shapes.append((8, LANES))
    return pl.pallas_call(
        finish_kernel,
        out_shape=[jax.ShapeDtypeStruct(shape, F32) for shape in shapes],
        compiler_params=pltpu.CompilerParams(vmem_limit_bytes=40 * 1024 * 1024),
        name="finish",
    )(early, late, keys)


def rms_scale(values):
    return lax.rsqrt(jnp.mean(values * values, axis=-1, keepdims=True) + EPS)


def rms_back(values, scale, gain, grad):
    scaled = grad * gain
    inner = jnp.mean(values * scaled, axis=-1, keepdims=True)
    gain_grad = jnp.sum(grad * values * scale, axis=0)
    return scale * scaled - values * (scale * scale * scale * inner), gain_grad


def per_device(
    tokens,
    segment_ids,
    picks,
    attn_gain,
    qkv_weight,
    attn_proj,
    mem_gain,
    query_weight,
    half_keys,
    memory_values,
    gate_weight,
    out_weight,
    out_cotangent,
):
    rows, width = tokens.shape
    owners = lax.axis_size("grp") * lax.axis_size("mem")
    local_rows = memory_values.shape[0]
    total_picks = rows * MHEADS * TOPK
    flat_bits = (total_picks - 1).bit_length()
    capacity = 2 * total_picks // owners
    group_len = segment_ids.shape[0]
    linked = (lax.axis_size("grp"), lax.axis_size("mem"), rows) == (4, 8, LANES)
    position = lax.axis_index("mem").astype(jnp.int32)
    pos = position.reshape(1)

    def gather(x, axes="mem"):
        return lax.all_gather(x, axes, axis=0, tiled=True)

    flat_picks = picks.reshape(rows, MHEADS * TOPK)
    if linked:
        gain_block = jnp.concatenate(
            [attn_gain[None], mem_gain[None], jnp.zeros((14, LANES), BF)]
        )
    else:
        gains = lax.all_gather(jnp.stack([attn_gain, mem_gain]), "mem", axis=1, tiled=True)
        tokens_all = gather(tokens)
        qkv_full = gather(qkv_weight)
        proj_full = gather(attn_proj)
        query_full = gather(query_weight)
        keys_full = gather(half_keys)
        gate_full = gather(gate_weight)
        output_full = gather(out_weight)
        gains = gains.astype(F32)
        gain_one, gain_two = gains[0:1], gains[1:2]
    seg_row, seg_col = segment_ids.reshape(1, group_len), segment_ids.reshape(group_len, 1)

    requests = route(picks, owners, local_rows, capacity, flat_bits)
    arrived = lax.all_to_all(requests, ALL, split_axis=0, concat_axis=0, tiled=True)

    if linked:
        (
            keys_full,
            qkv_full,
            proj_full,
            gate_full,
            output_full,
            folded_full,
            qkv_all,
            attn_sum,
            lse,
            gains,
        ) = gather_weights(
            half_keys,
            qkv_weight,
            attn_proj,
            gate_weight,
            out_weight,
            tokens,
            gain_block,
            query_weight,
            seg_col,
            seg_row,
            rows,
        )
        gains = gains.reshape(8, 16, LANES)[:, :2].transpose(1, 0, 2).reshape(2, width)
        gains = gains.astype(F32)
        gain_one, gain_two = gains[0:1], gains[1:2]
    else:
        inputs_all = tokens_all.astype(F32)
        first_all = (inputs_all * rms_scale(inputs_all) * gain_one).astype(BF)
        qkv_all = dot(first_all, qkv_full).astype(BF)
        attn_sum, lse = attn_fwd(pos, qkv_all, seg_row, seg_col, rows)
    attended = attn_sum.astype(BF)
    inputs = tokens.astype(F32)
    residual = inputs + dot(attended, proj_full)
    scale_two = rms_scale(residual)
    second = (residual * scale_two * gain_two).astype(BF)
    gate_pre = dot(second, gate_full)
    mixed_grad = dot(out_cotangent, output_full, NT)
    sig = jax.nn.sigmoid(gate_pre)
    gate_act = gate_pre * sig
    memory_grad = (mixed_grad * gate_act).astype(BF)
    if linked:
        half_scores = dot(second, folded_full)
    else:
        mem_query = dot(second, query_full).astype(BF)
        key_table = keys_full.reshape(MHEADS * 2, NK, HALF)
        half_scores = jnp.einsum(
            "tcf,cnf->tcn",
            mem_query.reshape(rows, MHEADS * 2, HALF),
            key_table,
            preferred_element_type=F32,
        ).reshape(rows, KEYS)
    pick_weights, weights_low = pick_fwd(half_scores, flat_picks)

    payload = jnp.concatenate([memory_grad, weights_low], axis=1)
    if linked:
        back, values_grad = memory_call(payload, arrived, memory_values, flat_bits)
    else:
        sent = gather(payload, ALL)
        part, spread = owner_call(arrived, sent, memory_values, flat_bits)
        back = lax.psum_scatter(part, "grp", scatter_dimension=0, tiled=True)
        back = lax.psum_scatter(back, "mem", scatter_dimension=0, tiled=True)
        values_grad = jnp.einsum(
            "hkl,kd->hld", spread, sent[:, :width], preferred_element_type=F32
        )
    values_grad = values_grad.reshape(local_rows, width)

    memory_out = back[:, :width].astype(F32)
    mixed = (memory_out * gate_act).astype(BF)
    block_out = (residual + dot(mixed, output_full)).astype(BF)
    gate_grad = (mixed_grad * memory_out * (sig * (1.0 + gate_pre * (1.0 - sig)))).astype(BF)
    half_grad, values_grad = pick_bwd(
        pick_weights, back.astype(F32), flat_picks, values_grad
    )
    if linked:
        second_grad = dot(gate_grad, gate_full, NT) + dot(half_grad, folded_full, NT)
    else:
        half_cube = half_grad.reshape(rows, MHEADS * 2, NK)
        query_grad = (
            jnp.einsum("tcn,cnf->tcf", half_cube, key_table, preferred_element_type=F32)
            .astype(BF)
            .reshape(rows, QUERIES)
        )
        second_grad = dot(gate_grad, gate_full, NT) + dot(query_grad, query_full, NT)
    resid_from_norm, gain_two_grad = rms_back(residual, scale_two, gain_two, second_grad)
    resid_grad = out_cotangent.astype(F32) + resid_from_norm
    resid_low = resid_grad.astype(BF)
    attn_grad = dot(resid_low, proj_full, NT).astype(BF)
    heads = (iota((width, HEADS), 0) // HDIM == iota((width, HEADS), 1)).astype(F32)
    delta = jnp.dot(
        attn_grad.astype(F32) * attn_sum,
        heads,
        precision=lax.Precision.HIGHEST,
        preferred_element_type=F32,
    )
    stats = jnp.concatenate([lse[:, :HEADS], delta], axis=1)
    stats_high = lax.reduce_precision(stats, 8, 7)
    stats_low = stats - stats_high
    shared = jnp.concatenate(
        [
            resid_low,
            stats_high.astype(BF),
            stats_low.astype(BF),
            jnp.zeros((rows, LANES - 4 * HEADS), BF),
        ],
        axis=1,
    )
    if linked:
        early = (
            mixed,
            second,
            attended,
            out_cotangent,
            gate_grad,
            resid_low,
            half_grad,
        )
        early, qkv_rows = reduce_back(early, shared, qkv_all, proj_full, seg_col, seg_row)
    else:
        shared = gather(shared)
        stats_all = shared[:, width : width + 2 * HEADS].astype(F32) + shared[
            :, width + 2 * HEADS : width + 4 * HEADS
        ].astype(F32)
        attn_grad_all = dot(shared[:, :width], proj_full, NT).astype(BF)
        qkv_rows = attn_bwd(pos, qkv_all, attn_grad_all, stats_all, seg_row, seg_col, rows)
    scale_one = rms_scale(inputs)
    first_low = (inputs * scale_one * gain_one).astype(BF)
    first_grad = dot(qkv_rows, qkv_full, NT)
    input_from_norm, gain_one_grad = rms_back(inputs, scale_one, gain_one, first_grad)
    tokens_grad = resid_grad + input_from_norm

    if linked:
        sums = jnp.stack([gain_one_grad, gain_two_grad])
        sums_high = lax.reduce_precision(sums, 8, 7)
        gain_rows = jnp.stack([sums_high, sums - sums_high], axis=1).reshape(4, width)
        gain_rows = jnp.concatenate([gain_rows.astype(BF), jnp.zeros((12, width), BF)])
        late, keys_share = reduce_late(
            first_low, qkv_rows, gain_rows, early[:, E_HALF:], query_weight
        )
        (
            out_share,
            gate_share,
            proj_share,
            qkv_share,
            query_share,
            gain_sums,
        ) = finish(early, late, keys_full)
    else:
        keys_grad = jnp.einsum(
            "tcn,tcf->cnf",
            half_cube,
            mem_query.reshape(rows, MHEADS * 2, HALF),
            preferred_element_type=F32,
        ).reshape(KEYS, HALF)
        partials = (
            dot(mixed, out_cotangent, TN),
            dot(second, gate_grad, TN),
            keys_grad,
            dot(second, query_grad, TN),
            dot(attended, resid_low, TN),
            dot(first_low, qkv_rows, TN),
        )
        shares = [
            lax.psum_scatter(x.astype(BF), "mem", scatter_dimension=0, tiled=True)
            for x in partials
        ]
        shares = lax.psum(tuple(shares), "grp")
        gain_sums = lax.psum(jnp.stack([gain_one_grad, gain_two_grad]), ALL)
        gain_sums = lax.dynamic_slice_in_dim(
            gain_sums, position * attn_gain.shape[0], attn_gain.shape[0], axis=1
        )
        out_share, gate_share, keys_share, query_share, proj_share, qkv_share = (
            x.astype(F32) for x in shares
        )
    return (
        block_out,
        tokens_grad,
        gain_sums[0],
        qkv_share,
        proj_share,
        gain_sums[1],
        query_share,
        keys_share,
        values_grad,
        gate_share,
        out_share,
    )


def solution(mesh):
    placed = (
        P(ALL, None),
        P("grp"),
        P(ALL, None, None),
        P("mem"),
        P("mem", None),
        P("mem", None),
        P("mem"),
        P("mem", None),
        P("mem", None),
        P(ALL, None),
        P("mem", None),
        P("mem", None),
        P(ALL, None),
    )
    return jax.shard_map(
        per_device,
        mesh=mesh,
        in_specs=placed,
        out_specs=(
            P(ALL, None),
            P(ALL, None),
            P("mem"),
            P("mem", None),
            P("mem", None),
            P("mem"),
            P("mem", None),
            P("mem", None),
            P(ALL, None),
            P("mem", None),
            P("mem", None),
        ),
        check_vma=False,
    )
```
